32 devices in a mesh: tile: 8 (over z, y), attr: 4 (over x, core).
Axes of the slice: x: 2, y: 2, z: 4, core: 2. Of those that a mesh axis runs over, the one named last changes fastest.
Arguments:
- geometry: float32 [6, 65536], P(None, 'tile'), as said below
- sh_coeffs: float32 [48, 65536], P('attr', 'tile'), may hold values from -3 to 3
- view_angles: float32 [2, 65536], P(None, 'tile'), may hold values from -3.140625 to 3.140625
- visible: int32 [64, 16], P(('tile', 'attr')), may hold values from 0 to 255, as said below
- counts: int32 [64], P(('tile', 'attr')), may hold values from 1 to 16, as said below
- order: int32 [64, 16], P(('tile', 'attr')), may hold values from 0 to 15, each once within a row
- image_cot: float32 [64, 3, 256], P(('tile', 'attr')), may hold values from -6 to 6
Outputs:
- picture: float32 [64, 3, 256], P(('tile', 'attr'))
- grad_geometry: float32 [6, 65536], P(None, 'tile')
- grad_sh: float32 [48, 65536], P('attr', 'tile')
The draws below stay inside these ranges and needn't reach their ends.
Inputs may be any that keep to these rules, and one draw needn't show every extreme that they name: `visible`: each tile lists 16 distinct block ids. Tile i and tile i + 1 of one device list the same blocks. The tiles of one device name at most 2 distinct blocks of one owner (id // 32), and exactly that many of some owner. The first counts[t] entries of tile t's depth order are live. `order`: A permutation of the list positions of the tile. `geometry`: row 0 and 1 between -4 and 20, rows 2 and 3 the logarithms of 0.1 * 16 to 0.25 * 16, row 4 an angle, row 5 within 5 below log(100 / 4096).
All inputs are finite; a program needn't handle non-finite values.
Results may differ from the reference program's by a relative error of at most 0.0003.
Values sent between devices are 32-bit elements; how exact they have to be, the bound alone decides.
A program may use at most 64 MiB of HBM per device.

```python
import math
import jax
import jax.numpy as jnp
from jax import lax

TILES_DEV = 2
VIS = 16
BLK_DEV = 32
BLOCK = 256
SIDE = 16
SH = 48
PIX = 256
TILES = 64
NBLK = 256
GAUSS = 65536
N_TILE = 8
N_ATTR = 4


def draw_visible(key, part):
    device_count = N_TILE * N_ATTR
    distinct = TILES_DEV * VIS // 2
    dev_keys = jax.random.split(jax.random.fold_in(key, 11), device_count)

    def one_device(dev_key):
        key_perm, key_base = jax.random.split(dev_key)
        owners_perm = jax.random.permutation(key_perm, N_TILE)
        base_local = jax.random.randint(key_base, (N_TILE,), 0, BLK_DEV)
        slot_index = jnp.arange(TILES_DEV * VIS) % distinct
        owner_id = owners_perm[slot_index % N_TILE]
        local_id = (base_local[owner_id] + slot_index // N_TILE) % BLK_DEV
        return (owner_id * BLK_DEV + local_id).reshape(TILES_DEV, VIS)
    return jax.vmap(one_device)(dev_keys).reshape(device_count * TILES_DEV, VIS).astype(jnp.int32)


def draw_counts(key, part):
    key_live, key_full = jax.random.split(jax.random.fold_in(key, 23))
    live_counts = jax.random.randint(key_live, (TILES,), 1, VIS + 1)
    full_tile = jax.random.randint(key_full, (), 0, TILES)
    return live_counts.at[full_tile].set(VIS).astype(jnp.int32)


def draw_geometry(key, part):
    row_keys = jax.random.split(jax.random.fold_in(key, 37), 6)
    count_all = GAUSS
    upper = math.log(100.0 / (VIS * BLOCK))
    centre_x = jax.random.uniform(row_keys[0], (count_all,), jnp.float32, -0.25 * SIDE, 1.25 * SIDE)
    centre_y = jax.random.uniform(row_keys[1], (count_all,), jnp.float32, -0.25 * SIDE, 1.25 * SIDE)
    scale_one = jax.random.uniform(row_keys[2], (count_all,), jnp.float32, math.log(0.1 * SIDE), math.log(0.25 * SIDE))
    scale_two = jax.random.uniform(row_keys[3], (count_all,), jnp.float32, math.log(0.1 * SIDE), math.log(0.25 * SIDE))
    rotation = jax.random.uniform(row_keys[4], (count_all,), jnp.float32, -math.pi, math.pi)
    logits = jax.random.uniform(row_keys[5], (count_all,), jnp.float32, upper - 5.0, upper)
    return jnp.stack([centre_x, centre_y, scale_one, scale_two, rotation, logits], 0).astype(jnp.float32)


def steps_of(own_key, extent, shards, low, top_value):
    level = 1.0
    for dim, blocks in shards:
        heights = jax.random.uniform(jax.random.fold_in(jax.random.fold_in(own_key, 6), dim), (blocks,), jnp.float32, low / len(shards), top_value / len(shards))
        level = level * jnp.repeat(jnp.exp(heights), extent[dim] // blocks).reshape((-1,) + (1,) * (len(extent) - 1 - dim))
    return level


def centred(own_key, shape, width, reach, cuts=(), kind=jnp.bfloat16):
    values = width * jax.random.normal(own_key, shape, jnp.float32)
    if cuts:
        values = values * steps_of(own_key, shape, cuts, -0.22, 0.18)
    return jnp.clip(values, -reach, reach).astype(kind)


def setup_inputs(seed: int = 0) -> dict:
    keys = jax.random.split(jax.random.key(seed), 8)
    geometry = draw_geometry(jax.random.fold_in(keys[7], 71), 0)
    sh_coeffs = centred(keys[1], (SH, GAUSS), 0.5, 3.0, ((0, 4), (1, 8)), jnp.float32)
    view_angles = jnp.clip(jax.random.uniform(keys[2], (2, GAUSS), jnp.float32, -3.140625, 3.140625), -3.140625, 3.140625)
    visible = draw_visible(jax.random.fold_in(keys[7], 71), 0)
    counts = draw_counts(jax.random.fold_in(keys[7], 71), 0)
    order = jax.vmap(lambda own: jax.random.permutation(own, VIS))(jax.random.split(keys[5], TILES)).reshape((TILES, VIS)).astype(jnp.int32)
    image_cot = centred(keys[6], (TILES, 3, PIX), 1.0, 6.0, ((0, 32),), jnp.float32)
    return dict(geometry=geometry, sh_coeffs=sh_coeffs, view_angles=view_angles, visible=visible, counts=counts, order=order, image_cot=image_cot)


precise = lax.Precision.HIGHEST
band_zero = 0.28209479177387814
band_one = 0.4886025119029199
band_two = (1.0925484305920792, -1.0925484305920792, 0.31539156525252005, -1.0925484305920792, 0.5462742152960396)
band_three = (-0.5900435899266435, 2.890611442640554, -0.4570457994644658, 0.3731763325901154, -0.4570457994644658, 1.445305721320277, -0.5900435899266435)

def sh_basis(view_angles):
    azimuth = view_angles[0]
    elevation = view_angles[1]
    dir_x = jnp.cos(azimuth) * jnp.cos(elevation)
    dir_y = jnp.sin(azimuth) * jnp.cos(elevation)
    dir_z = jnp.sin(elevation)
    sq_x = dir_x * dir_x
    sq_y = dir_y * dir_y
    sq_z = dir_z * dir_z
    basis_rows = [band_zero * jnp.ones_like(dir_x), -band_one * dir_y, band_one * dir_z, -band_one * dir_x, band_two[0] * dir_x * dir_y, band_two[1] * dir_y * dir_z, band_two[2] * (2.0 * sq_z - sq_x - sq_y), band_two[3] * dir_x * dir_z, band_two[4] * (sq_x - sq_y), band_three[0] * dir_y * (3.0 * sq_x - sq_y), band_three[1] * dir_x * dir_y * dir_z, band_three[2] * dir_y * (4.0 * sq_z - sq_x - sq_y), band_three[3] * dir_z * (2.0 * sq_z - 3.0 * sq_x - 3.0 * sq_y), band_three[4] * dir_x * (4.0 * sq_z - sq_x - sq_y), band_three[5] * dir_z * (sq_x - sq_y), band_three[6] * dir_x * (sq_x - 3.0 * sq_y)]
    return jnp.stack(basis_rows, 0)

def blend_tile(held_rows, order_row, live_count):
    ordered = jnp.take(held_rows, order_row, axis=0)
    depth_rank = jnp.arange(ordered.shape[0]).astype(jnp.int32)
    live_mask = (depth_rank < live_count).astype(jnp.float32)
    pixels = jnp.arange(SIDE * SIDE).astype(jnp.int32)
    pixel_x = (pixels % SIDE).astype(jnp.float32) + 0.5
    pixel_y = (pixels // SIDE).astype(jnp.float32) + 0.5
    delta_x = pixel_x - ordered[:, 0, :, None]
    delta_y = pixel_y - ordered[:, 1, :, None]
    cosine = jnp.cos(ordered[:, 4, :, None])
    sine_rot = jnp.sin(ordered[:, 4, :, None])
    along_axis = (delta_x * cosine + delta_y * sine_rot) * jnp.exp(-ordered[:, 2, :, None])
    across = (delta_y * cosine - delta_x * sine_rot) * jnp.exp(-ordered[:, 3, :, None])
    opacity = jax.nn.sigmoid(ordered[:, 5, :, None]) * live_mask[:, None, None]
    alphas = opacity * jnp.exp(-0.5 * (along_axis * along_axis + across * across))
    log_keep = jnp.log1p(-alphas)
    inside = jnp.cumsum(log_keep, axis=1) - log_keep
    block_sums = lax.optimization_barrier(jnp.sum(log_keep, axis=1))
    earlier = jnp.cumsum(block_sums, axis=0) - block_sums
    weight = alphas * jnp.exp(inside + earlier[:, None, :])
    return jnp.einsum('kgp,kcg->cp', weight, ordered[:, 6:9, :], precision=precise)

def colours_of(view_angles, coeff_in):
    basis = sh_basis(view_angles)
    return 0.5 + jnp.einsum('kg,kcg->cg', basis, coeff_in.reshape(basis.shape[0], 3, basis.shape[1]), precision=precise)

def reference(geometry, sh_coeffs, view_angles, visible, counts, order, image_cot):

    def render(geometry_in, coeff_in):
        colour = colours_of(view_angles, coeff_in)
        lookup_table = jnp.concatenate([geometry_in, colour], 0).reshape(9, NBLK, BLOCK).transpose(1, 0, 2)

        def one_tile(packed):
            block_list, order_row, live_count = packed
            return blend_tile(jnp.take(lookup_table, block_list, axis=0), order_row, live_count)
        return lax.map(jax.checkpoint(one_tile), (visible, order, counts))
    picture, pullback = jax.vjp(render, geometry, sh_coeffs)
    grad_geometry, grad_sh = pullback(image_cot)
    return (picture, grad_geometry, grad_sh)
```

```python
import functools
import jax
import jax.numpy as jnp
from jax import lax
from jax.experimental import pallas as pl
from jax.experimental.pallas import tpu as pltpu
from jax.sharding import PartitionSpec as P

BLOCK = 256
SIDE = 16
PIX = SIDE * SIDE
MID = 0.5 * SIDE
LOG2E = 1.4426950408889634
LN2 = 0.6931471805599453


band_zero = 0.28209479177387814
band_one = 0.4886025119029199
band_two = (
    1.0925484305920792,
    -1.0925484305920792,
    0.31539156525252005,
    -1.0925484305920792,
    0.5462742152960396,
)
band_three = (
    -0.5900435899266435,
    2.890611442640554,
    -0.4570457994644658,
    0.3731763325901154,
    -0.4570457994644658,
    1.445305721320277,
    -0.5900435899266435,
)


def sh_basis(view_angles):
    azimuth = view_angles[0]
    elevation = view_angles[1]
    dir_x = jnp.cos(azimuth) * jnp.cos(elevation)
    dir_y = jnp.sin(azimuth) * jnp.cos(elevation)
    dir_z = jnp.sin(elevation)
    sq_x = dir_x * dir_x
    sq_y = dir_y * dir_y
    sq_z = dir_z * dir_z
    basis_rows = [
        band_zero * jnp.ones_like(dir_x),
        -band_one * dir_y,
        band_one * dir_z,
        -band_one * dir_x,
        band_two[0] * dir_x * dir_y,
        band_two[1] * dir_y * dir_z,
        band_two[2] * (2.0 * sq_z - sq_x - sq_y),
        band_two[3] * dir_x * dir_z,
        band_two[4] * (sq_x - sq_y),
        band_three[0] * dir_y * (3.0 * sq_x - sq_y),
        band_three[1] * dir_x * dir_y * dir_z,
        band_three[2] * dir_y * (4.0 * sq_z - sq_x - sq_y),
        band_three[3] * dir_z * (2.0 * sq_z - 3.0 * sq_x - 3.0 * sq_y),
        band_three[4] * dir_x * (4.0 * sq_z - sq_x - sq_y),
        band_three[5] * dir_z * (sq_x - sq_y),
        band_three[6] * dir_x * (sq_x - 3.0 * sq_y),
    ]
    return basis_rows


def split2(x):
    high = x.astype(jnp.bfloat16)
    low = (x - high.astype(jnp.float32)).astype(jnp.bfloat16)
    return jnp.concatenate([high, low], axis=1)


def dot(a, b):
    return jnp.dot(a, b, preferred_element_type=jnp.float32)


def blend_kernel(tiles, seq_ref, counts_ref, held_ref, cot_rows_ref, cot_cols_ref, pic_ref, grad_ref, part_ref, ratio_ref):
    f32, bf16 = jnp.float32, jnp.bfloat16
    row = lax.broadcasted_iota(jnp.int32, (2 * BLOCK, BLOCK), 0)
    row = jnp.where(row >= BLOCK, row - BLOCK, row)
    col = lax.broadcasted_iota(jnp.int32, (2 * BLOCK, BLOCK), 1)
    before = jnp.where(row < col, -1.0, 0.0).astype(bf16)
    upto = jnp.where(row <= col, 1.0, 0.0).astype(bf16)

    def monomials(shape, dim, width):
        pixel = lax.broadcasted_iota(jnp.int32, shape, dim)
        kind = lax.broadcasted_iota(jnp.int32, shape, 1 - dim) & (width - 1)
        x = (pixel & (SIDE - 1)).astype(f32) + (0.5 - MID)
        y = (pixel // SIDE).astype(f32) + (0.5 - MID)
        out = jnp.where(kind == 0, 1.0, 0.0)
        for k, value in ((1, x), (2, y), (3, x * x), (4, x * y), (5, y * y)):
            out = jnp.where(kind == k, value, out)
        return out.astype(bf16)

    mono_cols = monomials((PIX, 48), 0, 16)
    mono_rows = monomials((8, PIX), 1, 8)
    cot_lhs, cot_rows = [], []
    for t in range(tiles):
        g = cot_cols_ref[t]
        high = g.astype(bf16).astype(f32)
        lane = lax.broadcasted_iota(jnp.int32, g.shape, 1)
        cot_lhs.append(jnp.where(lane < 48, high, g - high).astype(bf16))
        g = cot_rows_ref[t]
        high = g.astype(bf16).astype(f32)
        cot_rows.append(jnp.concatenate([high, g - high], axis=0).astype(bf16))

    grad_ref[...] = jnp.zeros_like(grad_ref)
    lives = [counts_ref[t] for t in range(tiles)]
    longest = functools.reduce(jnp.maximum, lives)

    lhs = []
    for t in range(tiles):
        wide = jnp.concatenate([mono_cols.astype(f32), jnp.zeros((PIX, 48), f32)], axis=1)
        lhs.append(jnp.concatenate([wide.astype(bf16), cot_lhs[t]], axis=0))
    head = lax.broadcasted_iota(jnp.int32, (16, BLOCK), 0) == 0

    def forward(j, carry):
        keep_before, sum_before, pictures = carry
        alphas, values, losses, helds, spots = [], [], [], [], []
        for t in range(tiles):
            at = seq_ref[t, j]
            hidden = jnp.where(j < lives[t], 0.0, -16384.0)
            held = held_ref[at]
            parts = split3(jnp.where(head, held + hidden, held))
            rows = jnp.concatenate(parts, axis=0)
            both = dot(lhs[t], jnp.concatenate([rows, rows], axis=0))
            alpha = jnp.exp2(both[:PIX])
            alphas.append(alpha)
            values.append(both[PIX:])
            losses.append(jnp.log(1.0 - alpha) * -LOG2E)
            helds.append(jnp.concatenate(parts[:2], axis=0))
            spots.append(at)
        loss = jnp.concatenate(losses, axis=0)
        keep_in = dot(split2(loss), before) + keep_before
        keep_before = keep_in[:, BLOCK - 1 :] - loss[:, BLOCK - 1 :]
        alpha = jnp.concatenate(alphas, axis=0)
        weight = alpha * jnp.exp2(keep_in)
        value = weight * jnp.concatenate(values, axis=0)
        total = dot(split2(value), upto) + sum_before
        sum_before = total[:, BLOCK - 1 :]
        ratio = alpha * jnp.exp2(loss)
        part_ref[j] = value + ratio * total
        ratio_ref[j] = ratio
        w2 = split2(weight)
        shown = []
        for t in range(tiles):
            w_high, w_low = w2[t * PIX : (t + 1) * PIX, :BLOCK], w2[t * PIX : (t + 1) * PIX, BLOCK:]
            rows = lax.dot_general(helds[t], w_high, (((1,), (1,)), ((), ())), preferred_element_type=f32)
            rows = rows + lax.dot_general(helds[t], w_low, (((1,), (1,)), ((), ())), preferred_element_type=f32)
            shown.append(pictures[t] + rows[:16] + rows[16:])
            colour_grad = dot(cot_rows[t], w_high) + dot(cot_rows[t], w_low)
            grad_ref[spots[t], 0:8, :] += colour_grad[:8] + colour_grad[8:]
        return keep_before, sum_before, tuple(shown)

    zero = jnp.zeros((tiles * PIX, 1), f32)
    start = (zero, zero, tuple(jnp.zeros((16, PIX), f32) for _ in range(tiles)))
    _, ends, pictures = lax.fori_loop(0, longest, forward, start)
    for t in range(tiles):
        pic_ref[t] = pictures[t]

    def backward(j, _):
        for t in range(tiles):
            pixels = slice(t * PIX, (t + 1) * PIX)
            d2 = split2(part_ref[j, pixels] - ratio_ref[j, pixels] * ends[pixels])
            moments = dot(mono_rows, d2[:, :BLOCK]) + dot(mono_rows, d2[:, BLOCK:])
            grad_ref[seq_ref[t, j], 8:16, :] += moments
        return 0

    lax.fori_loop(0, longest, backward, 0)


def blend(seq, counts, held, image_cot):
    tiles = image_cot.shape[0]
    rows = held.shape[0]
    cot_rows = jnp.pad(image_cot, ((0, 0), (0, 5), (0, 0)))
    cot_cols = jnp.pad(jnp.swapaxes(image_cot, 1, 2), ((0, 0), (0, 0), (6, 7)))
    cot_cols = jnp.tile(cot_cols, (1, 1, 6))
    smem = pl.BlockSpec(memory_space=pltpu.SMEM)
    vmem = pl.BlockSpec(memory_space=pltpu.VMEM)
    picture, grads = pl.pallas_call(
        functools.partial(blend_kernel, tiles),
        name="blend",
        out_shape=(
            jax.ShapeDtypeStruct((tiles, 16, PIX), jnp.float32),
            jax.ShapeDtypeStruct((rows, 16, BLOCK), jnp.float32),
        ),
        in_specs=[smem, smem, vmem, vmem, vmem],
        out_specs=(vmem, vmem),
        scratch_shapes=[
            pltpu.VMEM((seq.shape[1], tiles * PIX, BLOCK), jnp.float32),
            pltpu.VMEM((seq.shape[1], tiles * PIX, BLOCK), jnp.float32),
        ],
        compiler_params=pltpu.CompilerParams(vmem_limit_bytes=28 * 1024 * 1024),
    )(seq, counts, held, cot_rows, cot_cols)
    return picture[:, 6:9], grads


def splat_terms(geometry):
    mx, my = geometry[0] - MID, geometry[1] - MID
    c, s = jnp.cos(geometry[4]), jnp.sin(geometry[4])
    e1, e2 = jnp.exp(-2.0 * geometry[2]), jnp.exp(-2.0 * geometry[3])
    cc, ss, cs = c * c, s * s, c * s
    a = cc * e1 + ss * e2
    b = cs * (e1 - e2)
    d = ss * e1 + cc * e2
    return mx, my, e1, e2, cc, ss, cs, a, b, d, geometry[5]


def exponent_rows(terms):
    mx, my, e1, e2, cc, ss, cs, a, b, d, logit = terms
    bx, by = a * mx + b * my, b * mx + d * my
    log_opacity = jnp.minimum(logit, 0.0) - jnp.log1p(jnp.exp(-jnp.abs(logit)))
    one = log_opacity - 0.5 * (mx * bx + my * by)
    return [LOG2E * r for r in (one, bx, by, -0.5 * a, -b, -0.5 * d)]


def geometry_grads(terms, m):
    mx, my, e1, e2, cc, ss, cs, a, b, d, logit = terms
    n0 = m[0]
    nx, ny = m[1] - mx * n0, m[2] - my * n0
    nxx = m[3] - mx * (m[1] + nx)
    nxy = m[4] - mx * m[2] - my * nx
    nyy = m[5] - my * (m[2] + ny)
    return [
        a * nx + b * ny,
        b * nx + d * ny,
        e1 * (cc * nxx + 2.0 * cs * nxy + ss * nyy),
        e2 * (ss * nxx - 2.0 * cs * nxy + cc * nyy),
        (e2 - e1) * (cs * (nyy - nxx) + (cc - ss) * nxy),
        n0 / (1.0 + jnp.exp(logit)),
    ]


MESH = pl.DeviceIdType.MESH


def greet(peers):
    barrier = pltpu.get_barrier_semaphore()
    tile, attr, owners, extra = peers

    def hello(step, _):
        other = (tile + step) % owners
        pl.semaphore_signal(barrier, inc=1, device_id=(other, attr), device_id_type=MESH)
        return 0

    lax.fori_loop(1, owners, hello, 0)
    for other in extra:
        pl.semaphore_signal(barrier, inc=1, device_id=(tile, other), device_id_type=MESH)
    return barrier, owners - 1 + len(extra)


def split3(x):
    high = x.astype(jnp.bfloat16)
    rest = x - high.astype(jnp.float32)
    mid = rest.astype(jnp.bfloat16)
    return high, mid, (rest - mid.astype(jnp.float32)).astype(jnp.bfloat16)


def exchange(src, dst, sems, k, device):
    return pltpu.make_async_remote_copy(
        src_ref=src, dst_ref=dst, send_sem=sems.at[0, k], recv_sem=sems.at[1, k],
        device_id=device, device_id_type=MESH,
    )


def fetch_kernel(dims, want_ref, coef_ref, part_ref, held_ref, asked_ref,
                 asks, answer, landed, first, summed, second, tile_sems, back_sems, attr_sems):
    owners, owned, cap, message, stride = dims
    f32 = jnp.float32
    tile, attr = lax.axis_index("tile"), lax.axis_index("attr")
    core = attr + 1 - 2 * (attr % 2)
    across = (attr + 2) % 4
    pl.semaphore_wait(*greet((tile, attr, owners, (core, across))))

    colour_one = exchange(part_ref, first, attr_sems, 0, (tile, core))
    colour_one.start()

    def ask(other, sender):
        return pltpu.make_async_remote_copy(
            src_ref=want_ref.at[other], dst_ref=asks.at[sender],
            send_sem=tile_sems.at[0, other], recv_sem=tile_sems.at[1, sender],
            device_id=(other, attr), device_id_type=MESH,
        )

    def send_ask(step, _):
        ask((tile + step) % owners, tile).start()
        return 0

    lax.fori_loop(1, owners, send_ask, 0)
    asks[tile] = want_ref[tile]

    colour_one.wait()
    summed[...] = part_ref[...] + first[...]
    colour_two = exchange(summed, second, attr_sems, 1, (tile, across))
    colour_two.start()

    def take_ask(step, _):
        other = (tile + step) % owners
        ask(other, other).wait()
        return 0

    lax.fori_loop(1, owners, take_ask, 0)

    per = 128 // stride
    lanes = owners // per
    rows = []
    for tile_at in range(lanes):
        rows.append(functools.reduce(jnp.add, [asks[tile_at * per + k] for k in range(per)]))
    asked = jnp.concatenate(rows, axis=1) - 1.0
    asked_ref[...] = asked
    wide = 9 * owned
    columns = []
    for tile_at in range(lanes):
        square = jnp.concatenate([rows[tile_at] - 1.0] * 16, axis=0)
        columns.append(jnp.transpose(square)[:, 0:1])
    column = jnp.concatenate(columns, axis=0)
    lane = lax.broadcasted_iota(jnp.int32, (owners * stride, wide), 1).astype(f32)
    pick = jnp.where(lane == column, 1.0, 0.0).astype(jnp.bfloat16)

    colour_two.wait()
    colour = summed[...] + second[...] + 0.5
    table = jnp.concatenate([coef_ref[...], colour], axis=0)
    high, mid, low = split3(table)
    answer[...] = (dot(pick, low) + dot(pick, mid)) + dot(pick, high)

    def back(other, sender):
        at = pl.multiple_of(other * stride, 8)
        return pltpu.make_async_remote_copy(
            src_ref=answer.at[pl.ds(at, message)], dst_ref=landed.at[sender],
            send_sem=back_sems.at[0, other], recv_sem=back_sems.at[1, sender],
            device_id=(other, attr), device_id_type=MESH,
        )

    def send_back(step, _):
        back((tile + step) % owners, tile).start()
        return 0

    lax.fori_loop(1, owners, send_back, 0)
    landed[tile] = answer[pl.ds(pl.multiple_of(tile * stride, 8), message), :]
    held_ref[...] = jnp.zeros_like(held_ref)

    def take_back(step, _):
        other = (tile + step) % owners
        back(other, other).wait()
        return 0

    lax.fori_loop(1, owners, take_back, 0)

    def unpack(o, _):
        for k in range(cap):
            held_ref[o * cap + k, 0:9, :] = landed[o, 9 * k : 9 * k + 9, :]
        return 0

    lax.fori_loop(0, owners, unpack, 0)


def give_kernel(dims, grads_ref, asked_ref, out_ref,
                packed, landed, sums, first, half, second, third, tile_sems, attr_sems):
    owners, owned, cap, message, stride = dims
    f32 = jnp.float32
    tile, attr = lax.axis_index("tile"), lax.axis_index("attr")
    core = attr + 1 - 2 * (attr % 2)
    across = (attr + 2) % 4
    mine = attr % 2

    if message < stride:
        landed[...] = jnp.zeros_like(landed)
    greeted = greet((tile, attr, owners, (core, across)))
    packed[...] = jnp.zeros_like(packed)

    def pack(o, _):
        for k in range(cap):
            packed[o, 9 * k : 9 * k + 6, :] = grads_ref[o * cap + k, 8:14, :]
            packed[o, 9 * k + 6 : 9 * k + 9, :] = grads_ref[o * cap + k, 0:3, :]
        return 0

    lax.fori_loop(0, owners, pack, 0)
    pl.semaphore_wait(*greeted)

    def give(other, sender):
        at = pl.multiple_of(sender * stride, 8)
        return pltpu.make_async_remote_copy(
            src_ref=packed.at[other], dst_ref=landed.at[pl.ds(at, message)],
            send_sem=tile_sems.at[0, other], recv_sem=tile_sems.at[1, sender],
            device_id=(other, attr), device_id_type=MESH,
        )

    def send_give(step, _):
        give((tile + step) % owners, tile).start()
        return 0

    lax.fori_loop(1, owners, send_give, 0)
    landed[pl.ds(pl.multiple_of(tile * stride, 8), message), :] = packed[tile]
    wide = 9 * owned
    row = lax.broadcasted_iota(jnp.int32, (wide, owners * stride), 0).astype(f32)
    pick = jnp.where(row == asked_ref[0:1, :], 1.0, 0.0).astype(jnp.bfloat16)

    def take_give(step, _):
        other = (tile + step) % owners
        give(other, other).wait()
        return 0

    lax.fori_loop(1, owners, take_give, 0)
    high, mid, low = split3(landed[...])
    total = (dot(pick, low) + dot(pick, mid)) + dot(pick, high)
    cut = wide // 2
    sums[0] = total[:cut]
    sums[1] = total[cut:]

    one = exchange(sums.at[1 - mine], first, attr_sems, 0, (tile, core))
    one.start()
    one.wait()
    half[...] = sums[mine] + first[...]
    two = exchange(half, second, attr_sems, 1, (tile, across))
    two.start()
    two.wait()
    half_sum = half[...] + second[...]
    first[...] = half_sum
    three = exchange(first, third, attr_sems, 2, (tile, core))
    three.start()
    three.wait()
    at = pl.multiple_of(mine * cut, 8)
    out_ref[pl.ds(at, cut), :] = half_sum
    at = pl.multiple_of((1 - mine) * cut, 8)
    out_ref[pl.ds(at, cut), :] = third[...]


def remote_call(kernel, dims, outs, ins, scratch, number, name):
    vmem = pl.BlockSpec(memory_space=pltpu.VMEM)
    return pl.pallas_call(
        functools.partial(kernel, dims),
        name=name,
        out_shape=tuple(jax.ShapeDtypeStruct(o, jnp.float32) for o in outs),
        in_specs=[vmem] * len(ins),
        out_specs=tuple(vmem for _ in outs),
        scratch_shapes=scratch,
        compiler_params=pltpu.CompilerParams(
            collective_id=number, has_side_effects=True, vmem_limit_bytes=20 * 1024 * 1024
        ),
    )(*ins)


def floats(*shape):
    return pltpu.VMEM(shape, jnp.float32)


def fetch(dims, want, coef, part):
    owners, owned, cap, message, stride = dims
    sems = pltpu.SemaphoreType.DMA
    return remote_call(
        fetch_kernel, dims,
        ((owners * cap, 16, BLOCK), (8, owners * stride)),
        (want, coef, part),
        [floats(owners, 8, 128), floats(owners * stride, BLOCK), floats(owners, message, BLOCK),
         floats(3 * owned, BLOCK), floats(3 * owned, BLOCK), floats(3 * owned, BLOCK),
         sems((2, owners)), sems((2, owners)), sems((2, 2))],
        1, "fetch",
    )


def give_back(dims, grads, asked):
    owners, owned, cap, message, stride = dims
    sems = pltpu.SemaphoreType.DMA
    cut = 9 * owned // 2
    return remote_call(
        give_kernel, dims, ((9 * owned, BLOCK),), (grads, asked),
        [floats(owners, message, BLOCK), floats(owners * stride, BLOCK), floats(2, cut, BLOCK),
         floats(cut, BLOCK), floats(cut, BLOCK), floats(cut, BLOCK), floats(cut, BLOCK),
         sems((2, owners)), sems((2, 3))],
        2, "give",
    )[0]


def prep_kernel(owned, bands, geometry_ref, angles_ref, coeffs_ref, coef_ref, part_ref, basis_ref, terms_ref,
                geo, ang, coe, rows):
    def relay(b, _):
        for h in range(BLOCK // 128):
            at = pl.ds(pl.multiple_of(b * BLOCK + h * 128, 128), 128)
            geo[h, pl.ds(pl.multiple_of(b * 8, 8), 6), :] = geometry_ref[:, at]
            ang[h, pl.ds(pl.multiple_of(b * 8, 8), 2), :] = angles_ref[:, at]
            coe[h, pl.ds(pl.multiple_of(b * 16, 8), 3 * bands), :] = coeffs_ref[:, at]
        return 0

    lax.fori_loop(0, owned, relay, 0, unroll=4)

    def plane(ref, k, pitch):
        halves = [ref[h, pl.ds(k, owned, stride=pitch), :] for h in range(BLOCK // 128)]
        return jnp.concatenate(halves, axis=1)

    terms = splat_terms([plane(geo, k, 8) for k in range(6)])
    for k, value in enumerate(terms):
        terms_ref[k] = value
    for k, value in enumerate(exponent_rows(terms)):
        coef_ref[k * owned : (k + 1) * owned, :] = value
    for k, value in enumerate(sh_basis([plane(ang, k, 8) for k in range(2)])):
        rows[k] = value
    first = lax.axis_index("attr") * bands
    total = [jnp.zeros((owned, BLOCK), jnp.float32) for _ in range(3)]
    for k in range(bands):
        value = rows[first + k]
        basis_ref[k] = value
        for c in range(3):
            total[c] = total[c] + value * plane(coe, 3 * k + c, 16)
    for c in range(3):
        part_ref[c * owned : (c + 1) * owned, :] = total[c]


def prep(geometry, view_angles, sh_coeffs, owned):
    bands = sh_coeffs.shape[0] // 3
    vmem = pl.BlockSpec(memory_space=pltpu.VMEM)
    shapes = ((6 * owned, BLOCK), (3 * owned, BLOCK), (bands, owned, BLOCK), (11, owned, BLOCK))
    return pl.pallas_call(
        functools.partial(prep_kernel, owned, bands),
        name="prep",
        out_shape=tuple(jax.ShapeDtypeStruct(o, jnp.float32) for o in shapes),
        in_specs=[vmem] * 3,
        out_specs=(vmem,) * 4,
        scratch_shapes=[
            floats(BLOCK // 128, 8 * owned, 128),
            floats(BLOCK // 128, 8 * owned, 128),
            floats(BLOCK // 128, 16 * owned, 128),
            floats(16, owned, BLOCK),
        ],
        compiler_params=pltpu.CompilerParams(vmem_limit_bytes=12 * 1024 * 1024),
    )(geometry, view_angles, sh_coeffs)


def final_kernel(owned, bands, sums_ref, terms_ref, basis_ref, geometry_ref, coeffs_ref, geo, coe):
    summed = [sums_ref[k * owned : (k + 1) * owned, :] for k in range(9)]

    def put(ref, k, pitch, value):
        for h in range(BLOCK // 128):
            ref[h, pl.ds(k, owned, stride=pitch), :] = value[:, h * 128 : (h + 1) * 128]

    for k, value in enumerate(geometry_grads([terms_ref[k] for k in range(11)], summed[:6])):
        put(geo, k, 8, value)
    for k in range(bands):
        for c in range(3):
            put(coe, 3 * k + c, 16, basis_ref[k] * summed[6 + c])

    def relay(b, _):
        for h in range(BLOCK // 128):
            at = pl.ds(pl.multiple_of(b * BLOCK + h * 128, 128), 128)
            geometry_ref[:, at] = geo[h, pl.ds(pl.multiple_of(b * 8, 8), 6), :]
            coeffs_ref[:, at] = coe[h, pl.ds(pl.multiple_of(b * 16, 8), 3 * bands), :]
        return 0

    lax.fori_loop(0, owned, relay, 0, unroll=4)


def final(sums, terms, basis, owned):
    bands = basis.shape[0]
    vmem = pl.BlockSpec(memory_space=pltpu.VMEM)
    shapes = ((6, owned * BLOCK), (3 * bands, owned * BLOCK))
    return pl.pallas_call(
        functools.partial(final_kernel, owned, bands),
        name="final",
        out_shape=tuple(jax.ShapeDtypeStruct(o, jnp.float32) for o in shapes),
        in_specs=[vmem] * 3,
        out_specs=(vmem,) * 2,
        scratch_shapes=[
            floats(BLOCK // 128, 8 * owned, 128),
            floats(BLOCK // 128, 16 * owned, 128),
        ],
        compiler_params=pltpu.CompilerParams(vmem_limit_bytes=12 * 1024 * 1024),
    )(sums, terms, basis)


def local_general(geometry, sh_coeffs, view_angles, visible, counts, order, image_cot):
    owners = lax.axis_size("tile")
    owned = geometry.shape[1] // BLOCK
    vis = visible.shape[1]
    cap = (vis + owners - 1) // owners
    coef, partial_colour, my_basis, terms = prep(geometry, view_angles, sh_coeffs, owned)

    ids = visible[0]
    owner_of, local_of = ids // owned, ids % owned
    position = jnp.arange(vis)
    rank = jnp.sum(((owner_of[None, :] == owner_of[:, None]) & (position[None, :] < position[:, None])).astype(jnp.int32), 1)
    slot = owner_of * cap + rank
    message = -(-9 * cap // 8) * 8
    stride = 16 if message <= 16 else 32
    dims = (owners, owned, cap, message, stride)
    lane = jnp.arange(128) - (lax.axis_index("tile") % (128 // stride)) * stride
    in_slot = lane[None, :, None] // 9 + jnp.arange(owners)[:, None, None] * cap
    hit = (slot[None, None, :] == in_slot) & (lane >= 0)[None, :, None] & (lane < 9 * cap)[None, :, None]
    want = jnp.sum(jnp.where(hit, 1 + local_of[None, None, :] + owned * (lane % 9)[None, :, None], 0), 2)
    want = jnp.broadcast_to(want.astype(jnp.float32)[:, None, :], (owners, 8, 128))
    slot_of = jnp.sum(jnp.where(visible[:, :, None] == ids[None, None, :], slot[None, None, :], 0), 2)
    seq = jnp.sum(jnp.where(order[:, :, None] == position[None, None, :], slot_of[:, None, :], 0), 2)

    held, asked = fetch(dims, want, coef, partial_colour)
    picture, grads = blend(seq, counts, held, image_cot)
    sums = give_back(dims, grads, asked)
    grad_geometry, grad_sh = final(sums, terms, my_basis, owned)
    return (picture, grad_geometry, grad_sh)


STEPS = 8
PAIR = 2
SLOTS = STEPS * PAIR
OWNED = 32
MSG = 24
TRIPLE = 3


def stack3(x):
    high, mid, low = split3(x)
    return jnp.concatenate([high, mid, low], axis=0)


def lane_halves(x):
    return [x[:, h * 128 : (h + 1) * 128] for h in range(BLOCK // 128)]


def put_rows(ref, rows, value):
    for h, part in enumerate(lane_halves(value)):
        ref[h, rows, :] = part


def get_rows(ref, rows):
    return jnp.concatenate([ref[h, rows, :] for h in range(BLOCK // 128)], axis=1)


def scatter(ref, at, pitch, value):
    put_rows(ref, pl.ds(at, STEPS, stride=pitch), value)


def gather(ref, at, pitch):
    return get_rows(ref, pl.ds(at, STEPS, stride=pitch))


def tile_of(ref, i, at):
    return jnp.concatenate([ref[i, h, at : at + 8, :] for h in range(BLOCK // 128)], axis=1)


def pixel_monomials(shape, dim):
    pixel = lax.broadcasted_iota(jnp.int32, shape, dim)
    kind = lax.broadcasted_iota(jnp.int32, shape, 1 - dim) & 7
    x = (pixel & (SIDE - 1)).astype(jnp.float32) + (0.5 - MID)
    y = (pixel // SIDE).astype(jnp.float32) + (0.5 - MID)
    out = jnp.where(kind == 0, 1.0, 0.0)
    for k, value in ((1, x), (2, y), (3, x * x), (4, x * y), (5, y * y)):
        out = jnp.where(kind == k, value, out)
    return out.astype(jnp.bfloat16)


def slot_tables(tile, visible, order, counts_ref):
    f32 = jnp.float32
    sub = lax.broadcasted_iota(jnp.int32, (SLOTS, SLOTS), 0)
    lane = lax.broadcasted_iota(jnp.int32, (SLOTS, SLOTS), 1)
    diagonal = sub == lane
    lane_f, sub_f = lane.astype(f32), sub.astype(f32)

    def to_column(row):
        return jnp.sum(jnp.where(diagonal, row, 0.0), axis=1, keepdims=True)

    def to_row(column):
        return jnp.sum(jnp.where(diagonal, column, 0.0), axis=0, keepdims=True)

    ids = visible[0:1]
    owner = ids // OWNED
    near = owner - tile
    near = jnp.where(near < 0, near + STEPS, near).astype(f32)
    ids_f = ids.astype(f32)
    inside = (ids - owner * OWNED).astype(f32)
    near_column = to_column(near)
    second = jnp.sum(jnp.where((near_column == near) & (sub < lane), 1.0, 0.0), axis=0, keepdims=True)
    slot = second * STEPS + near
    match = sub_f == slot
    local_id = jnp.sum(jnp.where(match, inside, 0.0), axis=1, keepdims=True)
    slot_id = jnp.sum(jnp.where(match, ids_f, 0.0), axis=1, keepdims=True)
    ahead, live = [], []
    for t in range(2):
        listed = to_column(visible[t : t + 1].astype(f32))
        here = sub == order[t : t + 1]
        sequence = jnp.sum(jnp.where(here, listed, 0.0), axis=0, keepdims=True)
        rank = jnp.sum(jnp.where(sequence == slot_id, lane_f, 0.0), axis=1, keepdims=True)
        ahead.append(jnp.where(to_row(rank) < rank, 1.0, 0.0))
        live.append(jnp.where(rank < counts_ref[t].astype(f32), 1.0, 0.0))
    return local_id, ahead, live


def fused_kernel(bands, counts_ref, geometry_hbm, angles_hbm, coeffs_hbm, visible_hbm, order_hbm, cot_hbm,
                 pic_ref, basis_ref, terms_ref, out_ref,
                 geometry, angles, coeffs, visible, order, cot, geo, ang, coe, rows,
                 coef, part, first, summed, second, colour,
                 asks_out, asks, answer, held, w_ref, ratio_ref, loss_ref, c_ref, a_ref,
                 packed, landed, sums, got_core, half, got_across, got_rest,
                 local_sems, ask_sems, back_sems, give_sems, attr_sems):
    f32, bf16 = jnp.float32, jnp.bfloat16
    tile, attr = lax.axis_index("tile"), lax.axis_index("attr")
    core = attr + 1 - 2 * (attr % 2)
    across = (attr + 2) % 4
    mine = attr % 2
    greeted = greet((tile, attr, STEPS, (core, across)))

    pairs = ((visible_hbm, visible), (order_hbm, order), (geometry_hbm, geometry), (angles_hbm, angles),
             (coeffs_hbm, coeffs), (cot_hbm, cot))
    loads = [pltpu.make_async_copy(a, b, local_sems.at[n]) for n, (a, b) in enumerate(pairs)]
    for load in loads:
        load.start()

    asks_out[...] = jnp.zeros_like(asks_out)
    answer[...] = jnp.zeros_like(answer)
    loss_ref[...] = jnp.zeros_like(loss_ref)
    loads[0].wait()
    loads[1].wait()
    local_id, ahead, live = slot_tables(tile, visible[...], order[...], counts_ref)
    lane = lax.broadcasted_iota(jnp.int32, (SLOTS, 128), 1)
    block = (lane & (OWNED - 1)).astype(f32)
    wanted = jnp.where((block == local_id) & (lane < TRIPLE * OWNED), 1.0, 0.0)
    for k in range(PAIR):
        asks_out[pl.ds(k, STEPS, stride=8), :] = wanted[k * STEPS : (k + 1) * STEPS]
    for load in loads[2:]:
        load.wait()

    def relay(b, _):
        for h in range(BLOCK // 128):
            at = pl.ds(pl.multiple_of(b * BLOCK + h * 128, 128), 128)
            geo[h, pl.ds(pl.multiple_of(b * 8, 8), 6), :] = geometry[:, at]
            ang[h, pl.ds(pl.multiple_of(b * 8, 8), 2), :] = angles[:, at]
            coe[h, pl.ds(pl.multiple_of(b * 16, 8), 3 * bands), :] = coeffs[:, at]
        return 0

    lax.fori_loop(0, OWNED, relay, 0, unroll=4)

    def plane(ref, k, pitch):
        halves = [ref[h, pl.ds(k, OWNED, stride=pitch), :] for h in range(BLOCK // 128)]
        return jnp.concatenate(halves, axis=1)

    for k, value in enumerate(sh_basis([plane(ang, k, 8) for k in range(2)])):
        rows[k] = value
    first_band = attr * bands
    total = [jnp.zeros((OWNED, BLOCK), f32) for _ in range(3)]
    for k in range(bands):
        value = rows[first_band + k]
        basis_ref[k] = value
        for c in range(3):
            total[c] = total[c] + value * plane(coe, 3 * k + c, 16)
    for c in range(3):
        part[c * OWNED : (c + 1) * OWNED, :] = total[c]
    pl.semaphore_wait(*greeted)

    def ask(i):
        return pltpu.make_async_remote_copy(
            src_ref=asks_out.at[pl.ds(pl.multiple_of(i * 8, 8), 8)], dst_ref=asks.at[pl.ds(pl.multiple_of(i * 8, 8), 8)],
            send_sem=ask_sems.at[0, i], recv_sem=ask_sems.at[1, i],
            device_id=((tile + i) % STEPS, attr), device_id_type=MESH,
        )

    def back(i):
        return pltpu.make_async_remote_copy(
            src_ref=answer.at[:, pl.ds(pl.multiple_of(i * MSG, 8), MSG)], dst_ref=held.at[i],
            send_sem=back_sems.at[0, i], recv_sem=back_sems.at[1, i],
            device_id=((tile + STEPS - i) % STEPS, attr), device_id_type=MESH,
        )

    def give(i):
        return pltpu.make_async_remote_copy(
            src_ref=packed.at[i], dst_ref=landed.at[:, pl.ds(pl.multiple_of(i * MSG, 8), MSG)],
            send_sem=give_sems.at[0, i], recv_sem=give_sems.at[1, i],
            device_id=((tile + i) % STEPS, attr), device_id_type=MESH,
        )

    def each(act):
        def step(i, _):
            act(i)
            return 0

        lax.fori_loop(1, STEPS, step, 0)

    each(lambda i: ask(i).start())
    colour_one = exchange(part, first, attr_sems, 0, (tile, core))
    colour_one.start()
    asks[0:8, :] = asks_out[0:8, :]

    terms = splat_terms([plane(geo, k, 8) for k in range(6)])
    for k, value in enumerate(terms):
        terms_ref[k] = value
    for k, value in enumerate(exponent_rows(terms)):
        coef[k] = stack3(value)

    colour_one.wait()
    summed[...] = part[...] + first[...]
    colour_two = exchange(summed, second, attr_sems, 1, (tile, across))
    colour_two.start()

    each(lambda i: ask(i).wait_recv())
    picks = jnp.concatenate([asks[pl.ds(k, STEPS, stride=8), :] for k in range(PAIR)], axis=0)
    pick = picks.astype(bf16)[:, : TRIPLE * OWNED]
    tall = jnp.concatenate([picks] * TRIPLE + [jnp.zeros((128 - TRIPLE * SLOTS, 128), f32)], axis=0)
    put = jnp.transpose(tall)[:OWNED, : TRIPLE * SLOTS].astype(bf16)

    def pick_row(values, at):
        found = dot(pick, values)
        for k in range(PAIR):
            scatter(answer, at[k], MSG, found[k * STEPS : (k + 1) * STEPS])

    for r in range(6):
        pick_row(coef[r], (r, 8 + r))
    colour_two.wait()
    for c in range(3):
        piece = slice(c * OWNED, (c + 1) * OWNED)
        pick_row(stack3(summed[piece] + second[piece] + 0.5), (16 + c, 20 + c))
    each(lambda i: back(i).start())
    held[0] = answer[:, 0:MSG, :]

    row = lax.broadcasted_iota(jnp.int32, (2 * BLOCK, BLOCK), 0) & (BLOCK - 1)
    col = lax.broadcasted_iota(jnp.int32, (2 * BLOCK, BLOCK), 1)
    before = jnp.where(row < col, -1.0, 0.0).astype(bf16)
    upto = jnp.where(row <= col, 1.0, 0.0).astype(bf16)
    mono_cols = pixel_monomials((PIX, 32), 0)
    mono_rows = pixel_monomials((8, PIX), 1)
    slot_lane = lax.broadcasted_iota(jnp.int32, (PIX, 128), 1)
    eight = lax.broadcasted_iota(jnp.int32, (8, BLOCK), 0)
    own_rows = [(eight >= 4 * k) & (eight < 4 * k + 3) for k in range(PAIR)]

    def halves(x):
        high = x.astype(bf16).astype(f32)
        return high, x - high

    def forward(i, _):
        @pl.when(i > 0)
        def _():
            back(i).wait_recv()

        c_high, c_low = halves(tile_of(held, i, 16))
        seen = None
        losses = loss_ref[...]
        for k in range(PAIR):
            high, mid, low = [p.astype(f32) for p in split3(tile_of(held, i, 8 * k))]
            coefs = jnp.concatenate([high, mid, low, jnp.zeros_like(low)], axis=0).astype(bf16)
            alpha = jnp.exp2(dot(mono_cols, coefs))
            loss = jnp.log(1.0 - alpha) * -LOG2E
            keep = dot(split2(loss), before)
            losses = jnp.where(slot_lane == i + k * STEPS, loss[:, BLOCK - 1 :] - keep[:, BLOCK - 1 :], losses)
            w2 = split2(alpha * jnp.exp2(keep))
            w_ref[i, k] = w2
            ratio_ref[i, k] = alpha * jnp.exp2(loss)
            lhs = jnp.concatenate([jnp.where(own_rows[k], c_high, 0.0), jnp.where(own_rows[k], c_low, 0.0)], axis=0)
            lhs = lhs.astype(bf16)
            contract = (((1,), (1,)), ((), ()))
            shown = lax.dot_general(lhs, w2[:, :BLOCK], contract, preferred_element_type=f32)
            shown = shown + lax.dot_general(lhs, w2[:, BLOCK:], contract, preferred_element_type=f32)
            shown = shown[:8] + shown[8:]
            seen = shown if seen is None else seen + shown
        loss_ref[...] = losses
        put_rows(c_ref, pl.ds(pl.multiple_of(i * 8, 8), 8), seen)
        return 0

    lax.fori_loop(0, STEPS, forward, 0)

    def by_slot(ref, c):
        return jnp.concatenate([gather(ref, c + 4 * k, 8) for k in range(PAIR)], axis=0)

    losses = jnp.transpose(loss_ref[...])[:SLOTS]
    local = [by_slot(c_ref, c) for c in range(3)]
    spread = [jnp.zeros((SLOTS, PIX), f32) for _ in range(4)]
    for t in range(2):
        def earlier(values):
            out = jnp.zeros((SLOTS, PIX), f32)
            for s in range(SLOTS):
                out = out + ahead[t][:, s : s + 1] * values[s : s + 1, :]
            return out

        through = jnp.exp2(-earlier(losses)) * live[t]
        shade = jnp.zeros((SLOTS, PIX), f32)
        for c in range(3):
            g = cot[c, t : t + 1, :]
            lit = through * local[c]
            pic_ref[c, t : t + 1, :] = jnp.sum(lit, axis=0, keepdims=True)
            shade = shade + lit * g
            spread[c] = spread[c] + through * g
        behind = earlier(shade) - jnp.sum(shade, axis=0, keepdims=True)
        spread[3] = spread[3] + live[t] * behind
    for c in range(4):
        for k in range(PAIR):
            scatter(a_ref, c + 4 * k, 8, spread[c][k * STEPS : (k + 1) * STEPS])

    def backward(n, _):
        i = (n + 1) % STEPS
        a = get_rows(a_ref, pl.ds(pl.multiple_of(i * 8, 8), 8))
        a_high, a_low = halves(a)
        c_high, c_low = halves(tile_of(held, i, 16))
        columns = jnp.transpose(jnp.concatenate([a_high, a_low, a_high, a], axis=0))
        v_lhs = columns.astype(bf16)
        tint = None
        for k in range(PAIR):
            ch, cl = jnp.where(own_rows[k], c_high, 0.0), jnp.where(own_rows[k], c_low, 0.0)
            v_rhs = jnp.concatenate([ch, ch, cl, jnp.zeros_like(cl)], axis=0).astype(bf16)
            w2 = w_ref[i, k]
            w_high, w_low = w2[:, :BLOCK], w2[:, BLOCK:]
            value = (w_high.astype(f32) + w_low.astype(f32)) * dot(v_lhs, v_rhs)
            beyond = dot(split2(value), upto) + columns[:, 27 + 4 * k : 28 + 4 * k]
            d2 = split2(value + ratio_ref[i, k] * beyond)
            moments = dot(mono_rows, d2[:, :BLOCK]) + dot(mono_rows, d2[:, BLOCK:])
            put_rows(packed.at[i], pl.ds(8 * k, 8), moments)
            lhs = jnp.concatenate([jnp.where(own_rows[k], a_high, 0.0), jnp.where(own_rows[k], a_low, 0.0)], axis=0)
            lhs = lhs.astype(bf16)
            grads = dot(lhs, w_high) + dot(lhs, w_low)
            grads = grads[:8] + grads[8:]
            tint = grads if tint is None else tint + grads
        put_rows(packed.at[i], pl.ds(16, 8), tint)

        @pl.when(i > 0)
        def _():
            give(i).start()

        return 0

    lax.fori_loop(0, STEPS, backward, 0)
    landed[:, 0:MSG, :] = packed[0]
    each(lambda i: give(i).wait_recv())
    cut = 9 * OWNED // 2
    for r in range(9):
        at = (r, 8 + r) if r < 6 else (10 + r, 14 + r)
        found = jnp.concatenate([gather(landed, at[k], MSG) for k in range(PAIR)], axis=0)
        sums[r * OWNED : (r + 1) * OWNED, :] = dot(put, stack3(found))

    at_mine = pl.multiple_of(mine * cut, 8)
    at_other = pl.multiple_of((1 - mine) * cut, 8)
    one = exchange(sums.at[pl.ds(at_other, cut)], got_core, attr_sems, 2, (tile, core))
    one.start()
    one.wait()
    half[...] = sums[pl.ds(at_mine, cut), :] + got_core[...]
    two = exchange(half, got_across, attr_sems, 3, (tile, across))
    two.start()
    two.wait()
    half_sum = half[...] + got_across[...]
    half[...] = half_sum
    three = exchange(half, got_rest, attr_sems, 4, (tile, core))
    three.start()
    out_ref[pl.ds(at_mine, cut), :] = half_sum
    three.wait()
    out_ref[pl.ds(at_other, cut), :] = got_rest[...]
    each(lambda i: ask(i).wait_send())
    each(lambda i: back(i).wait_send())
    each(lambda i: give(i).wait_send())


def fused(geometry, view_angles, sh_coeffs, visible, order, cot, counts):
    bands = sh_coeffs.shape[0] // 3
    sems = pltpu.SemaphoreType.DMA
    vmem = pl.BlockSpec(memory_space=pltpu.VMEM)
    whole = pl.BlockSpec(memory_space=pl.ANY)
    ins = (geometry, view_angles, sh_coeffs, visible, order, cot)
    colours, cut = 3 * OWNED, 9 * OWNED // 2
    shapes = (cot.shape, (bands, OWNED, BLOCK), (11, OWNED, BLOCK), (9 * OWNED, BLOCK))
    return pl.pallas_call(
        functools.partial(fused_kernel, bands),
        name="splat",
        out_shape=tuple(jax.ShapeDtypeStruct(o, jnp.float32) for o in shapes),
        in_specs=[pl.BlockSpec(memory_space=pltpu.SMEM)] + [whole] * len(ins),
        out_specs=tuple(vmem for _ in shapes),
        scratch_shapes=[pltpu.VMEM(x.shape, x.dtype) for x in ins] + [
            floats(BLOCK // 128, 8 * OWNED, 128), floats(BLOCK // 128, 8 * OWNED, 128),
            floats(BLOCK // 128, 16 * OWNED, 128), floats(16, OWNED, BLOCK),
            pltpu.VMEM((6, TRIPLE * OWNED, BLOCK), jnp.bfloat16), floats(colours, BLOCK), floats(colours, BLOCK),
            floats(colours, BLOCK), floats(colours, BLOCK), floats(8, 128),
            floats(8 * STEPS, 128), floats(8 * STEPS, 128), floats(2, STEPS * MSG, 128), floats(STEPS, 2, MSG, 128),
            pltpu.VMEM((STEPS, PAIR, PIX, 2 * BLOCK), jnp.bfloat16), floats(STEPS, PAIR, PIX, BLOCK),
            floats(PIX, 128), floats(2, 8 * STEPS, 128), floats(2, 8 * STEPS, 128),
            floats(STEPS, 2, MSG, 128), floats(2, STEPS * MSG, 128), floats(9 * OWNED, BLOCK),
            floats(cut, BLOCK), floats(cut, BLOCK), floats(cut, BLOCK), floats(cut, BLOCK),
            sems((len(ins),)), sems((2, STEPS)), sems((2, STEPS)), sems((2, STEPS)), sems((2, 5)),
        ],
        compiler_params=pltpu.CompilerParams(
            collective_id=3, has_side_effects=True, vmem_limit_bytes=40 * 1024 * 1024
        ),
    )(counts, *ins)


def finish_kernel(bands, sums_ref, terms_ref, basis_ref, pic_ref, geometry_ref, coeffs_ref, picture_ref, geo, coe):
    final_kernel(OWNED, bands, sums_ref, terms_ref, basis_ref, geometry_ref, coeffs_ref, geo, coe)
    picture_ref[...] = pic_ref[...]


def finish(sums, terms, basis, pic):
    bands = basis.shape[0]
    vmem = pl.BlockSpec(memory_space=pltpu.VMEM)
    shapes = ((6, OWNED * BLOCK), (3 * bands, OWNED * BLOCK), pic.shape)
    return pl.pallas_call(
        functools.partial(finish_kernel, bands),
        name="finish",
        out_shape=tuple(jax.ShapeDtypeStruct(o, jnp.float32) for o in shapes),
        in_specs=[vmem] * 4,
        out_specs=(vmem,) * 3,
        scratch_shapes=[
            floats(BLOCK // 128, 8 * OWNED, 128),
            floats(BLOCK // 128, 16 * OWNED, 128),
        ],
        compiler_params=pltpu.CompilerParams(vmem_limit_bytes=12 * 1024 * 1024),
    )(sums, terms, basis, pic)


def local_fused(geometry, sh_coeffs, view_angles, visible, counts, order, image_cot):
    cot = jnp.swapaxes(image_cot, 0, 1)
    pic, basis, terms, sums = fused(geometry, view_angles, sh_coeffs, visible, order, cot, counts)
    grad_geometry, grad_sh, picture = finish(sums, terms, basis, pic)
    return (jnp.swapaxes(picture, 0, 1), grad_geometry, grad_sh)


def local(geometry, sh_coeffs, view_angles, visible, counts, order, image_cot):
    owners = lax.axis_size("tile")
    tiles, vis = visible.shape
    owned = geometry.shape[1] // BLOCK
    fits = (owners, vis, tiles, owned, lax.axis_size("attr")) == (8, 16, 2, 32, 4)
    run = local_fused if fits else local_general
    return run(geometry, sh_coeffs, view_angles, visible, counts, order, image_cot)


def solution(mesh):
    in_specs = (
        P(None, "tile"),
        P("attr", "tile"),
        P(None, "tile"),
        P(("tile", "attr"), None),
        P(("tile", "attr")),
        P(("tile", "attr"), None),
        P(("tile", "attr"), None, None),
    )
    out_specs = (P(("tile", "attr"), None, None), P(None, "tile"), P("attr", "tile"))
    return jax.shard_map(local, mesh=mesh, in_specs=in_specs, out_specs=out_specs, check_vma=False)
```

```python
import functools
import jax
import jax.numpy as jnp
from jax import lax
from jax.experimental import pallas as pl
from jax.experimental.pallas import tpu as pltpu
from jax.sharding import PartitionSpec as P

BLOCK = 256
SIDE = 16
PIX = SIDE * SIDE
MID = 0.5 * SIDE
LOG2E = 1.4426950408889634
LN2 = 0.6931471805599453


band_zero = 0.28209479177387814
band_one = 0.4886025119029199
band_two = (
    1.0925484305920792,
    -1.0925484305920792,
    0.31539156525252005,
    -1.0925484305920792,
    0.5462742152960396,
)
band_three = (
    -0.5900435899266435,
    2.890611442640554,
    -0.4570457994644658,
    0.3731763325901154,
    -0.4570457994644658,
    1.445305721320277,
    -0.5900435899266435,
)


def sh_basis(view_angles):
    azimuth = view_angles[0]
    elevation = view_angles[1]
    dir_x = jnp.cos(azimuth) * jnp.cos(elevation)
    dir_y = jnp.sin(azimuth) * jnp.cos(elevation)
    dir_z = jnp.sin(elevation)
    sq_x = dir_x * dir_x
    sq_y = dir_y * dir_y
    sq_z = dir_z * dir_z
    basis_rows = [
        band_zero * jnp.ones_like(dir_x),
        -band_one * dir_y,
        band_one * dir_z,
        -band_one * dir_x,
        band_two[0] * dir_x * dir_y,
        band_two[1] * dir_y * dir_z,
        band_two[2] * (2.0 * sq_z - sq_x - sq_y),
        band_two[3] * dir_x * dir_z,
        band_two[4] * (sq_x - sq_y),
        band_three[0] * dir_y * (3.0 * sq_x - sq_y),
        band_three[1] * dir_x * dir_y * dir_z,
        band_three[2] * dir_y * (4.0 * sq_z - sq_x - sq_y),
        band_three[3] * dir_z * (2.0 * sq_z - 3.0 * sq_x - 3.0 * sq_y),
        band_three[4] * dir_x * (4.0 * sq_z - sq_x - sq_y),
        band_three[5] * dir_z * (sq_x - sq_y),
        band_three[6] * dir_x * (sq_x - 3.0 * sq_y),
    ]
    return basis_rows


def split2(x):
    high = x.astype(jnp.bfloat16)
    low = (x - high.astype(jnp.float32)).astype(jnp.bfloat16)
    return jnp.concatenate([high, low], axis=1)


def dot(a, b):
    return jnp.dot(a, b, preferred_element_type=jnp.float32)


def blend_kernel(tiles, seq_ref, counts_ref, held_ref, cot_rows_ref, cot_cols_ref, pic_ref, grad_ref, part_ref, ratio_ref):
    f32, bf16 = jnp.float32, jnp.bfloat16
    row = lax.broadcasted_iota(jnp.int32, (2 * BLOCK, BLOCK), 0)
    row = jnp.where(row >= BLOCK, row - BLOCK, row)
    col = lax.broadcasted_iota(jnp.int32, (2 * BLOCK, BLOCK), 1)
    before = jnp.where(row < col, -1.0, 0.0).astype(bf16)
    upto = jnp.where(row <= col, 1.0, 0.0).astype(bf16)

    def monomials(shape, dim, width):
        pixel = lax.broadcasted_iota(jnp.int32, shape, dim)
        kind = lax.broadcasted_iota(jnp.int32, shape, 1 - dim) & (width - 1)
        x = (pixel & (SIDE - 1)).astype(f32) + (0.5 - MID)
        y = (pixel // SIDE).astype(f32) + (0.5 - MID)
        out = jnp.where(kind == 0, 1.0, 0.0)
        for k, value in ((1, x), (2, y), (3, x * x), (4, x * y), (5, y * y)):
            out = jnp.where(kind == k, value, out)
        return out.astype(bf16)

    mono_cols = monomials((PIX, 48), 0, 16)
    mono_rows = monomials((8, PIX), 1, 8)
    cot_lhs, cot_rows = [], []
    for t in range(tiles):
        g = cot_cols_ref[t]
        high = g.astype(bf16).astype(f32)
        lane = lax.broadcasted_iota(jnp.int32, g.shape, 1)
        cot_lhs.append(jnp.where(lane < 48, high, g - high).astype(bf16))
        g = cot_rows_ref[t]
        high = g.astype(bf16).astype(f32)
        cot_rows.append(jnp.concatenate([high, g - high], axis=0).astype(bf16))

    grad_ref[...] = jnp.zeros_like(grad_ref)
    lives = [counts_ref[t] for t in range(tiles)]
    longest = functools.reduce(jnp.maximum, lives)

    lhs = []
    for t in range(tiles):
        wide = jnp.concatenate([mono_cols.astype(f32), jnp.zeros((PIX, 48), f32)], axis=1)
        lhs.append(jnp.concatenate([wide.astype(bf16), cot_lhs[t]], axis=0))
    head = lax.broadcasted_iota(jnp.int32, (16, BLOCK), 0) == 0

    def forward(j, carry):
        keep_before, sum_before, pictures = carry
        alphas, values, losses, helds, spots = [], [], [], [], []
        for t in range(tiles):
            at = seq_ref[t, j]
            hidden = jnp.where(j < lives[t], 0.0, -16384.0)
            held = held_ref[at]
            parts = split3(jnp.where(head, held + hidden, held))
            rows = jnp.concatenate(parts, axis=0)
            both = dot(lhs[t], jnp.concatenate([rows, rows], axis=0))
            alpha = jnp.exp2(both[:PIX])
            alphas.append(alpha)
            values.append(both[PIX:])
            losses.append(jnp.log(1.0 - alpha) * -LOG2E)
            helds.append(jnp.concatenate(parts[:2], axis=0))
            spots.append(at)
        loss = jnp.concatenate(losses, axis=0)
        keep_in = dot(split2(loss), before) + keep_before
        keep_before = keep_in[:, BLOCK - 1 :] - loss[:, BLOCK - 1 :]
        alpha = jnp.concatenate(alphas, axis=0)
        weight = alpha * jnp.exp2(keep_in)
        value = weight * jnp.concatenate(values, axis=0)
        total = dot(split2(value), upto) + sum_before
        sum_before = total[:, BLOCK - 1 :]
        ratio = alpha * jnp.exp2(loss)
        part_ref[j] = value + ratio * total
        ratio_ref[j] = ratio
        w2 = split2(weight)
        shown = []
        for t in range(tiles):
            w_high, w_low = w2[t * PIX : (t + 1) * PIX, :BLOCK], w2[t * PIX : (t + 1) * PIX, BLOCK:]
            rows = lax.dot_general(helds[t], w_high, (((1,), (1,)), ((), ())), preferred_element_type=f32)
            rows = rows + lax.dot_general(helds[t], w_low, (((1,), (1,)), ((), ())), preferred_element_type=f32)
            shown.append(pictures[t] + rows[:16] + rows[16:])
            colour_grad = dot(cot_rows[t], w_high) + dot(cot_rows[t], w_low)
            grad_ref[spots[t], 0:8, :] += colour_grad[:8] + colour_grad[8:]
        return keep_before, sum_before, tuple(shown)

    zero = jnp.zeros((tiles * PIX, 1), f32)
    start = (zero, zero, tuple(jnp.zeros((16, PIX), f32) for _ in range(tiles)))
    _, ends, pictures = lax.fori_loop(0, longest, forward, start)
    for t in range(tiles):
        pic_ref[t] = pictures[t]

    def backward(j, _):
        for t in range(tiles):
            pixels = slice(t * PIX, (t + 1) * PIX)
            d2 = split2(part_ref[j, pixels] - ratio_ref[j, pixels] * ends[pixels])
            moments = dot(mono_rows, d2[:, :BLOCK]) + dot(mono_rows, d2[:, BLOCK:])
            grad_ref[seq_ref[t, j], 8:16, :] += moments
        return 0

    lax.fori_loop(0, longest, backward, 0)


def blend(seq, counts, held, image_cot):
    tiles = image_cot.shape[0]
    rows = held.shape[0]
    cot_rows = jnp.pad(image_cot, ((0, 0), (0, 5), (0, 0)))
    cot_cols = jnp.pad(jnp.swapaxes(image_cot, 1, 2), ((0, 0), (0, 0), (6, 7)))
    cot_cols = jnp.tile(cot_cols, (1, 1, 6))
    smem = pl.BlockSpec(memory_space=pltpu.SMEM)
    vmem = pl.BlockSpec(memory_space=pltpu.VMEM)
    picture, grads = pl.pallas_call(
        functools.partial(blend_kernel, tiles),
        name="blend",
        out_shape=(
            jax.ShapeDtypeStruct((tiles, 16, PIX), jnp.float32),
            jax.ShapeDtypeStruct((rows, 16, BLOCK), jnp.float32),
        ),
        in_specs=[smem, smem, vmem, vmem, vmem],
        out_specs=(vmem, vmem),
        scratch_shapes=[
            pltpu.VMEM((seq.shape[1], tiles * PIX, BLOCK), jnp.float32),
            pltpu.VMEM((seq.shape[1], tiles * PIX, BLOCK), jnp.float32),
        ],
        compiler_params=pltpu.CompilerParams(vmem_limit_bytes=28 * 1024 * 1024),
    )(seq, counts, held, cot_rows, cot_cols)
    return picture[:, 6:9], grads


def splat_terms(geometry):
    mx, my = geometry[0] - MID, geometry[1] - MID
    c, s = jnp.cos(geometry[4]), jnp.sin(geometry[4])
    e1, e2 = jnp.exp(-2.0 * geometry[2]), jnp.exp(-2.0 * geometry[3])
    cc, ss, cs = c * c, s * s, c * s
    a = cc * e1 + ss * e2
    b = cs * (e1 - e2)
    d = ss * e1 + cc * e2
    return mx, my, e1, e2, cc, ss, cs, a, b, d, geometry[5]


def exponent_rows(terms):
    mx, my, e1, e2, cc, ss, cs, a, b, d, logit = terms
    bx, by = a * mx + b * my, b * mx + d * my
    log_opacity = jnp.minimum(logit, 0.0) - jnp.log1p(jnp.exp(-jnp.abs(logit)))
    one = log_opacity - 0.5 * (mx * bx + my * by)
    return [LOG2E * r for r in (one, bx, by, -0.5 * a, -b, -0.5 * d)]


def geometry_grads(terms, m):
    mx, my, e1, e2, cc, ss, cs, a, b, d, logit = terms
    n0 = m[0]
    nx, ny = m[1] - mx * n0, m[2] - my * n0
    nxx = m[3] - mx * (m[1] + nx)
    nxy = m[4] - mx * m[2] - my * nx
    nyy = m[5] - my * (m[2] + ny)
    return [
        a * nx + b * ny,
        b * nx + d * ny,
        e1 * (cc * nxx + 2.0 * cs * nxy + ss * nyy),
        e2 * (ss * nxx - 2.0 * cs * nxy + cc * nyy),
        (e2 - e1) * (cs * (nyy - nxx) + (cc - ss) * nxy),
        n0 / (1.0 + jnp.exp(logit)),
    ]


MESH = pl.DeviceIdType.MESH


def greet(peers):
    barrier = pltpu.get_barrier_semaphore()
    tile, attr, owners, extra = peers

    def hello(step, _):
        other = (tile + step) % owners
        pl.semaphore_signal(barrier, inc=1, device_id=(other, attr), device_id_type=MESH)
        return 0

    lax.fori_loop(1, owners, hello, 0)
    for other in extra:
        pl.semaphore_signal(barrier, inc=1, device_id=(tile, other), device_id_type=MESH)
    return barrier, owners - 1 + len(extra)


def split3(x):
    high = x.astype(jnp.bfloat16)
    rest = x - high.astype(jnp.float32)
    mid = rest.astype(jnp.bfloat16)
    return high, mid, (rest - mid.astype(jnp.float32)).astype(jnp.bfloat16)


def exchange(src, dst, sems, k, device):
    return pltpu.make_async_remote_copy(
        src_ref=src, dst_ref=dst, send_sem=sems.at[0, k], recv_sem=sems.at[1, k],
        device_id=device, device_id_type=MESH,
    )


def fetch_kernel(dims, want_ref, coef_ref, part_ref, held_ref, asked_ref,
                 asks, answer, landed, first, summed, second, tile_sems, back_sems, attr_sems):
    owners, owned, cap, message, stride = dims
    f32 = jnp.float32
    tile, attr = lax.axis_index("tile"), lax.axis_index("attr")
    core = attr + 1 - 2 * (attr % 2)
    across = (attr + 2) % 4
    pl.semaphore_wait(*greet((tile, attr, owners, (core, across))))

    colour_one = exchange(part_ref, first, attr_sems, 0, (tile, core))
    colour_one.start()

    def ask(other, sender):
        return pltpu.make_async_remote_copy(
            src_ref=want_ref.at[other], dst_ref=asks.at[sender],
            send_sem=tile_sems.at[0, other], recv_sem=tile_sems.at[1, sender],
            device_id=(other, attr), device_id_type=MESH,
        )

    def send_ask(step, _):
        ask((tile + step) % owners, tile).start()
        return 0

    lax.fori_loop(1, owners, send_ask, 0)
    asks[tile] = want_ref[tile]

    colour_one.wait()
    summed[...] = part_ref[...] + first[...]
    colour_two = exchange(summed, second, attr_sems, 1, (tile, across))
    colour_two.start()

    def take_ask(step, _):
        other = (tile + step) % owners
        ask(other, other).wait()
        return 0

    lax.fori_loop(1, owners, take_ask, 0)

    per = 128 // stride
    lanes = owners // per
    rows = []
    for tile_at in range(lanes):
        rows.append(functools.reduce(jnp.add, [asks[tile_at * per + k] for k in range(per)]))
    asked = jnp.concatenate(rows, axis=1) - 1.0
    asked_ref[...] = asked
    wide = 9 * owned
    columns = []
    for tile_at in range(lanes):
        square = jnp.concatenate([rows[tile_at] - 1.0] * 16, axis=0)
        columns.append(jnp.transpose(square)[:, 0:1])
    column = jnp.concatenate(columns, axis=0)
    lane = lax.broadcasted_iota(jnp.int32, (owners * stride, wide), 1).astype(f32)
    pick = jnp.where(lane == column, 1.0, 0.0).astype(jnp.bfloat16)

    colour_two.wait()
    colour = summed[...] + second[...] + 0.5
    table = jnp.concatenate([coef_ref[...], colour], axis=0)
    high, mid, low = split3(table)
    answer[...] = (dot(pick, low) + dot(pick, mid)) + dot(pick, high)

    def back(other, sender):
        at = pl.multiple_of(other * stride, 8)
        return pltpu.make_async_remote_copy(
            src_ref=answer.at[pl.ds(at, message)], dst_ref=landed.at[sender],
            send_sem=back_sems.at[0, other], recv_sem=back_sems.at[1, sender],
            device_id=(other, attr), device_id_type=MESH,
        )

    def send_back(step, _):
        back((tile + step) % owners, tile).start()
        return 0

    lax.fori_loop(1, owners, send_back, 0)
    landed[tile] = answer[pl.ds(pl.multiple_of(tile * stride, 8), message), :]
    held_ref[...] = jnp.zeros_like(held_ref)

    def take_back(step, _):
        other = (tile + step) % owners
        back(other, other).wait()
        return 0

    lax.fori_loop(1, owners, take_back, 0)

    def unpack(o, _):
        for k in range(cap):
            held_ref[o * cap + k, 0:9, :] = landed[o, 9 * k : 9 * k + 9, :]
        return 0

    lax.fori_loop(0, owners, unpack, 0)


def give_kernel(dims, grads_ref, asked_ref, out_ref,
                packed, landed, sums, first, half, second, third, tile_sems, attr_sems):
    owners, owned, cap, message, stride = dims
    f32 = jnp.float32
    tile, attr = lax.axis_index("tile"), lax.axis_index("attr")
    core = attr + 1 - 2 * (attr % 2)
    across = (attr + 2) % 4
    mine = attr % 2

    if message < stride:
        landed[...] = jnp.zeros_like(landed)
    greeted = greet((tile, attr, owners, (core, across)))
    packed[...] = jnp.zeros_like(packed)

    def pack(o, _):
        for k in range(cap):
            packed[o, 9 * k : 9 * k + 6, :] = grads_ref[o * cap + k, 8:14, :]
            packed[o, 9 * k + 6 : 9 * k + 9, :] = grads_ref[o * cap + k, 0:3, :]
        return 0

    lax.fori_loop(0, owners, pack, 0)
    pl.semaphore_wait(*greeted)

    def give(other, sender):
        at = pl.multiple_of(sender * stride, 8)
        return pltpu.make_async_remote_copy(
            src_ref=packed.at[other], dst_ref=landed.at[pl.ds(at, message)],
            send_sem=tile_sems.at[0, other], recv_sem=tile_sems.at[1, sender],
            device_id=(other, attr), device_id_type=MESH,
        )

    def send_give(step, _):
        give((tile + step) % owners, tile).start()
        return 0

    lax.fori_loop(1, owners, send_give, 0)
    landed[pl.ds(pl.multiple_of(tile * stride, 8), message), :] = packed[tile]
    wide = 9 * owned
    row = lax.broadcasted_iota(jnp.int32, (wide, owners * stride), 0).astype(f32)
    pick = jnp.where(row == asked_ref[0:1, :], 1.0, 0.0).astype(jnp.bfloat16)

    def take_give(step, _):
        other = (tile + step) % owners
        give(other, other).wait()
        return 0

    lax.fori_loop(1, owners, take_give, 0)
    high, mid, low = split3(landed[...])
    total = (dot(pick, low) + dot(pick, mid)) + dot(pick, high)
    cut = wide // 2
    sums[0] = total[:cut]
    sums[1] = total[cut:]

    one = exchange(sums.at[1 - mine], first, attr_sems, 0, (tile, core))
    one.start()
    one.wait()
    half[...] = sums[mine] + first[...]
    two = exchange(half, second, attr_sems, 1, (tile, across))
    two.start()
    two.wait()
    half_sum = half[...] + second[...]
    first[...] = half_sum
    three = exchange(first, third, attr_sems, 2, (tile, core))
    three.start()
    three.wait()
    at = pl.multiple_of(mine * cut, 8)
    out_ref[pl.ds(at, cut), :] = half_sum
    at = pl.multiple_of((1 - mine) * cut, 8)
    out_ref[pl.ds(at, cut), :] = third[...]


def remote_call(kernel, dims, outs, ins, scratch, number, name):
    vmem = pl.BlockSpec(memory_space=pltpu.VMEM)
    return pl.pallas_call(
        functools.partial(kernel, dims),
        name=name,
        out_shape=tuple(jax.ShapeDtypeStruct(o, jnp.float32) for o in outs),
        in_specs=[vmem] * len(ins),
        out_specs=tuple(vmem for _ in outs),
        scratch_shapes=scratch,
        compiler_params=pltpu.CompilerParams(
            collective_id=number, has_side_effects=True, vmem_limit_bytes=20 * 1024 * 1024
        ),
    )(*ins)


def floats(*shape):
    return pltpu.VMEM(shape, jnp.float32)


def fetch(dims, want, coef, part):
    owners, owned, cap, message, stride = dims
    sems = pltpu.SemaphoreType.DMA
    return remote_call(
        fetch_kernel, dims,
        ((owners * cap, 16, BLOCK), (8, owners * stride)),
        (want, coef, part),
        [floats(owners, 8, 128), floats(owners * stride, BLOCK), floats(owners, message, BLOCK),
         floats(3 * owned, BLOCK), floats(3 * owned, BLOCK), floats(3 * owned, BLOCK),
         sems((2, owners)), sems((2, owners)), sems((2, 2))],
        1, "fetch",
    )


def give_back(dims, grads, asked):
    owners, owned, cap, message, stride = dims
    sems = pltpu.SemaphoreType.DMA
    cut = 9 * owned // 2
    return remote_call(
        give_kernel, dims, ((9 * owned, BLOCK),), (grads, asked),
        [floats(owners, message, BLOCK), floats(owners * stride, BLOCK), floats(2, cut, BLOCK),
         floats(cut, BLOCK), floats(cut, BLOCK), floats(cut, BLOCK), floats(cut, BLOCK),
         sems((2, owners)), sems((2, 3))],
        2, "give",
    )[0]


def prep_kernel(owned, bands, geometry_ref, angles_ref, coeffs_ref, coef_ref, part_ref, basis_ref, terms_ref,
                geo, ang, coe, rows):
    def relay(b, _):
        for h in range(BLOCK // 128):
            at = pl.ds(pl.multiple_of(b * BLOCK + h * 128, 128), 128)
            geo[h, pl.ds(pl.multiple_of(b * 8, 8), 6), :] = geometry_ref[:, at]
            ang[h, pl.ds(pl.multiple_of(b * 8, 8), 2), :] = angles_ref[:, at]
            coe[h, pl.ds(pl.multiple_of(b * 16, 8), 3 * bands), :] = coeffs_ref[:, at]
        return 0

    lax.fori_loop(0, owned, relay, 0, unroll=4)

    def plane(ref, k, pitch):
        halves = [ref[h, pl.ds(k, owned, stride=pitch), :] for h in range(BLOCK // 128)]
        return jnp.concatenate(halves, axis=1)

    terms = splat_terms([plane(geo, k, 8) for k in range(6)])
    for k, value in enumerate(terms):
        terms_ref[k] = value
    for k, value in enumerate(exponent_rows(terms)):
        coef_ref[k * owned : (k + 1) * owned, :] = value
    for k, value in enumerate(sh_basis([plane(ang, k, 8) for k in range(2)])):
        rows[k] = value
    first = lax.axis_index("attr") * bands
    total = [jnp.zeros((owned, BLOCK), jnp.float32) for _ in range(3)]
    for k in range(bands):
        value = rows[first + k]
        basis_ref[k] = value
        for c in range(3):
            total[c] = total[c] + value * plane(coe, 3 * k + c, 16)
    for c in range(3):
        part_ref[c * owned : (c + 1) * owned, :] = total[c]


def prep(geometry, view_angles, sh_coeffs, owned):
    bands = sh_coeffs.shape[0] // 3
    vmem = pl.BlockSpec(memory_space=pltpu.VMEM)
    shapes = ((6 * owned, BLOCK), (3 * owned, BLOCK), (bands, owned, BLOCK), (11, owned, BLOCK))
    return pl.pallas_call(
        functools.partial(prep_kernel, owned, bands),
        name="prep",
        out_shape=tuple(jax.ShapeDtypeStruct(o, jnp.float32) for o in shapes),
        in_specs=[vmem] * 3,
        out_specs=(vmem,) * 4,
        scratch_shapes=[
            floats(BLOCK // 128, 8 * owned, 128),
            floats(BLOCK // 128, 8 * owned, 128),
            floats(BLOCK // 128, 16 * owned, 128),
            floats(16, owned, BLOCK),
        ],
        compiler_params=pltpu.CompilerParams(vmem_limit_bytes=12 * 1024 * 1024),
    )(geometry, view_angles, sh_coeffs)


def final_kernel(owned, bands, sums_ref, terms_ref, basis_ref, geometry_ref, coeffs_ref, geo, coe):
    summed = [sums_ref[k * owned : (k + 1) * owned, :] for k in range(9)]

    def put(ref, k, pitch, value):
        for h in range(BLOCK // 128):
            ref[h, pl.ds(k, owned, stride=pitch), :] = value[:, h * 128 : (h + 1) * 128]

    for k, value in enumerate(geometry_grads([terms_ref[k] for k in range(11)], summed[:6])):
        put(geo, k, 8, value)
    for k in range(bands):
        for c in range(3):
            put(coe, 3 * k + c, 16, basis_ref[k] * summed[6 + c])

    def relay(b, _):
        for h in range(BLOCK // 128):
            at = pl.ds(pl.multiple_of(b * BLOCK + h * 128, 128), 128)
            geometry_ref[:, at] = geo[h, pl.ds(pl.multiple_of(b * 8, 8), 6), :]
            coeffs_ref[:, at] = coe[h, pl.ds(pl.multiple_of(b * 16, 8), 3 * bands), :]
        return 0

    lax.fori_loop(0, owned, relay, 0, unroll=4)


def final(sums, terms, basis, owned):
    bands = basis.shape[0]
    vmem = pl.BlockSpec(memory_space=pltpu.VMEM)
    shapes = ((6, owned * BLOCK), (3 * bands, owned * BLOCK))
    return pl.pallas_call(
        functools.partial(final_kernel, owned, bands),
        name="final",
        out_shape=tuple(jax.ShapeDtypeStruct(o, jnp.float32) for o in shapes),
        in_specs=[vmem] * 3,
        out_specs=(vmem,) * 2,
        scratch_shapes=[
            floats(BLOCK // 128, 8 * owned, 128),
            floats(BLOCK // 128, 16 * owned, 128),
        ],
        compiler_params=pltpu.CompilerParams(vmem_limit_bytes=12 * 1024 * 1024),
    )(sums, terms, basis)


def local_general(geometry, sh_coeffs, view_angles, visible, counts, order, image_cot):
    owners = lax.axis_size("tile")
    owned = geometry.shape[1] // BLOCK
    vis = visible.shape[1]
    cap = (vis + owners - 1) // owners
    coef, partial_colour, my_basis, terms = prep(geometry, view_angles, sh_coeffs, owned)

    ids = visible[0]
    owner_of, local_of = ids // owned, ids % owned
    position = jnp.arange(vis)
    rank = jnp.sum(((owner_of[None, :] == owner_of[:, None]) & (position[None, :] < position[:, None])).astype(jnp.int32), 1)
    slot = owner_of * cap + rank
    message = -(-9 * cap // 8) * 8
    stride = 16 if message <= 16 else 32
    dims = (owners, owned, cap, message, stride)
    lane = jnp.arange(128) - (lax.axis_index("tile") % (128 // stride)) * stride
    in_slot = lane[None, :, None] // 9 + jnp.arange(owners)[:, None, None] * cap
    hit = (slot[None, None, :] == in_slot) & (lane >= 0)[None, :, None] & (lane < 9 * cap)[None, :, None]
    want = jnp.sum(jnp.where(hit, 1 + local_of[None, None, :] + owned * (lane % 9)[None, :, None], 0), 2)
    want = jnp.broadcast_to(want.astype(jnp.float32)[:, None, :], (owners, 8, 128))
    slot_of = jnp.sum(jnp.where(visible[:, :, None] == ids[None, None, :], slot[None, None, :], 0), 2)
    seq = jnp.sum(jnp.where(order[:, :, None] == position[None, None, :], slot_of[:, None, :], 0), 2)

    held, asked = fetch(dims, want, coef, partial_colour)
    picture, grads = blend(seq, counts, held, image_cot)
    sums = give_back(dims, grads, asked)
    grad_geometry, grad_sh = final(sums, terms, my_basis, owned)
    return (picture, grad_geometry, grad_sh)


STEPS = 8
PAIR = 2
SLOTS = STEPS * PAIR
OWNED = 32
MSG = 24
TRIPLE = 3


def stack3(x):
    high, mid, low = split3(x)
    return jnp.concatenate([high, mid, low], axis=0)


def lane_halves(x):
    return [x[:, h * 128 : (h + 1) * 128] for h in range(BLOCK // 128)]


def put_rows(ref, rows, value):
    for h, part in enumerate(lane_halves(value)):
        ref[h, rows, :] = part


def get_rows(ref, rows):
    return jnp.concatenate([ref[h, rows, :] for h in range(BLOCK // 128)], axis=1)


def scatter(ref, at, pitch, value):
    put_rows(ref, pl.ds(at, STEPS, stride=pitch), value)


def gather(ref, at, pitch):
    return get_rows(ref, pl.ds(at, STEPS, stride=pitch))


def tile_of(ref, i, at):
    return jnp.concatenate([ref[i, h, at : at + 8, :] for h in range(BLOCK // 128)], axis=1)


def pixel_monomials(shape, dim):
    pixel = lax.broadcasted_iota(jnp.int32, shape, dim)
    kind = lax.broadcasted_iota(jnp.int32, shape, 1 - dim) & 7
    x = (pixel & (SIDE - 1)).astype(jnp.float32) + (0.5 - MID)
    y = (pixel // SIDE).astype(jnp.float32) + (0.5 - MID)
    out = jnp.where(kind == 0, 1.0, 0.0)
    for k, value in ((1, x), (2, y), (3, x * x), (4, x * y), (5, y * y)):
        out = jnp.where(kind == k, value, out)
    return out.astype(jnp.bfloat16)


def slot_tables(tile, visible, order, counts_ref):
    f32 = jnp.float32
    sub = lax.broadcasted_iota(jnp.int32, (SLOTS, SLOTS), 0)
    lane = lax.broadcasted_iota(jnp.int32, (SLOTS, SLOTS), 1)
    diagonal = sub == lane
    lane_f, sub_f = lane.astype(f32), sub.astype(f32)

    def to_column(row):
        return jnp.sum(jnp.where(diagonal, row, 0.0), axis=1, keepdims=True)

    def to_row(column):
        return jnp.sum(jnp.where(diagonal, column, 0.0), axis=0, keepdims=True)

    ids = visible[0:1]
    owner = ids // OWNED
    near = owner - tile
    near = jnp.where(near < 0, near + STEPS, near).astype(f32)
    ids_f = ids.astype(f32)
    inside = (ids - owner * OWNED).astype(f32)
    near_column = to_column(near)
    second = jnp.sum(jnp.where((near_column == near) & (sub < lane), 1.0, 0.0), axis=0, keepdims=True)
    slot = second * STEPS + near
    match = sub_f == slot
    local_id = jnp.sum(jnp.where(match, inside, 0.0), axis=1, keepdims=True)
    slot_id = jnp.sum(jnp.where(match, ids_f, 0.0), axis=1, keepdims=True)
    ahead, live = [], []
    for t in range(2):
        listed = to_column(visible[t : t + 1].astype(f32))
        here = sub == order[t : t + 1]
        sequence = jnp.sum(jnp.where(here, listed, 0.0), axis=0, keepdims=True)
        rank = jnp.sum(jnp.where(sequence == slot_id, lane_f, 0.0), axis=1, keepdims=True)
        ahead.append(jnp.where(to_row(rank) < rank, 1.0, 0.0))
        live.append(jnp.where(rank < counts_ref[t].astype(f32), 1.0, 0.0))
    return local_id, ahead, live


def fused_kernel(bands, geometry_hbm, angles_hbm, coeffs_hbm, visible_hbm, order_hbm, cot_hbm, counts_hbm,
                 pic_ref, basis_ref, terms_ref, out_ref,
                 geometry, angles, coeffs, visible, order, cot, counts_ref, geo, ang, coe, rows,
                 coef, part, first, summed, second, colour,
                 asks_out, asks, answer, held, w_ref, ratio_ref, loss_ref, c_ref, a_ref,
                 packed, landed, sums, got_core, half, got_across, got_rest,
                 local_sems, ask_sems, back_sems, give_sems, attr_sems):
    f32, bf16 = jnp.float32, jnp.bfloat16
    tile, attr = lax.axis_index("tile"), lax.axis_index("attr")
    core = attr + 1 - 2 * (attr % 2)
    across = (attr + 2) % 4
    mine = attr % 2
    greeted = greet((tile, attr, STEPS, (core, across)))

    pairs = ((visible_hbm, visible), (order_hbm, order), (counts_hbm, counts_ref), (angles_hbm, angles),
             (coeffs_hbm, coeffs), (geometry_hbm, geometry), (cot_hbm, cot))
    loads = [pltpu.make_async_copy(a, b, local_sems.at[n]) for n, (a, b) in enumerate(pairs)]
    for load in loads:
        load.start()

    asks_out[...] = jnp.zeros_like(asks_out)
    answer[...] = jnp.zeros_like(answer)
    loss_ref[...] = jnp.zeros_like(loss_ref)
    for load in loads[:3]:
        load.wait()
    local_id, ahead, live = slot_tables(tile, visible[...], order[...], counts_ref)
    lane = lax.broadcasted_iota(jnp.int32, (SLOTS, 128), 1)
    block = (lane & (OWNED - 1)).astype(f32)
    wanted = jnp.where((block == local_id) & (lane < TRIPLE * OWNED), 1.0, 0.0)
    for k in range(PAIR):
        asks_out[pl.ds(k, STEPS, stride=8), :] = wanted[k * STEPS : (k + 1) * STEPS]
    for load in loads[3:]:
        load.wait()

    def relay(b, _):
        for h in range(BLOCK // 128):
            at = pl.ds(pl.multiple_of(b * BLOCK + h * 128, 128), 128)
            geo[h, pl.ds(pl.multiple_of(b * 8, 8), 6), :] = geometry[:, at]
            ang[h, pl.ds(pl.multiple_of(b * 8, 8), 2), :] = angles[:, at]
            coe[h, pl.ds(pl.multiple_of(b * 16, 8), 3 * bands), :] = coeffs[:, at]
        return 0

    lax.fori_loop(0, OWNED, relay, 0, unroll=4)

    def plane(ref, k, pitch):
        halves = [ref[h, pl.ds(k, OWNED, stride=pitch), :] for h in range(BLOCK // 128)]
        return jnp.concatenate(halves, axis=1)

    for k, value in enumerate(sh_basis([plane(ang, k, 8) for k in range(2)])):
        rows[k] = value
    first_band = attr * bands
    total = [jnp.zeros((OWNED, BLOCK), f32) for _ in range(3)]
    for k in range(bands):
        value = rows[first_band + k]
        basis_ref[k] = value
        for c in range(3):
            total[c] = total[c] + value * plane(coe, 3 * k + c, 16)
    for c in range(3):
        part[c * OWNED : (c + 1) * OWNED, :] = total[c]
    pl.semaphore_wait(*greeted)

    def ask(i):
        return pltpu.make_async_remote_copy(
            src_ref=asks_out.at[pl.ds(pl.multiple_of(i * 8, 8), 8)], dst_ref=asks.at[pl.ds(pl.multiple_of(i * 8, 8), 8)],
            send_sem=ask_sems.at[0, i], recv_sem=ask_sems.at[1, i],
            device_id=((tile + i) % STEPS, attr), device_id_type=MESH,
        )

    def back(i):
        return pltpu.make_async_remote_copy(
            src_ref=answer.at[:, pl.ds(pl.multiple_of(i * MSG, 8), MSG)], dst_ref=held.at[i],
            send_sem=back_sems.at[0, i], recv_sem=back_sems.at[1, i],
            device_id=((tile + STEPS - i) % STEPS, attr), device_id_type=MESH,
        )

    def give(i):
        return pltpu.make_async_remote_copy(
            src_ref=packed.at[i], dst_ref=landed.at[:, pl.ds(pl.multiple_of(i * MSG, 8), MSG)],
            send_sem=give_sems.at[0, i], recv_sem=give_sems.at[1, i],
            device_id=((tile + i) % STEPS, attr), device_id_type=MESH,
        )

    def each(act):
        def step(i, _):
            act(i)
            return 0

        lax.fori_loop(1, STEPS, step, 0)

    each(lambda i: ask(i).start())
    colour_one = exchange(part, first, attr_sems, 0, (tile, core))
    colour_one.start()
    asks[0:8, :] = asks_out[0:8, :]

    terms = splat_terms([plane(geo, k, 8) for k in range(6)])
    for k, value in enumerate(terms):
        terms_ref[k] = value
    for k, value in enumerate(exponent_rows(terms)):
        coef[k] = stack3(value)

    colour_one.wait()
    summed[...] = part[...] + first[...]
    colour_two = exchange(summed, second, attr_sems, 1, (tile, across))
    colour_two.start()

    each(lambda i: ask(i).wait_recv())
    picks = jnp.concatenate([asks[pl.ds(k, STEPS, stride=8), :] for k in range(PAIR)], axis=0)
    pick = picks.astype(bf16)[:, : TRIPLE * OWNED]
    tall = jnp.concatenate([picks] * TRIPLE + [jnp.zeros((128 - TRIPLE * SLOTS, 128), f32)], axis=0)
    put = jnp.transpose(tall)[:OWNED, : TRIPLE * SLOTS].astype(bf16)

    def pick_row(values, at):
        found = dot(pick, values)
        for k in range(PAIR):
            scatter(answer, at[k], MSG, found[k * STEPS : (k + 1) * STEPS])

    for r in range(6):
        pick_row(coef[r], (r, 8 + r))
    colour_two.wait()
    for c in range(3):
        piece = slice(c * OWNED, (c + 1) * OWNED)
        pick_row(stack3(summed[piece] + second[piece] + 0.5), (16 + c, 20 + c))
    each(lambda i: back(i).start())
    held[0] = answer[:, 0:MSG, :]

    row = lax.broadcasted_iota(jnp.int32, (2 * BLOCK, BLOCK), 0) & (BLOCK - 1)
    col = lax.broadcasted_iota(jnp.int32, (2 * BLOCK, BLOCK), 1)
    before = jnp.where(row < col, -1.0, 0.0).astype(bf16)
    upto = jnp.where(row <= col, 1.0, 0.0).astype(bf16)
    mono_cols = pixel_monomials((PIX, 32), 0)
    mono_rows = pixel_monomials((8, PIX), 1)
    slot_lane = lax.broadcasted_iota(jnp.int32, (PIX, 128), 1)
    eight = lax.broadcasted_iota(jnp.int32, (8, BLOCK), 0)
    own_rows = [(eight >= 4 * k) & (eight < 4 * k + 3) for k in range(PAIR)]

    def halves(x):
        high = x.astype(bf16).astype(f32)
        return high, x - high

    def forward(i, _):
        @pl.when(i > 0)
        def _():
            back(i).wait_recv()

        c_high, c_low = halves(tile_of(held, i, 16))
        seen = None
        losses = loss_ref[...]
        for k in range(PAIR):
            high, mid, low = [p.astype(f32) for p in split3(tile_of(held, i, 8 * k))]
            coefs = jnp.concatenate([high, mid, low, jnp.zeros_like(low)], axis=0).astype(bf16)
            alpha = jnp.exp2(dot(mono_cols, coefs))
            loss = jnp.log(1.0 - alpha) * -LOG2E
            keep = dot(split2(loss), before)
            losses = jnp.where(slot_lane == i + k * STEPS, loss[:, BLOCK - 1 :] - keep[:, BLOCK - 1 :], losses)
            w2 = split2(alpha * jnp.exp2(keep))
            w_ref[i, k] = w2
            ratio_ref[i, k] = alpha * jnp.exp2(loss)
            lhs = jnp.concatenate([jnp.where(own_rows[k], c_high, 0.0), jnp.where(own_rows[k], c_low, 0.0)], axis=0)
            lhs = lhs.astype(bf16)
            contract = (((1,), (1,)), ((), ()))
            shown = lax.dot_general(lhs, w2[:, :BLOCK], contract, preferred_element_type=f32)
            shown = shown + lax.dot_general(lhs, w2[:, BLOCK:], contract, preferred_element_type=f32)
            shown = shown[:8] + shown[8:]
            seen = shown if seen is None else seen + shown
        loss_ref[...] = losses
        put_rows(c_ref, pl.ds(pl.multiple_of(i * 8, 8), 8), seen)
        return 0

    lax.fori_loop(0, STEPS, forward, 0)

    def by_slot(ref, c):
        return jnp.concatenate([gather(ref, c + 4 * k, 8) for k in range(PAIR)], axis=0)

    losses = jnp.transpose(loss_ref[...])[:SLOTS]
    local = [by_slot(c_ref, c) for c in range(3)]
    spread = [jnp.zeros((SLOTS, PIX), f32) for _ in range(4)]
    for t in range(2):
        def earlier(values):
            out = jnp.zeros((SLOTS, PIX), f32)
            for s in range(SLOTS):
                out = out + ahead[t][:, s : s + 1] * values[s : s + 1, :]
            return out

        through = jnp.exp2(-earlier(losses)) * live[t]
        shade = jnp.zeros((SLOTS, PIX), f32)
        for c in range(3):
            g = cot[c, t : t + 1, :]
            lit = through * local[c]
            pic_ref[c, t : t + 1, :] = jnp.sum(lit, axis=0, keepdims=True)
            shade = shade + lit * g
            spread[c] = spread[c] + through * g
        behind = earlier(shade) - jnp.sum(shade, axis=0, keepdims=True)
        spread[3] = spread[3] + live[t] * behind
    for c in range(4):
        for k in range(PAIR):
            scatter(a_ref, c + 4 * k, 8, spread[c][k * STEPS : (k + 1) * STEPS])

    def backward(n, _):
        i = (n + 1) % STEPS
        a = get_rows(a_ref, pl.ds(pl.multiple_of(i * 8, 8), 8))
        a_high, a_low = halves(a)
        c_high, c_low = halves(tile_of(held, i, 16))
        columns = jnp.transpose(jnp.concatenate([a_high, a_low, a_high, a], axis=0))
        v_lhs = columns.astype(bf16)
        tint = None
        for k in range(PAIR):
            ch, cl = jnp.where(own_rows[k], c_high, 0.0), jnp.where(own_rows[k], c_low, 0.0)
            v_rhs = jnp.concatenate([ch, ch, cl, jnp.zeros_like(cl)], axis=0).astype(bf16)
            w2 = w_ref[i, k]
            w_high, w_low = w2[:, :BLOCK], w2[:, BLOCK:]
            value = (w_high.astype(f32) + w_low.astype(f32)) * dot(v_lhs, v_rhs)
            beyond = dot(split2(value), upto) + columns[:, 27 + 4 * k : 28 + 4 * k]
            d2 = split2(value + ratio_ref[i, k] * beyond)
            moments = dot(mono_rows, d2[:, :BLOCK]) + dot(mono_rows, d2[:, BLOCK:])
            put_rows(packed.at[i], pl.ds(8 * k, 8), moments)
            lhs = jnp.concatenate([jnp.where(own_rows[k], a_high, 0.0), jnp.where(own_rows[k], a_low, 0.0)], axis=0)
            lhs = lhs.astype(bf16)
            grads = dot(lhs, w_high) + dot(lhs, w_low)
            grads = grads[:8] + grads[8:]
            tint = grads if tint is None else tint + grads
        put_rows(packed.at[i], pl.ds(16, 8), tint)

        @pl.when(i > 0)
        def _():
            give(i).start()

        return 0

    lax.fori_loop(0, STEPS, backward, 0)
    landed[:, 0:MSG, :] = packed[0]
    each(lambda i: give(i).wait_recv())
    cut = 9 * OWNED // 2
    for r in range(9):
        at = (r, 8 + r) if r < 6 else (10 + r, 14 + r)
        found = jnp.concatenate([gather(landed, at[k], MSG) for k in range(PAIR)], axis=0)
        sums[r * OWNED : (r + 1) * OWNED, :] = dot(put, stack3(found))

    at_mine = pl.multiple_of(mine * cut, 8)
    at_other = pl.multiple_of((1 - mine) * cut, 8)
    one = exchange(sums.at[pl.ds(at_other, cut)], got_core, attr_sems, 2, (tile, core))
    one.start()
    one.wait()
    half[...] = sums[pl.ds(at_mine, cut), :] + got_core[...]
    two = exchange(half, got_across, attr_sems, 3, (tile, across))
    two.start()
    two.wait()
    half_sum = half[...] + got_across[...]
    half[...] = half_sum
    three = exchange(half, got_rest, attr_sems, 4, (tile, core))
    three.start()
    out_ref[pl.ds(at_mine, cut), :] = half_sum
    three.wait()
    out_ref[pl.ds(at_other, cut), :] = got_rest[...]
    each(lambda i: ask(i).wait_send())
    each(lambda i: back(i).wait_send())
    each(lambda i: give(i).wait_send())


def fused(geometry, view_angles, sh_coeffs, visible, order, cot, counts):
    bands = sh_coeffs.shape[0] // 3
    sems = pltpu.SemaphoreType.DMA
    vmem = pl.BlockSpec(memory_space=pltpu.VMEM)
    ins = (geometry, view_angles, sh_coeffs, visible, order, cot, counts)
    colours, cut = 3 * OWNED, 9 * OWNED // 2
    shapes = (cot.shape, (bands, OWNED, BLOCK), (11, OWNED, BLOCK), (9 * OWNED, BLOCK))
    return pl.pallas_call(
        functools.partial(fused_kernel, bands),
        name="splat",
        out_shape=tuple(jax.ShapeDtypeStruct(o, jnp.float32) for o in shapes),
        in_specs=[pl.BlockSpec(memory_space=pltpu.HBM)] * len(ins),
        out_specs=tuple(vmem for _ in shapes),
        scratch_shapes=[pltpu.VMEM(x.shape, x.dtype) for x in ins[:-1]] + [
            pltpu.SMEM(counts.shape, counts.dtype),
            floats(BLOCK // 128, 8 * OWNED, 128), floats(BLOCK // 128, 8 * OWNED, 128),
            floats(BLOCK // 128, 16 * OWNED, 128), floats(16, OWNED, BLOCK),
            pltpu.VMEM((6, TRIPLE * OWNED, BLOCK), jnp.bfloat16), floats(colours, BLOCK), floats(colours, BLOCK),
            floats(colours, BLOCK), floats(colours, BLOCK), floats(8, 128),
            floats(8 * STEPS, 128), floats(8 * STEPS, 128), floats(2, STEPS * MSG, 128), floats(STEPS, 2, MSG, 128),
            pltpu.VMEM((STEPS, PAIR, PIX, 2 * BLOCK), jnp.bfloat16), floats(STEPS, PAIR, PIX, BLOCK),
            floats(PIX, 128), floats(2, 8 * STEPS, 128), floats(2, 8 * STEPS, 128),
            floats(STEPS, 2, MSG, 128), floats(2, STEPS * MSG, 128), floats(9 * OWNED, BLOCK),
            floats(cut, BLOCK), floats(cut, BLOCK), floats(cut, BLOCK), floats(cut, BLOCK),
            sems((len(ins),)), sems((2, STEPS)), sems((2, STEPS)), sems((2, STEPS)), sems((2, 5)),
        ],
        compiler_params=pltpu.CompilerParams(
            collective_id=3, has_side_effects=True, vmem_limit_bytes=40 * 1024 * 1024
        ),
    )(*[pltpu.with_memory_space_constraint(x, pltpu.HBM) for x in ins])


def finish_kernel(bands, sums_ref, terms_ref, basis_ref, pic_ref, geometry_ref, coeffs_ref, picture_ref, geo, coe):
    final_kernel(OWNED, bands, sums_ref, terms_ref, basis_ref, geometry_ref, coeffs_ref, geo, coe)
    picture_ref[...] = pic_ref[...]


def finish(sums, terms, basis, pic):
    bands = basis.shape[0]
    vmem = pl.BlockSpec(memory_space=pltpu.VMEM)
    shapes = ((6, OWNED * BLOCK), (3 * bands, OWNED * BLOCK), pic.shape)
    return pl.pallas_call(
        functools.partial(finish_kernel, bands),
        name="finish",
        out_shape=tuple(jax.ShapeDtypeStruct(o, jnp.float32) for o in shapes),
        in_specs=[vmem] * 4,
        out_specs=(vmem,) * 3,
        scratch_shapes=[
            floats(BLOCK // 128, 8 * OWNED, 128),
            floats(BLOCK // 128, 16 * OWNED, 128),
        ],
        compiler_params=pltpu.CompilerParams(vmem_limit_bytes=12 * 1024 * 1024),
    )(sums, terms, basis, pic)


def local_fused(geometry, sh_coeffs, view_angles, visible, counts, order, image_cot):
    cot = jnp.swapaxes(image_cot, 0, 1)
    pic, basis, terms, sums = fused(geometry, view_angles, sh_coeffs, visible, order, cot, counts)
    grad_geometry, grad_sh, picture = finish(sums, terms, basis, pic)
    return (jnp.swapaxes(picture, 0, 1), grad_geometry, grad_sh)


def local(geometry, sh_coeffs, view_angles, visible, counts, order, image_cot):
    owners = lax.axis_size("tile")
    tiles, vis = visible.shape
    owned = geometry.shape[1] // BLOCK
    fits = (owners, vis, tiles, owned, lax.axis_size("attr")) == (8, 16, 2, 32, 4)
    run = local_fused if fits else local_general
    return run(geometry, sh_coeffs, view_angles, visible, counts, order, image_cot)


def solution(mesh):
    in_specs = (
        P(None, "tile"),
        P("attr", "tile"),
        P(None, "tile"),
        P(("tile", "attr"), None),
        P(("tile", "attr")),
        P(("tile", "attr"), None),
        P(("tile", "attr"), None, None),
    )
    out_specs = (P(("tile", "attr"), None, None), P(None, "tile"), P("attr", "tile"))
    return jax.shard_map(local, mesh=mesh, in_specs=in_specs, out_specs=out_specs, check_vma=False)
```

```python
import functools
import jax
import jax.numpy as jnp
from jax import lax
from jax.experimental import pallas as pl
from jax.experimental.pallas import tpu as pltpu
from jax.sharding import PartitionSpec as P

BLOCK = 256
SIDE = 16
PIX = SIDE * SIDE
MID = 0.5 * SIDE
LOG2E = 1.4426950408889634
LN2 = 0.6931471805599453


band_zero = 0.28209479177387814
band_one = 0.4886025119029199
band_two = (
    1.0925484305920792,
    -1.0925484305920792,
    0.31539156525252005,
    -1.0925484305920792,
    0.5462742152960396,
)
band_three = (
    -0.5900435899266435,
    2.890611442640554,
    -0.4570457994644658,
    0.3731763325901154,
    -0.4570457994644658,
    1.445305721320277,
    -0.5900435899266435,
)


def sh_basis(view_angles):
    azimuth = view_angles[0]
    elevation = view_angles[1]
    dir_x = jnp.cos(azimuth) * jnp.cos(elevation)
    dir_y = jnp.sin(azimuth) * jnp.cos(elevation)
    dir_z = jnp.sin(elevation)
    sq_x = dir_x * dir_x
    sq_y = dir_y * dir_y
    sq_z = dir_z * dir_z
    basis_rows = [
        band_zero * jnp.ones_like(dir_x),
        -band_one * dir_y,
        band_one * dir_z,
        -band_one * dir_x,
        band_two[0] * dir_x * dir_y,
        band_two[1] * dir_y * dir_z,
        band_two[2] * (2.0 * sq_z - sq_x - sq_y),
        band_two[3] * dir_x * dir_z,
        band_two[4] * (sq_x - sq_y),
        band_three[0] * dir_y * (3.0 * sq_x - sq_y),
        band_three[1] * dir_x * dir_y * dir_z,
        band_three[2] * dir_y * (4.0 * sq_z - sq_x - sq_y),
        band_three[3] * dir_z * (2.0 * sq_z - 3.0 * sq_x - 3.0 * sq_y),
        band_three[4] * dir_x * (4.0 * sq_z - sq_x - sq_y),
        band_three[5] * dir_z * (sq_x - sq_y),
        band_three[6] * dir_x * (sq_x - 3.0 * sq_y),
    ]
    return basis_rows


def split2(x):
    high = x.astype(jnp.bfloat16)
    low = (x - high.astype(jnp.float32)).astype(jnp.bfloat16)
    return jnp.concatenate([high, low], axis=1)


def dot(a, b):
    return jnp.dot(a, b, preferred_element_type=jnp.float32)


def blend_kernel(tiles, seq_ref, counts_ref, held_ref, cot_rows_ref, cot_cols_ref, pic_ref, grad_ref, part_ref, ratio_ref):
    f32, bf16 = jnp.float32, jnp.bfloat16
    row = lax.broadcasted_iota(jnp.int32, (2 * BLOCK, BLOCK), 0)
    row = jnp.where(row >= BLOCK, row - BLOCK, row)
    col = lax.broadcasted_iota(jnp.int32, (2 * BLOCK, BLOCK), 1)
    before = jnp.where(row < col, -1.0, 0.0).astype(bf16)
    upto = jnp.where(row <= col, 1.0, 0.0).astype(bf16)

    def monomials(shape, dim, width):
        pixel = lax.broadcasted_iota(jnp.int32, shape, dim)
        kind = lax.broadcasted_iota(jnp.int32, shape, 1 - dim) & (width - 1)
        x = (pixel & (SIDE - 1)).astype(f32) + (0.5 - MID)
        y = (pixel // SIDE).astype(f32) + (0.5 - MID)
        out = jnp.where(kind == 0, 1.0, 0.0)
        for k, value in ((1, x), (2, y), (3, x * x), (4, x * y), (5, y * y)):
            out = jnp.where(kind == k, value, out)
        return out.astype(bf16)

    mono_cols = monomials((PIX, 48), 0, 16)
    mono_rows = monomials((8, PIX), 1, 8)
    cot_lhs, cot_rows = [], []
    for t in range(tiles):
        g = cot_cols_ref[t]
        high = g.astype(bf16).astype(f32)
        lane = lax.broadcasted_iota(jnp.int32, g.shape, 1)
        cot_lhs.append(jnp.where(lane < 48, high, g - high).astype(bf16))
        g = cot_rows_ref[t]
        high = g.astype(bf16).astype(f32)
        cot_rows.append(jnp.concatenate([high, g - high], axis=0).astype(bf16))

    grad_ref[...] = jnp.zeros_like(grad_ref)
    lives = [counts_ref[t] for t in range(tiles)]
    longest = functools.reduce(jnp.maximum, lives)

    lhs = []
    for t in range(tiles):
        wide = jnp.concatenate([mono_cols.astype(f32), jnp.zeros((PIX, 48), f32)], axis=1)
        lhs.append(jnp.concatenate([wide.astype(bf16), cot_lhs[t]], axis=0))
    head = lax.broadcasted_iota(jnp.int32, (16, BLOCK), 0) == 0

    def forward(j, carry):
        keep_before, sum_before, pictures = carry
        alphas, values, losses, helds, spots = [], [], [], [], []
        for t in range(tiles):
            at = seq_ref[t, j]
            hidden = jnp.where(j < lives[t], 0.0, -16384.0)
            held = held_ref[at]
            parts = split3(jnp.where(head, held + hidden, held))
            rows = jnp.concatenate(parts, axis=0)
            both = dot(lhs[t], jnp.concatenate([rows, rows], axis=0))
            alpha = jnp.exp2(both[:PIX])
            alphas.append(alpha)
            values.append(both[PIX:])
            losses.append(jnp.log(1.0 - alpha) * -LOG2E)
            helds.append(jnp.concatenate(parts[:2], axis=0))
            spots.append(at)
        loss = jnp.concatenate(losses, axis=0)
        keep_in = dot(split2(loss), before) + keep_before
        keep_before = keep_in[:, BLOCK - 1 :] - loss[:, BLOCK - 1 :]
        alpha = jnp.concatenate(alphas, axis=0)
        weight = alpha * jnp.exp2(keep_in)
        value = weight * jnp.concatenate(values, axis=0)
        total = dot(split2(value), upto) + sum_before
        sum_before = total[:, BLOCK - 1 :]
        ratio = alpha * jnp.exp2(loss)
        part_ref[j] = value + ratio * total
        ratio_ref[j] = ratio
        w2 = split2(weight)
        shown = []
        for t in range(tiles):
            w_high, w_low = w2[t * PIX : (t + 1) * PIX, :BLOCK], w2[t * PIX : (t + 1) * PIX, BLOCK:]
            rows = lax.dot_general(helds[t], w_high, (((1,), (1,)), ((), ())), preferred_element_type=f32)
            rows = rows + lax.dot_general(helds[t], w_low, (((1,), (1,)), ((), ())), preferred_element_type=f32)
            shown.append(pictures[t] + rows[:16] + rows[16:])
            colour_grad = dot(cot_rows[t], w_high) + dot(cot_rows[t], w_low)
            grad_ref[spots[t], 0:8, :] += colour_grad[:8] + colour_grad[8:]
        return keep_before, sum_before, tuple(shown)

    zero = jnp.zeros((tiles * PIX, 1), f32)
    start = (zero, zero, tuple(jnp.zeros((16, PIX), f32) for _ in range(tiles)))
    _, ends, pictures = lax.fori_loop(0, longest, forward, start)
    for t in range(tiles):
        pic_ref[t] = pictures[t]

    def backward(j, _):
        for t in range(tiles):
            pixels = slice(t * PIX, (t + 1) * PIX)
            d2 = split2(part_ref[j, pixels] - ratio_ref[j, pixels] * ends[pixels])
            moments = dot(mono_rows, d2[:, :BLOCK]) + dot(mono_rows, d2[:, BLOCK:])
            grad_ref[seq_ref[t, j], 8:16, :] += moments
        return 0

    lax.fori_loop(0, longest, backward, 0)


def blend(seq, counts, held, image_cot):
    tiles = image_cot.shape[0]
    rows = held.shape[0]
    cot_rows = jnp.pad(image_cot, ((0, 0), (0, 5), (0, 0)))
    cot_cols = jnp.pad(jnp.swapaxes(image_cot, 1, 2), ((0, 0), (0, 0), (6, 7)))
    cot_cols = jnp.tile(cot_cols, (1, 1, 6))
    smem = pl.BlockSpec(memory_space=pltpu.SMEM)
    vmem = pl.BlockSpec(memory_space=pltpu.VMEM)
    picture, grads = pl.pallas_call(
        functools.partial(blend_kernel, tiles),
        name="blend",
        out_shape=(
            jax.ShapeDtypeStruct((tiles, 16, PIX), jnp.float32),
            jax.ShapeDtypeStruct((rows, 16, BLOCK), jnp.float32),
        ),
        in_specs=[smem, smem, vmem, vmem, vmem],
        out_specs=(vmem, vmem),
        scratch_shapes=[
            pltpu.VMEM((seq.shape[1], tiles * PIX, BLOCK), jnp.float32),
            pltpu.VMEM((seq.shape[1], tiles * PIX, BLOCK), jnp.float32),
        ],
        compiler_params=pltpu.CompilerParams(vmem_limit_bytes=28 * 1024 * 1024),
    )(seq, counts, held, cot_rows, cot_cols)
    return picture[:, 6:9], grads


def splat_terms(geometry):
    mx, my = geometry[0] - MID, geometry[1] - MID
    c, s = jnp.cos(geometry[4]), jnp.sin(geometry[4])
    e1, e2 = jnp.exp(-2.0 * geometry[2]), jnp.exp(-2.0 * geometry[3])
    cc, ss, cs = c * c, s * s, c * s
    a = cc * e1 + ss * e2
    b = cs * (e1 - e2)
    d = ss * e1 + cc * e2
    return mx, my, e1, e2, cc, ss, cs, a, b, d, geometry[5]


def exponent_rows(terms):
    mx, my, e1, e2, cc, ss, cs, a, b, d, logit = terms
    bx, by = a * mx + b * my, b * mx + d * my
    log_opacity = jnp.minimum(logit, 0.0) - jnp.log1p(jnp.exp(-jnp.abs(logit)))
    one = log_opacity - 0.5 * (mx * bx + my * by)
    return [LOG2E * r for r in (one, bx, by, -0.5 * a, -b, -0.5 * d)]


def geometry_grads(terms, m):
    mx, my, e1, e2, cc, ss, cs, a, b, d, logit = terms
    n0 = m[0]
    nx, ny = m[1] - mx * n0, m[2] - my * n0
    nxx = m[3] - mx * (m[1] + nx)
    nxy = m[4] - mx * m[2] - my * nx
    nyy = m[5] - my * (m[2] + ny)
    return [
        a * nx + b * ny,
        b * nx + d * ny,
        e1 * (cc * nxx + 2.0 * cs * nxy + ss * nyy),
        e2 * (ss * nxx - 2.0 * cs * nxy + cc * nyy),
        (e2 - e1) * (cs * (nyy - nxx) + (cc - ss) * nxy),
        n0 / (1.0 + jnp.exp(logit)),
    ]


MESH = pl.DeviceIdType.MESH


def greet(peers):
    barrier = pltpu.get_barrier_semaphore()
    tile, attr, owners, extra = peers

    def hello(step, _):
        other = (tile + step) % owners
        pl.semaphore_signal(barrier, inc=1, device_id=(other, attr), device_id_type=MESH)
        return 0

    lax.fori_loop(1, owners, hello, 0)
    for other in extra:
        pl.semaphore_signal(barrier, inc=1, device_id=(tile, other), device_id_type=MESH)
    return barrier, owners - 1 + len(extra)


def split3(x):
    high = x.astype(jnp.bfloat16)
    rest = x - high.astype(jnp.float32)
    mid = rest.astype(jnp.bfloat16)
    return high, mid, (rest - mid.astype(jnp.float32)).astype(jnp.bfloat16)


def exchange(src, dst, sems, k, device):
    return pltpu.make_async_remote_copy(
        src_ref=src, dst_ref=dst, send_sem=sems.at[0, k], recv_sem=sems.at[1, k],
        device_id=device, device_id_type=MESH,
    )


def fetch_kernel(dims, want_ref, coef_ref, part_ref, held_ref, asked_ref,
                 asks, answer, landed, first, summed, second, tile_sems, back_sems, attr_sems):
    owners, owned, cap, message, stride = dims
    f32 = jnp.float32
    tile, attr = lax.axis_index("tile"), lax.axis_index("attr")
    core = attr + 1 - 2 * (attr % 2)
    across = (attr + 2) % 4
    pl.semaphore_wait(*greet((tile, attr, owners, (core, across))))

    colour_one = exchange(part_ref, first, attr_sems, 0, (tile, core))
    colour_one.start()

    def ask(other, sender):
        return pltpu.make_async_remote_copy(
            src_ref=want_ref.at[other], dst_ref=asks.at[sender],
            send_sem=tile_sems.at[0, other], recv_sem=tile_sems.at[1, sender],
            device_id=(other, attr), device_id_type=MESH,
        )

    def send_ask(step, _):
        ask((tile + step) % owners, tile).start()
        return 0

    lax.fori_loop(1, owners, send_ask, 0)
    asks[tile] = want_ref[tile]

    colour_one.wait()
    summed[...] = part_ref[...] + first[...]
    colour_two = exchange(summed, second, attr_sems, 1, (tile, across))
    colour_two.start()

    def take_ask(step, _):
        other = (tile + step) % owners
        ask(other, other).wait()
        return 0

    lax.fori_loop(1, owners, take_ask, 0)

    per = 128 // stride
    lanes = owners // per
    rows = []
    for tile_at in range(lanes):
        rows.append(functools.reduce(jnp.add, [asks[tile_at * per + k] for k in range(per)]))
    asked = jnp.concatenate(rows, axis=1) - 1.0
    asked_ref[...] = asked
    wide = 9 * owned
    columns = []
    for tile_at in range(lanes):
        square = jnp.concatenate([rows[tile_at] - 1.0] * 16, axis=0)
        columns.append(jnp.transpose(square)[:, 0:1])
    column = jnp.concatenate(columns, axis=0)
    lane = lax.broadcasted_iota(jnp.int32, (owners * stride, wide), 1).astype(f32)
    pick = jnp.where(lane == column, 1.0, 0.0).astype(jnp.bfloat16)

    colour_two.wait()
    colour = summed[...] + second[...] + 0.5
    table = jnp.concatenate([coef_ref[...], colour], axis=0)
    high, mid, low = split3(table)
    answer[...] = (dot(pick, low) + dot(pick, mid)) + dot(pick, high)

    def back(other, sender):
        at = pl.multiple_of(other * stride, 8)
        return pltpu.make_async_remote_copy(
            src_ref=answer.at[pl.ds(at, message)], dst_ref=landed.at[sender],
            send_sem=back_sems.at[0, other], recv_sem=back_sems.at[1, sender],
            device_id=(other, attr), device_id_type=MESH,
        )

    def send_back(step, _):
        back((tile + step) % owners, tile).start()
        return 0

    lax.fori_loop(1, owners, send_back, 0)
    landed[tile] = answer[pl.ds(pl.multiple_of(tile * stride, 8), message), :]
    held_ref[...] = jnp.zeros_like(held_ref)

    def take_back(step, _):
        other = (tile + step) % owners
        back(other, other).wait()
        return 0

    lax.fori_loop(1, owners, take_back, 0)

    def unpack(o, _):
        for k in range(cap):
            held_ref[o * cap + k, 0:9, :] = landed[o, 9 * k : 9 * k + 9, :]
        return 0

    lax.fori_loop(0, owners, unpack, 0)


def give_kernel(dims, grads_ref, asked_ref, out_ref,
                packed, landed, sums, first, half, second, third, tile_sems, attr_sems):
    owners, owned, cap, message, stride = dims
    f32 = jnp.float32
    tile, attr = lax.axis_index("tile"), lax.axis_index("attr")
    core = attr + 1 - 2 * (attr % 2)
    across = (attr + 2) % 4
    mine = attr % 2

    if message < stride:
        landed[...] = jnp.zeros_like(landed)
    greeted = greet((tile, attr, owners, (core, across)))
    packed[...] = jnp.zeros_like(packed)

    def pack(o, _):
        for k in range(cap):
            packed[o, 9 * k : 9 * k + 6, :] = grads_ref[o * cap + k, 8:14, :]
            packed[o, 9 * k + 6 : 9 * k + 9, :] = grads_ref[o * cap + k, 0:3, :]
        return 0

    lax.fori_loop(0, owners, pack, 0)
    pl.semaphore_wait(*greeted)

    def give(other, sender):
        at = pl.multiple_of(sender * stride, 8)
        return pltpu.make_async_remote_copy(
            src_ref=packed.at[other], dst_ref=landed.at[pl.ds(at, message)],
            send_sem=tile_sems.at[0, other], recv_sem=tile_sems.at[1, sender],
            device_id=(other, attr), device_id_type=MESH,
        )

    def send_give(step, _):
        give((tile + step) % owners, tile).start()
        return 0

    lax.fori_loop(1, owners, send_give, 0)
    landed[pl.ds(pl.multiple_of(tile * stride, 8), message), :] = packed[tile]
    wide = 9 * owned
    row = lax.broadcasted_iota(jnp.int32, (wide, owners * stride), 0).astype(f32)
    pick = jnp.where(row == asked_ref[0:1, :], 1.0, 0.0).astype(jnp.bfloat16)

    def take_give(step, _):
        other = (tile + step) % owners
        give(other, other).wait()
        return 0

    lax.fori_loop(1, owners, take_give, 0)
    high, mid, low = split3(landed[...])
    total = (dot(pick, low) + dot(pick, mid)) + dot(pick, high)
    cut = wide // 2
    sums[0] = total[:cut]
    sums[1] = total[cut:]

    one = exchange(sums.at[1 - mine], first, attr_sems, 0, (tile, core))
    one.start()
    one.wait()
    half[...] = sums[mine] + first[...]
    two = exchange(half, second, attr_sems, 1, (tile, across))
    two.start()
    two.wait()
    half_sum = half[...] + second[...]
    first[...] = half_sum
    three = exchange(first, third, attr_sems, 2, (tile, core))
    three.start()
    three.wait()
    at = pl.multiple_of(mine * cut, 8)
    out_ref[pl.ds(at, cut), :] = half_sum
    at = pl.multiple_of((1 - mine) * cut, 8)
    out_ref[pl.ds(at, cut), :] = third[...]


def remote_call(kernel, dims, outs, ins, scratch, number, name):
    vmem = pl.BlockSpec(memory_space=pltpu.VMEM)
    return pl.pallas_call(
        functools.partial(kernel, dims),
        name=name,
        out_shape=tuple(jax.ShapeDtypeStruct(o, jnp.float32) for o in outs),
        in_specs=[vmem] * len(ins),
        out_specs=tuple(vmem for _ in outs),
        scratch_shapes=scratch,
        compiler_params=pltpu.CompilerParams(
            collective_id=number, has_side_effects=True, vmem_limit_bytes=20 * 1024 * 1024
        ),
    )(*ins)


def floats(*shape):
    return pltpu.VMEM(shape, jnp.float32)


def fetch(dims, want, coef, part):
    owners, owned, cap, message, stride = dims
    sems = pltpu.SemaphoreType.DMA
    return remote_call(
        fetch_kernel, dims,
        ((owners * cap, 16, BLOCK), (8, owners * stride)),
        (want, coef, part),
        [floats(owners, 8, 128), floats(owners * stride, BLOCK), floats(owners, message, BLOCK),
         floats(3 * owned, BLOCK), floats(3 * owned, BLOCK), floats(3 * owned, BLOCK),
         sems((2, owners)), sems((2, owners)), sems((2, 2))],
        1, "fetch",
    )


def give_back(dims, grads, asked):
    owners, owned, cap, message, stride = dims
    sems = pltpu.SemaphoreType.DMA
    cut = 9 * owned // 2
    return remote_call(
        give_kernel, dims, ((9 * owned, BLOCK),), (grads, asked),
        [floats(owners, message, BLOCK), floats(owners * stride, BLOCK), floats(2, cut, BLOCK),
         floats(cut, BLOCK), floats(cut, BLOCK), floats(cut, BLOCK), floats(cut, BLOCK),
         sems((2, owners)), sems((2, 3))],
        2, "give",
    )[0]


def prep_kernel(owned, bands, geometry_ref, angles_ref, coeffs_ref, coef_ref, part_ref, basis_ref, terms_ref,
                geo, ang, coe, rows):
    def relay(b, _):
        for h in range(BLOCK // 128):
            at = pl.ds(pl.multiple_of(b * BLOCK + h * 128, 128), 128)
            geo[h, pl.ds(pl.multiple_of(b * 8, 8), 6), :] = geometry_ref[:, at]
            ang[h, pl.ds(pl.multiple_of(b * 8, 8), 2), :] = angles_ref[:, at]
            coe[h, pl.ds(pl.multiple_of(b * 16, 8), 3 * bands), :] = coeffs_ref[:, at]
        return 0

    lax.fori_loop(0, owned, relay, 0, unroll=4)

    def plane(ref, k, pitch):
        halves = [ref[h, pl.ds(k, owned, stride=pitch), :] for h in range(BLOCK // 128)]
        return jnp.concatenate(halves, axis=1)

    terms = splat_terms([plane(geo, k, 8) for k in range(6)])
    for k, value in enumerate(terms):
        terms_ref[k] = value
    for k, value in enumerate(exponent_rows(terms)):
        coef_ref[k * owned : (k + 1) * owned, :] = value
    for k, value in enumerate(sh_basis([plane(ang, k, 8) for k in range(2)])):
        rows[k] = value
    first = lax.axis_index("attr") * bands
    total = [jnp.zeros((owned, BLOCK), jnp.float32) for _ in range(3)]
    for k in range(bands):
        value = rows[first + k]
        basis_ref[k] = value
        for c in range(3):
            total[c] = total[c] + value * plane(coe, 3 * k + c, 16)
    for c in range(3):
        part_ref[c * owned : (c + 1) * owned, :] = total[c]


def prep(geometry, view_angles, sh_coeffs, owned):
    bands = sh_coeffs.shape[0] // 3
    vmem = pl.BlockSpec(memory_space=pltpu.VMEM)
    shapes = ((6 * owned, BLOCK), (3 * owned, BLOCK), (bands, owned, BLOCK), (11, owned, BLOCK))
    return pl.pallas_call(
        functools.partial(prep_kernel, owned, bands),
        name="prep",
        out_shape=tuple(jax.ShapeDtypeStruct(o, jnp.float32) for o in shapes),
        in_specs=[vmem] * 3,
        out_specs=(vmem,) * 4,
        scratch_shapes=[
            floats(BLOCK // 128, 8 * owned, 128),
            floats(BLOCK // 128, 8 * owned, 128),
            floats(BLOCK // 128, 16 * owned, 128),
            floats(16, owned, BLOCK),
        ],
        compiler_params=pltpu.CompilerParams(vmem_limit_bytes=12 * 1024 * 1024),
    )(geometry, view_angles, sh_coeffs)


def final_kernel(owned, bands, sums_ref, terms_ref, basis_ref, geometry_ref, coeffs_ref, geo, coe):
    summed = [sums_ref[k * owned : (k + 1) * owned, :] for k in range(9)]

    def put(ref, k, pitch, value):
        for h in range(BLOCK // 128):
            ref[h, pl.ds(k, owned, stride=pitch), :] = value[:, h * 128 : (h + 1) * 128]

    for k, value in enumerate(geometry_grads([terms_ref[k] for k in range(11)], summed[:6])):
        put(geo, k, 8, value)
    for k in range(bands):
        for c in range(3):
            put(coe, 3 * k + c, 16, basis_ref[k] * summed[6 + c])

    def relay(b, _):
        for h in range(BLOCK // 128):
            at = pl.ds(pl.multiple_of(b * BLOCK + h * 128, 128), 128)
            geometry_ref[:, at] = geo[h, pl.ds(pl.multiple_of(b * 8, 8), 6), :]
            coeffs_ref[:, at] = coe[h, pl.ds(pl.multiple_of(b * 16, 8), 3 * bands), :]
        return 0

    lax.fori_loop(0, owned, relay, 0, unroll=4)


def final(sums, terms, basis, owned):
    bands = basis.shape[0]
    vmem = pl.BlockSpec(memory_space=pltpu.VMEM)
    shapes = ((6, owned * BLOCK), (3 * bands, owned * BLOCK))
    return pl.pallas_call(
        functools.partial(final_kernel, owned, bands),
        name="final",
        out_shape=tuple(jax.ShapeDtypeStruct(o, jnp.float32) for o in shapes),
        in_specs=[vmem] * 3,
        out_specs=(vmem,) * 2,
        scratch_shapes=[
            floats(BLOCK // 128, 8 * owned, 128),
            floats(BLOCK // 128, 16 * owned, 128),
        ],
        compiler_params=pltpu.CompilerParams(vmem_limit_bytes=12 * 1024 * 1024),
    )(sums, terms, basis)


def local_general(geometry, sh_coeffs, view_angles, visible, counts, order, image_cot):
    owners = lax.axis_size("tile")
    owned = geometry.shape[1] // BLOCK
    vis = visible.shape[1]
    cap = (vis + owners - 1) // owners
    coef, partial_colour, my_basis, terms = prep(geometry, view_angles, sh_coeffs, owned)

    ids = visible[0]
    owner_of, local_of = ids // owned, ids % owned
    position = jnp.arange(vis)
    rank = jnp.sum(((owner_of[None, :] == owner_of[:, None]) & (position[None, :] < position[:, None])).astype(jnp.int32), 1)
    slot = owner_of * cap + rank
    message = -(-9 * cap // 8) * 8
    stride = 16 if message <= 16 else 32
    dims = (owners, owned, cap, message, stride)
    lane = jnp.arange(128) - (lax.axis_index("tile") % (128 // stride)) * stride
    in_slot = lane[None, :, None] // 9 + jnp.arange(owners)[:, None, None] * cap
    hit = (slot[None, None, :] == in_slot) & (lane >= 0)[None, :, None] & (lane < 9 * cap)[None, :, None]
    want = jnp.sum(jnp.where(hit, 1 + local_of[None, None, :] + owned * (lane % 9)[None, :, None], 0), 2)
    want = jnp.broadcast_to(want.astype(jnp.float32)[:, None, :], (owners, 8, 128))
    slot_of = jnp.sum(jnp.where(visible[:, :, None] == ids[None, None, :], slot[None, None, :], 0), 2)
    seq = jnp.sum(jnp.where(order[:, :, None] == position[None, None, :], slot_of[:, None, :], 0), 2)

    held, asked = fetch(dims, want, coef, partial_colour)
    picture, grads = blend(seq, counts, held, image_cot)
    sums = give_back(dims, grads, asked)
    grad_geometry, grad_sh = final(sums, terms, my_basis, owned)
    return (picture, grad_geometry, grad_sh)


STEPS = 8
PAIR = 2
SLOTS = STEPS * PAIR
OWNED = 32
MSG = 24
TRIPLE = 3


def stack3(x):
    high, mid, low = split3(x)
    return jnp.concatenate([high, mid, low], axis=0)


def lane_halves(x):
    return [x[:, h * 128 : (h + 1) * 128] for h in range(BLOCK // 128)]


def put_rows(ref, rows, value):
    for h, part in enumerate(lane_halves(value)):
        ref[h, rows, :] = part


def get_rows(ref, rows):
    return jnp.concatenate([ref[h, rows, :] for h in range(BLOCK // 128)], axis=1)


def scatter(ref, at, pitch, value):
    put_rows(ref, pl.ds(at, STEPS, stride=pitch), value)


def gather(ref, at, pitch):
    return get_rows(ref, pl.ds(at, STEPS, stride=pitch))


def tile_of(ref, i, at):
    return jnp.concatenate([ref[i, h, at : at + 8, :] for h in range(BLOCK // 128)], axis=1)


def pixel_monomials(shape, dim):
    pixel = lax.broadcasted_iota(jnp.int32, shape, dim)
    kind = lax.broadcasted_iota(jnp.int32, shape, 1 - dim) & 7
    x = (pixel & (SIDE - 1)).astype(jnp.float32) + (0.5 - MID)
    y = (pixel // SIDE).astype(jnp.float32) + (0.5 - MID)
    out = jnp.where(kind == 0, 1.0, 0.0)
    for k, value in ((1, x), (2, y), (3, x * x), (4, x * y), (5, y * y)):
        out = jnp.where(kind == k, value, out)
    return out.astype(jnp.bfloat16)


def slot_tables(tile, visible, order, counts_ref):
    f32 = jnp.float32
    sub = lax.broadcasted_iota(jnp.int32, (SLOTS, SLOTS), 0)
    lane = lax.broadcasted_iota(jnp.int32, (SLOTS, SLOTS), 1)
    diagonal = sub == lane
    lane_f, sub_f = lane.astype(f32), sub.astype(f32)

    def to_column(row):
        return jnp.sum(jnp.where(diagonal, row, 0.0), axis=1, keepdims=True)

    def to_row(column):
        return jnp.sum(jnp.where(diagonal, column, 0.0), axis=0, keepdims=True)

    ids = visible[0:1]
    owner = ids // OWNED
    near = owner - tile
    near = jnp.where(near < 0, near + STEPS, near).astype(f32)
    ids_f = ids.astype(f32)
    inside = (ids - owner * OWNED).astype(f32)
    near_column = to_column(near)
    second = jnp.sum(jnp.where((near_column == near) & (sub < lane), 1.0, 0.0), axis=0, keepdims=True)
    slot = second * STEPS + near
    match = sub_f == slot
    local_id = jnp.sum(jnp.where(match, inside, 0.0), axis=1, keepdims=True)
    slot_id = jnp.sum(jnp.where(match, ids_f, 0.0), axis=1, keepdims=True)
    ahead, live = [], []
    for t in range(2):
        listed = to_column(visible[t : t + 1].astype(f32))
        here = sub == order[t : t + 1]
        sequence = jnp.sum(jnp.where(here, listed, 0.0), axis=0, keepdims=True)
        rank = jnp.sum(jnp.where(sequence == slot_id, lane_f, 0.0), axis=1, keepdims=True)
        ahead.append(jnp.where(to_row(rank) < rank, 1.0, 0.0))
        live.append(jnp.where(rank < counts_ref[t].astype(f32), 1.0, 0.0))
    return local_id, ahead, live


def fused_kernel(bands, geometry_hbm, angles_hbm, coeffs_hbm, visible_hbm, order_hbm, cot_hbm, counts_hbm,
                 pic_ref, basis_ref, terms_ref, out_ref,
                 geometry, angles, coeffs, visible, order, cot, counts_ref, geo, ang, coe, rows,
                 coef, part, first, summed, second, colour,
                 asks_out, asks, answer, held, w_ref, ratio_ref, loss_ref, c_ref, a_ref,
                 packed, landed, sums, got_core, all_picks, d_ref,
                 local_sems, ask_sems, back_sems, give_sems, share_sems, attr_sems):
    f32, bf16 = jnp.float32, jnp.bfloat16
    tile, attr = lax.axis_index("tile"), lax.axis_index("attr")
    core = attr + 1 - 2 * (attr % 2)
    across = (attr + 2) % 4
    mine = attr % 2
    greeted = greet((tile, attr, STEPS, (core, across, (core + 2) % 4)))

    pairs = ((visible_hbm, visible), (order_hbm, order), (counts_hbm, counts_ref), (angles_hbm, angles),
             (coeffs_hbm, coeffs), (geometry_hbm, geometry), (cot_hbm, cot))
    loads = [pltpu.make_async_copy(a, b, local_sems.at[n]) for n, (a, b) in enumerate(pairs)]
    for load in loads:
        load.start()

    asks_out[...] = jnp.zeros_like(asks_out)
    answer[...] = jnp.zeros_like(answer)
    loss_ref[...] = jnp.zeros_like(loss_ref)
    for load in loads[:3]:
        load.wait()
    local_id, ahead, live = slot_tables(tile, visible[...], order[...], counts_ref)
    lane = lax.broadcasted_iota(jnp.int32, (SLOTS, 128), 1)
    block = (lane & (OWNED - 1)).astype(f32)
    wanted = jnp.where((block == local_id) & (lane < TRIPLE * OWNED), 1.0, 0.0)
    for k in range(PAIR):
        asks_out[pl.ds(k, STEPS, stride=8), :] = wanted[k * STEPS : (k + 1) * STEPS]
    for load in loads[3:]:
        load.wait()

    def relay(b, _):
        for h in range(BLOCK // 128):
            at = pl.ds(pl.multiple_of(b * BLOCK + h * 128, 128), 128)
            geo[h, pl.ds(pl.multiple_of(b * 8, 8), 6), :] = geometry[:, at]
            ang[h, pl.ds(pl.multiple_of(b * 8, 8), 2), :] = angles[:, at]
            coe[h, pl.ds(pl.multiple_of(b * 16, 8), 3 * bands), :] = coeffs[:, at]
        return 0

    lax.fori_loop(0, OWNED, relay, 0, unroll=4)

    def plane(ref, k, pitch):
        halves = [ref[h, pl.ds(k, OWNED, stride=pitch), :] for h in range(BLOCK // 128)]
        return jnp.concatenate(halves, axis=1)

    for k, value in enumerate(sh_basis([plane(ang, k, 8) for k in range(2)])):
        rows[k] = value
    first_band = attr * bands
    total = [jnp.zeros((OWNED, BLOCK), f32) for _ in range(3)]
    for k in range(bands):
        value = rows[first_band + k]
        basis_ref[k] = value
        for c in range(3):
            total[c] = total[c] + value * plane(coe, 3 * k + c, 16)
    for c in range(3):
        part[c * OWNED : (c + 1) * OWNED, :] = total[c]
    pl.semaphore_wait(*greeted)

    def ask(i):
        return pltpu.make_async_remote_copy(
            src_ref=asks_out.at[pl.ds(pl.multiple_of(i * 8, 8), 8)], dst_ref=asks.at[pl.ds(pl.multiple_of(i * 8, 8), 8)],
            send_sem=ask_sems.at[0, i], recv_sem=ask_sems.at[1, i],
            device_id=((tile + i) % STEPS, attr), device_id_type=MESH,
        )

    def back(i):
        return pltpu.make_async_remote_copy(
            src_ref=answer.at[:, pl.ds(pl.multiple_of(i * MSG, 8), MSG)], dst_ref=held.at[i],
            send_sem=back_sems.at[0, i], recv_sem=back_sems.at[1, i],
            device_id=((tile + STEPS - i) % STEPS, attr), device_id_type=MESH,
        )

    def give(i, d):
        slot = d * STEPS + i
        return pltpu.make_async_remote_copy(
            src_ref=packed.at[i, (attr + d) % 2], dst_ref=landed.at[pl.ds(pl.multiple_of(slot * MSG, 8), MSG)],
            send_sem=give_sems.at[0, slot], recv_sem=give_sems.at[1, slot],
            device_id=((tile + i) % STEPS, (attr + d) % 4), device_id_type=MESH,
        )

    def share(d):
        return exchange(all_picks.at[0], all_picks.at[d], share_sems, d, (tile, (attr + d) % 4))

    def each(act):
        def step(i, _):
            act(i)
            return 0

        lax.fori_loop(1, STEPS, step, 0)

    each(lambda i: ask(i).start())
    colour_one = exchange(part, first, attr_sems, 0, (tile, core))
    colour_one.start()
    asks[0:8, :] = asks_out[0:8, :]

    terms = splat_terms([plane(geo, k, 8) for k in range(6)])
    for k, value in enumerate(terms):
        terms_ref[k] = value
    for k, value in enumerate(exponent_rows(terms)):
        coef[k] = stack3(value)

    colour_one.wait()
    summed[...] = part[...] + first[...]
    colour_two = exchange(summed, second, attr_sems, 1, (tile, across))
    colour_two.start()

    each(lambda i: ask(i).wait_recv())
    picks = jnp.concatenate([asks[pl.ds(k, STEPS, stride=8), :] for k in range(PAIR)], axis=0)
    pick = picks.astype(bf16)[:, : TRIPLE * OWNED]
    all_picks[0] = picks
    for d in range(1, 4):
        share(d).start()

    def pick_row(values, at):
        found = dot(pick, values)
        for k in range(PAIR):
            scatter(answer, at[k], MSG, found[k * STEPS : (k + 1) * STEPS])

    for r in range(6):
        pick_row(coef[r], (r, 8 + r))
    colour_two.wait()
    for c in range(3):
        piece = slice(c * OWNED, (c + 1) * OWNED)
        pick_row(stack3(summed[piece] + second[piece] + 0.5), (16 + c, 20 + c))
    each(lambda i: back(i).start())
    held[0] = answer[:, 0:MSG, :]

    row = lax.broadcasted_iota(jnp.int32, (2 * BLOCK, BLOCK), 0) & (BLOCK - 1)
    col = lax.broadcasted_iota(jnp.int32, (2 * BLOCK, BLOCK), 1)
    before = jnp.where(row < col, -1.0, 0.0).astype(bf16)
    upto = jnp.where(row <= col, 1.0, 0.0).astype(bf16)
    mono_cols = pixel_monomials((PIX, 32), 0)
    mono_rows = pixel_monomials((8, PIX), 1)
    slot_lane = lax.broadcasted_iota(jnp.int32, (PIX, 128), 1)
    eight = lax.broadcasted_iota(jnp.int32, (8, BLOCK), 0)
    own_rows = [(eight >= 4 * k) & (eight < 4 * k + 3) for k in range(PAIR)]

    def halves(x):
        high = x.astype(bf16).astype(f32)
        return high, x - high

    def shape_pair(i):
        losses = loss_ref[...]
        for k in range(PAIR):
            high, mid, low = [p.astype(f32) for p in split3(tile_of(held, i, 8 * k))]
            coefs = jnp.concatenate([high, mid, low, jnp.zeros_like(low)], axis=0).astype(bf16)
            alpha = jnp.exp2(dot(mono_cols, coefs))
            loss = jnp.log(1.0 - alpha) * -LOG2E
            keep = dot(split2(loss), before)
            losses = jnp.where(slot_lane == i + k * STEPS, loss[:, BLOCK - 1 :] - keep[:, BLOCK - 1 :], losses)
            w_ref[i, k] = split2(alpha * jnp.exp2(keep))
            ratio_ref[i, k] = alpha * jnp.exp2(loss)
        loss_ref[...] = losses

    def show_pair(i):
        c_high, c_low = halves(tile_of(held, i, 16))
        seen = None
        for k in range(PAIR):
            w2 = w_ref[i, k]
            lhs = jnp.concatenate([jnp.where(own_rows[k], c_high, 0.0), jnp.where(own_rows[k], c_low, 0.0)], axis=0)
            lhs = lhs.astype(bf16)
            contract = (((1,), (1,)), ((), ()))
            shown = lax.dot_general(lhs, w2[:, :BLOCK], contract, preferred_element_type=f32)
            shown = shown + lax.dot_general(lhs, w2[:, BLOCK:], contract, preferred_element_type=f32)
            shown = shown[:8] + shown[8:]
            seen = shown if seen is None else seen + shown
        put_rows(c_ref, pl.ds(pl.multiple_of(i * 8, 8), 8), seen)

    def forward(i, _):
        back(i).wait_recv()
        show_pair(i - 1)
        shape_pair(i)
        return 0

    shape_pair(0)
    lax.fori_loop(1, STEPS, forward, 0)
    show_pair(STEPS - 1)

    def by_slot(ref, c):
        return jnp.concatenate([gather(ref, c + 4 * k, 8) for k in range(PAIR)], axis=0)

    losses = jnp.transpose(loss_ref[...])[:SLOTS]
    local = [by_slot(c_ref, c) for c in range(3)]
    spread = [jnp.zeros((SLOTS, PIX), f32) for _ in range(4)]
    for t in range(2):
        def earlier(values):
            out = jnp.zeros((SLOTS, PIX), f32)
            for s in range(SLOTS):
                out = out + ahead[t][:, s : s + 1] * values[s : s + 1, :]
            return out

        through = jnp.exp2(-earlier(losses)) * live[t]
        shade = jnp.zeros((SLOTS, PIX), f32)
        for c in range(3):
            g = cot[c, t : t + 1, :]
            lit = through * local[c]
            pic_ref[c, t : t + 1, :] = jnp.sum(lit, axis=0, keepdims=True)
            shade = shade + lit * g
            spread[c] = spread[c] + through * g
        behind = earlier(shade) - jnp.sum(shade, axis=0, keepdims=True)
        spread[3] = spread[3] + live[t] * behind
    for c in range(4):
        for k in range(PAIR):
            scatter(a_ref, c + 4 * k, 8, spread[c][k * STEPS : (k + 1) * STEPS])

    def slope_pair(i):
        a = get_rows(a_ref, pl.ds(pl.multiple_of(i * 8, 8), 8))
        a_high, a_low = halves(a)
        c_high, c_low = halves(tile_of(held, i, 16))
        columns = jnp.transpose(jnp.concatenate([a_high, a_low, a_high, a], axis=0))
        v_lhs = columns.astype(bf16)
        for k in range(PAIR):
            ch, cl = jnp.where(own_rows[k], c_high, 0.0), jnp.where(own_rows[k], c_low, 0.0)
            v_rhs = jnp.concatenate([ch, ch, cl, jnp.zeros_like(cl)], axis=0).astype(bf16)
            w2 = w_ref[i, k]
            value = (w2[:, :BLOCK].astype(f32) + w2[:, BLOCK:].astype(f32)) * dot(v_lhs, v_rhs)
            beyond = dot(split2(value), upto) + columns[:, 27 + 4 * k : 28 + 4 * k]
            d_ref[k] = split2(value + ratio_ref[i, k] * beyond)

    def sum_pair(i):
        a_high, a_low = halves(get_rows(a_ref, pl.ds(pl.multiple_of(i * 8, 8), 8)))
        tint = None
        for k in range(PAIR):
            d2, w2 = d_ref[k], w_ref[i, k]
            moments = dot(mono_rows, d2[:, :BLOCK]) + dot(mono_rows, d2[:, BLOCK:])
            put_rows(packed.at[i], pl.ds(8 * k, 8), moments)
            lhs = jnp.concatenate([jnp.where(own_rows[k], a_high, 0.0), jnp.where(own_rows[k], a_low, 0.0)], axis=0)
            lhs = lhs.astype(bf16)
            grads = dot(lhs, w2[:, :BLOCK]) + dot(lhs, w2[:, BLOCK:])
            grads = grads[:8] + grads[8:]
            tint = grads if tint is None else tint + grads
        put_rows(packed.at[i], pl.ds(16, 8), tint)

    def backward(n, _):
        sum_pair(n)
        slope_pair((n + 1) % STEPS)
        for d in range(4):
            give(n, d).start()
        return 0

    slope_pair(1)
    lax.fori_loop(1, STEPS, backward, 0)
    sum_pair(0)
    for d in range(1, 4):
        give(0, d).start()
    landed[0:MSG, :] = packed[0, mine]

    for d in range(1, 4):
        share(d).wait_recv()
    chosen = [all_picks[d, k * STEPS : (k + 1) * STEPS, :] for k in range(PAIR) for d in range(4)]
    tall = jnp.concatenate(chosen * TRIPLE + [jnp.zeros((256 - TRIPLE * 4 * SLOTS, 128), f32)], axis=0)
    put = jnp.transpose(tall)[:OWNED, : TRIPLE * 4 * SLOTS].astype(bf16)

    def take_give(n, _):
        for d in range(4):
            give(n, d).wait_recv()
        return 0

    lax.fori_loop(1, STEPS, take_give, 0)
    for d in range(1, 4):
        give(0, d).wait_recv()
    for r in range(0, 9, 2):
        both = []
        for q in range(r, min(r + 2, 9)):
            at = (q, 8 + q) if q < 6 else (10 + q, 14 + q)
            both.append(jnp.concatenate([landed[pl.ds(at[k], 4 * STEPS, stride=MSG), :] for k in range(PAIR)], axis=0))
        found = dot(put, stack3(jnp.concatenate(both, axis=1)))
        for q in range(len(both)):
            sums[(r + q) * OWNED : (r + q + 1) * OWNED, :] = found[:, q * 128 : (q + 1) * 128]

    swap = exchange(sums, got_core, attr_sems, 2, (tile, core))
    swap.start()
    out_ref[mine] = sums[...]
    for d in range(1, 4):
        share(d).wait_send()
        give(0, d).wait_send()

    def sent_give(n, _):
        for d in range(4):
            give(n, d).wait_send()
        return 0

    lax.fori_loop(1, STEPS, sent_give, 0)
    each(lambda i: ask(i).wait_send())
    each(lambda i: back(i).wait_send())
    swap.wait()
    out_ref[1 - mine] = got_core[...]


def fused(geometry, view_angles, sh_coeffs, visible, order, cot, counts):
    bands = sh_coeffs.shape[0] // 3
    sems = pltpu.SemaphoreType.DMA
    vmem = pl.BlockSpec(memory_space=pltpu.VMEM)
    ins = (geometry, view_angles, sh_coeffs, visible, order, cot, counts)
    colours = 3 * OWNED
    shapes = (cot.shape, (bands, OWNED, BLOCK), (11, OWNED, BLOCK), (2, 9 * OWNED, 128))
    return pl.pallas_call(
        functools.partial(fused_kernel, bands),
        name="splat",
        out_shape=tuple(jax.ShapeDtypeStruct(o, jnp.float32) for o in shapes),
        in_specs=[pl.BlockSpec(memory_space=pltpu.HBM)] * len(ins),
        out_specs=tuple(vmem for _ in shapes),
        scratch_shapes=[pltpu.VMEM(x.shape, x.dtype) for x in ins[:-1]] + [
            pltpu.SMEM(counts.shape, counts.dtype),
            floats(BLOCK // 128, 8 * OWNED, 128), floats(BLOCK // 128, 8 * OWNED, 128),
            floats(BLOCK // 128, 16 * OWNED, 128), floats(16, OWNED, BLOCK),
            pltpu.VMEM((6, TRIPLE * OWNED, BLOCK), jnp.bfloat16), floats(colours, BLOCK), floats(colours, BLOCK),
            floats(colours, BLOCK), floats(colours, BLOCK), floats(8, 128),
            floats(8 * STEPS, 128), floats(8 * STEPS, 128), floats(2, STEPS * MSG, 128), floats(STEPS, 2, MSG, 128),
            pltpu.VMEM((STEPS, PAIR, PIX, 2 * BLOCK), jnp.bfloat16), floats(STEPS, PAIR, PIX, BLOCK),
            floats(PIX, 128), floats(2, 8 * STEPS, 128), floats(2, 8 * STEPS, 128),
            floats(STEPS, 2, MSG, 128), floats(4 * STEPS * MSG, 128), floats(9 * OWNED, 128), floats(9 * OWNED, 128),
            floats(4, SLOTS, 128), pltpu.VMEM((PAIR, PIX, 2 * BLOCK), jnp.bfloat16),
            sems((len(ins),)), sems((2, STEPS)), sems((2, STEPS)), sems((2, 4 * STEPS)), sems((2, 4)), sems((2, 3)),
        ],
        compiler_params=pltpu.CompilerParams(
            collective_id=3, has_side_effects=True, vmem_limit_bytes=40 * 1024 * 1024
        ),
    )(*[pltpu.with_memory_space_constraint(x, pltpu.HBM) for x in ins])


def finish_kernel(bands, sums_ref, terms_ref, basis_ref, pic_ref, geometry_ref, coeffs_ref, picture_ref, both, geo, coe):
    for h in range(BLOCK // 128):
        both[:, h * 128 : (h + 1) * 128] = sums_ref[h]
    final_kernel(OWNED, bands, both, terms_ref, basis_ref, geometry_ref, coeffs_ref, geo, coe)
    picture_ref[...] = pic_ref[...]


def finish(sums, terms, basis, pic):
    bands = basis.shape[0]
    vmem = pl.BlockSpec(memory_space=pltpu.VMEM)
    shapes = ((6, OWNED * BLOCK), (3 * bands, OWNED * BLOCK), pic.shape)
    return pl.pallas_call(
        functools.partial(finish_kernel, bands),
        name="finish",
        out_shape=tuple(jax.ShapeDtypeStruct(o, jnp.float32) for o in shapes),
        in_specs=[vmem] * 4,
        out_specs=(vmem,) * 3,
        scratch_shapes=[
            floats(9 * OWNED, BLOCK),
            floats(BLOCK // 128, 8 * OWNED, 128),
            floats(BLOCK // 128, 16 * OWNED, 128),
        ],
        compiler_params=pltpu.CompilerParams(vmem_limit_bytes=12 * 1024 * 1024),
    )(sums, terms, basis, pic)


def local_fused(geometry, sh_coeffs, view_angles, visible, counts, order, image_cot):
    cot = jnp.swapaxes(image_cot, 0, 1)
    pic, basis, terms, sums = fused(geometry, view_angles, sh_coeffs, visible, order, cot, counts)
    grad_geometry, grad_sh, picture = finish(sums, terms, basis, pic)
    return (jnp.swapaxes(picture, 0, 1), grad_geometry, grad_sh)


def local(geometry, sh_coeffs, view_angles, visible, counts, order, image_cot):
    owners = lax.axis_size("tile")
    tiles, vis = visible.shape
    owned = geometry.shape[1] // BLOCK
    fits = (owners, vis, tiles, owned, lax.axis_size("attr")) == (8, 16, 2, 32, 4)
    run = local_fused if fits else local_general
    return run(geometry, sh_coeffs, view_angles, visible, counts, order, image_cot)


def solution(mesh):
    in_specs = (
        P(None, "tile"),
        P("attr", "tile"),
        P(None, "tile"),
        P(("tile", "attr"), None),
        P(("tile", "attr")),
        P(("tile", "attr"), None),
        P(("tile", "attr"), None, None),
    )
    out_specs = (P(("tile", "attr"), None, None), P(None, "tile"), P("attr", "tile"))
    return jax.shard_map(local, mesh=mesh, in_specs=in_specs, out_specs=out_specs, check_vma=False)
```

```python
import functools
import jax
import jax.numpy as jnp
from jax import lax
from jax.experimental import pallas as pl
from jax.experimental.pallas import tpu as pltpu
from jax.sharding import PartitionSpec as P

BLOCK = 256
SIDE = 16
PIX = SIDE * SIDE
MID = 0.5 * SIDE
LOG2E = 1.4426950408889634
LN2 = 0.6931471805599453


band_zero = 0.28209479177387814
band_one = 0.4886025119029199
band_two = (
    1.0925484305920792,
    -1.0925484305920792,
    0.31539156525252005,
    -1.0925484305920792,
    0.5462742152960396,
)
band_three = (
    -0.5900435899266435,
    2.890611442640554,
    -0.4570457994644658,
    0.3731763325901154,
    -0.4570457994644658,
    1.445305721320277,
    -0.5900435899266435,
)


def sh_basis(view_angles):
    azimuth = view_angles[0]
    elevation = view_angles[1]
    dir_x = jnp.cos(azimuth) * jnp.cos(elevation)
    dir_y = jnp.sin(azimuth) * jnp.cos(elevation)
    dir_z = jnp.sin(elevation)
    sq_x = dir_x * dir_x
    sq_y = dir_y * dir_y
    sq_z = dir_z * dir_z
    basis_rows = [
        band_zero * jnp.ones_like(dir_x),
        -band_one * dir_y,
        band_one * dir_z,
        -band_one * dir_x,
        band_two[0] * dir_x * dir_y,
        band_two[1] * dir_y * dir_z,
        band_two[2] * (2.0 * sq_z - sq_x - sq_y),
        band_two[3] * dir_x * dir_z,
        band_two[4] * (sq_x - sq_y),
        band_three[0] * dir_y * (3.0 * sq_x - sq_y),
        band_three[1] * dir_x * dir_y * dir_z,
        band_three[2] * dir_y * (4.0 * sq_z - sq_x - sq_y),
        band_three[3] * dir_z * (2.0 * sq_z - 3.0 * sq_x - 3.0 * sq_y),
        band_three[4] * dir_x * (4.0 * sq_z - sq_x - sq_y),
        band_three[5] * dir_z * (sq_x - sq_y),
        band_three[6] * dir_x * (sq_x - 3.0 * sq_y),
    ]
    return basis_rows


def split2(x):
    high = x.astype(jnp.bfloat16)
    low = (x - high.astype(jnp.float32)).astype(jnp.bfloat16)
    return jnp.concatenate([high, low], axis=1)


def dot(a, b):
    return jnp.dot(a, b, preferred_element_type=jnp.float32)


def blend_kernel(tiles, seq_ref, counts_ref, held_ref, cot_rows_ref, cot_cols_ref, pic_ref, grad_ref, part_ref, ratio_ref):
    f32, bf16 = jnp.float32, jnp.bfloat16
    row = lax.broadcasted_iota(jnp.int32, (2 * BLOCK, BLOCK), 0)
    row = jnp.where(row >= BLOCK, row - BLOCK, row)
    col = lax.broadcasted_iota(jnp.int32, (2 * BLOCK, BLOCK), 1)
    before = jnp.where(row < col, -1.0, 0.0).astype(bf16)
    upto = jnp.where(row <= col, 1.0, 0.0).astype(bf16)

    def monomials(shape, dim, width):
        pixel = lax.broadcasted_iota(jnp.int32, shape, dim)
        kind = lax.broadcasted_iota(jnp.int32, shape, 1 - dim) & (width - 1)
        x = (pixel & (SIDE - 1)).astype(f32) + (0.5 - MID)
        y = (pixel // SIDE).astype(f32) + (0.5 - MID)
        out = jnp.where(kind == 0, 1.0, 0.0)
        for k, value in ((1, x), (2, y), (3, x * x), (4, x * y), (5, y * y)):
            out = jnp.where(kind == k, value, out)
        return out.astype(bf16)

    mono_cols = monomials((PIX, 48), 0, 16)
    mono_rows = monomials((8, PIX), 1, 8)
    cot_lhs, cot_rows = [], []
    for t in range(tiles):
        g = cot_cols_ref[t]
        high = g.astype(bf16).astype(f32)
        lane = lax.broadcasted_iota(jnp.int32, g.shape, 1)
        cot_lhs.append(jnp.where(lane < 48, high, g - high).astype(bf16))
        g = cot_rows_ref[t]
        high = g.astype(bf16).astype(f32)
        cot_rows.append(jnp.concatenate([high, g - high], axis=0).astype(bf16))

    grad_ref[...] = jnp.zeros_like(grad_ref)
    lives = [counts_ref[t] for t in range(tiles)]
    longest = functools.reduce(jnp.maximum, lives)

    lhs = []
    for t in range(tiles):
        wide = jnp.concatenate([mono_cols.astype(f32), jnp.zeros((PIX, 48), f32)], axis=1)
        lhs.append(jnp.concatenate([wide.astype(bf16), cot_lhs[t]], axis=0))
    head = lax.broadcasted_iota(jnp.int32, (16, BLOCK), 0) == 0

    def forward(j, carry):
        keep_before, sum_before, pictures = carry
        alphas, values, losses, helds, spots = [], [], [], [], []
        for t in range(tiles):
            at = seq_ref[t, j]
            hidden = jnp.where(j < lives[t], 0.0, -16384.0)
            held = held_ref[at]
            parts = split3(jnp.where(head, held + hidden, held))
            rows = jnp.concatenate(parts, axis=0)
            both = dot(lhs[t], jnp.concatenate([rows, rows], axis=0))
            alpha = jnp.exp2(both[:PIX])
            alphas.append(alpha)
            values.append(both[PIX:])
            losses.append(jnp.log(1.0 - alpha) * -LOG2E)
            helds.append(jnp.concatenate(parts[:2], axis=0))
            spots.append(at)
        loss = jnp.concatenate(losses, axis=0)
        keep_in = dot(split2(loss), before) + keep_before
        keep_before = keep_in[:, BLOCK - 1 :] - loss[:, BLOCK - 1 :]
        alpha = jnp.concatenate(alphas, axis=0)
        weight = alpha * jnp.exp2(keep_in)
        value = weight * jnp.concatenate(values, axis=0)
        total = dot(split2(value), upto) + sum_before
        sum_before = total[:, BLOCK - 1 :]
        ratio = alpha * jnp.exp2(loss)
        part_ref[j] = value + ratio * total
        ratio_ref[j] = ratio
        w2 = split2(weight)
        shown = []
        for t in range(tiles):
            w_high, w_low = w2[t * PIX : (t + 1) * PIX, :BLOCK], w2[t * PIX : (t + 1) * PIX, BLOCK:]
            rows = lax.dot_general(helds[t], w_high, (((1,), (1,)), ((), ())), preferred_element_type=f32)
            rows = rows + lax.dot_general(helds[t], w_low, (((1,), (1,)), ((), ())), preferred_element_type=f32)
            shown.append(pictures[t] + rows[:16] + rows[16:])
            colour_grad = dot(cot_rows[t], w_high) + dot(cot_rows[t], w_low)
            grad_ref[spots[t], 0:8, :] += colour_grad[:8] + colour_grad[8:]
        return keep_before, sum_before, tuple(shown)

    zero = jnp.zeros((tiles * PIX, 1), f32)
    start = (zero, zero, tuple(jnp.zeros((16, PIX), f32) for _ in range(tiles)))
    _, ends, pictures = lax.fori_loop(0, longest, forward, start)
    for t in range(tiles):
        pic_ref[t] = pictures[t]

    def backward(j, _):
        for t in range(tiles):
            pixels = slice(t * PIX, (t + 1) * PIX)
            d2 = split2(part_ref[j, pixels] - ratio_ref[j, pixels] * ends[pixels])
            moments = dot(mono_rows, d2[:, :BLOCK]) + dot(mono_rows, d2[:, BLOCK:])
            grad_ref[seq_ref[t, j], 8:16, :] += moments
        return 0

    lax.fori_loop(0, longest, backward, 0)


def blend(seq, counts, held, image_cot):
    tiles = image_cot.shape[0]
    rows = held.shape[0]
    cot_rows = jnp.pad(image_cot, ((0, 0), (0, 5), (0, 0)))
    cot_cols = jnp.pad(jnp.swapaxes(image_cot, 1, 2), ((0, 0), (0, 0), (6, 7)))
    cot_cols = jnp.tile(cot_cols, (1, 1, 6))
    smem = pl.BlockSpec(memory_space=pltpu.SMEM)
    vmem = pl.BlockSpec(memory_space=pltpu.VMEM)
    picture, grads = pl.pallas_call(
        functools.partial(blend_kernel, tiles),
        name="blend",
        out_shape=(
            jax.ShapeDtypeStruct((tiles, 16, PIX), jnp.float32),
            jax.ShapeDtypeStruct((rows, 16, BLOCK), jnp.float32),
        ),
        in_specs=[smem, smem, vmem, vmem, vmem],
        out_specs=(vmem, vmem),
        scratch_shapes=[
            pltpu.VMEM((seq.shape[1], tiles * PIX, BLOCK), jnp.float32),
            pltpu.VMEM((seq.shape[1], tiles * PIX, BLOCK), jnp.float32),
        ],
        compiler_params=pltpu.CompilerParams(vmem_limit_bytes=28 * 1024 * 1024),
    )(seq, counts, held, cot_rows, cot_cols)
    return picture[:, 6:9], grads


def splat_terms(geometry):
    mx, my = geometry[0] - MID, geometry[1] - MID
    c, s = jnp.cos(geometry[4]), jnp.sin(geometry[4])
    e1, e2 = jnp.exp(-2.0 * geometry[2]), jnp.exp(-2.0 * geometry[3])
    cc, ss, cs = c * c, s * s, c * s
    a = cc * e1 + ss * e2
    b = cs * (e1 - e2)
    d = ss * e1 + cc * e2
    return mx, my, e1, e2, cc, ss, cs, a, b, d, geometry[5]


def exponent_rows(terms):
    mx, my, e1, e2, cc, ss, cs, a, b, d, logit = terms
    bx, by = a * mx + b * my, b * mx + d * my
    log_opacity = jnp.minimum(logit, 0.0) - jnp.log1p(jnp.exp(-jnp.abs(logit)))
    one = log_opacity - 0.5 * (mx * bx + my * by)
    return [LOG2E * r for r in (one, bx, by, -0.5 * a, -b, -0.5 * d)]


def geometry_grads(terms, m):
    mx, my, e1, e2, cc, ss, cs, a, b, d, logit = terms
    n0 = m[0]
    nx, ny = m[1] - mx * n0, m[2] - my * n0
    nxx = m[3] - mx * (m[1] + nx)
    nxy = m[4] - mx * m[2] - my * nx
    nyy = m[5] - my * (m[2] + ny)
    return [
        a * nx + b * ny,
        b * nx + d * ny,
        e1 * (cc * nxx + 2.0 * cs * nxy + ss * nyy),
        e2 * (ss * nxx - 2.0 * cs * nxy + cc * nyy),
        (e2 - e1) * (cs * (nyy - nxx) + (cc - ss) * nxy),
        n0 / (1.0 + jnp.exp(logit)),
    ]


MESH = pl.DeviceIdType.MESH


def greet(peers):
    barrier = pltpu.get_barrier_semaphore()
    tile, attr, owners, extra = peers

    def hello(step, _):
        other = (tile + step) % owners
        pl.semaphore_signal(barrier, inc=1, device_id=(other, attr), device_id_type=MESH)
        return 0

    lax.fori_loop(1, owners, hello, 0)
    for other in extra:
        pl.semaphore_signal(barrier, inc=1, device_id=(tile, other), device_id_type=MESH)
    return barrier, owners - 1 + len(extra)


def split3(x):
    high = x.astype(jnp.bfloat16)
    rest = x - high.astype(jnp.float32)
    mid = rest.astype(jnp.bfloat16)
    return high, mid, (rest - mid.astype(jnp.float32)).astype(jnp.bfloat16)


def exchange(src, dst, sems, k, device):
    return pltpu.make_async_remote_copy(
        src_ref=src, dst_ref=dst, send_sem=sems.at[0, k], recv_sem=sems.at[1, k],
        device_id=device, device_id_type=MESH,
    )


def fetch_kernel(dims, want_ref, coef_ref, part_ref, held_ref, asked_ref,
                 asks, answer, landed, first, summed, second, tile_sems, back_sems, attr_sems):
    owners, owned, cap, message, stride = dims
    f32 = jnp.float32
    tile, attr = lax.axis_index("tile"), lax.axis_index("attr")
    core = attr + 1 - 2 * (attr % 2)
    across = (attr + 2) % 4
    pl.semaphore_wait(*greet((tile, attr, owners, (core, across))))

    colour_one = exchange(part_ref, first, attr_sems, 0, (tile, core))
    colour_one.start()

    def ask(other, sender):
        return pltpu.make_async_remote_copy(
            src_ref=want_ref.at[other], dst_ref=asks.at[sender],
            send_sem=tile_sems.at[0, other], recv_sem=tile_sems.at[1, sender],
            device_id=(other, attr), device_id_type=MESH,
        )

    def send_ask(step, _):
        ask((tile + step) % owners, tile).start()
        return 0

    lax.fori_loop(1, owners, send_ask, 0)
    asks[tile] = want_ref[tile]

    colour_one.wait()
    summed[...] = part_ref[...] + first[...]
    colour_two = exchange(summed, second, attr_sems, 1, (tile, across))
    colour_two.start()

    def take_ask(step, _):
        other = (tile + step) % owners
        ask(other, other).wait()
        return 0

    lax.fori_loop(1, owners, take_ask, 0)

    per = 128 // stride
    lanes = owners // per
    rows = []
    for tile_at in range(lanes):
        rows.append(functools.reduce(jnp.add, [asks[tile_at * per + k] for k in range(per)]))
    asked = jnp.concatenate(rows, axis=1) - 1.0
    asked_ref[...] = asked
    wide = 9 * owned
    columns = []
    for tile_at in range(lanes):
        square = jnp.concatenate([rows[tile_at] - 1.0] * 16, axis=0)
        columns.append(jnp.transpose(square)[:, 0:1])
    column = jnp.concatenate(columns, axis=0)
    lane = lax.broadcasted_iota(jnp.int32, (owners * stride, wide), 1).astype(f32)
    pick = jnp.where(lane == column, 1.0, 0.0).astype(jnp.bfloat16)

    colour_two.wait()
    colour = summed[...] + second[...] + 0.5
    table = jnp.concatenate([coef_ref[...], colour], axis=0)
    high, mid, low = split3(table)
    answer[...] = (dot(pick, low) + dot(pick, mid)) + dot(pick, high)

    def back(other, sender):
        at = pl.multiple_of(other * stride, 8)
        return pltpu.make_async_remote_copy(
            src_ref=answer.at[pl.ds(at, message)], dst_ref=landed.at[sender],
            send_sem=back_sems.at[0, other], recv_sem=back_sems.at[1, sender],
            device_id=(other, attr), device_id_type=MESH,
        )

    def send_back(step, _):
        back((tile + step) % owners, tile).start()
        return 0

    lax.fori_loop(1, owners, send_back, 0)
    landed[tile] = answer[pl.ds(pl.multiple_of(tile * stride, 8), message), :]
    held_ref[...] = jnp.zeros_like(held_ref)

    def take_back(step, _):
        other = (tile + step) % owners
        back(other, other).wait()
        return 0

    lax.fori_loop(1, owners, take_back, 0)

    def unpack(o, _):
        for k in range(cap):
            held_ref[o * cap + k, 0:9, :] = landed[o, 9 * k : 9 * k + 9, :]
        return 0

    lax.fori_loop(0, owners, unpack, 0)


def give_kernel(dims, grads_ref, asked_ref, out_ref,
                packed, landed, sums, first, half, second, third, tile_sems, attr_sems):
    owners, owned, cap, message, stride = dims
    f32 = jnp.float32
    tile, attr = lax.axis_index("tile"), lax.axis_index("attr")
    core = attr + 1 - 2 * (attr % 2)
    across = (attr + 2) % 4
    mine = attr % 2

    if message < stride:
        landed[...] = jnp.zeros_like(landed)
    greeted = greet((tile, attr, owners, (core, across)))
    packed[...] = jnp.zeros_like(packed)

    def pack(o, _):
        for k in range(cap):
            packed[o, 9 * k : 9 * k + 6, :] = grads_ref[o * cap + k, 8:14, :]
            packed[o, 9 * k + 6 : 9 * k + 9, :] = grads_ref[o * cap + k, 0:3, :]
        return 0

    lax.fori_loop(0, owners, pack, 0)
    pl.semaphore_wait(*greeted)

    def give(other, sender):
        at = pl.multiple_of(sender * stride, 8)
        return pltpu.make_async_remote_copy(
            src_ref=packed.at[other], dst_ref=landed.at[pl.ds(at, message)],
            send_sem=tile_sems.at[0, other], recv_sem=tile_sems.at[1, sender],
            device_id=(other, attr), device_id_type=MESH,
        )

    def send_give(step, _):
        give((tile + step) % owners, tile).start()
        return 0

    lax.fori_loop(1, owners, send_give, 0)
    landed[pl.ds(pl.multiple_of(tile * stride, 8), message), :] = packed[tile]
    wide = 9 * owned
    row = lax.broadcasted_iota(jnp.int32, (wide, owners * stride), 0).astype(f32)
    pick = jnp.where(row == asked_ref[0:1, :], 1.0, 0.0).astype(jnp.bfloat16)

    def take_give(step, _):
        other = (tile + step) % owners
        give(other, other).wait()
        return 0

    lax.fori_loop(1, owners, take_give, 0)
    high, mid, low = split3(landed[...])
    total = (dot(pick, low) + dot(pick, mid)) + dot(pick, high)
    cut = wide // 2
    sums[0] = total[:cut]
    sums[1] = total[cut:]

    one = exchange(sums.at[1 - mine], first, attr_sems, 0, (tile, core))
    one.start()
    one.wait()
    half[...] = sums[mine] + first[...]
    two = exchange(half, second, attr_sems, 1, (tile, across))
    two.start()
    two.wait()
    half_sum = half[...] + second[...]
    first[...] = half_sum
    three = exchange(first, third, attr_sems, 2, (tile, core))
    three.start()
    three.wait()
    at = pl.multiple_of(mine * cut, 8)
    out_ref[pl.ds(at, cut), :] = half_sum
    at = pl.multiple_of((1 - mine) * cut, 8)
    out_ref[pl.ds(at, cut), :] = third[...]


def remote_call(kernel, dims, outs, ins, scratch, number, name):
    vmem = pl.BlockSpec(memory_space=pltpu.VMEM)
    return pl.pallas_call(
        functools.partial(kernel, dims),
        name=name,
        out_shape=tuple(jax.ShapeDtypeStruct(o, jnp.float32) for o in outs),
        in_specs=[vmem] * len(ins),
        out_specs=tuple(vmem for _ in outs),
        scratch_shapes=scratch,
        compiler_params=pltpu.CompilerParams(
            collective_id=number, has_side_effects=True, vmem_limit_bytes=20 * 1024 * 1024
        ),
    )(*ins)


def floats(*shape):
    return pltpu.VMEM(shape, jnp.float32)


def fetch(dims, want, coef, part):
    owners, owned, cap, message, stride = dims
    sems = pltpu.SemaphoreType.DMA
    return remote_call(
        fetch_kernel, dims,
        ((owners * cap, 16, BLOCK), (8, owners * stride)),
        (want, coef, part),
        [floats(owners, 8, 128), floats(owners * stride, BLOCK), floats(owners, message, BLOCK),
         floats(3 * owned, BLOCK), floats(3 * owned, BLOCK), floats(3 * owned, BLOCK),
         sems((2, owners)), sems((2, owners)), sems((2, 2))],
        1, "fetch",
    )


def give_back(dims, grads, asked):
    owners, owned, cap, message, stride = dims
    sems = pltpu.SemaphoreType.DMA
    cut = 9 * owned // 2
    return remote_call(
        give_kernel, dims, ((9 * owned, BLOCK),), (grads, asked),
        [floats(owners, message, BLOCK), floats(owners * stride, BLOCK), floats(2, cut, BLOCK),
         floats(cut, BLOCK), floats(cut, BLOCK), floats(cut, BLOCK), floats(cut, BLOCK),
         sems((2, owners)), sems((2, 3))],
        2, "give",
    )[0]


def prep_kernel(owned, bands, geometry_ref, angles_ref, coeffs_ref, coef_ref, part_ref, basis_ref, terms_ref,
                geo, ang, coe, rows):
    def relay(b, _):
        for h in range(BLOCK // 128):
            at = pl.ds(pl.multiple_of(b * BLOCK + h * 128, 128), 128)
            geo[h, pl.ds(pl.multiple_of(b * 8, 8), 6), :] = geometry_ref[:, at]
            ang[h, pl.ds(pl.multiple_of(b * 8, 8), 2), :] = angles_ref[:, at]
            coe[h, pl.ds(pl.multiple_of(b * 16, 8), 3 * bands), :] = coeffs_ref[:, at]
        return 0

    lax.fori_loop(0, owned, relay, 0, unroll=4)

    def plane(ref, k, pitch):
        halves = [ref[h, pl.ds(k, owned, stride=pitch), :] for h in range(BLOCK // 128)]
        return jnp.concatenate(halves, axis=1)

    terms = splat_terms([plane(geo, k, 8) for k in range(6)])
    for k, value in enumerate(terms):
        terms_ref[k] = value
    for k, value in enumerate(exponent_rows(terms)):
        coef_ref[k * owned : (k + 1) * owned, :] = value
    for k, value in enumerate(sh_basis([plane(ang, k, 8) for k in range(2)])):
        rows[k] = value
    first = lax.axis_index("attr") * bands
    total = [jnp.zeros((owned, BLOCK), jnp.float32) for _ in range(3)]
    for k in range(bands):
        value = rows[first + k]
        basis_ref[k] = value
        for c in range(3):
            total[c] = total[c] + value * plane(coe, 3 * k + c, 16)
    for c in range(3):
        part_ref[c * owned : (c + 1) * owned, :] = total[c]


def prep(geometry, view_angles, sh_coeffs, owned):
    bands = sh_coeffs.shape[0] // 3
    vmem = pl.BlockSpec(memory_space=pltpu.VMEM)
    shapes = ((6 * owned, BLOCK), (3 * owned, BLOCK), (bands, owned, BLOCK), (11, owned, BLOCK))
    return pl.pallas_call(
        functools.partial(prep_kernel, owned, bands),
        name="prep",
        out_shape=tuple(jax.ShapeDtypeStruct(o, jnp.float32) for o in shapes),
        in_specs=[vmem] * 3,
        out_specs=(vmem,) * 4,
        scratch_shapes=[
            floats(BLOCK // 128, 8 * owned, 128),
            floats(BLOCK // 128, 8 * owned, 128),
            floats(BLOCK // 128, 16 * owned, 128),
            floats(16, owned, BLOCK),
        ],
        compiler_params=pltpu.CompilerParams(vmem_limit_bytes=12 * 1024 * 1024),
    )(geometry, view_angles, sh_coeffs)


def final_kernel(owned, bands, sums_ref, terms_ref, basis_ref, geometry_ref, coeffs_ref, geo, coe):
    summed = [sums_ref[k * owned : (k + 1) * owned, :] for k in range(9)]

    def put(ref, k, pitch, value):
        for h in range(BLOCK // 128):
            ref[h, pl.ds(k, owned, stride=pitch), :] = value[:, h * 128 : (h + 1) * 128]

    for k, value in enumerate(geometry_grads([terms_ref[k] for k in range(11)], summed[:6])):
        put(geo, k, 8, value)
    for k in range(bands):
        for c in range(3):
            put(coe, 3 * k + c, 16, basis_ref[k] * summed[6 + c])

    def relay(b, _):
        for h in range(BLOCK // 128):
            at = pl.ds(pl.multiple_of(b * BLOCK + h * 128, 128), 128)
            geometry_ref[:, at] = geo[h, pl.ds(pl.multiple_of(b * 8, 8), 6), :]
            coeffs_ref[:, at] = coe[h, pl.ds(pl.multiple_of(b * 16, 8), 3 * bands), :]
        return 0

    lax.fori_loop(0, owned, relay, 0, unroll=4)


def final(sums, terms, basis, owned):
    bands = basis.shape[0]
    vmem = pl.BlockSpec(memory_space=pltpu.VMEM)
    shapes = ((6, owned * BLOCK), (3 * bands, owned * BLOCK))
    return pl.pallas_call(
        functools.partial(final_kernel, owned, bands),
        name="final",
        out_shape=tuple(jax.ShapeDtypeStruct(o, jnp.float32) for o in shapes),
        in_specs=[vmem] * 3,
        out_specs=(vmem,) * 2,
        scratch_shapes=[
            floats(BLOCK // 128, 8 * owned, 128),
            floats(BLOCK // 128, 16 * owned, 128),
        ],
        compiler_params=pltpu.CompilerParams(vmem_limit_bytes=12 * 1024 * 1024),
    )(sums, terms, basis)


def local_general(geometry, sh_coeffs, view_angles, visible, counts, order, image_cot):
    owners = lax.axis_size("tile")
    owned = geometry.shape[1] // BLOCK
    vis = visible.shape[1]
    cap = (vis + owners - 1) // owners
    coef, partial_colour, my_basis, terms = prep(geometry, view_angles, sh_coeffs, owned)

    ids = visible[0]
    owner_of, local_of = ids // owned, ids % owned
    position = jnp.arange(vis)
    rank = jnp.sum(((owner_of[None, :] == owner_of[:, None]) & (position[None, :] < position[:, None])).astype(jnp.int32), 1)
    slot = owner_of * cap + rank
    message = -(-9 * cap // 8) * 8
    stride = 16 if message <= 16 else 32
    dims = (owners, owned, cap, message, stride)
    lane = jnp.arange(128) - (lax.axis_index("tile") % (128 // stride)) * stride
    in_slot = lane[None, :, None] // 9 + jnp.arange(owners)[:, None, None] * cap
    hit = (slot[None, None, :] == in_slot) & (lane >= 0)[None, :, None] & (lane < 9 * cap)[None, :, None]
    want = jnp.sum(jnp.where(hit, 1 + local_of[None, None, :] + owned * (lane % 9)[None, :, None], 0), 2)
    want = jnp.broadcast_to(want.astype(jnp.float32)[:, None, :], (owners, 8, 128))
    slot_of = jnp.sum(jnp.where(visible[:, :, None] == ids[None, None, :], slot[None, None, :], 0), 2)
    seq = jnp.sum(jnp.where(order[:, :, None] == position[None, None, :], slot_of[:, None, :], 0), 2)

    held, asked = fetch(dims, want, coef, partial_colour)
    picture, grads = blend(seq, counts, held, image_cot)
    sums = give_back(dims, grads, asked)
    grad_geometry, grad_sh = final(sums, terms, my_basis, owned)
    return (picture, grad_geometry, grad_sh)


STEPS = 8
PAIR = 2
SLOTS = STEPS * PAIR
OWNED = 32
MSG = 24
TRIPLE = 3
LAG = 3


def stack3(x):
    high, mid, low = split3(x)
    return jnp.concatenate([high, mid, low], axis=0)


def lane_halves(x):
    return [x[:, h * 128 : (h + 1) * 128] for h in range(BLOCK // 128)]


def put_rows(ref, rows, value):
    for h, part in enumerate(lane_halves(value)):
        ref[h, rows, :] = part


def get_rows(ref, rows):
    return jnp.concatenate([ref[h, rows, :] for h in range(BLOCK // 128)], axis=1)


def scatter(ref, at, pitch, value):
    put_rows(ref, pl.ds(at, STEPS, stride=pitch), value)


def gather(ref, at, pitch):
    return get_rows(ref, pl.ds(at, STEPS, stride=pitch))


def tile_of(ref, i, at):
    return jnp.concatenate([ref[i, h, at : at + 8, :] for h in range(BLOCK // 128)], axis=1)


def pixel_monomials(shape, dim):
    pixel = lax.broadcasted_iota(jnp.int32, shape, dim)
    kind = lax.broadcasted_iota(jnp.int32, shape, 1 - dim) & 7
    x = (pixel & (SIDE - 1)).astype(jnp.float32) + (0.5 - MID)
    y = (pixel // SIDE).astype(jnp.float32) + (0.5 - MID)
    out = jnp.where(kind == 0, 1.0, 0.0)
    for k, value in ((1, x), (2, y), (3, x * x), (4, x * y), (5, y * y)):
        out = jnp.where(kind == k, value, out)
    return out.astype(jnp.bfloat16)


def slot_tables(tile, visible, order, counts_ref):
    f32 = jnp.float32
    sub = lax.broadcasted_iota(jnp.int32, (SLOTS, SLOTS), 0)
    lane = lax.broadcasted_iota(jnp.int32, (SLOTS, SLOTS), 1)
    diagonal = sub == lane
    lane_f, sub_f = lane.astype(f32), sub.astype(f32)

    def to_column(row):
        return jnp.sum(jnp.where(diagonal, row, 0.0), axis=1, keepdims=True)

    def to_row(column):
        return jnp.sum(jnp.where(diagonal, column, 0.0), axis=0, keepdims=True)

    ids = visible[0:1]
    owner = ids // OWNED
    near = owner - tile
    near = jnp.where(near < 0, near + STEPS, near).astype(f32)
    ids_f = ids.astype(f32)
    inside = (ids - owner * OWNED).astype(f32)
    near_column = to_column(near)
    second = jnp.sum(jnp.where((near_column == near) & (sub < lane), 1.0, 0.0), axis=0, keepdims=True)
    slot = second * STEPS + near
    match = sub_f == slot
    local_id = jnp.sum(jnp.where(match, inside, 0.0), axis=1, keepdims=True)
    slot_id = jnp.sum(jnp.where(match, ids_f, 0.0), axis=1, keepdims=True)
    ahead, live = [], []
    for t in range(2):
        listed = to_column(visible[t : t + 1].astype(f32))
        here = sub == order[t : t + 1]
        sequence = jnp.sum(jnp.where(here, listed, 0.0), axis=0, keepdims=True)
        rank = jnp.sum(jnp.where(sequence == slot_id, lane_f, 0.0), axis=1, keepdims=True)
        ahead.append(jnp.where(to_row(rank) < rank, 1.0, 0.0))
        live.append(jnp.where(rank < counts_ref[t].astype(f32), 1.0, 0.0))
    return local_id, ahead, live


def fused_kernel(bands, geometry_hbm, angles_hbm, coeffs_hbm, visible_hbm, order_hbm, cot_hbm, counts_hbm,
                 pic_ref, basis_ref, terms_ref, out_ref,
                 geometry, angles, coeffs, visible, order, cot, counts_ref, geo, ang, coe, rows,
                 coef, part, first, summed, second, colour,
                 asks_out, asks, answer, held, w_ref, ratio_ref, c_ref, a_ref,
                 packed, landed, sums, got_core, all_picks, d_ref,
                 local_sems, ask_sems, back_sems, give_sems, share_sems, attr_sems):
    f32, bf16 = jnp.float32, jnp.bfloat16
    tile, attr = lax.axis_index("tile"), lax.axis_index("attr")
    core = attr + 1 - 2 * (attr % 2)
    across = (attr + 2) % 4
    mine = attr % 2
    greeted = greet((tile, attr, STEPS, (core, across, (core + 2) % 4)))

    pairs = ((visible_hbm, visible), (order_hbm, order), (counts_hbm, counts_ref), (angles_hbm, angles),
             (coeffs_hbm, coeffs), (geometry_hbm, geometry), (cot_hbm, cot))
    loads = [pltpu.make_async_copy(a, b, local_sems.at[n]) for n, (a, b) in enumerate(pairs)]
    for load in loads:
        load.start()

    asks_out[...] = jnp.zeros_like(asks_out)
    answer[...] = jnp.zeros_like(answer)
    for load in loads[:3]:
        load.wait()
    local_id, ahead, live = slot_tables(tile, visible[...], order[...], counts_ref)
    lane = lax.broadcasted_iota(jnp.int32, (SLOTS, 128), 1)
    block = (lane & (OWNED - 1)).astype(f32)
    wanted = jnp.where((block == local_id) & (lane < TRIPLE * OWNED), 1.0, 0.0)
    for k in range(PAIR):
        asks_out[pl.ds(k, STEPS, stride=8), :] = wanted[k * STEPS : (k + 1) * STEPS]
    for load in loads[3:]:
        load.wait()

    def relay(b, _):
        for h in range(BLOCK // 128):
            at = pl.ds(pl.multiple_of(b * BLOCK + h * 128, 128), 128)
            geo[h, pl.ds(pl.multiple_of(b * 8, 8), 6), :] = geometry[:, at]
            ang[h, pl.ds(pl.multiple_of(b * 8, 8), 2), :] = angles[:, at]
            coe[h, pl.ds(pl.multiple_of(b * 16, 8), 3 * bands), :] = coeffs[:, at]
        return 0

    lax.fori_loop(0, OWNED, relay, 0, unroll=4)

    def plane(ref, k, pitch):
        halves = [ref[h, pl.ds(k, OWNED, stride=pitch), :] for h in range(BLOCK // 128)]
        return jnp.concatenate(halves, axis=1)

    for k, value in enumerate(sh_basis([plane(ang, k, 8) for k in range(2)])):
        rows[k] = value
    first_band = attr * bands
    total = [jnp.zeros((OWNED, BLOCK), f32) for _ in range(3)]
    for k in range(bands):
        value = rows[first_band + k]
        basis_ref[k] = value
        for c in range(3):
            total[c] = total[c] + value * plane(coe, 3 * k + c, 16)
    for c in range(3):
        part[c * OWNED : (c + 1) * OWNED, :] = total[c]
    pl.semaphore_wait(*greeted)

    def ask(i):
        return pltpu.make_async_remote_copy(
            src_ref=asks_out.at[pl.ds(pl.multiple_of(i * 8, 8), 8)], dst_ref=asks.at[pl.ds(pl.multiple_of(i * 8, 8), 8)],
            send_sem=ask_sems.at[0, i], recv_sem=ask_sems.at[1, i],
            device_id=((tile + i) % STEPS, attr), device_id_type=MESH,
        )

    def back(i, part):
        at, size = ((0, 16), (16, 8))[part]
        return pltpu.make_async_remote_copy(
            src_ref=answer.at[:, pl.ds(pl.multiple_of(i * MSG + at, 8), size)], dst_ref=held.at[i, :, pl.ds(at, size)],
            send_sem=back_sems.at[0, part, i], recv_sem=back_sems.at[1, part, i],
            device_id=((tile + STEPS - i) % STEPS, attr), device_id_type=MESH,
        )

    def give(i, d):
        slot = d * STEPS + i
        return pltpu.make_async_remote_copy(
            src_ref=packed.at[i, (attr + d) % 2], dst_ref=landed.at[pl.ds(pl.multiple_of(slot * MSG, 8), MSG)],
            send_sem=give_sems.at[0, slot], recv_sem=give_sems.at[1, slot],
            device_id=((tile + i) % STEPS, (attr + d) % 4), device_id_type=MESH,
        )

    def share(d):
        return exchange(all_picks.at[0], all_picks.at[d], share_sems, d, (tile, (attr + d) % 4))

    upper = tile // (STEPS // 2)

    def near(n):
        return (n + upper * (STEPS - 2 * n)) % STEPS

    def far(n):
        return (STEPS - n + upper * (2 * n - STEPS)) % STEPS

    def each(act):
        def step(n, _):
            act(far(n))
            return 0

        lax.fori_loop(1, STEPS, step, 0)

    each(lambda i: ask(i).start())
    colour_one = exchange(part, first, attr_sems, 0, (tile, core))
    colour_one.start()
    asks[0:8, :] = asks_out[0:8, :]

    terms = splat_terms([plane(geo, k, 8) for k in range(6)])
    for k, value in enumerate(terms):
        terms_ref[k] = value
    for k, value in enumerate(exponent_rows(terms)):
        coef[k] = stack3(value)

    colour_one.wait()
    summed[...] = part[...] + first[...]
    colour_two = exchange(summed, second, attr_sems, 1, (tile, across))
    colour_two.start()

    each(lambda i: ask(i).wait_recv())
    picks = jnp.concatenate([asks[pl.ds(k, STEPS, stride=8), :] for k in range(PAIR)], axis=0)
    pick = picks.astype(bf16)[:, : TRIPLE * OWNED]
    all_picks[0] = picks
    for d in range(1, 4):
        share(d).start()

    def pick_row(values, at):
        found = dot(pick, values)
        for k in range(PAIR):
            scatter(answer, at[k], MSG, found[k * STEPS : (k + 1) * STEPS])

    for r in range(6):
        pick_row(coef[r], (r, 8 + r))
    each(lambda i: back(i, 0).start())
    held[0, :, 0:16] = answer[:, 0:16, :]

    row = lax.broadcasted_iota(jnp.int32, (2 * BLOCK, BLOCK), 0) & (BLOCK - 1)
    col = lax.broadcasted_iota(jnp.int32, (2 * BLOCK, BLOCK), 1)
    before = jnp.where(row < col, -1.0, 0.0).astype(bf16)
    upto = jnp.where(row <= col, 1.0, 0.0).astype(bf16)
    mono_cols = pixel_monomials((PIX, 32), 0)
    mono_rows = pixel_monomials((8, PIX), 1)
    eight = lax.broadcasted_iota(jnp.int32, (8, BLOCK), 0)
    own_rows = [(eight >= 4 * k) & (eight < 4 * k + 3) for k in range(PAIR)]

    def halves(x):
        high = x.astype(bf16).astype(f32)
        return high, x - high

    def shape_pair(i):
        alphas, losses = [], []
        for k in range(PAIR):
            high, mid, low = [p.astype(f32) for p in split3(tile_of(held, i, 8 * k))]
            coefs = jnp.concatenate([high, mid, low, jnp.zeros_like(low)], axis=0).astype(bf16)
            alpha = jnp.exp2(dot(mono_cols, coefs))
            loss = jnp.log(1.0 - alpha) * -LOG2E
            alphas.append(alpha)
            losses.append(split2(loss))
            ratio_ref[i, k] = alpha * jnp.exp2(loss)
        keep = dot(jnp.concatenate(losses, axis=0), before)
        for k in range(PAIR):
            w_ref[i, k] = split2(alphas[k] * jnp.exp2(keep[k * PIX : (k + 1) * PIX]))

    def show_pair(i):
        c_high, c_low = halves(tile_of(held, i, 16))
        seen = None
        for k in range(PAIR):
            w2 = w_ref[i, k]
            one = jnp.where(eight == 4 * k + 3, 1.0, 0.0)
            lhs = jnp.concatenate([jnp.where(own_rows[k], c_high, one), jnp.where(own_rows[k], c_low, 0.0)], axis=0)
            lhs = lhs.astype(bf16)
            contract = (((1,), (1,)), ((), ()))
            shown = lax.dot_general(lhs, w2[:, :BLOCK], contract, preferred_element_type=f32)
            shown = shown + lax.dot_general(lhs, w2[:, BLOCK:], contract, preferred_element_type=f32)
            shown = shown[:8] + shown[8:]
            seen = shown if seen is None else seen + shown
        put_rows(c_ref, pl.ds(pl.multiple_of(i * 8, 8), 8), seen)

    def forward_early(n, _):
        i = near(n)
        back(i, 0).wait_recv()
        shape_pair(i)
        return 0

    def forward(n, _):
        i, shown = near(n), near(n - LAG)
        back(i, 0).wait_recv()

        @pl.when(n > LAG)
        def _():
            back(shown, 1).wait_recv()

        show_pair(shown)
        shape_pair(i)
        return 0

    shape_pair(0)
    colour_two.wait()
    for c in range(3):
        piece = slice(c * OWNED, (c + 1) * OWNED)
        pick_row(stack3(summed[piece] + second[piece] + 0.5), (16 + c, 20 + c))
    each(lambda i: back(i, 1).start())
    held[0, :, 16:24] = answer[:, 16:24, :]
    lax.fori_loop(1, LAG, forward_early, 0)
    lax.fori_loop(LAG, STEPS, forward, 0)
    for n in range(STEPS - LAG, STEPS):
        back(near(n), 1).wait_recv()
    for n in range(STEPS - LAG, STEPS):
        show_pair(near(n))

    def by_slot(ref, c):
        return jnp.concatenate([gather(ref, c + 4 * k, 8) for k in range(PAIR)], axis=0)

    local = [by_slot(c_ref, c) for c in range(4)]
    spread = [jnp.zeros((SLOTS, PIX), f32) for _ in range(4)]
    for t in range(2):
        def earlier(values):
            out = jnp.zeros((SLOTS, PIX), f32)
            for s in range(SLOTS):
                out = out + ahead[t][:, s : s + 1] * values[s : s + 1, :]
            return out

        through = jnp.broadcast_to(live[t], (SLOTS, PIX))
        for s in range(SLOTS):
            through = through * (1.0 - ahead[t][:, s : s + 1] * local[3][s : s + 1, :])
        shade = jnp.zeros((SLOTS, PIX), f32)
        for c in range(3):
            g = cot[c, t : t + 1, :]
            lit = through * local[c]
            pic_ref[c, t : t + 1, :] = jnp.sum(lit, axis=0, keepdims=True)
            shade = shade + lit * g
            spread[c] = spread[c] + through * g
        behind = earlier(shade) - jnp.sum(shade, axis=0, keepdims=True)
        spread[3] = spread[3] + live[t] * behind
    for c in range(4):
        for k in range(PAIR):
            scatter(a_ref, c + 4 * k, 8, spread[c][k * STEPS : (k + 1) * STEPS])

    def slope_pair(i):
        a = get_rows(a_ref, pl.ds(pl.multiple_of(i * 8, 8), 8))
        a_high, a_low = halves(a)
        c_high, c_low = halves(tile_of(held, i, 16))
        columns = jnp.transpose(jnp.concatenate([a_high, a_low, a_high, a], axis=0))
        v_lhs = columns.astype(bf16)
        values = []
        for k in range(PAIR):
            ch, cl = jnp.where(own_rows[k], c_high, 0.0), jnp.where(own_rows[k], c_low, 0.0)
            v_rhs = jnp.concatenate([ch, ch, cl, jnp.zeros_like(cl)], axis=0).astype(bf16)
            w2 = w_ref[i, k]
            values.append((w2[:, :BLOCK].astype(f32) + w2[:, BLOCK:].astype(f32)) * dot(v_lhs, v_rhs))
        total = dot(jnp.concatenate([split2(value) for value in values], axis=0), upto)
        for k in range(PAIR):
            beyond = total[k * PIX : (k + 1) * PIX] + columns[:, 27 + 4 * k : 28 + 4 * k]
            d_ref[k] = split2(values[k] + ratio_ref[i, k] * beyond)

    def sum_pair(i):
        a_high, a_low = halves(get_rows(a_ref, pl.ds(pl.multiple_of(i * 8, 8), 8)))
        tint = None
        for k in range(PAIR):
            d2, w2 = d_ref[k], w_ref[i, k]
            moments = dot(mono_rows, d2[:, :BLOCK]) + dot(mono_rows, d2[:, BLOCK:])
            put_rows(packed.at[i], pl.ds(8 * k, 8), moments)
            lhs = jnp.concatenate([jnp.where(own_rows[k], a_high, 0.0), jnp.where(own_rows[k], a_low, 0.0)], axis=0)
            lhs = lhs.astype(bf16)
            grads = dot(lhs, w2[:, :BLOCK]) + dot(lhs, w2[:, BLOCK:])
            grads = grads[:8] + grads[8:]
            tint = grads if tint is None else tint + grads
        put_rows(packed.at[i], pl.ds(16, 8), tint)

    def backward(n, _):
        i = far(n)
        sum_pair(i)
        slope_pair(far(n + 1))
        for d in range(4):
            give(i, d).start()
        return 0

    slope_pair(far(1))
    lax.fori_loop(1, STEPS, backward, 0)
    sum_pair(0)
    for d in range(1, 4):
        give(0, d).start()
    landed[0:MSG, :] = packed[0, mine]

    for d in range(1, 4):
        share(d).wait_recv()
    chosen = [all_picks[d, k * STEPS : (k + 1) * STEPS, :] for k in range(PAIR) for d in range(4)]
    tall = jnp.concatenate(chosen * TRIPLE + [jnp.zeros((256 - TRIPLE * 4 * SLOTS, 128), f32)], axis=0)
    put = jnp.transpose(tall)[:OWNED, : TRIPLE * 4 * SLOTS].astype(bf16)

    def take_give(n, _):
        for d in range(4):
            give(n, d).wait_recv()
        return 0

    lax.fori_loop(1, STEPS, take_give, 0)
    for d in range(1, 4):
        give(0, d).wait_recv()
    for r in range(0, 9, 2):
        both = []
        for q in range(r, min(r + 2, 9)):
            at = (q, 8 + q) if q < 6 else (10 + q, 14 + q)
            both.append(jnp.concatenate([landed[pl.ds(at[k], 4 * STEPS, stride=MSG), :] for k in range(PAIR)], axis=0))
        found = dot(put, stack3(jnp.concatenate(both, axis=1)))
        for q in range(len(both)):
            sums[(r + q) * OWNED : (r + q + 1) * OWNED, :] = found[:, q * 128 : (q + 1) * 128]

    swap = exchange(sums, got_core, attr_sems, 2, (tile, core))
    swap.start()
    out_ref[mine] = sums[...]
    for d in range(1, 4):
        share(d).wait_send()
        give(0, d).wait_send()

    def sent_give(n, _):
        for d in range(4):
            give(n, d).wait_send()
        return 0

    lax.fori_loop(1, STEPS, sent_give, 0)
    each(lambda i: ask(i).wait_send())
    each(lambda i: back(i, 0).wait_send())
    each(lambda i: back(i, 1).wait_send())
    swap.wait()
    out_ref[1 - mine] = got_core[...]


def fused(geometry, view_angles, sh_coeffs, visible, order, cot, counts):
    bands = sh_coeffs.shape[0] // 3
    sems = pltpu.SemaphoreType.DMA
    vmem = pl.BlockSpec(memory_space=pltpu.VMEM)
    ins = (geometry, view_angles, sh_coeffs, visible, order, cot, counts)
    colours = 3 * OWNED
    shapes = (cot.shape, (bands, OWNED, BLOCK), (11, OWNED, BLOCK), (2, 9 * OWNED, 128))
    return pl.pallas_call(
        functools.partial(fused_kernel, bands),
        name="splat",
        out_shape=tuple(jax.ShapeDtypeStruct(o, jnp.float32) for o in shapes),
        in_specs=[pl.BlockSpec(memory_space=pltpu.HBM)] * len(ins),
        out_specs=tuple(vmem for _ in shapes),
        scratch_shapes=[pltpu.VMEM(x.shape, x.dtype) for x in ins[:-1]] + [
            pltpu.SMEM(counts.shape, counts.dtype),
            floats(BLOCK // 128, 8 * OWNED, 128), floats(BLOCK // 128, 8 * OWNED, 128),
            floats(BLOCK // 128, 16 * OWNED, 128), floats(16, OWNED, BLOCK),
            pltpu.VMEM((6, TRIPLE * OWNED, BLOCK), jnp.bfloat16), floats(colours, BLOCK), floats(colours, BLOCK),
            floats(colours, BLOCK), floats(colours, BLOCK), floats(8, 128),
            floats(8 * STEPS, 128), floats(8 * STEPS, 128), floats(2, STEPS * MSG, 128), floats(STEPS, 2, MSG, 128),
            pltpu.VMEM((STEPS, PAIR, PIX, 2 * BLOCK), jnp.bfloat16), floats(STEPS, PAIR, PIX, BLOCK),
            floats(2, 8 * STEPS, 128), floats(2, 8 * STEPS, 128),
            floats(STEPS, 2, MSG, 128), floats(4 * STEPS * MSG, 128), floats(9 * OWNED, 128), floats(9 * OWNED, 128),
            floats(4, SLOTS, 128), pltpu.VMEM((PAIR, PIX, 2 * BLOCK), jnp.bfloat16),
            sems((len(ins),)), sems((2, STEPS)), sems((2, 2, STEPS)), sems((2, 4 * STEPS)), sems((2, 4)), sems((2, 3)),
        ],
        compiler_params=pltpu.CompilerParams(
            collective_id=3, has_side_effects=True, vmem_limit_bytes=40 * 1024 * 1024
        ),
    )(*[pltpu.with_memory_space_constraint(x, pltpu.HBM) for x in ins])


def finish_kernel(bands, sums_ref, terms_ref, basis_ref, pic_ref, geometry_ref, coeffs_ref, picture_ref, both, geo, coe):
    for h in range(BLOCK // 128):
        both[:, h * 128 : (h + 1) * 128] = sums_ref[h]
    final_kernel(OWNED, bands, both, terms_ref, basis_ref, geometry_ref, coeffs_ref, geo, coe)
    picture_ref[...] = pic_ref[...]


def finish(sums, terms, basis, pic):
    bands = basis.shape[0]
    vmem = pl.BlockSpec(memory_space=pltpu.VMEM)
    shapes = ((6, OWNED * BLOCK), (3 * bands, OWNED * BLOCK), pic.shape)
    return pl.pallas_call(
        functools.partial(finish_kernel, bands),
        name="finish",
        out_shape=tuple(jax.ShapeDtypeStruct(o, jnp.float32) for o in shapes),
        in_specs=[vmem] * 4,
        out_specs=(vmem,) * 3,
        scratch_shapes=[
            floats(9 * OWNED, BLOCK),
            floats(BLOCK // 128, 8 * OWNED, 128),
            floats(BLOCK // 128, 16 * OWNED, 128),
        ],
        compiler_params=pltpu.CompilerParams(vmem_limit_bytes=12 * 1024 * 1024),
    )(sums, terms, basis, pic)


def local_fused(geometry, sh_coeffs, view_angles, visible, counts, order, image_cot):
    cot = jnp.swapaxes(image_cot, 0, 1)
    pic, basis, terms, sums = fused(geometry, view_angles, sh_coeffs, visible, order, cot, counts)
    grad_geometry, grad_sh, picture = finish(sums, terms, basis, pic)
    return (jnp.swapaxes(picture, 0, 1), grad_geometry, grad_sh)


def local(geometry, sh_coeffs, view_angles, visible, counts, order, image_cot):
    owners = lax.axis_size("tile")
    tiles, vis = visible.shape
    owned = geometry.shape[1] // BLOCK
    fits = (owners, vis, tiles, owned, lax.axis_size("attr")) == (8, 16, 2, 32, 4)
    run = local_fused if fits else local_general
    return run(geometry, sh_coeffs, view_angles, visible, counts, order, image_cot)


def solution(mesh):
    in_specs = (
        P(None, "tile"),
        P("attr", "tile"),
        P(None, "tile"),
        P(("tile", "attr"), None),
        P(("tile", "attr")),
        P(("tile", "attr"), None),
        P(("tile", "attr"), None, None),
    )
    out_specs = (P(("tile", "attr"), None, None), P(None, "tile"), P("attr", "tile"))
    return jax.shard_map(local, mesh=mesh, in_specs=in_specs, out_specs=out_specs, check_vma=False)
```

```python
import functools
import jax
import jax.numpy as jnp
from jax import lax
from jax.experimental import pallas as pl
from jax.experimental.pallas import tpu as pltpu
from jax.sharding import PartitionSpec as P

BLOCK = 256
SIDE = 16
PIX = SIDE * SIDE
MID = 0.5 * SIDE
LOG2E = 1.4426950408889634
LN2 = 0.6931471805599453


band_zero = 0.28209479177387814
band_one = 0.4886025119029199
band_two = (
    1.0925484305920792,
    -1.0925484305920792,
    0.31539156525252005,
    -1.0925484305920792,
    0.5462742152960396,
)
band_three = (
    -0.5900435899266435,
    2.890611442640554,
    -0.4570457994644658,
    0.3731763325901154,
    -0.4570457994644658,
    1.445305721320277,
    -0.5900435899266435,
)


def sh_basis(view_angles):
    azimuth = view_angles[0]
    elevation = view_angles[1]
    dir_x = jnp.cos(azimuth) * jnp.cos(elevation)
    dir_y = jnp.sin(azimuth) * jnp.cos(elevation)
    dir_z = jnp.sin(elevation)
    sq_x = dir_x * dir_x
    sq_y = dir_y * dir_y
    sq_z = dir_z * dir_z
    basis_rows = [
        band_zero * jnp.ones_like(dir_x),
        -band_one * dir_y,
        band_one * dir_z,
        -band_one * dir_x,
        band_two[0] * dir_x * dir_y,
        band_two[1] * dir_y * dir_z,
        band_two[2] * (2.0 * sq_z - sq_x - sq_y),
        band_two[3] * dir_x * dir_z,
        band_two[4] * (sq_x - sq_y),
        band_three[0] * dir_y * (3.0 * sq_x - sq_y),
        band_three[1] * dir_x * dir_y * dir_z,
        band_three[2] * dir_y * (4.0 * sq_z - sq_x - sq_y),
        band_three[3] * dir_z * (2.0 * sq_z - 3.0 * sq_x - 3.0 * sq_y),
        band_three[4] * dir_x * (4.0 * sq_z - sq_x - sq_y),
        band_three[5] * dir_z * (sq_x - sq_y),
        band_three[6] * dir_x * (sq_x - 3.0 * sq_y),
    ]
    return basis_rows


def split2(x):
    high = x.astype(jnp.bfloat16)
    low = (x - high.astype(jnp.float32)).astype(jnp.bfloat16)
    return jnp.concatenate([high, low], axis=1)


def dot(a, b):
    return jnp.dot(a, b, preferred_element_type=jnp.float32)


def blend_kernel(tiles, seq_ref, counts_ref, held_ref, cot_rows_ref, cot_cols_ref, pic_ref, grad_ref, part_ref, ratio_ref):
    f32, bf16 = jnp.float32, jnp.bfloat16
    row = lax.broadcasted_iota(jnp.int32, (2 * BLOCK, BLOCK), 0)
    row = jnp.where(row >= BLOCK, row - BLOCK, row)
    col = lax.broadcasted_iota(jnp.int32, (2 * BLOCK, BLOCK), 1)
    before = jnp.where(row < col, -1.0, 0.0).astype(bf16)
    upto = jnp.where(row <= col, 1.0, 0.0).astype(bf16)

    def monomials(shape, dim, width):
        pixel = lax.broadcasted_iota(jnp.int32, shape, dim)
        kind = lax.broadcasted_iota(jnp.int32, shape, 1 - dim) & (width - 1)
        x = (pixel & (SIDE - 1)).astype(f32) + (0.5 - MID)
        y = (pixel // SIDE).astype(f32) + (0.5 - MID)
        out = jnp.where(kind == 0, 1.0, 0.0)
        for k, value in ((1, x), (2, y), (3, x * x), (4, x * y), (5, y * y)):
            out = jnp.where(kind == k, value, out)
        return out.astype(bf16)

    mono_cols = monomials((PIX, 48), 0, 16)
    mono_rows = monomials((8, PIX), 1, 8)
    cot_lhs, cot_rows = [], []
    for t in range(tiles):
        g = cot_cols_ref[t]
        high = g.astype(bf16).astype(f32)
        lane = lax.broadcasted_iota(jnp.int32, g.shape, 1)
        cot_lhs.append(jnp.where(lane < 48, high, g - high).astype(bf16))
        g = cot_rows_ref[t]
        high = g.astype(bf16).astype(f32)
        cot_rows.append(jnp.concatenate([high, g - high], axis=0).astype(bf16))

    grad_ref[...] = jnp.zeros_like(grad_ref)
    lives = [counts_ref[t] for t in range(tiles)]
    longest = functools.reduce(jnp.maximum, lives)

    lhs = []
    for t in range(tiles):
        wide = jnp.concatenate([mono_cols.astype(f32), jnp.zeros((PIX, 48), f32)], axis=1)
        lhs.append(jnp.concatenate([wide.astype(bf16), cot_lhs[t]], axis=0))
    head = lax.broadcasted_iota(jnp.int32, (16, BLOCK), 0) == 0

    def forward(j, carry):
        keep_before, sum_before, pictures = carry
        alphas, values, losses, helds, spots = [], [], [], [], []
        for t in range(tiles):
            at = seq_ref[t, j]
            hidden = jnp.where(j < lives[t], 0.0, -16384.0)
            held = held_ref[at]
            parts = split3(jnp.where(head, held + hidden, held))
            rows = jnp.concatenate(parts, axis=0)
            both = dot(lhs[t], jnp.concatenate([rows, rows], axis=0))
            alpha = jnp.exp2(both[:PIX])
            alphas.append(alpha)
            values.append(both[PIX:])
            losses.append(jnp.log(1.0 - alpha) * -LOG2E)
            helds.append(jnp.concatenate(parts[:2], axis=0))
            spots.append(at)
        loss = jnp.concatenate(losses, axis=0)
        keep_in = dot(split2(loss), before) + keep_before
        keep_before = keep_in[:, BLOCK - 1 :] - loss[:, BLOCK - 1 :]
        alpha = jnp.concatenate(alphas, axis=0)
        weight = alpha * jnp.exp2(keep_in)
        value = weight * jnp.concatenate(values, axis=0)
        total = dot(split2(value), upto) + sum_before
        sum_before = total[:, BLOCK - 1 :]
        ratio = alpha * jnp.exp2(loss)
        part_ref[j] = value + ratio * total
        ratio_ref[j] = ratio
        w2 = split2(weight)
        shown = []
        for t in range(tiles):
            w_high, w_low = w2[t * PIX : (t + 1) * PIX, :BLOCK], w2[t * PIX : (t + 1) * PIX, BLOCK:]
            rows = lax.dot_general(helds[t], w_high, (((1,), (1,)), ((), ())), preferred_element_type=f32)
            rows = rows + lax.dot_general(helds[t], w_low, (((1,), (1,)), ((), ())), preferred_element_type=f32)
            shown.append(pictures[t] + rows[:16] + rows[16:])
            colour_grad = dot(cot_rows[t], w_high) + dot(cot_rows[t], w_low)
            grad_ref[spots[t], 0:8, :] += colour_grad[:8] + colour_grad[8:]
        return keep_before, sum_before, tuple(shown)

    zero = jnp.zeros((tiles * PIX, 1), f32)
    start = (zero, zero, tuple(jnp.zeros((16, PIX), f32) for _ in range(tiles)))
    _, ends, pictures = lax.fori_loop(0, longest, forward, start)
    for t in range(tiles):
        pic_ref[t] = pictures[t]

    def backward(j, _):
        for t in range(tiles):
            pixels = slice(t * PIX, (t + 1) * PIX)
            d2 = split2(part_ref[j, pixels] - ratio_ref[j, pixels] * ends[pixels])
            moments = dot(mono_rows, d2[:, :BLOCK]) + dot(mono_rows, d2[:, BLOCK:])
            grad_ref[seq_ref[t, j], 8:16, :] += moments
        return 0

    lax.fori_loop(0, longest, backward, 0)


def blend(seq, counts, held, image_cot):
    tiles = image_cot.shape[0]
    rows = held.shape[0]
    cot_rows = jnp.pad(image_cot, ((0, 0), (0, 5), (0, 0)))
    cot_cols = jnp.pad(jnp.swapaxes(image_cot, 1, 2), ((0, 0), (0, 0), (6, 7)))
    cot_cols = jnp.tile(cot_cols, (1, 1, 6))
    smem = pl.BlockSpec(memory_space=pltpu.SMEM)
    vmem = pl.BlockSpec(memory_space=pltpu.VMEM)
    picture, grads = pl.pallas_call(
        functools.partial(blend_kernel, tiles),
        name="blend",
        out_shape=(
            jax.ShapeDtypeStruct((tiles, 16, PIX), jnp.float32),
            jax.ShapeDtypeStruct((rows, 16, BLOCK), jnp.float32),
        ),
        in_specs=[smem, smem, vmem, vmem, vmem],
        out_specs=(vmem, vmem),
        scratch_shapes=[
            pltpu.VMEM((seq.shape[1], tiles * PIX, BLOCK), jnp.float32),
            pltpu.VMEM((seq.shape[1], tiles * PIX, BLOCK), jnp.float32),
        ],
        compiler_params=pltpu.CompilerParams(vmem_limit_bytes=28 * 1024 * 1024),
    )(seq, counts, held, cot_rows, cot_cols)
    return picture[:, 6:9], grads


def splat_terms(geometry):
    mx, my = geometry[0] - MID, geometry[1] - MID
    c, s = jnp.cos(geometry[4]), jnp.sin(geometry[4])
    e1, e2 = jnp.exp(-2.0 * geometry[2]), jnp.exp(-2.0 * geometry[3])
    cc, ss, cs = c * c, s * s, c * s
    a = cc * e1 + ss * e2
    b = cs * (e1 - e2)
    d = ss * e1 + cc * e2
    return mx, my, e1, e2, cc, ss, cs, a, b, d, geometry[5]


def exponent_rows(terms):
    mx, my, e1, e2, cc, ss, cs, a, b, d, logit = terms
    bx, by = a * mx + b * my, b * mx + d * my
    log_opacity = jnp.minimum(logit, 0.0) - jnp.log1p(jnp.exp(-jnp.abs(logit)))
    one = log_opacity - 0.5 * (mx * bx + my * by)
    return [LOG2E * r for r in (one, bx, by, -0.5 * a, -b, -0.5 * d)]


def geometry_grads(terms, m):
    mx, my, e1, e2, cc, ss, cs, a, b, d, logit = terms
    n0 = m[0]
    nx, ny = m[1] - mx * n0, m[2] - my * n0
    nxx = m[3] - mx * (m[1] + nx)
    nxy = m[4] - mx * m[2] - my * nx
    nyy = m[5] - my * (m[2] + ny)
    return [
        a * nx + b * ny,
        b * nx + d * ny,
        e1 * (cc * nxx + 2.0 * cs * nxy + ss * nyy),
        e2 * (ss * nxx - 2.0 * cs * nxy + cc * nyy),
        (e2 - e1) * (cs * (nyy - nxx) + (cc - ss) * nxy),
        n0 / (1.0 + jnp.exp(logit)),
    ]


MESH = pl.DeviceIdType.MESH


def greet(peers):
    barrier = pltpu.get_barrier_semaphore()
    tile, attr, owners, extra = peers

    def hello(step, _):
        other = (tile + step) % owners
        pl.semaphore_signal(barrier, inc=1, device_id=(other, attr), device_id_type=MESH)
        return 0

    lax.fori_loop(1, owners, hello, 0)
    for other in extra:
        pl.semaphore_signal(barrier, inc=1, device_id=(tile, other), device_id_type=MESH)
    return barrier, owners - 1 + len(extra)


def split3(x):
    high = x.astype(jnp.bfloat16)
    rest = x - high.astype(jnp.float32)
    mid = rest.astype(jnp.bfloat16)
    return high, mid, (rest - mid.astype(jnp.float32)).astype(jnp.bfloat16)


def exchange(src, dst, sems, k, device):
    return pltpu.make_async_remote_copy(
        src_ref=src, dst_ref=dst, send_sem=sems.at[0, k], recv_sem=sems.at[1, k],
        device_id=device, device_id_type=MESH,
    )


def fetch_kernel(dims, want_ref, coef_ref, part_ref, held_ref, asked_ref,
                 asks, answer, landed, first, summed, second, tile_sems, back_sems, attr_sems):
    owners, owned, cap, message, stride = dims
    f32 = jnp.float32
    tile, attr = lax.axis_index("tile"), lax.axis_index("attr")
    core = attr + 1 - 2 * (attr % 2)
    across = (attr + 2) % 4
    pl.semaphore_wait(*greet((tile, attr, owners, (core, across))))

    colour_one = exchange(part_ref, first, attr_sems, 0, (tile, core))
    colour_one.start()

    def ask(other, sender):
        return pltpu.make_async_remote_copy(
            src_ref=want_ref.at[other], dst_ref=asks.at[sender],
            send_sem=tile_sems.at[0, other], recv_sem=tile_sems.at[1, sender],
            device_id=(other, attr), device_id_type=MESH,
        )

    def send_ask(step, _):
        ask((tile + step) % owners, tile).start()
        return 0

    lax.fori_loop(1, owners, send_ask, 0)
    asks[tile] = want_ref[tile]

    colour_one.wait()
    summed[...] = part_ref[...] + first[...]
    colour_two = exchange(summed, second, attr_sems, 1, (tile, across))
    colour_two.start()

    def take_ask(step, _):
        other = (tile + step) % owners
        ask(other, other).wait()
        return 0

    lax.fori_loop(1, owners, take_ask, 0)

    per = 128 // stride
    lanes = owners // per
    rows = []
    for tile_at in range(lanes):
        rows.append(functools.reduce(jnp.add, [asks[tile_at * per + k] for k in range(per)]))
    asked = jnp.concatenate(rows, axis=1) - 1.0
    asked_ref[...] = asked
    wide = 9 * owned
    columns = []
    for tile_at in range(lanes):
        square = jnp.concatenate([rows[tile_at] - 1.0] * 16, axis=0)
        columns.append(jnp.transpose(square)[:, 0:1])
    column = jnp.concatenate(columns, axis=0)
    lane = lax.broadcasted_iota(jnp.int32, (owners * stride, wide), 1).astype(f32)
    pick = jnp.where(lane == column, 1.0, 0.0).astype(jnp.bfloat16)

    colour_two.wait()
    colour = summed[...] + second[...] + 0.5
    table = jnp.concatenate([coef_ref[...], colour], axis=0)
    high, mid, low = split3(table)
    answer[...] = (dot(pick, low) + dot(pick, mid)) + dot(pick, high)

    def back(other, sender):
        at = pl.multiple_of(other * stride, 8)
        return pltpu.make_async_remote_copy(
            src_ref=answer.at[pl.ds(at, message)], dst_ref=landed.at[sender],
            send_sem=back_sems.at[0, other], recv_sem=back_sems.at[1, sender],
            device_id=(other, attr), device_id_type=MESH,
        )

    def send_back(step, _):
        back((tile + step) % owners, tile).start()
        return 0

    lax.fori_loop(1, owners, send_back, 0)
    landed[tile] = answer[pl.ds(pl.multiple_of(tile * stride, 8), message), :]
    held_ref[...] = jnp.zeros_like(held_ref)

    def take_back(step, _):
        other = (tile + step) % owners
        back(other, other).wait()
        return 0

    lax.fori_loop(1, owners, take_back, 0)

    def unpack(o, _):
        for k in range(cap):
            held_ref[o * cap + k, 0:9, :] = landed[o, 9 * k : 9 * k + 9, :]
        return 0

    lax.fori_loop(0, owners, unpack, 0)


def give_kernel(dims, grads_ref, asked_ref, out_ref,
                packed, landed, sums, first, half, second, third, tile_sems, attr_sems):
    owners, owned, cap, message, stride = dims
    f32 = jnp.float32
    tile, attr = lax.axis_index("tile"), lax.axis_index("attr")
    core = attr + 1 - 2 * (attr % 2)
    across = (attr + 2) % 4
    mine = attr % 2

    if message < stride:
        landed[...] = jnp.zeros_like(landed)
    greeted = greet((tile, attr, owners, (core, across)))
    packed[...] = jnp.zeros_like(packed)

    def pack(o, _):
        for k in range(cap):
            packed[o, 9 * k : 9 * k + 6, :] = grads_ref[o * cap + k, 8:14, :]
            packed[o, 9 * k + 6 : 9 * k + 9, :] = grads_ref[o * cap + k, 0:3, :]
        return 0

    lax.fori_loop(0, owners, pack, 0)
    pl.semaphore_wait(*greeted)

    def give(other, sender):
        at = pl.multiple_of(sender * stride, 8)
        return pltpu.make_async_remote_copy(
            src_ref=packed.at[other], dst_ref=landed.at[pl.ds(at, message)],
            send_sem=tile_sems.at[0, other], recv_sem=tile_sems.at[1, sender],
            device_id=(other, attr), device_id_type=MESH,
        )

    def send_give(step, _):
        give((tile + step) % owners, tile).start()
        return 0

    lax.fori_loop(1, owners, send_give, 0)
    landed[pl.ds(pl.multiple_of(tile * stride, 8), message), :] = packed[tile]
    wide = 9 * owned
    row = lax.broadcasted_iota(jnp.int32, (wide, owners * stride), 0).astype(f32)
    pick = jnp.where(row == asked_ref[0:1, :], 1.0, 0.0).astype(jnp.bfloat16)

    def take_give(step, _):
        other = (tile + step) % owners
        give(other, other).wait()
        return 0

    lax.fori_loop(1, owners, take_give, 0)
    high, mid, low = split3(landed[...])
    total = (dot(pick, low) + dot(pick, mid)) + dot(pick, high)
    cut = wide // 2
    sums[0] = total[:cut]
    sums[1] = total[cut:]

    one = exchange(sums.at[1 - mine], first, attr_sems, 0, (tile, core))
    one.start()
    one.wait()
    half[...] = sums[mine] + first[...]
    two = exchange(half, second, attr_sems, 1, (tile, across))
    two.start()
    two.wait()
    half_sum = half[...] + second[...]
    first[...] = half_sum
    three = exchange(first, third, attr_sems, 2, (tile, core))
    three.start()
    three.wait()
    at = pl.multiple_of(mine * cut, 8)
    out_ref[pl.ds(at, cut), :] = half_sum
    at = pl.multiple_of((1 - mine) * cut, 8)
    out_ref[pl.ds(at, cut), :] = third[...]


def remote_call(kernel, dims, outs, ins, scratch, number, name):
    vmem = pl.BlockSpec(memory_space=pltpu.VMEM)
    return pl.pallas_call(
        functools.partial(kernel, dims),
        name=name,
        out_shape=tuple(jax.ShapeDtypeStruct(o, jnp.float32) for o in outs),
        in_specs=[vmem] * len(ins),
        out_specs=tuple(vmem for _ in outs),
        scratch_shapes=scratch,
        compiler_params=pltpu.CompilerParams(
            collective_id=number, has_side_effects=True, vmem_limit_bytes=20 * 1024 * 1024
        ),
    )(*ins)


def floats(*shape):
    return pltpu.VMEM(shape, jnp.float32)


def fetch(dims, want, coef, part):
    owners, owned, cap, message, stride = dims
    sems = pltpu.SemaphoreType.DMA
    return remote_call(
        fetch_kernel, dims,
        ((owners * cap, 16, BLOCK), (8, owners * stride)),
        (want, coef, part),
        [floats(owners, 8, 128), floats(owners * stride, BLOCK), floats(owners, message, BLOCK),
         floats(3 * owned, BLOCK), floats(3 * owned, BLOCK), floats(3 * owned, BLOCK),
         sems((2, owners)), sems((2, owners)), sems((2, 2))],
        1, "fetch",
    )


def give_back(dims, grads, asked):
    owners, owned, cap, message, stride = dims
    sems = pltpu.SemaphoreType.DMA
    cut = 9 * owned // 2
    return remote_call(
        give_kernel, dims, ((9 * owned, BLOCK),), (grads, asked),
        [floats(owners, message, BLOCK), floats(owners * stride, BLOCK), floats(2, cut, BLOCK),
         floats(cut, BLOCK), floats(cut, BLOCK), floats(cut, BLOCK), floats(cut, BLOCK),
         sems((2, owners)), sems((2, 3))],
        2, "give",
    )[0]


def prep_kernel(owned, bands, geometry_ref, angles_ref, coeffs_ref, coef_ref, part_ref, basis_ref, terms_ref,
                geo, ang, coe, rows):
    def relay(b, _):
        for h in range(BLOCK // 128):
            at = pl.ds(pl.multiple_of(b * BLOCK + h * 128, 128), 128)
            geo[h, pl.ds(pl.multiple_of(b * 8, 8), 6), :] = geometry_ref[:, at]
            ang[h, pl.ds(pl.multiple_of(b * 8, 8), 2), :] = angles_ref[:, at]
            coe[h, pl.ds(pl.multiple_of(b * 16, 8), 3 * bands), :] = coeffs_ref[:, at]
        return 0

    lax.fori_loop(0, owned, relay, 0, unroll=4)

    def plane(ref, k, pitch):
        halves = [ref[h, pl.ds(k, owned, stride=pitch), :] for h in range(BLOCK // 128)]
        return jnp.concatenate(halves, axis=1)

    terms = splat_terms([plane(geo, k, 8) for k in range(6)])
    for k, value in enumerate(terms):
        terms_ref[k] = value
    for k, value in enumerate(exponent_rows(terms)):
        coef_ref[k * owned : (k + 1) * owned, :] = value
    for k, value in enumerate(sh_basis([plane(ang, k, 8) for k in range(2)])):
        rows[k] = value
    first = lax.axis_index("attr") * bands
    total = [jnp.zeros((owned, BLOCK), jnp.float32) for _ in range(3)]
    for k in range(bands):
        value = rows[first + k]
        basis_ref[k] = value
        for c in range(3):
            total[c] = total[c] + value * plane(coe, 3 * k + c, 16)
    for c in range(3):
        part_ref[c * owned : (c + 1) * owned, :] = total[c]


def prep(geometry, view_angles, sh_coeffs, owned):
    bands = sh_coeffs.shape[0] // 3
    vmem = pl.BlockSpec(memory_space=pltpu.VMEM)
    shapes = ((6 * owned, BLOCK), (3 * owned, BLOCK), (bands, owned, BLOCK), (11, owned, BLOCK))
    return pl.pallas_call(
        functools.partial(prep_kernel, owned, bands),
        name="prep",
        out_shape=tuple(jax.ShapeDtypeStruct(o, jnp.float32) for o in shapes),
        in_specs=[vmem] * 3,
        out_specs=(vmem,) * 4,
        scratch_shapes=[
            floats(BLOCK // 128, 8 * owned, 128),
            floats(BLOCK // 128, 8 * owned, 128),
            floats(BLOCK // 128, 16 * owned, 128),
            floats(16, owned, BLOCK),
        ],
        compiler_params=pltpu.CompilerParams(vmem_limit_bytes=12 * 1024 * 1024),
    )(geometry, view_angles, sh_coeffs)


def final_kernel(owned, bands, sums_ref, terms_ref, basis_ref, geometry_ref, coeffs_ref, geo, coe):
    summed = [sums_ref[k * owned : (k + 1) * owned, :] for k in range(9)]

    def put(ref, k, pitch, value):
        for h in range(BLOCK // 128):
            ref[h, pl.ds(k, owned, stride=pitch), :] = value[:, h * 128 : (h + 1) * 128]

    for k, value in enumerate(geometry_grads([terms_ref[k] for k in range(11)], summed[:6])):
        put(geo, k, 8, value)
    for k in range(bands):
        for c in range(3):
            put(coe, 3 * k + c, 16, basis_ref[k] * summed[6 + c])

    def relay(b, _):
        for h in range(BLOCK // 128):
            at = pl.ds(pl.multiple_of(b * BLOCK + h * 128, 128), 128)
            geometry_ref[:, at] = geo[h, pl.ds(pl.multiple_of(b * 8, 8), 6), :]
            coeffs_ref[:, at] = coe[h, pl.ds(pl.multiple_of(b * 16, 8), 3 * bands), :]
        return 0

    lax.fori_loop(0, owned, relay, 0, unroll=4)


def final(sums, terms, basis, owned):
    bands = basis.shape[0]
    vmem = pl.BlockSpec(memory_space=pltpu.VMEM)
    shapes = ((6, owned * BLOCK), (3 * bands, owned * BLOCK))
    return pl.pallas_call(
        functools.partial(final_kernel, owned, bands),
        name="final",
        out_shape=tuple(jax.ShapeDtypeStruct(o, jnp.float32) for o in shapes),
        in_specs=[vmem] * 3,
        out_specs=(vmem,) * 2,
        scratch_shapes=[
            floats(BLOCK // 128, 8 * owned, 128),
            floats(BLOCK // 128, 16 * owned, 128),
        ],
        compiler_params=pltpu.CompilerParams(vmem_limit_bytes=12 * 1024 * 1024),
    )(sums, terms, basis)


def local_general(geometry, sh_coeffs, view_angles, visible, counts, order, image_cot):
    owners = lax.axis_size("tile")
    owned = geometry.shape[1] // BLOCK
    vis = visible.shape[1]
    cap = (vis + owners - 1) // owners
    coef, partial_colour, my_basis, terms = prep(geometry, view_angles, sh_coeffs, owned)

    ids = visible[0]
    owner_of, local_of = ids // owned, ids % owned
    position = jnp.arange(vis)
    rank = jnp.sum(((owner_of[None, :] == owner_of[:, None]) & (position[None, :] < position[:, None])).astype(jnp.int32), 1)
    slot = owner_of * cap + rank
    message = -(-9 * cap // 8) * 8
    stride = 16 if message <= 16 else 32
    dims = (owners, owned, cap, message, stride)
    lane = jnp.arange(128) - (lax.axis_index("tile") % (128 // stride)) * stride
    in_slot = lane[None, :, None] // 9 + jnp.arange(owners)[:, None, None] * cap
    hit = (slot[None, None, :] == in_slot) & (lane >= 0)[None, :, None] & (lane < 9 * cap)[None, :, None]
    want = jnp.sum(jnp.where(hit, 1 + local_of[None, None, :] + owned * (lane % 9)[None, :, None], 0), 2)
    want = jnp.broadcast_to(want.astype(jnp.float32)[:, None, :], (owners, 8, 128))
    slot_of = jnp.sum(jnp.where(visible[:, :, None] == ids[None, None, :], slot[None, None, :], 0), 2)
    seq = jnp.sum(jnp.where(order[:, :, None] == position[None, None, :], slot_of[:, None, :], 0), 2)

    held, asked = fetch(dims, want, coef, partial_colour)
    picture, grads = blend(seq, counts, held, image_cot)
    sums = give_back(dims, grads, asked)
    grad_geometry, grad_sh = final(sums, terms, my_basis, owned)
    return (picture, grad_geometry, grad_sh)


STEPS = 8
PAIR = 2
SLOTS = STEPS * PAIR
OWNED = 32
MSG = 24
TRIPLE = 3
LAG = 3
GIVEN = 9 * PAIR


def stack3(x):
    high, mid, low = split3(x)
    return jnp.concatenate([high, mid, low], axis=0)


def lane_halves(x):
    return [x[:, h * 128 : (h + 1) * 128] for h in range(BLOCK // 128)]


def put_rows(ref, rows, value):
    for h, part in enumerate(lane_halves(value)):
        ref[h, rows, :] = part


def get_rows(ref, rows):
    return jnp.concatenate([ref[h, rows, :] for h in range(BLOCK // 128)], axis=1)


def scatter(ref, at, pitch, value):
    put_rows(ref, pl.ds(at, STEPS, stride=pitch), value)


def gather(ref, at, pitch):
    return get_rows(ref, pl.ds(at, STEPS, stride=pitch))


def tile_of(ref, i, at):
    return jnp.concatenate([ref[i, h, at : at + 8, :] for h in range(BLOCK // 128)], axis=1)


def pixel_monomials(shape, dim):
    pixel = lax.broadcasted_iota(jnp.int32, shape, dim)
    kind = lax.broadcasted_iota(jnp.int32, shape, 1 - dim) & 7
    x = (pixel & (SIDE - 1)).astype(jnp.float32) + (0.5 - MID)
    y = (pixel // SIDE).astype(jnp.float32) + (0.5 - MID)
    out = jnp.where(kind == 0, 1.0, 0.0)
    for k, value in ((1, x), (2, y), (3, x * x), (4, x * y), (5, y * y)):
        out = jnp.where(kind == k, value, out)
    return out.astype(jnp.bfloat16)


def slot_tables(tile, visible, order, counts_ref):
    f32 = jnp.float32
    sub = lax.broadcasted_iota(jnp.int32, (SLOTS, SLOTS), 0)
    lane = lax.broadcasted_iota(jnp.int32, (SLOTS, SLOTS), 1)
    diagonal = sub == lane
    lane_f, sub_f = lane.astype(f32), sub.astype(f32)

    def to_column(row):
        return jnp.sum(jnp.where(diagonal, row, 0.0), axis=1, keepdims=True)

    def to_row(column):
        return jnp.sum(jnp.where(diagonal, column, 0.0), axis=0, keepdims=True)

    ids = visible[0:1]
    owner = ids // OWNED
    near = owner - tile
    near = jnp.where(near < 0, near + STEPS, near).astype(f32)
    ids_f = ids.astype(f32)
    inside = (ids - owner * OWNED).astype(f32)
    near_column = to_column(near)
    second = jnp.sum(jnp.where((near_column == near) & (sub < lane), 1.0, 0.0), axis=0, keepdims=True)
    slot = second * STEPS + near
    match = sub_f == slot
    local_id = jnp.sum(jnp.where(match, inside, 0.0), axis=1, keepdims=True)
    slot_id = jnp.sum(jnp.where(match, ids_f, 0.0), axis=1, keepdims=True)
    ahead, live = [], []
    for t in range(2):
        listed = to_column(visible[t : t + 1].astype(f32))
        here = sub == order[t : t + 1]
        sequence = jnp.sum(jnp.where(here, listed, 0.0), axis=0, keepdims=True)
        rank = jnp.sum(jnp.where(sequence == slot_id, lane_f, 0.0), axis=1, keepdims=True)
        ahead.append(jnp.where(to_row(rank) < rank, 1.0, 0.0))
        live.append(jnp.where(rank < counts_ref[t].astype(f32), 1.0, 0.0))
    return local_id, ahead, live


def fused_kernel(bands, geometry_hbm, angles_hbm, coeffs_hbm, visible_hbm, order_hbm, cot_hbm, counts_hbm,
                 pic_ref, basis_ref, terms_ref, out_ref,
                 geometry, angles, coeffs, visible, order, cot, counts_ref, geo, ang, coe, rows,
                 coef, part, first, summed, second, colour,
                 asks_out, asks, answer, held, w_ref, ratio_ref, c_ref, a_ref,
                 packed, landed, sums, got_core, all_picks, d_ref,
                 local_sems, ask_sems, back_sems, give_sems, share_sems, attr_sems):
    f32, bf16 = jnp.float32, jnp.bfloat16
    tile, attr = lax.axis_index("tile"), lax.axis_index("attr")
    core = attr + 1 - 2 * (attr % 2)
    across = (attr + 2) % 4
    mine = attr % 2
    greeted = greet((tile, attr, STEPS, (core, across, (core + 2) % 4)))

    pairs = ((visible_hbm, visible), (order_hbm, order), (counts_hbm, counts_ref), (angles_hbm, angles),
             (coeffs_hbm, coeffs), (geometry_hbm, geometry), (cot_hbm, cot))
    loads = [pltpu.make_async_copy(a, b, local_sems.at[n]) for n, (a, b) in enumerate(pairs)]
    for load in loads:
        load.start()

    asks_out[...] = jnp.zeros_like(asks_out)
    answer[...] = jnp.zeros_like(answer)
    for load in loads[:3]:
        load.wait()
    local_id, ahead, live = slot_tables(tile, visible[...], order[...], counts_ref)
    lane = lax.broadcasted_iota(jnp.int32, (SLOTS, 128), 1)
    block = (lane & (OWNED - 1)).astype(f32)
    wanted = jnp.where((block == local_id) & (lane < TRIPLE * OWNED), 1.0, 0.0)
    for k in range(PAIR):
        asks_out[pl.ds(k, STEPS, stride=8), :] = wanted[k * STEPS : (k + 1) * STEPS]
    for load in loads[3:]:
        load.wait()

    def relay(b, _):
        for h in range(BLOCK // 128):
            at = pl.ds(pl.multiple_of(b * BLOCK + h * 128, 128), 128)
            geo[h, pl.ds(pl.multiple_of(b * 8, 8), 6), :] = geometry[:, at]
            ang[h, pl.ds(pl.multiple_of(b * 8, 8), 2), :] = angles[:, at]
            coe[h, pl.ds(pl.multiple_of(b * 16, 8), 3 * bands), :] = coeffs[:, at]
        return 0

    lax.fori_loop(0, OWNED, relay, 0, unroll=4)

    def plane(ref, k, pitch):
        halves = [ref[h, pl.ds(k, OWNED, stride=pitch), :] for h in range(BLOCK // 128)]
        return jnp.concatenate(halves, axis=1)

    for k, value in enumerate(sh_basis([plane(ang, k, 8) for k in range(2)])):
        rows[k] = value
    first_band = attr * bands
    total = [jnp.zeros((OWNED, BLOCK), f32) for _ in range(3)]
    for k in range(bands):
        value = rows[first_band + k]
        basis_ref[k] = value
        for c in range(3):
            total[c] = total[c] + value * plane(coe, 3 * k + c, 16)
    for c in range(3):
        part[c * OWNED : (c + 1) * OWNED, :] = total[c]
    pl.semaphore_wait(*greeted)

    def ask(i):
        return pltpu.make_async_remote_copy(
            src_ref=asks_out.at[pl.ds(pl.multiple_of(i * 8, 8), 8)], dst_ref=asks.at[pl.ds(pl.multiple_of(i * 8, 8), 8)],
            send_sem=ask_sems.at[0, i], recv_sem=ask_sems.at[1, i],
            device_id=((tile + i) % STEPS, attr), device_id_type=MESH,
        )

    def back(i, part):
        at, size = ((0, 16), (16, 8))[part]
        return pltpu.make_async_remote_copy(
            src_ref=answer.at[:, pl.ds(pl.multiple_of(i * MSG + at, 8), size)], dst_ref=held.at[i, :, pl.ds(at, size)],
            send_sem=back_sems.at[0, part, i], recv_sem=back_sems.at[1, part, i],
            device_id=((tile + STEPS - i) % STEPS, attr), device_id_type=MESH,
        )

    def give(i, d):
        slot = d * STEPS + i
        return pltpu.make_async_remote_copy(
            src_ref=packed.at[i, (attr + d) % 2, pl.ds(0, GIVEN)],
            dst_ref=landed.at[pl.ds(pl.multiple_of(slot * MSG, 8), GIVEN)],
            send_sem=give_sems.at[0, slot], recv_sem=give_sems.at[1, slot],
            device_id=((tile + i) % STEPS, (attr + d) % 4), device_id_type=MESH,
        )

    def share(d):
        return exchange(all_picks.at[0], all_picks.at[d], share_sems, d, (tile, (attr + d) % 4))

    upper = tile // (STEPS // 2)

    def near(n):
        return (n + upper * (STEPS - 2 * n)) % STEPS

    def far(n):
        return (STEPS - n + upper * (2 * n - STEPS)) % STEPS

    def each(act):
        def step(n, _):
            act(far(n))
            return 0

        lax.fori_loop(1, STEPS, step, 0)

    each(lambda i: ask(i).start())
    colour_one = exchange(part, first, attr_sems, 0, (tile, core))
    colour_one.start()
    asks[0:8, :] = asks_out[0:8, :]

    terms = splat_terms([plane(geo, k, 8) for k in range(6)])
    for k, value in enumerate(terms):
        terms_ref[k] = value
    for k, value in enumerate(exponent_rows(terms)):
        coef[k] = stack3(value)

    colour_one.wait()
    summed[...] = part[...] + first[...]
    colour_two = exchange(summed, second, attr_sems, 1, (tile, across))
    colour_two.start()

    each(lambda i: ask(i).wait_recv())
    picks = jnp.concatenate([asks[pl.ds(k, STEPS, stride=8), :] for k in range(PAIR)], axis=0)
    pick = picks.astype(bf16)[:, : TRIPLE * OWNED]
    all_picks[0] = picks
    for d in range(1, 4):
        share(d).start()

    def pick_row(values, at):
        found = dot(pick, values)
        for k in range(PAIR):
            scatter(answer, at[k], MSG, found[k * STEPS : (k + 1) * STEPS])

    for r in range(6):
        pick_row(coef[r], (r, 8 + r))
    each(lambda i: back(i, 0).start())
    held[0, :, 0:16] = answer[:, 0:16, :]

    row = lax.broadcasted_iota(jnp.int32, (2 * BLOCK, BLOCK), 0) & (BLOCK - 1)
    col = lax.broadcasted_iota(jnp.int32, (2 * BLOCK, BLOCK), 1)
    before = jnp.where(row < col, -1.0, 0.0).astype(bf16)
    upto = jnp.where(row <= col, 1.0, 0.0).astype(bf16)
    mono_cols = pixel_monomials((PIX, 32), 0)
    mono_rows = pixel_monomials((8, PIX), 1)
    eight = lax.broadcasted_iota(jnp.int32, (8, BLOCK), 0)
    own_rows = [(eight >= 4 * k) & (eight < 4 * k + 3) for k in range(PAIR)]

    def halves(x):
        high = x.astype(bf16).astype(f32)
        return high, x - high

    def shape_pair(i):
        alphas, losses = [], []
        for k in range(PAIR):
            high, mid, low = [p.astype(f32) for p in split3(tile_of(held, i, 8 * k))]
            coefs = jnp.concatenate([high, mid, low, jnp.zeros_like(low)], axis=0).astype(bf16)
            alpha = jnp.exp2(dot(mono_cols, coefs))
            loss = jnp.log(1.0 - alpha) * -LOG2E
            alphas.append(alpha)
            losses.append(split2(loss))
            ratio_ref[i, k] = alpha * jnp.exp2(loss)
        keep = dot(jnp.concatenate(losses, axis=0), before)
        for k in range(PAIR):
            w_ref[i, k] = split2(alphas[k] * jnp.exp2(keep[k * PIX : (k + 1) * PIX]))

    def show_pair(i):
        c_high, c_low = halves(tile_of(held, i, 16))
        seen = None
        for k in range(PAIR):
            w2 = w_ref[i, k]
            one = jnp.where(eight == 4 * k + 3, 1.0, 0.0)
            lhs = jnp.concatenate([jnp.where(own_rows[k], c_high, one), jnp.where(own_rows[k], c_low, 0.0)], axis=0)
            lhs = lhs.astype(bf16)
            contract = (((1,), (1,)), ((), ()))
            shown = lax.dot_general(lhs, w2[:, :BLOCK], contract, preferred_element_type=f32)
            shown = shown + lax.dot_general(lhs, w2[:, BLOCK:], contract, preferred_element_type=f32)
            shown = shown[:8] + shown[8:]
            seen = shown if seen is None else seen + shown
        put_rows(c_ref, pl.ds(pl.multiple_of(i * 8, 8), 8), seen)

    def forward_early(n, _):
        i = near(n)
        back(i, 0).wait_recv()
        shape_pair(i)
        return 0

    def forward(n, _):
        i, shown = near(n), near(n - LAG)
        back(i, 0).wait_recv()

        @pl.when(n > LAG)
        def _():
            back(shown, 1).wait_recv()

        show_pair(shown)
        shape_pair(i)
        return 0

    shape_pair(0)
    colour_two.wait()
    for c in range(3):
        piece = slice(c * OWNED, (c + 1) * OWNED)
        pick_row(stack3(summed[piece] + second[piece] + 0.5), (16 + c, 20 + c))
    each(lambda i: back(i, 1).start())
    held[0, :, 16:24] = answer[:, 16:24, :]
    lax.fori_loop(1, LAG, forward_early, 0)
    lax.fori_loop(LAG, STEPS, forward, 0)
    for n in range(STEPS - LAG, STEPS):
        back(near(n), 1).wait_recv()
    for n in range(STEPS - LAG, STEPS):
        show_pair(near(n))

    def by_slot(ref, c):
        return jnp.concatenate([gather(ref, c + 4 * k, 8) for k in range(PAIR)], axis=0)

    local = [by_slot(c_ref, c) for c in range(4)]
    spread = [jnp.zeros((SLOTS, PIX), f32) for _ in range(4)]
    for t in range(2):
        def earlier(values):
            out = jnp.zeros((SLOTS, PIX), f32)
            for s in range(SLOTS):
                out = out + ahead[t][:, s : s + 1] * values[s : s + 1, :]
            return out

        through = jnp.broadcast_to(live[t], (SLOTS, PIX))
        for s in range(SLOTS):
            through = through * (1.0 - ahead[t][:, s : s + 1] * local[3][s : s + 1, :])
        shade = jnp.zeros((SLOTS, PIX), f32)
        for c in range(3):
            g = cot[c, t : t + 1, :]
            lit = through * local[c]
            pic_ref[c, t : t + 1, :] = jnp.sum(lit, axis=0, keepdims=True)
            shade = shade + lit * g
            spread[c] = spread[c] + through * g
        behind = earlier(shade) - jnp.sum(shade, axis=0, keepdims=True)
        spread[3] = spread[3] + live[t] * behind
    for c in range(4):
        for k in range(PAIR):
            scatter(a_ref, c + 4 * k, 8, spread[c][k * STEPS : (k + 1) * STEPS])

    def slope_pair(i):
        a = get_rows(a_ref, pl.ds(pl.multiple_of(i * 8, 8), 8))
        a_high, a_low = halves(a)
        c_high, c_low = halves(tile_of(held, i, 16))
        columns = jnp.transpose(jnp.concatenate([a_high, a_low, a_high, a], axis=0))
        v_lhs = columns.astype(bf16)
        values = []
        for k in range(PAIR):
            ch, cl = jnp.where(own_rows[k], c_high, 0.0), jnp.where(own_rows[k], c_low, 0.0)
            v_rhs = jnp.concatenate([ch, ch, cl, jnp.zeros_like(cl)], axis=0).astype(bf16)
            w2 = w_ref[i, k]
            values.append((w2[:, :BLOCK].astype(f32) + w2[:, BLOCK:].astype(f32)) * dot(v_lhs, v_rhs))
        total = dot(jnp.concatenate([split2(value) for value in values], axis=0), upto)
        for k in range(PAIR):
            beyond = total[k * PIX : (k + 1) * PIX] + columns[:, 27 + 4 * k : 28 + 4 * k]
            d_ref[k] = split2(values[k] + ratio_ref[i, k] * beyond)

    def sum_pair(i):
        a_high, a_low = halves(get_rows(a_ref, pl.ds(pl.multiple_of(i * 8, 8), 8)))
        moments, tint = [], None
        for k in range(PAIR):
            d2, w2 = d_ref[k], w_ref[i, k]
            moments.append(dot(mono_rows, d2[:, :BLOCK]) + dot(mono_rows, d2[:, BLOCK:]))
            lhs = jnp.concatenate([jnp.where(own_rows[k], a_high, 0.0), jnp.where(own_rows[k], a_low, 0.0)], axis=0)
            lhs = lhs.astype(bf16)
            grads = dot(lhs, w2[:, :BLOCK]) + dot(lhs, w2[:, BLOCK:])
            grads = grads[:8] + grads[8:]
            tint = grads if tint is None else tint + grads
        pieces = [m[:6] for m in moments] + [tint[0:3], tint[4:7], jnp.zeros((6, BLOCK), f32)]
        put_rows(packed.at[i], pl.ds(0, MSG), jnp.concatenate(pieces, axis=0))

    def backward(n, _):
        i = far(n)
        sum_pair(i)
        slope_pair(far(n + 1))
        for d in range(4):
            give(i, d).start()
        return 0

    slope_pair(far(1))
    lax.fori_loop(1, STEPS, backward, 0)
    sum_pair(0)
    for d in range(1, 4):
        give(0, d).start()
    landed[0:MSG, :] = packed[0, mine]

    for d in range(1, 4):
        share(d).wait_recv()
    chosen = [all_picks[d, k * STEPS : (k + 1) * STEPS, :] for k in range(PAIR) for d in range(4)]
    tall = jnp.concatenate(chosen * TRIPLE + [jnp.zeros((256 - TRIPLE * 4 * SLOTS, 128), f32)], axis=0)
    put = jnp.transpose(tall)[:OWNED, : TRIPLE * 4 * SLOTS].astype(bf16)

    def take_give(n, _):
        for d in range(4):
            give(n, d).wait_recv()
        return 0

    lax.fori_loop(1, STEPS, take_give, 0)
    for d in range(1, 4):
        give(0, d).wait_recv()
    for r in range(0, 9, 2):
        both = []
        for q in range(r, min(r + 2, 9)):
            at = (q, 6 + q) if q < 6 else (6 + q, 9 + q)
            both.append(jnp.concatenate([landed[pl.ds(at[k], 4 * STEPS, stride=MSG), :] for k in range(PAIR)], axis=0))
        found = dot(put, stack3(jnp.concatenate(both, axis=1)))
        for q in range(len(both)):
            sums[(r + q) * OWNED : (r + q + 1) * OWNED, :] = found[:, q * 128 : (q + 1) * 128]

    swap = exchange(sums, got_core, attr_sems, 2, (tile, core))
    swap.start()
    out_ref[mine] = sums[...]
    for d in range(1, 4):
        share(d).wait_send()
        give(0, d).wait_send()

    def sent_give(n, _):
        for d in range(4):
            give(n, d).wait_send()
        return 0

    lax.fori_loop(1, STEPS, sent_give, 0)
    each(lambda i: ask(i).wait_send())
    each(lambda i: back(i, 0).wait_send())
    each(lambda i: back(i, 1).wait_send())
    swap.wait()
    out_ref[1 - mine] = got_core[...]


def fused(geometry, view_angles, sh_coeffs, visible, order, cot, counts):
    bands = sh_coeffs.shape[0] // 3
    sems = pltpu.SemaphoreType.DMA
    vmem = pl.BlockSpec(memory_space=pltpu.VMEM)
    ins = (geometry, view_angles, sh_coeffs, visible, order, cot, counts)
    colours = 3 * OWNED
    shapes = (cot.shape, (bands, OWNED, BLOCK), (11, OWNED, BLOCK), (2, 9 * OWNED, 128))
    return pl.pallas_call(
        functools.partial(fused_kernel, bands),
        name="splat",
        out_shape=tuple(jax.ShapeDtypeStruct(o, jnp.float32) for o in shapes),
        in_specs=[pl.BlockSpec(memory_space=pltpu.HBM)] * len(ins),
        out_specs=tuple(vmem for _ in shapes),
        scratch_shapes=[pltpu.VMEM(x.shape, x.dtype) for x in ins[:-1]] + [
            pltpu.SMEM(counts.shape, counts.dtype),
            floats(BLOCK // 128, 8 * OWNED, 128), floats(BLOCK // 128, 8 * OWNED, 128),
            floats(BLOCK // 128, 16 * OWNED, 128), floats(16, OWNED, BLOCK),
            pltpu.VMEM((6, TRIPLE * OWNED, BLOCK), jnp.bfloat16), floats(colours, BLOCK), floats(colours, BLOCK),
            floats(colours, BLOCK), floats(colours, BLOCK), floats(8, 128),
            floats(8 * STEPS, 128), floats(8 * STEPS, 128), floats(2, STEPS * MSG, 128), floats(STEPS, 2, MSG, 128),
            pltpu.VMEM((STEPS, PAIR, PIX, 2 * BLOCK), jnp.bfloat16), floats(STEPS, PAIR, PIX, BLOCK),
            floats(2, 8 * STEPS, 128), floats(2, 8 * STEPS, 128),
            floats(STEPS, 2, MSG, 128), floats(4 * STEPS * MSG, 128), floats(9 * OWNED, 128), floats(9 * OWNED, 128),
            floats(4, SLOTS, 128), pltpu.VMEM((PAIR, PIX, 2 * BLOCK), jnp.bfloat16),
            sems((len(ins),)), sems((2, STEPS)), sems((2, 2, STEPS)), sems((2, 4 * STEPS)), sems((2, 4)), sems((2, 3)),
        ],
        compiler_params=pltpu.CompilerParams(
            collective_id=3, has_side_effects=True, vmem_limit_bytes=40 * 1024 * 1024
        ),
    )(*[pltpu.with_memory_space_constraint(x, pltpu.HBM) for x in ins])


def finish_kernel(bands, sums_ref, terms_ref, basis_ref, pic_ref, geometry_ref, coeffs_ref, picture_ref, both, geo, coe):
    for h in range(BLOCK // 128):
        both[:, h * 128 : (h + 1) * 128] = sums_ref[h]
    final_kernel(OWNED, bands, both, terms_ref, basis_ref, geometry_ref, coeffs_ref, geo, coe)
    picture_ref[...] = pic_ref[...]


def finish(sums, terms, basis, pic):
    bands = basis.shape[0]
    vmem = pl.BlockSpec(memory_space=pltpu.VMEM)
    shapes = ((6, OWNED * BLOCK), (3 * bands, OWNED * BLOCK), pic.shape)
    return pl.pallas_call(
        functools.partial(finish_kernel, bands),
        name="finish",
        out_shape=tuple(jax.ShapeDtypeStruct(o, jnp.float32) for o in shapes),
        in_specs=[vmem] * 4,
        out_specs=(vmem,) * 3,
        scratch_shapes=[
            floats(9 * OWNED, BLOCK),
            floats(BLOCK // 128, 8 * OWNED, 128),
            floats(BLOCK // 128, 16 * OWNED, 128),
        ],
        compiler_params=pltpu.CompilerParams(vmem_limit_bytes=12 * 1024 * 1024),
    )(sums, terms, basis, pic)


def local_fused(geometry, sh_coeffs, view_angles, visible, counts, order, image_cot):
    cot = jnp.swapaxes(image_cot, 0, 1)
    pic, basis, terms, sums = fused(geometry, view_angles, sh_coeffs, visible, order, cot, counts)
    grad_geometry, grad_sh, picture = finish(sums, terms, basis, pic)
    return (jnp.swapaxes(picture, 0, 1), grad_geometry, grad_sh)


def local(geometry, sh_coeffs, view_angles, visible, counts, order, image_cot):
    owners = lax.axis_size("tile")
    tiles, vis = visible.shape
    owned = geometry.shape[1] // BLOCK
    fits = (owners, vis, tiles, owned, lax.axis_size("attr")) == (8, 16, 2, 32, 4)
    run = local_fused if fits else local_general
    return run(geometry, sh_coeffs, view_angles, visible, counts, order, image_cot)


def solution(mesh):
    in_specs = (
        P(None, "tile"),
        P("attr", "tile"),
        P(None, "tile"),
        P(("tile", "attr"), None),
        P(("tile", "attr")),
        P(("tile", "attr"), None),
        P(("tile", "attr"), None, None),
    )
    out_specs = (P(("tile", "attr"), None, None), P(None, "tile"), P("attr", "tile"))
    return jax.shard_map(local, mesh=mesh, in_specs=in_specs, out_specs=out_specs, check_vma=False)
```

```python
import functools
import jax
import jax.numpy as jnp
from jax import lax
from jax.experimental import pallas as pl
from jax.experimental.pallas import tpu as pltpu
from jax.sharding import PartitionSpec as P

BLOCK = 256
SIDE = 16
PIX = SIDE * SIDE
MID = 0.5 * SIDE
LOG2E = 1.4426950408889634
LN2 = 0.6931471805599453


band_zero = 0.28209479177387814
band_one = 0.4886025119029199
band_two = (
    1.0925484305920792,
    -1.0925484305920792,
    0.31539156525252005,
    -1.0925484305920792,
    0.5462742152960396,
)
band_three = (
    -0.5900435899266435,
    2.890611442640554,
    -0.4570457994644658,
    0.3731763325901154,
    -0.4570457994644658,
    1.445305721320277,
    -0.5900435899266435,
)


def sh_basis(view_angles):
    azimuth = view_angles[0]
    elevation = view_angles[1]
    dir_x = jnp.cos(azimuth) * jnp.cos(elevation)
    dir_y = jnp.sin(azimuth) * jnp.cos(elevation)
    dir_z = jnp.sin(elevation)
    sq_x = dir_x * dir_x
    sq_y = dir_y * dir_y
    sq_z = dir_z * dir_z
    basis_rows = [
        band_zero * jnp.ones_like(dir_x),
        -band_one * dir_y,
        band_one * dir_z,
        -band_one * dir_x,
        band_two[0] * dir_x * dir_y,
        band_two[1] * dir_y * dir_z,
        band_two[2] * (2.0 * sq_z - sq_x - sq_y),
        band_two[3] * dir_x * dir_z,
        band_two[4] * (sq_x - sq_y),
        band_three[0] * dir_y * (3.0 * sq_x - sq_y),
        band_three[1] * dir_x * dir_y * dir_z,
        band_three[2] * dir_y * (4.0 * sq_z - sq_x - sq_y),
        band_three[3] * dir_z * (2.0 * sq_z - 3.0 * sq_x - 3.0 * sq_y),
        band_three[4] * dir_x * (4.0 * sq_z - sq_x - sq_y),
        band_three[5] * dir_z * (sq_x - sq_y),
        band_three[6] * dir_x * (sq_x - 3.0 * sq_y),
    ]
    return basis_rows


def split2(x):
    high = x.astype(jnp.bfloat16)
    low = (x - high.astype(jnp.float32)).astype(jnp.bfloat16)
    return jnp.concatenate([high, low], axis=1)


def dot(a, b):
    return jnp.dot(a, b, preferred_element_type=jnp.float32)


def blend_kernel(tiles, seq_ref, counts_ref, held_ref, cot_rows_ref, cot_cols_ref, pic_ref, grad_ref, part_ref, ratio_ref):
    f32, bf16 = jnp.float32, jnp.bfloat16
    row = lax.broadcasted_iota(jnp.int32, (2 * BLOCK, BLOCK), 0)
    row = jnp.where(row >= BLOCK, row - BLOCK, row)
    col = lax.broadcasted_iota(jnp.int32, (2 * BLOCK, BLOCK), 1)
    before = jnp.where(row < col, -1.0, 0.0).astype(bf16)
    upto = jnp.where(row <= col, 1.0, 0.0).astype(bf16)

    def monomials(shape, dim, width):
        pixel = lax.broadcasted_iota(jnp.int32, shape, dim)
        kind = lax.broadcasted_iota(jnp.int32, shape, 1 - dim) & (width - 1)
        x = (pixel & (SIDE - 1)).astype(f32) + (0.5 - MID)
        y = (pixel // SIDE).astype(f32) + (0.5 - MID)
        out = jnp.where(kind == 0, 1.0, 0.0)
        for k, value in ((1, x), (2, y), (3, x * x), (4, x * y), (5, y * y)):
            out = jnp.where(kind == k, value, out)
        return out.astype(bf16)

    mono_cols = monomials((PIX, 48), 0, 16)
    mono_rows = monomials((8, PIX), 1, 8)
    cot_lhs, cot_rows = [], []
    for t in range(tiles):
        g = cot_cols_ref[t]
        high = g.astype(bf16).astype(f32)
        lane = lax.broadcasted_iota(jnp.int32, g.shape, 1)
        cot_lhs.append(jnp.where(lane < 48, high, g - high).astype(bf16))
        g = cot_rows_ref[t]
        high = g.astype(bf16).astype(f32)
        cot_rows.append(jnp.concatenate([high, g - high], axis=0).astype(bf16))

    grad_ref[...] = jnp.zeros_like(grad_ref)
    lives = [counts_ref[t] for t in range(tiles)]
    longest = functools.reduce(jnp.maximum, lives)

    lhs = []
    for t in range(tiles):
        wide = jnp.concatenate([mono_cols.astype(f32), jnp.zeros((PIX, 48), f32)], axis=1)
        lhs.append(jnp.concatenate([wide.astype(bf16), cot_lhs[t]], axis=0))
    head = lax.broadcasted_iota(jnp.int32, (16, BLOCK), 0) == 0

    def forward(j, carry):
        keep_before, sum_before, pictures = carry
        alphas, values, losses, helds, spots = [], [], [], [], []
        for t in range(tiles):
            at = seq_ref[t, j]
            hidden = jnp.where(j < lives[t], 0.0, -16384.0)
            held = held_ref[at]
            parts = split3(jnp.where(head, held + hidden, held))
            rows = jnp.concatenate(parts, axis=0)
            both = dot(lhs[t], jnp.concatenate([rows, rows], axis=0))
            alpha = jnp.exp2(both[:PIX])
            alphas.append(alpha)
            values.append(both[PIX:])
            losses.append(jnp.log(1.0 - alpha) * -LOG2E)
            helds.append(jnp.concatenate(parts[:2], axis=0))
            spots.append(at)
        loss = jnp.concatenate(losses, axis=0)
        keep_in = dot(split2(loss), before) + keep_before
        keep_before = keep_in[:, BLOCK - 1 :] - loss[:, BLOCK - 1 :]
        alpha = jnp.concatenate(alphas, axis=0)
        weight = alpha * jnp.exp2(keep_in)
        value = weight * jnp.concatenate(values, axis=0)
        total = dot(split2(value), upto) + sum_before
        sum_before = total[:, BLOCK - 1 :]
        ratio = alpha * jnp.exp2(loss)
        part_ref[j] = value + ratio * total
        ratio_ref[j] = ratio
        w2 = split2(weight)
        shown = []
        for t in range(tiles):
            w_high, w_low = w2[t * PIX : (t + 1) * PIX, :BLOCK], w2[t * PIX : (t + 1) * PIX, BLOCK:]
            rows = lax.dot_general(helds[t], w_high, (((1,), (1,)), ((), ())), preferred_element_type=f32)
            rows = rows + lax.dot_general(helds[t], w_low, (((1,), (1,)), ((), ())), preferred_element_type=f32)
            shown.append(pictures[t] + rows[:16] + rows[16:])
            colour_grad = dot(cot_rows[t], w_high) + dot(cot_rows[t], w_low)
            grad_ref[spots[t], 0:8, :] += colour_grad[:8] + colour_grad[8:]
        return keep_before, sum_before, tuple(shown)

    zero = jnp.zeros((tiles * PIX, 1), f32)
    start = (zero, zero, tuple(jnp.zeros((16, PIX), f32) for _ in range(tiles)))
    _, ends, pictures = lax.fori_loop(0, longest, forward, start)
    for t in range(tiles):
        pic_ref[t] = pictures[t]

    def backward(j, _):
        for t in range(tiles):
            pixels = slice(t * PIX, (t + 1) * PIX)
            d2 = split2(part_ref[j, pixels] - ratio_ref[j, pixels] * ends[pixels])
            moments = dot(mono_rows, d2[:, :BLOCK]) + dot(mono_rows, d2[:, BLOCK:])
            grad_ref[seq_ref[t, j], 8:16, :] += moments
        return 0

    lax.fori_loop(0, longest, backward, 0)


def blend(seq, counts, held, image_cot):
    tiles = image_cot.shape[0]
    rows = held.shape[0]
    cot_rows = jnp.pad(image_cot, ((0, 0), (0, 5), (0, 0)))
    cot_cols = jnp.pad(jnp.swapaxes(image_cot, 1, 2), ((0, 0), (0, 0), (6, 7)))
    cot_cols = jnp.tile(cot_cols, (1, 1, 6))
    smem = pl.BlockSpec(memory_space=pltpu.SMEM)
    vmem = pl.BlockSpec(memory_space=pltpu.VMEM)
    picture, grads = pl.pallas_call(
        functools.partial(blend_kernel, tiles),
        name="blend",
        out_shape=(
            jax.ShapeDtypeStruct((tiles, 16, PIX), jnp.float32),
            jax.ShapeDtypeStruct((rows, 16, BLOCK), jnp.float32),
        ),
        in_specs=[smem, smem, vmem, vmem, vmem],
        out_specs=(vmem, vmem),
        scratch_shapes=[
            pltpu.VMEM((seq.shape[1], tiles * PIX, BLOCK), jnp.float32),
            pltpu.VMEM((seq.shape[1], tiles * PIX, BLOCK), jnp.float32),
        ],
        compiler_params=pltpu.CompilerParams(vmem_limit_bytes=28 * 1024 * 1024),
    )(seq, counts, held, cot_rows, cot_cols)
    return picture[:, 6:9], grads


def splat_terms(geometry):
    mx, my = geometry[0] - MID, geometry[1] - MID
    c, s = jnp.cos(geometry[4]), jnp.sin(geometry[4])
    e1, e2 = jnp.exp(-2.0 * geometry[2]), jnp.exp(-2.0 * geometry[3])
    cc, ss, cs = c * c, s * s, c * s
    a = cc * e1 + ss * e2
    b = cs * (e1 - e2)
    d = ss * e1 + cc * e2
    return mx, my, e1, e2, cc, ss, cs, a, b, d, geometry[5]


def exponent_rows(terms):
    mx, my, e1, e2, cc, ss, cs, a, b, d, logit = terms
    bx, by = a * mx + b * my, b * mx + d * my
    log_opacity = jnp.minimum(logit, 0.0) - jnp.log1p(jnp.exp(-jnp.abs(logit)))
    one = log_opacity - 0.5 * (mx * bx + my * by)
    return [LOG2E * r for r in (one, bx, by, -0.5 * a, -b, -0.5 * d)]


def geometry_grads(terms, m):
    mx, my, e1, e2, cc, ss, cs, a, b, d, logit = terms
    n0 = m[0]
    nx, ny = m[1] - mx * n0, m[2] - my * n0
    nxx = m[3] - mx * (m[1] + nx)
    nxy = m[4] - mx * m[2] - my * nx
    nyy = m[5] - my * (m[2] + ny)
    return [
        a * nx + b * ny,
        b * nx + d * ny,
        e1 * (cc * nxx + 2.0 * cs * nxy + ss * nyy),
        e2 * (ss * nxx - 2.0 * cs * nxy + cc * nyy),
        (e2 - e1) * (cs * (nyy - nxx) + (cc - ss) * nxy),
        n0 / (1.0 + jnp.exp(logit)),
    ]


MESH = pl.DeviceIdType.MESH


def greet(peers):
    barrier = pltpu.get_barrier_semaphore()
    tile, attr, owners, extra = peers

    def hello(step, _):
        other = (tile + step) % owners
        pl.semaphore_signal(barrier, inc=1, device_id=(other, attr), device_id_type=MESH)
        return 0

    lax.fori_loop(1, owners, hello, 0)
    for other in extra:
        pl.semaphore_signal(barrier, inc=1, device_id=(tile, other), device_id_type=MESH)
    return barrier, owners - 1 + len(extra)


def split3(x):
    high = x.astype(jnp.bfloat16)
    rest = x - high.astype(jnp.float32)
    mid = rest.astype(jnp.bfloat16)
    return high, mid, (rest - mid.astype(jnp.float32)).astype(jnp.bfloat16)


def exchange(src, dst, sems, k, device):
    return pltpu.make_async_remote_copy(
        src_ref=src, dst_ref=dst, send_sem=sems.at[0, k], recv_sem=sems.at[1, k],
        device_id=device, device_id_type=MESH,
    )


def fetch_kernel(dims, want_ref, coef_ref, part_ref, held_ref, asked_ref,
                 asks, answer, landed, first, summed, second, tile_sems, back_sems, attr_sems):
    owners, owned, cap, message, stride = dims
    f32 = jnp.float32
    tile, attr = lax.axis_index("tile"), lax.axis_index("attr")
    core = attr + 1 - 2 * (attr % 2)
    across = (attr + 2) % 4
    pl.semaphore_wait(*greet((tile, attr, owners, (core, across))))

    colour_one = exchange(part_ref, first, attr_sems, 0, (tile, core))
    colour_one.start()

    def ask(other, sender):
        return pltpu.make_async_remote_copy(
            src_ref=want_ref.at[other], dst_ref=asks.at[sender],
            send_sem=tile_sems.at[0, other], recv_sem=tile_sems.at[1, sender],
            device_id=(other, attr), device_id_type=MESH,
        )

    def send_ask(step, _):
        ask((tile + step) % owners, tile).start()
        return 0

    lax.fori_loop(1, owners, send_ask, 0)
    asks[tile] = want_ref[tile]

    colour_one.wait()
    summed[...] = part_ref[...] + first[...]
    colour_two = exchange(summed, second, attr_sems, 1, (tile, across))
    colour_two.start()

    def take_ask(step, _):
        other = (tile + step) % owners
        ask(other, other).wait()
        return 0

    lax.fori_loop(1, owners, take_ask, 0)

    per = 128 // stride
    lanes = owners // per
    rows = []
    for tile_at in range(lanes):
        rows.append(functools.reduce(jnp.add, [asks[tile_at * per + k] for k in range(per)]))
    asked = jnp.concatenate(rows, axis=1) - 1.0
    asked_ref[...] = asked
    wide = 9 * owned
    columns = []
    for tile_at in range(lanes):
        square = jnp.concatenate([rows[tile_at] - 1.0] * 16, axis=0)
        columns.append(jnp.transpose(square)[:, 0:1])
    column = jnp.concatenate(columns, axis=0)
    lane = lax.broadcasted_iota(jnp.int32, (owners * stride, wide), 1).astype(f32)
    pick = jnp.where(lane == column, 1.0, 0.0).astype(jnp.bfloat16)

    colour_two.wait()
    colour = summed[...] + second[...] + 0.5
    table = jnp.concatenate([coef_ref[...], colour], axis=0)
    high, mid, low = split3(table)
    answer[...] = (dot(pick, low) + dot(pick, mid)) + dot(pick, high)

    def back(other, sender):
        at = pl.multiple_of(other * stride, 8)
        return pltpu.make_async_remote_copy(
            src_ref=answer.at[pl.ds(at, message)], dst_ref=landed.at[sender],
            send_sem=back_sems.at[0, other], recv_sem=back_sems.at[1, sender],
            device_id=(other, attr), device_id_type=MESH,
        )

    def send_back(step, _):
        back((tile + step) % owners, tile).start()
        return 0

    lax.fori_loop(1, owners, send_back, 0)
    landed[tile] = answer[pl.ds(pl.multiple_of(tile * stride, 8), message), :]
    held_ref[...] = jnp.zeros_like(held_ref)

    def take_back(step, _):
        other = (tile + step) % owners
        back(other, other).wait()
        return 0

    lax.fori_loop(1, owners, take_back, 0)

    def unpack(o, _):
        for k in range(cap):
            held_ref[o * cap + k, 0:9, :] = landed[o, 9 * k : 9 * k + 9, :]
        return 0

    lax.fori_loop(0, owners, unpack, 0)


def give_kernel(dims, grads_ref, asked_ref, out_ref,
                packed, landed, sums, first, half, second, third, tile_sems, attr_sems):
    owners, owned, cap, message, stride = dims
    f32 = jnp.float32
    tile, attr = lax.axis_index("tile"), lax.axis_index("attr")
    core = attr + 1 - 2 * (attr % 2)
    across = (attr + 2) % 4
    mine = attr % 2

    if message < stride:
        landed[...] = jnp.zeros_like(landed)
    greeted = greet((tile, attr, owners, (core, across)))
    packed[...] = jnp.zeros_like(packed)

    def pack(o, _):
        for k in range(cap):
            packed[o, 9 * k : 9 * k + 6, :] = grads_ref[o * cap + k, 8:14, :]
            packed[o, 9 * k + 6 : 9 * k + 9, :] = grads_ref[o * cap + k, 0:3, :]
        return 0

    lax.fori_loop(0, owners, pack, 0)
    pl.semaphore_wait(*greeted)

    def give(other, sender):
        at = pl.multiple_of(sender * stride, 8)
        return pltpu.make_async_remote_copy(
            src_ref=packed.at[other], dst_ref=landed.at[pl.ds(at, message)],
            send_sem=tile_sems.at[0, other], recv_sem=tile_sems.at[1, sender],
            device_id=(other, attr), device_id_type=MESH,
        )

    def send_give(step, _):
        give((tile + step) % owners, tile).start()
        return 0

    lax.fori_loop(1, owners, send_give, 0)
    landed[pl.ds(pl.multiple_of(tile * stride, 8), message), :] = packed[tile]
    wide = 9 * owned
    row = lax.broadcasted_iota(jnp.int32, (wide, owners * stride), 0).astype(f32)
    pick = jnp.where(row == asked_ref[0:1, :], 1.0, 0.0).astype(jnp.bfloat16)

    def take_give(step, _):
        other = (tile + step) % owners
        give(other, other).wait()
        return 0

    lax.fori_loop(1, owners, take_give, 0)
    high, mid, low = split3(landed[...])
    total = (dot(pick, low) + dot(pick, mid)) + dot(pick, high)
    cut = wide // 2
    sums[0] = total[:cut]
    sums[1] = total[cut:]

    one = exchange(sums.at[1 - mine], first, attr_sems, 0, (tile, core))
    one.start()
    one.wait()
    half[...] = sums[mine] + first[...]
    two = exchange(half, second, attr_sems, 1, (tile, across))
    two.start()
    two.wait()
    half_sum = half[...] + second[...]
    first[...] = half_sum
    three = exchange(first, third, attr_sems, 2, (tile, core))
    three.start()
    three.wait()
    at = pl.multiple_of(mine * cut, 8)
    out_ref[pl.ds(at, cut), :] = half_sum
    at = pl.multiple_of((1 - mine) * cut, 8)
    out_ref[pl.ds(at, cut), :] = third[...]


def remote_call(kernel, dims, outs, ins, scratch, number, name):
    vmem = pl.BlockSpec(memory_space=pltpu.VMEM)
    return pl.pallas_call(
        functools.partial(kernel, dims),
        name=name,
        out_shape=tuple(jax.ShapeDtypeStruct(o, jnp.float32) for o in outs),
        in_specs=[vmem] * len(ins),
        out_specs=tuple(vmem for _ in outs),
        scratch_shapes=scratch,
        compiler_params=pltpu.CompilerParams(
            collective_id=number, has_side_effects=True, vmem_limit_bytes=20 * 1024 * 1024
        ),
    )(*ins)


def floats(*shape):
    return pltpu.VMEM(shape, jnp.float32)


def fetch(dims, want, coef, part):
    owners, owned, cap, message, stride = dims
    sems = pltpu.SemaphoreType.DMA
    return remote_call(
        fetch_kernel, dims,
        ((owners * cap, 16, BLOCK), (8, owners * stride)),
        (want, coef, part),
        [floats(owners, 8, 128), floats(owners * stride, BLOCK), floats(owners, message, BLOCK),
         floats(3 * owned, BLOCK), floats(3 * owned, BLOCK), floats(3 * owned, BLOCK),
         sems((2, owners)), sems((2, owners)), sems((2, 2))],
        1, "fetch",
    )


def give_back(dims, grads, asked):
    owners, owned, cap, message, stride = dims
    sems = pltpu.SemaphoreType.DMA
    cut = 9 * owned // 2
    return remote_call(
        give_kernel, dims, ((9 * owned, BLOCK),), (grads, asked),
        [floats(owners, message, BLOCK), floats(owners * stride, BLOCK), floats(2, cut, BLOCK),
         floats(cut, BLOCK), floats(cut, BLOCK), floats(cut, BLOCK), floats(cut, BLOCK),
         sems((2, owners)), sems((2, 3))],
        2, "give",
    )[0]


def prep_kernel(owned, bands, geometry_ref, angles_ref, coeffs_ref, coef_ref, part_ref, basis_ref, terms_ref,
                geo, ang, coe, rows):
    def relay(b, _):
        for h in range(BLOCK // 128):
            at = pl.ds(pl.multiple_of(b * BLOCK + h * 128, 128), 128)
            geo[h, pl.ds(pl.multiple_of(b * 8, 8), 6), :] = geometry_ref[:, at]
            ang[h, pl.ds(pl.multiple_of(b * 8, 8), 2), :] = angles_ref[:, at]
            coe[h, pl.ds(pl.multiple_of(b * 16, 8), 3 * bands), :] = coeffs_ref[:, at]
        return 0

    lax.fori_loop(0, owned, relay, 0, unroll=4)

    def plane(ref, k, pitch):
        halves = [ref[h, pl.ds(k, owned, stride=pitch), :] for h in range(BLOCK // 128)]
        return jnp.concatenate(halves, axis=1)

    terms = splat_terms([plane(geo, k, 8) for k in range(6)])
    for k, value in enumerate(terms):
        terms_ref[k] = value
    for k, value in enumerate(exponent_rows(terms)):
        coef_ref[k * owned : (k + 1) * owned, :] = value
    for k, value in enumerate(sh_basis([plane(ang, k, 8) for k in range(2)])):
        rows[k] = value
    first = lax.axis_index("attr") * bands
    total = [jnp.zeros((owned, BLOCK), jnp.float32) for _ in range(3)]
    for k in range(bands):
        value = rows[first + k]
        basis_ref[k] = value
        for c in range(3):
            total[c] = total[c] + value * plane(coe, 3 * k + c, 16)
    for c in range(3):
        part_ref[c * owned : (c + 1) * owned, :] = total[c]


def prep(geometry, view_angles, sh_coeffs, owned):
    bands = sh_coeffs.shape[0] // 3
    vmem = pl.BlockSpec(memory_space=pltpu.VMEM)
    shapes = ((6 * owned, BLOCK), (3 * owned, BLOCK), (bands, owned, BLOCK), (11, owned, BLOCK))
    return pl.pallas_call(
        functools.partial(prep_kernel, owned, bands),
        name="prep",
        out_shape=tuple(jax.ShapeDtypeStruct(o, jnp.float32) for o in shapes),
        in_specs=[vmem] * 3,
        out_specs=(vmem,) * 4,
        scratch_shapes=[
            floats(BLOCK // 128, 8 * owned, 128),
            floats(BLOCK // 128, 8 * owned, 128),
            floats(BLOCK // 128, 16 * owned, 128),
            floats(16, owned, BLOCK),
        ],
        compiler_params=pltpu.CompilerParams(vmem_limit_bytes=12 * 1024 * 1024),
    )(geometry, view_angles, sh_coeffs)


def final_kernel(owned, bands, sums_ref, terms_ref, basis_ref, geometry_ref, coeffs_ref, geo, coe):
    summed = [sums_ref[k * owned : (k + 1) * owned, :] for k in range(9)]

    def put(ref, k, pitch, value):
        for h in range(BLOCK // 128):
            ref[h, pl.ds(k, owned, stride=pitch), :] = value[:, h * 128 : (h + 1) * 128]

    for k, value in enumerate(geometry_grads([terms_ref[k] for k in range(11)], summed[:6])):
        put(geo, k, 8, value)
    for k in range(bands):
        for c in range(3):
            put(coe, 3 * k + c, 16, basis_ref[k] * summed[6 + c])

    def relay(b, _):
        for h in range(BLOCK // 128):
            at = pl.ds(pl.multiple_of(b * BLOCK + h * 128, 128), 128)
            geometry_ref[:, at] = geo[h, pl.ds(pl.multiple_of(b * 8, 8), 6), :]
            coeffs_ref[:, at] = coe[h, pl.ds(pl.multiple_of(b * 16, 8), 3 * bands), :]
        return 0

    lax.fori_loop(0, owned, relay, 0, unroll=4)


def final(sums, terms, basis, owned):
    bands = basis.shape[0]
    vmem = pl.BlockSpec(memory_space=pltpu.VMEM)
    shapes = ((6, owned * BLOCK), (3 * bands, owned * BLOCK))
    return pl.pallas_call(
        functools.partial(final_kernel, owned, bands),
        name="final",
        out_shape=tuple(jax.ShapeDtypeStruct(o, jnp.float32) for o in shapes),
        in_specs=[vmem] * 3,
        out_specs=(vmem,) * 2,
        scratch_shapes=[
            floats(BLOCK // 128, 8 * owned, 128),
            floats(BLOCK // 128, 16 * owned, 128),
        ],
        compiler_params=pltpu.CompilerParams(vmem_limit_bytes=12 * 1024 * 1024),
    )(sums, terms, basis)


def local_general(geometry, sh_coeffs, view_angles, visible, counts, order, image_cot):
    owners = lax.axis_size("tile")
    owned = geometry.shape[1] // BLOCK
    vis = visible.shape[1]
    cap = (vis + owners - 1) // owners
    coef, partial_colour, my_basis, terms = prep(geometry, view_angles, sh_coeffs, owned)

    ids = visible[0]
    owner_of, local_of = ids // owned, ids % owned
    position = jnp.arange(vis)
    rank = jnp.sum(((owner_of[None, :] == owner_of[:, None]) & (position[None, :] < position[:, None])).astype(jnp.int32), 1)
    slot = owner_of * cap + rank
    message = -(-9 * cap // 8) * 8
    stride = 16 if message <= 16 else 32
    dims = (owners, owned, cap, message, stride)
    lane = jnp.arange(128) - (lax.axis_index("tile") % (128 // stride)) * stride
    in_slot = lane[None, :, None] // 9 + jnp.arange(owners)[:, None, None] * cap
    hit = (slot[None, None, :] == in_slot) & (lane >= 0)[None, :, None] & (lane < 9 * cap)[None, :, None]
    want = jnp.sum(jnp.where(hit, 1 + local_of[None, None, :] + owned * (lane % 9)[None, :, None], 0), 2)
    want = jnp.broadcast_to(want.astype(jnp.float32)[:, None, :], (owners, 8, 128))
    slot_of = jnp.sum(jnp.where(visible[:, :, None] == ids[None, None, :], slot[None, None, :], 0), 2)
    seq = jnp.sum(jnp.where(order[:, :, None] == position[None, None, :], slot_of[:, None, :], 0), 2)

    held, asked = fetch(dims, want, coef, partial_colour)
    picture, grads = blend(seq, counts, held, image_cot)
    sums = give_back(dims, grads, asked)
    grad_geometry, grad_sh = final(sums, terms, my_basis, owned)
    return (picture, grad_geometry, grad_sh)


STEPS = 8
PAIR = 2
SLOTS = STEPS * PAIR
OWNED = 32
MSG = 24
TRIPLE = 3
LAG = 3
GIVEN = 9 * PAIR


def stack3(x):
    high, mid, low = split3(x)
    return jnp.concatenate([high, mid, low], axis=0)


def lane_halves(x):
    return [x[:, h * 128 : (h + 1) * 128] for h in range(BLOCK // 128)]


def put_rows(ref, rows, value):
    for h, part in enumerate(lane_halves(value)):
        ref[h, rows, :] = part


def get_rows(ref, rows):
    return jnp.concatenate([ref[h, rows, :] for h in range(BLOCK // 128)], axis=1)


def scatter(ref, at, pitch, value):
    put_rows(ref, pl.ds(at, STEPS, stride=pitch), value)


def gather(ref, at, pitch):
    return get_rows(ref, pl.ds(at, STEPS, stride=pitch))


def tile_of(ref, i, at):
    return jnp.concatenate([ref[i, h, at : at + 8, :] for h in range(BLOCK // 128)], axis=1)


def pixel_monomials(shape, dim):
    pixel = lax.broadcasted_iota(jnp.int32, shape, dim)
    kind = lax.broadcasted_iota(jnp.int32, shape, 1 - dim) & 7
    x = (pixel & (SIDE - 1)).astype(jnp.float32) + (0.5 - MID)
    y = (pixel // SIDE).astype(jnp.float32) + (0.5 - MID)
    out = jnp.where(kind == 0, 1.0, 0.0)
    for k, value in ((1, x), (2, y), (3, x * x), (4, x * y), (5, y * y)):
        out = jnp.where(kind == k, value, out)
    return out.astype(jnp.bfloat16)


def slot_tables(tile, visible, order, counts_ref):
    f32 = jnp.float32
    sub = lax.broadcasted_iota(jnp.int32, (SLOTS, SLOTS), 0)
    lane = lax.broadcasted_iota(jnp.int32, (SLOTS, SLOTS), 1)
    diagonal = sub == lane
    lane_f, sub_f = lane.astype(f32), sub.astype(f32)

    def to_column(row):
        return jnp.sum(jnp.where(diagonal, row, 0.0), axis=1, keepdims=True)

    def to_row(column):
        return jnp.sum(jnp.where(diagonal, column, 0.0), axis=0, keepdims=True)

    ids = visible[0:1]
    owner = ids // OWNED
    near = owner - tile
    near = jnp.where(near < 0, near + STEPS, near).astype(f32)
    ids_f = ids.astype(f32)
    inside = (ids - owner * OWNED).astype(f32)
    near_column = to_column(near)
    second = jnp.sum(jnp.where((near_column == near) & (sub < lane), 1.0, 0.0), axis=0, keepdims=True)
    slot = second * STEPS + near
    match = sub_f == slot
    local_id = jnp.sum(jnp.where(match, inside, 0.0), axis=1, keepdims=True)
    slot_id = jnp.sum(jnp.where(match, ids_f, 0.0), axis=1, keepdims=True)
    ahead, live = [], []
    for t in range(2):
        listed = to_column(visible[t : t + 1].astype(f32))
        here = sub == order[t : t + 1]
        sequence = jnp.sum(jnp.where(here, listed, 0.0), axis=0, keepdims=True)
        rank = jnp.sum(jnp.where(sequence == slot_id, lane_f, 0.0), axis=1, keepdims=True)
        ahead.append(jnp.where(to_row(rank) < rank, 1.0, 0.0))
        live.append(jnp.where(rank < counts_ref[t].astype(f32), 1.0, 0.0))
    return local_id, ahead, live


def fused_kernel(bands, geometry_hbm, angles_hbm, coeffs_hbm, visible_hbm, order_hbm, cot_hbm, counts_hbm,
                 pic_ref, basis_ref, terms_ref, out_ref,
                 geometry, angles, coeffs, visible, order, cot, counts_ref, geo, ang, coe, rows,
                 coef, part, first, summed, second, colour,
                 asks_out, asks, answer, held, w_ref, ratio_ref, c_ref, a_ref,
                 packed, landed, sums, got_core, all_picks, d_ref, columns_ref,
                 local_sems, ask_sems, back_sems, give_sems, share_sems, attr_sems):
    f32, bf16 = jnp.float32, jnp.bfloat16
    tile, attr = lax.axis_index("tile"), lax.axis_index("attr")
    core = attr + 1 - 2 * (attr % 2)
    across = (attr + 2) % 4
    mine = attr % 2
    greeted = greet((tile, attr, STEPS, (core, across, (core + 2) % 4)))

    pairs = ((visible_hbm, visible), (order_hbm, order), (counts_hbm, counts_ref), (angles_hbm, angles),
             (coeffs_hbm, coeffs), (geometry_hbm, geometry), (cot_hbm, cot))
    loads = [pltpu.make_async_copy(a, b, local_sems.at[n]) for n, (a, b) in enumerate(pairs)]
    for load in loads:
        load.start()

    asks_out[...] = jnp.zeros_like(asks_out)
    answer[...] = jnp.zeros_like(answer)
    for load in loads[:3]:
        load.wait()
    local_id, ahead, live = slot_tables(tile, visible[...], order[...], counts_ref)
    lane = lax.broadcasted_iota(jnp.int32, (SLOTS, 128), 1)
    block = (lane & (OWNED - 1)).astype(f32)
    wanted = jnp.where((block == local_id) & (lane < TRIPLE * OWNED), 1.0, 0.0)
    for k in range(PAIR):
        asks_out[pl.ds(k, STEPS, stride=8), :] = wanted[k * STEPS : (k + 1) * STEPS]
    for load in loads[3:]:
        load.wait()

    def relay(b, _):
        for h in range(BLOCK // 128):
            at = pl.ds(pl.multiple_of(b * BLOCK + h * 128, 128), 128)
            geo[h, pl.ds(pl.multiple_of(b * 8, 8), 6), :] = geometry[:, at]
            ang[h, pl.ds(pl.multiple_of(b * 8, 8), 2), :] = angles[:, at]
            coe[h, pl.ds(pl.multiple_of(b * 16, 8), 3 * bands), :] = coeffs[:, at]
        return 0

    lax.fori_loop(0, OWNED, relay, 0, unroll=4)

    def plane(ref, k, pitch):
        halves = [ref[h, pl.ds(k, OWNED, stride=pitch), :] for h in range(BLOCK // 128)]
        return jnp.concatenate(halves, axis=1)

    for k, value in enumerate(sh_basis([plane(ang, k, 8) for k in range(2)])):
        rows[k] = value
    first_band = attr * bands
    total = [jnp.zeros((OWNED, BLOCK), f32) for _ in range(3)]
    for k in range(bands):
        value = rows[first_band + k]
        basis_ref[k] = value
        for c in range(3):
            total[c] = total[c] + value * plane(coe, 3 * k + c, 16)
    for c in range(3):
        part[c * OWNED : (c + 1) * OWNED, :] = total[c]
    pl.semaphore_wait(*greeted)

    def ask(i):
        return pltpu.make_async_remote_copy(
            src_ref=asks_out.at[pl.ds(pl.multiple_of(i * 8, 8), 8)], dst_ref=asks.at[pl.ds(pl.multiple_of(i * 8, 8), 8)],
            send_sem=ask_sems.at[0, i], recv_sem=ask_sems.at[1, i],
            device_id=((tile + i) % STEPS, attr), device_id_type=MESH,
        )

    def back(i, part):
        at, size = ((0, 16), (16, 8))[part]
        return pltpu.make_async_remote_copy(
            src_ref=answer.at[:, pl.ds(pl.multiple_of(i * MSG + at, 8), size)], dst_ref=held.at[i, :, pl.ds(at, size)],
            send_sem=back_sems.at[0, part, i], recv_sem=back_sems.at[1, part, i],
            device_id=((tile + STEPS - i) % STEPS, attr), device_id_type=MESH,
        )

    def give(i, d):
        slot = d * STEPS + i
        return pltpu.make_async_remote_copy(
            src_ref=packed.at[i, (attr + d) % 2, pl.ds(0, GIVEN)],
            dst_ref=landed.at[pl.ds(pl.multiple_of(slot * MSG, 8), GIVEN)],
            send_sem=give_sems.at[0, slot], recv_sem=give_sems.at[1, slot],
            device_id=((tile + i) % STEPS, (attr + d) % 4), device_id_type=MESH,
        )

    def share(d):
        return exchange(all_picks.at[0], all_picks.at[d], share_sems, d, (tile, (attr + d) % 4))

    upper = tile // (STEPS // 2)

    def near(n):
        return (n + upper * (STEPS - 2 * n)) % STEPS

    def far(n):
        return (2 * STEPS - n + upper * (2 * n - STEPS)) % STEPS

    def each(act):
        def step(n, _):
            act(far(n))
            return 0

        lax.fori_loop(1, STEPS, step, 0)

    colour_one = exchange(part, first, attr_sems, 0, (tile, core))
    colour_one.start()
    each(lambda i: ask(i).start())
    asks[0:8, :] = asks_out[0:8, :]

    terms = splat_terms([plane(geo, k, 8) for k in range(6)])
    for k, value in enumerate(terms):
        terms_ref[k] = value
    for k, value in enumerate(exponent_rows(terms)):
        coef[k] = stack3(value)

    colour_one.wait()
    summed[...] = part[...] + first[...]
    colour_two = exchange(summed, second, attr_sems, 1, (tile, across))
    colour_two.start()

    each(lambda i: ask(i).wait_recv())
    picks = jnp.concatenate([asks[pl.ds(k, STEPS, stride=8), :] for k in range(PAIR)], axis=0)
    pick = picks.astype(bf16)[:, : TRIPLE * OWNED]
    all_picks[0] = picks
    for d in range(1, 4):
        share(d).start()

    def pick_row(values, at):
        found = dot(pick, values)
        for k in range(PAIR):
            scatter(answer, at[k], MSG, found[k * STEPS : (k + 1) * STEPS])

    for r in range(6):
        pick_row(coef[r], (r, 8 + r))
    each(lambda i: back(i, 0).start())
    held[0, :, 0:16] = answer[:, 0:16, :]

    row = lax.broadcasted_iota(jnp.int32, (2 * BLOCK, BLOCK), 0) & (BLOCK - 1)
    col = lax.broadcasted_iota(jnp.int32, (2 * BLOCK, BLOCK), 1)
    before = jnp.where(row < col, -1.0, 0.0).astype(bf16)
    upto = jnp.where(row <= col, 1.0, 0.0).astype(bf16)
    mono_cols = pixel_monomials((PIX, 32), 0)
    mono_rows = pixel_monomials((8, PIX), 1)
    eight = lax.broadcasted_iota(jnp.int32, (8, BLOCK), 0)
    own_rows = [(eight >= 4 * k) & (eight < 4 * k + 3) for k in range(PAIR)]

    def halves(x):
        high = x.astype(bf16).astype(f32)
        return high, x - high

    def powers_of(i):
        powers = []
        for k in range(PAIR):
            high, mid, low = [p.astype(f32) for p in split3(tile_of(held, i, 8 * k))]
            coefs = jnp.concatenate([high, mid, low, jnp.zeros_like(low)], axis=0).astype(bf16)
            powers.append(dot(mono_cols, coefs))
        return powers

    def shape_pair(i, powers):
        alphas, losses = [], []
        for k in range(PAIR):
            alpha = jnp.exp2(powers[k])
            loss = jnp.log(1.0 - alpha) * -LOG2E
            alphas.append(alpha)
            losses.append(split2(loss))
            ratio_ref[i, k] = alpha * jnp.exp2(loss)
        keep = dot(jnp.concatenate(losses, axis=0), before)
        for k in range(PAIR):
            w_ref[i, k] = split2(alphas[k] * jnp.exp2(keep[k * PIX : (k + 1) * PIX]))

    def show_pair(i):
        c_high, c_low = halves(tile_of(held, i, 16))
        seen = None
        for k in range(PAIR):
            w2 = w_ref[i, k]
            one = jnp.where(eight == 4 * k + 3, 1.0, 0.0)
            lhs = jnp.concatenate([jnp.where(own_rows[k], c_high, one), jnp.where(own_rows[k], c_low, 0.0)], axis=0)
            lhs = lhs.astype(bf16)
            contract = (((1,), (1,)), ((), ()))
            shown = lax.dot_general(lhs, w2[:, :BLOCK], contract, preferred_element_type=f32)
            shown = shown + lax.dot_general(lhs, w2[:, BLOCK:], contract, preferred_element_type=f32)
            shown = shown[:8] + shown[8:]
            seen = shown if seen is None else seen + shown
        put_rows(c_ref, pl.ds(pl.multiple_of(i * 8, 8), 8), seen)

    def forward_early(n, _):
        i = near(n)
        back(i, 0).wait_recv()
        shape_pair(i, powers_of(i))
        return 0

    def forward(n, _):
        i, shown = near(n), near(n - LAG)
        back(i, 0).wait_recv()

        @pl.when(n > LAG)
        def _():
            back(shown, 1).wait_recv()

        powers = powers_of(i)
        show_pair(shown)
        shape_pair(i, powers)
        return 0

    shape_pair(0, powers_of(0))
    colour_two.wait()
    for c in range(3):
        piece = slice(c * OWNED, (c + 1) * OWNED)
        pick_row(stack3(summed[piece] + second[piece] + 0.5), (16 + c, 20 + c))
    each(lambda i: back(i, 1).start())
    held[0, :, 16:24] = answer[:, 16:24, :]
    lax.fori_loop(1, LAG, forward_early, 0)
    lax.fori_loop(LAG, STEPS, forward, 0)
    for n in range(STEPS - LAG, STEPS):
        back(near(n), 1).wait_recv()
    for n in range(STEPS - LAG, STEPS):
        show_pair(near(n))

    def by_slot(ref, c):
        return jnp.concatenate([gather(ref, c + 4 * k, 8) for k in range(PAIR)], axis=0)

    local = [by_slot(c_ref, c) for c in range(4)]
    spread = [jnp.zeros((SLOTS, PIX), f32) for _ in range(4)]
    for t in range(2):
        def earlier(values):
            out = jnp.zeros((SLOTS, PIX), f32)
            for s in range(SLOTS):
                out = out + ahead[t][:, s : s + 1] * values[s : s + 1, :]
            return out

        through = jnp.broadcast_to(live[t], (SLOTS, PIX))
        for s in range(SLOTS):
            through = through * (1.0 - ahead[t][:, s : s + 1] * local[3][s : s + 1, :])
        shade = jnp.zeros((SLOTS, PIX), f32)
        for c in range(3):
            g = cot[c, t : t + 1, :]
            lit = through * local[c]
            pic_ref[c, t : t + 1, :] = jnp.sum(lit, axis=0, keepdims=True)
            shade = shade + lit * g
            spread[c] = spread[c] + through * g
        behind = earlier(shade) - jnp.sum(shade, axis=0, keepdims=True)
        spread[3] = spread[3] + live[t] * behind
    for c in range(4):
        for k in range(PAIR):
            scatter(a_ref, c + 4 * k, 8, spread[c][k * STEPS : (k + 1) * STEPS])

    def turn(i):
        a = get_rows(a_ref, pl.ds(pl.multiple_of(i * 8, 8), 8))
        a_high, a_low = halves(a)
        columns_ref[...] = jnp.transpose(jnp.concatenate([a_high, a_low, a_high, a], axis=0))

    def tints_of(i, columns):
        c_high, c_low = halves(tile_of(held, i, 16))
        tints = []
        for k in range(PAIR):
            ch, cl = jnp.where(own_rows[k], c_high, 0.0), jnp.where(own_rows[k], c_low, 0.0)
            tints.append(dot(columns.astype(bf16), jnp.concatenate([ch, ch, cl, jnp.zeros_like(cl)], axis=0).astype(bf16)))
        return tints

    def slope_pair(i, columns, tints):
        values = []
        for k in range(PAIR):
            w2 = w_ref[i, k]
            values.append((w2[:, :BLOCK].astype(f32) + w2[:, BLOCK:].astype(f32)) * tints[k])
        total = dot(jnp.concatenate([split2(value) for value in values], axis=0), upto)
        for k in range(PAIR):
            beyond = total[k * PIX : (k + 1) * PIX] + columns[:, 27 + 4 * k : 28 + 4 * k]
            d_ref[k] = split2(values[k] + ratio_ref[i, k] * beyond)

    def sum_pair(i):
        a_high, a_low = halves(get_rows(a_ref, pl.ds(pl.multiple_of(i * 8, 8), 8)))
        moments, tint = [], None
        for k in range(PAIR):
            d2, w2 = d_ref[k], w_ref[i, k]
            moments.append(dot(mono_rows, d2[:, :BLOCK]) + dot(mono_rows, d2[:, BLOCK:]))
            lhs = jnp.concatenate([jnp.where(own_rows[k], a_high, 0.0), jnp.where(own_rows[k], a_low, 0.0)], axis=0)
            lhs = lhs.astype(bf16)
            grads = dot(lhs, w2[:, :BLOCK]) + dot(lhs, w2[:, BLOCK:])
            grads = grads[:8] + grads[8:]
            tint = grads if tint is None else tint + grads
        pieces = [m[:6] for m in moments] + [tint[0:3], tint[4:7], jnp.zeros((6, BLOCK), f32)]
        put_rows(packed.at[i], pl.ds(0, MSG), jnp.concatenate(pieces, axis=0))

    def backward(n, _):
        i, after = far(n), far(n + 1)
        columns = columns_ref[...]
        tints = tints_of(after, columns)
        sum_pair(i)
        slope_pair(after, columns, tints)
        turn(far(n + 2))
        for d in range(4):
            give(i, d).start()
        return 0

    turn(far(1))
    columns = columns_ref[...]
    slope_pair(far(1), columns, tints_of(far(1), columns))
    turn(far(2))
    lax.fori_loop(1, STEPS, backward, 0)
    sum_pair(0)
    for d in range(1, 4):
        give(0, d).start()
    landed[0:MSG, :] = packed[0, mine]

    for d in range(1, 4):
        share(d).wait_recv()
    chosen = [all_picks[d, k * STEPS : (k + 1) * STEPS, :] for k in range(PAIR) for d in range(4)]
    tall = jnp.concatenate(chosen * TRIPLE + [jnp.zeros((256 - TRIPLE * 4 * SLOTS, 128), f32)], axis=0)
    put = jnp.transpose(tall)[:OWNED, : TRIPLE * 4 * SLOTS].astype(bf16)

    def take_give(n, _):
        for d in range(4):
            give(n, d).wait_recv()
        return 0

    lax.fori_loop(1, STEPS, take_give, 0)
    for d in range(1, 4):
        give(0, d).wait_recv()
    for r in range(0, 9, 2):
        both = []
        for q in range(r, min(r + 2, 9)):
            at = (q, 6 + q) if q < 6 else (6 + q, 9 + q)
            both.append(jnp.concatenate([landed[pl.ds(at[k], 4 * STEPS, stride=MSG), :] for k in range(PAIR)], axis=0))
        found = dot(put, stack3(jnp.concatenate(both, axis=1)))
        for q in range(len(both)):
            sums[(r + q) * OWNED : (r + q + 1) * OWNED, :] = found[:, q * 128 : (q + 1) * 128]

    swap = exchange(sums, got_core, attr_sems, 2, (tile, core))
    swap.start()
    out_ref[mine] = sums[...]
    for d in range(1, 4):
        share(d).wait_send()
        give(0, d).wait_send()

    def sent_give(n, _):
        for d in range(4):
            give(n, d).wait_send()
        return 0

    lax.fori_loop(1, STEPS, sent_give, 0)
    each(lambda i: ask(i).wait_send())
    each(lambda i: back(i, 0).wait_send())
    each(lambda i: back(i, 1).wait_send())
    swap.wait()
    out_ref[1 - mine] = got_core[...]


def fused(geometry, view_angles, sh_coeffs, visible, order, cot, counts):
    bands = sh_coeffs.shape[0] // 3
    sems = pltpu.SemaphoreType.DMA
    vmem = pl.BlockSpec(memory_space=pltpu.VMEM)
    ins = (geometry, view_angles, sh_coeffs, visible, order, cot, counts)
    colours = 3 * OWNED
    shapes = (cot.shape, (bands, OWNED, BLOCK), (11, OWNED, BLOCK), (2, 9 * OWNED, 128))
    return pl.pallas_call(
        functools.partial(fused_kernel, bands),
        name="splat",
        out_shape=tuple(jax.ShapeDtypeStruct(o, jnp.float32) for o in shapes),
        in_specs=[pl.BlockSpec(memory_space=pltpu.HBM)] * len(ins),
        out_specs=tuple(vmem for _ in shapes),
        scratch_shapes=[pltpu.VMEM(x.shape, x.dtype) for x in ins[:-1]] + [
            pltpu.SMEM(counts.shape, counts.dtype),
            floats(BLOCK // 128, 8 * OWNED, 128), floats(BLOCK // 128, 8 * OWNED, 128),
            floats(BLOCK // 128, 16 * OWNED, 128), floats(16, OWNED, BLOCK),
            pltpu.VMEM((6, TRIPLE * OWNED, BLOCK), jnp.bfloat16), floats(colours, BLOCK), floats(colours, BLOCK),
            floats(colours, BLOCK), floats(colours, BLOCK), floats(8, 128),
            floats(8 * STEPS, 128), floats(8 * STEPS, 128), floats(2, STEPS * MSG, 128), floats(STEPS, 2, MSG, 128),
            pltpu.VMEM((STEPS, PAIR, PIX, 2 * BLOCK), jnp.bfloat16), floats(STEPS, PAIR, PIX, BLOCK),
            floats(2, 8 * STEPS, 128), floats(2, 8 * STEPS, 128),
            floats(STEPS, 2, MSG, 128), floats(4 * STEPS * MSG, 128), floats(9 * OWNED, 128), floats(9 * OWNED, 128),
            floats(4, SLOTS, 128), pltpu.VMEM((PAIR, PIX, 2 * BLOCK), jnp.bfloat16), floats(PIX, 32),
            sems((len(ins),)), sems((2, STEPS)), sems((2, 2, STEPS)), sems((2, 4 * STEPS)), sems((2, 4)), sems((2, 3)),
        ],
        compiler_params=pltpu.CompilerParams(
            collective_id=3, has_side_effects=True, vmem_limit_bytes=40 * 1024 * 1024
        ),
    )(*[pltpu.with_memory_space_constraint(x, pltpu.HBM) for x in ins])


def finish_kernel(bands, sums_ref, terms_ref, basis_ref, pic_ref, geometry_hbm, coeffs_hbm, picture_hbm,
                  geo, coe, geometry_ref, coeffs_ref, sems):
    pairs = ((pic_ref, picture_hbm), (coeffs_ref, coeffs_hbm), (geometry_ref, geometry_hbm))
    stores = [pltpu.make_async_copy(a, b, sems.at[n]) for n, (a, b) in enumerate(pairs)]
    stores[0].start()

    def summed(r):
        return jnp.concatenate([sums_ref[h, r * OWNED : (r + 1) * OWNED, :] for h in range(BLOCK // 128)], axis=1)

    def put(ref, k, pitch, value):
        for h, part in enumerate(lane_halves(value)):
            ref[h, pl.ds(k, OWNED, stride=pitch), :] = part

    def relay(ref, out, pitch, count):
        def step(b, _):
            for h in range(BLOCK // 128):
                at = pl.ds(pl.multiple_of(b * BLOCK + h * 128, 128), 128)
                out[:, at] = ref[h, pl.ds(pl.multiple_of(b * pitch, 8), count), :]
            return 0

        lax.fori_loop(0, OWNED, step, 0, unroll=4)

    for c in range(3):
        tint = summed(6 + c)
        for k in range(bands):
            put(coe, 3 * k + c, 16, basis_ref[k] * tint)
    relay(coe, coeffs_ref, 16, 3 * bands)
    stores[1].start()
    grads = geometry_grads([terms_ref[k] for k in range(11)], [summed(r) for r in range(6)])
    for k, value in enumerate(grads):
        put(geo, k, 8, value)
    relay(geo, geometry_ref, 8, 6)
    stores[2].start()
    for store in stores:
        store.wait()


def finish(sums, terms, basis, pic):
    bands = basis.shape[0]
    vmem = pl.BlockSpec(memory_space=pltpu.VMEM)
    shapes = ((6, OWNED * BLOCK), (3 * bands, OWNED * BLOCK), pic.shape)
    return pl.pallas_call(
        functools.partial(finish_kernel, bands),
        name="finish",
        out_shape=tuple(jax.ShapeDtypeStruct(o, jnp.float32) for o in shapes),
        in_specs=[vmem] * 4,
        out_specs=tuple(pl.BlockSpec(memory_space=pltpu.HBM) for _ in shapes),
        scratch_shapes=[
            floats(BLOCK // 128, 8 * OWNED, 128),
            floats(BLOCK // 128, 16 * OWNED, 128),
            floats(*shapes[0]), floats(*shapes[1]), pltpu.SemaphoreType.DMA((3,)),
        ],
        compiler_params=pltpu.CompilerParams(vmem_limit_bytes=12 * 1024 * 1024),
    )(sums, terms, basis, pic)


def local_fused(geometry, sh_coeffs, view_angles, visible, counts, order, image_cot):
    cot = jnp.swapaxes(image_cot, 0, 1)
    pic, basis, terms, sums = fused(geometry, view_angles, sh_coeffs, visible, order, cot, counts)
    grad_geometry, grad_sh, picture = finish(sums, terms, basis, pic)
    return (jnp.swapaxes(picture, 0, 1), grad_geometry, grad_sh)


def local(geometry, sh_coeffs, view_angles, visible, counts, order, image_cot):
    owners = lax.axis_size("tile")
    tiles, vis = visible.shape
    owned = geometry.shape[1] // BLOCK
    fits = (owners, vis, tiles, owned, lax.axis_size("attr")) == (8, 16, 2, 32, 4)
    run = local_fused if fits else local_general
    return run(geometry, sh_coeffs, view_angles, visible, counts, order, image_cot)


def solution(mesh):
    in_specs = (
        P(None, "tile"),
        P("attr", "tile"),
        P(None, "tile"),
        P(("tile", "attr"), None),
        P(("tile", "attr")),
        P(("tile", "attr"), None),
        P(("tile", "attr"), None, None),
    )
    out_specs = (P(("tile", "attr"), None, None), P(None, "tile"), P("attr", "tile"))
    return jax.shard_map(local, mesh=mesh, in_specs=in_specs, out_specs=out_specs, check_vma=False)
```

```python
import functools
import jax
import jax.numpy as jnp
from jax import lax
from jax.experimental import pallas as pl
from jax.experimental.pallas import tpu as pltpu
from jax.sharding import PartitionSpec as P

BLOCK = 256
SIDE = 16
PIX = SIDE * SIDE
MID = 0.5 * SIDE
LOG2E = 1.4426950408889634
LN2 = 0.6931471805599453


band_zero = 0.28209479177387814
band_one = 0.4886025119029199
band_two = (
    1.0925484305920792,
    -1.0925484305920792,
    0.31539156525252005,
    -1.0925484305920792,
    0.5462742152960396,
)
band_three = (
    -0.5900435899266435,
    2.890611442640554,
    -0.4570457994644658,
    0.3731763325901154,
    -0.4570457994644658,
    1.445305721320277,
    -0.5900435899266435,
)


def sh_basis(view_angles):
    azimuth = view_angles[0]
    elevation = view_angles[1]
    dir_x = jnp.cos(azimuth) * jnp.cos(elevation)
    dir_y = jnp.sin(azimuth) * jnp.cos(elevation)
    dir_z = jnp.sin(elevation)
    sq_x = dir_x * dir_x
    sq_y = dir_y * dir_y
    sq_z = dir_z * dir_z
    basis_rows = [
        band_zero * jnp.ones_like(dir_x),
        -band_one * dir_y,
        band_one * dir_z,
        -band_one * dir_x,
        band_two[0] * dir_x * dir_y,
        band_two[1] * dir_y * dir_z,
        band_two[2] * (2.0 * sq_z - sq_x - sq_y),
        band_two[3] * dir_x * dir_z,
        band_two[4] * (sq_x - sq_y),
        band_three[0] * dir_y * (3.0 * sq_x - sq_y),
        band_three[1] * dir_x * dir_y * dir_z,
        band_three[2] * dir_y * (4.0 * sq_z - sq_x - sq_y),
        band_three[3] * dir_z * (2.0 * sq_z - 3.0 * sq_x - 3.0 * sq_y),
        band_three[4] * dir_x * (4.0 * sq_z - sq_x - sq_y),
        band_three[5] * dir_z * (sq_x - sq_y),
        band_three[6] * dir_x * (sq_x - 3.0 * sq_y),
    ]
    return basis_rows


def split2(x):
    high = x.astype(jnp.bfloat16)
    low = (x - high.astype(jnp.float32)).astype(jnp.bfloat16)
    return jnp.concatenate([high, low], axis=1)


def dot(a, b):
    return jnp.dot(a, b, preferred_element_type=jnp.float32)


def blend_kernel(tiles, seq_ref, counts_ref, held_ref, cot_rows_ref, cot_cols_ref, pic_ref, grad_ref, part_ref, ratio_ref):
    f32, bf16 = jnp.float32, jnp.bfloat16
    row = lax.broadcasted_iota(jnp.int32, (2 * BLOCK, BLOCK), 0)
    row = jnp.where(row >= BLOCK, row - BLOCK, row)
    col = lax.broadcasted_iota(jnp.int32, (2 * BLOCK, BLOCK), 1)
    before = jnp.where(row < col, -1.0, 0.0).astype(bf16)
    upto = jnp.where(row <= col, 1.0, 0.0).astype(bf16)

    def monomials(shape, dim, width):
        pixel = lax.broadcasted_iota(jnp.int32, shape, dim)
        kind = lax.broadcasted_iota(jnp.int32, shape, 1 - dim) & (width - 1)
        x = (pixel & (SIDE - 1)).astype(f32) + (0.5 - MID)
        y = (pixel // SIDE).astype(f32) + (0.5 - MID)
        out = jnp.where(kind == 0, 1.0, 0.0)
        for k, value in ((1, x), (2, y), (3, x * x), (4, x * y), (5, y * y)):
            out = jnp.where(kind == k, value, out)
        return out.astype(bf16)

    mono_cols = monomials((PIX, 48), 0, 16)
    mono_rows = monomials((8, PIX), 1, 8)
    cot_lhs, cot_rows = [], []
    for t in range(tiles):
        g = cot_cols_ref[t]
        high = g.astype(bf16).astype(f32)
        lane = lax.broadcasted_iota(jnp.int32, g.shape, 1)
        cot_lhs.append(jnp.where(lane < 48, high, g - high).astype(bf16))
        g = cot_rows_ref[t]
        high = g.astype(bf16).astype(f32)
        cot_rows.append(jnp.concatenate([high, g - high], axis=0).astype(bf16))

    grad_ref[...] = jnp.zeros_like(grad_ref)
    lives = [counts_ref[t] for t in range(tiles)]
    longest = functools.reduce(jnp.maximum, lives)

    lhs = []
    for t in range(tiles):
        wide = jnp.concatenate([mono_cols.astype(f32), jnp.zeros((PIX, 48), f32)], axis=1)
        lhs.append(jnp.concatenate([wide.astype(bf16), cot_lhs[t]], axis=0))
    head = lax.broadcasted_iota(jnp.int32, (16, BLOCK), 0) == 0

    def forward(j, carry):
        keep_before, sum_before, pictures = carry
        alphas, values, losses, helds, spots = [], [], [], [], []
        for t in range(tiles):
            at = seq_ref[t, j]
            hidden = jnp.where(j < lives[t], 0.0, -16384.0)
            held = held_ref[at]
            parts = split3(jnp.where(head, held + hidden, held))
            rows = jnp.concatenate(parts, axis=0)
            both = dot(lhs[t], jnp.concatenate([rows, rows], axis=0))
            alpha = jnp.exp2(both[:PIX])
            alphas.append(alpha)
            values.append(both[PIX:])
            losses.append(jnp.log(1.0 - alpha) * -LOG2E)
            helds.append(jnp.concatenate(parts[:2], axis=0))
            spots.append(at)
        loss = jnp.concatenate(losses, axis=0)
        keep_in = dot(split2(loss), before) + keep_before
        keep_before = keep_in[:, BLOCK - 1 :] - loss[:, BLOCK - 1 :]
        alpha = jnp.concatenate(alphas, axis=0)
        weight = alpha * jnp.exp2(keep_in)
        value = weight * jnp.concatenate(values, axis=0)
        total = dot(split2(value), upto) + sum_before
        sum_before = total[:, BLOCK - 1 :]
        ratio = alpha * jnp.exp2(loss)
        part_ref[j] = value + ratio * total
        ratio_ref[j] = ratio
        w2 = split2(weight)
        shown = []
        for t in range(tiles):
            w_high, w_low = w2[t * PIX : (t + 1) * PIX, :BLOCK], w2[t * PIX : (t + 1) * PIX, BLOCK:]
            rows = lax.dot_general(helds[t], w_high, (((1,), (1,)), ((), ())), preferred_element_type=f32)
            rows = rows + lax.dot_general(helds[t], w_low, (((1,), (1,)), ((), ())), preferred_element_type=f32)
            shown.append(pictures[t] + rows[:16] + rows[16:])
            colour_grad = dot(cot_rows[t], w_high) + dot(cot_rows[t], w_low)
            grad_ref[spots[t], 0:8, :] += colour_grad[:8] + colour_grad[8:]
        return keep_before, sum_before, tuple(shown)

    zero = jnp.zeros((tiles * PIX, 1), f32)
    start = (zero, zero, tuple(jnp.zeros((16, PIX), f32) for _ in range(tiles)))
    _, ends, pictures = lax.fori_loop(0, longest, forward, start)
    for t in range(tiles):
        pic_ref[t] = pictures[t]

    def backward(j, _):
        for t in range(tiles):
            pixels = slice(t * PIX, (t + 1) * PIX)
            d2 = split2(part_ref[j, pixels] - ratio_ref[j, pixels] * ends[pixels])
            moments = dot(mono_rows, d2[:, :BLOCK]) + dot(mono_rows, d2[:, BLOCK:])
            grad_ref[seq_ref[t, j], 8:16, :] += moments
        return 0

    lax.fori_loop(0, longest, backward, 0)


def blend(seq, counts, held, image_cot):
    tiles = image_cot.shape[0]
    rows = held.shape[0]
    cot_rows = jnp.pad(image_cot, ((0, 0), (0, 5), (0, 0)))
    cot_cols = jnp.pad(jnp.swapaxes(image_cot, 1, 2), ((0, 0), (0, 0), (6, 7)))
    cot_cols = jnp.tile(cot_cols, (1, 1, 6))
    smem = pl.BlockSpec(memory_space=pltpu.SMEM)
    vmem = pl.BlockSpec(memory_space=pltpu.VMEM)
    picture, grads = pl.pallas_call(
        functools.partial(blend_kernel, tiles),
        name="blend",
        out_shape=(
            jax.ShapeDtypeStruct((tiles, 16, PIX), jnp.float32),
            jax.ShapeDtypeStruct((rows, 16, BLOCK), jnp.float32),
        ),
        in_specs=[smem, smem, vmem, vmem, vmem],
        out_specs=(vmem, vmem),
        scratch_shapes=[
            pltpu.VMEM((seq.shape[1], tiles * PIX, BLOCK), jnp.float32),
            pltpu.VMEM((seq.shape[1], tiles * PIX, BLOCK), jnp.float32),
        ],
        compiler_params=pltpu.CompilerParams(vmem_limit_bytes=28 * 1024 * 1024),
    )(seq, counts, held, cot_rows, cot_cols)
    return picture[:, 6:9], grads


def splat_terms(geometry):
    mx, my = geometry[0] - MID, geometry[1] - MID
    c, s = jnp.cos(geometry[4]), jnp.sin(geometry[4])
    e1, e2 = jnp.exp(-2.0 * geometry[2]), jnp.exp(-2.0 * geometry[3])
    cc, ss, cs = c * c, s * s, c * s
    a = cc * e1 + ss * e2
    b = cs * (e1 - e2)
    d = ss * e1 + cc * e2
    return mx, my, e1, e2, cc, ss, cs, a, b, d, geometry[5]


def exponent_rows(terms):
    mx, my, e1, e2, cc, ss, cs, a, b, d, logit = terms
    bx, by = a * mx + b * my, b * mx + d * my
    log_opacity = jnp.minimum(logit, 0.0) - jnp.log1p(jnp.exp(-jnp.abs(logit)))
    one = log_opacity - 0.5 * (mx * bx + my * by)
    return [LOG2E * r for r in (one, bx, by, -0.5 * a, -b, -0.5 * d)]


def geometry_grads(terms, m):
    mx, my, e1, e2, cc, ss, cs, a, b, d, logit = terms
    n0 = m[0]
    nx, ny = m[1] - mx * n0, m[2] - my * n0
    nxx = m[3] - mx * (m[1] + nx)
    nxy = m[4] - mx * m[2] - my * nx
    nyy = m[5] - my * (m[2] + ny)
    return [
        a * nx + b * ny,
        b * nx + d * ny,
        e1 * (cc * nxx + 2.0 * cs * nxy + ss * nyy),
        e2 * (ss * nxx - 2.0 * cs * nxy + cc * nyy),
        (e2 - e1) * (cs * (nyy - nxx) + (cc - ss) * nxy),
        n0 / (1.0 + jnp.exp(logit)),
    ]


MESH = pl.DeviceIdType.MESH


def greet(peers):
    barrier = pltpu.get_barrier_semaphore()
    tile, attr, owners, extra = peers

    def hello(step, _):
        other = (tile + step) % owners
        pl.semaphore_signal(barrier, inc=1, device_id=(other, attr), device_id_type=MESH)
        return 0

    lax.fori_loop(1, owners, hello, 0)
    for other in extra:
        pl.semaphore_signal(barrier, inc=1, device_id=(tile, other), device_id_type=MESH)
    return barrier, owners - 1 + len(extra)


def split3(x):
    high = x.astype(jnp.bfloat16)
    rest = x - high.astype(jnp.float32)
    mid = rest.astype(jnp.bfloat16)
    return high, mid, (rest - mid.astype(jnp.float32)).astype(jnp.bfloat16)


def exchange(src, dst, sems, k, device):
    return pltpu.make_async_remote_copy(
        src_ref=src, dst_ref=dst, send_sem=sems.at[0, k], recv_sem=sems.at[1, k],
        device_id=device, device_id_type=MESH,
    )


def fetch_kernel(dims, want_ref, coef_ref, part_ref, held_ref, asked_ref,
                 asks, answer, landed, first, summed, second, tile_sems, back_sems, attr_sems):
    owners, owned, cap, message, stride = dims
    f32 = jnp.float32
    tile, attr = lax.axis_index("tile"), lax.axis_index("attr")
    core = attr + 1 - 2 * (attr % 2)
    across = (attr + 2) % 4
    pl.semaphore_wait(*greet((tile, attr, owners, (core, across))))

    colour_one = exchange(part_ref, first, attr_sems, 0, (tile, core))
    colour_one.start()

    def ask(other, sender):
        return pltpu.make_async_remote_copy(
            src_ref=want_ref.at[other], dst_ref=asks.at[sender],
            send_sem=tile_sems.at[0, other], recv_sem=tile_sems.at[1, sender],
            device_id=(other, attr), device_id_type=MESH,
        )

    def send_ask(step, _):
        ask((tile + step) % owners, tile).start()
        return 0

    lax.fori_loop(1, owners, send_ask, 0)
    asks[tile] = want_ref[tile]

    colour_one.wait()
    summed[...] = part_ref[...] + first[...]
    colour_two = exchange(summed, second, attr_sems, 1, (tile, across))
    colour_two.start()

    def take_ask(step, _):
        other = (tile + step) % owners
        ask(other, other).wait()
        return 0

    lax.fori_loop(1, owners, take_ask, 0)

    per = 128 // stride
    lanes = owners // per
    rows = []
    for tile_at in range(lanes):
        rows.append(functools.reduce(jnp.add, [asks[tile_at * per + k] for k in range(per)]))
    asked = jnp.concatenate(rows, axis=1) - 1.0
    asked_ref[...] = asked
    wide = 9 * owned
    columns = []
    for tile_at in range(lanes):
        square = jnp.concatenate([rows[tile_at] - 1.0] * 16, axis=0)
        columns.append(jnp.transpose(square)[:, 0:1])
    column = jnp.concatenate(columns, axis=0)
    lane = lax.broadcasted_iota(jnp.int32, (owners * stride, wide), 1).astype(f32)
    pick = jnp.where(lane == column, 1.0, 0.0).astype(jnp.bfloat16)

    colour_two.wait()
    colour = summed[...] + second[...] + 0.5
    table = jnp.concatenate([coef_ref[...], colour], axis=0)
    high, mid, low = split3(table)
    answer[...] = (dot(pick, low) + dot(pick, mid)) + dot(pick, high)

    def back(other, sender):
        at = pl.multiple_of(other * stride, 8)
        return pltpu.make_async_remote_copy(
            src_ref=answer.at[pl.ds(at, message)], dst_ref=landed.at[sender],
            send_sem=back_sems.at[0, other], recv_sem=back_sems.at[1, sender],
            device_id=(other, attr), device_id_type=MESH,
        )

    def send_back(step, _):
        back((tile + step) % owners, tile).start()
        return 0

    lax.fori_loop(1, owners, send_back, 0)
    landed[tile] = answer[pl.ds(pl.multiple_of(tile * stride, 8), message), :]
    held_ref[...] = jnp.zeros_like(held_ref)

    def take_back(step, _):
        other = (tile + step) % owners
        back(other, other).wait()
        return 0

    lax.fori_loop(1, owners, take_back, 0)

    def unpack(o, _):
        for k in range(cap):
            held_ref[o * cap + k, 0:9, :] = landed[o, 9 * k : 9 * k + 9, :]
        return 0

    lax.fori_loop(0, owners, unpack, 0)


def give_kernel(dims, grads_ref, asked_ref, out_ref,
                packed, landed, sums, first, half, second, third, tile_sems, attr_sems):
    owners, owned, cap, message, stride = dims
    f32 = jnp.float32
    tile, attr = lax.axis_index("tile"), lax.axis_index("attr")
    core = attr + 1 - 2 * (attr % 2)
    across = (attr + 2) % 4
    mine = attr % 2

    if message < stride:
        landed[...] = jnp.zeros_like(landed)
    greeted = greet((tile, attr, owners, (core, across)))
    packed[...] = jnp.zeros_like(packed)

    def pack(o, _):
        for k in range(cap):
            packed[o, 9 * k : 9 * k + 6, :] = grads_ref[o * cap + k, 8:14, :]
            packed[o, 9 * k + 6 : 9 * k + 9, :] = grads_ref[o * cap + k, 0:3, :]
        return 0

    lax.fori_loop(0, owners, pack, 0)
    pl.semaphore_wait(*greeted)

    def give(other, sender):
        at = pl.multiple_of(sender * stride, 8)
        return pltpu.make_async_remote_copy(
            src_ref=packed.at[other], dst_ref=landed.at[pl.ds(at, message)],
            send_sem=tile_sems.at[0, other], recv_sem=tile_sems.at[1, sender],
            device_id=(other, attr), device_id_type=MESH,
        )

    def send_give(step, _):
        give((tile + step) % owners, tile).start()
        return 0

    lax.fori_loop(1, owners, send_give, 0)
    landed[pl.ds(pl.multiple_of(tile * stride, 8), message), :] = packed[tile]
    wide = 9 * owned
    row = lax.broadcasted_iota(jnp.int32, (wide, owners * stride), 0).astype(f32)
    pick = jnp.where(row == asked_ref[0:1, :], 1.0, 0.0).astype(jnp.bfloat16)

    def take_give(step, _):
        other = (tile + step) % owners
        give(other, other).wait()
        return 0

    lax.fori_loop(1, owners, take_give, 0)
    high, mid, low = split3(landed[...])
    total = (dot(pick, low) + dot(pick, mid)) + dot(pick, high)
    cut = wide // 2
    sums[0] = total[:cut]
    sums[1] = total[cut:]

    one = exchange(sums.at[1 - mine], first, attr_sems, 0, (tile, core))
    one.start()
    one.wait()
    half[...] = sums[mine] + first[...]
    two = exchange(half, second, attr_sems, 1, (tile, across))
    two.start()
    two.wait()
    half_sum = half[...] + second[...]
    first[...] = half_sum
    three = exchange(first, third, attr_sems, 2, (tile, core))
    three.start()
    three.wait()
    at = pl.multiple_of(mine * cut, 8)
    out_ref[pl.ds(at, cut), :] = half_sum
    at = pl.multiple_of((1 - mine) * cut, 8)
    out_ref[pl.ds(at, cut), :] = third[...]


def remote_call(kernel, dims, outs, ins, scratch, number, name):
    vmem = pl.BlockSpec(memory_space=pltpu.VMEM)
    return pl.pallas_call(
        functools.partial(kernel, dims),
        name=name,
        out_shape=tuple(jax.ShapeDtypeStruct(o, jnp.float32) for o in outs),
        in_specs=[vmem] * len(ins),
        out_specs=tuple(vmem for _ in outs),
        scratch_shapes=scratch,
        compiler_params=pltpu.CompilerParams(
            collective_id=number, has_side_effects=True, vmem_limit_bytes=20 * 1024 * 1024
        ),
    )(*ins)


def floats(*shape):
    return pltpu.VMEM(shape, jnp.float32)


def fetch(dims, want, coef, part):
    owners, owned, cap, message, stride = dims
    sems = pltpu.SemaphoreType.DMA
    return remote_call(
        fetch_kernel, dims,
        ((owners * cap, 16, BLOCK), (8, owners * stride)),
        (want, coef, part),
        [floats(owners, 8, 128), floats(owners * stride, BLOCK), floats(owners, message, BLOCK),
         floats(3 * owned, BLOCK), floats(3 * owned, BLOCK), floats(3 * owned, BLOCK),
         sems((2, owners)), sems((2, owners)), sems((2, 2))],
        1, "fetch",
    )


def give_back(dims, grads, asked):
    owners, owned, cap, message, stride = dims
    sems = pltpu.SemaphoreType.DMA
    cut = 9 * owned // 2
    return remote_call(
        give_kernel, dims, ((9 * owned, BLOCK),), (grads, asked),
        [floats(owners, message, BLOCK), floats(owners * stride, BLOCK), floats(2, cut, BLOCK),
         floats(cut, BLOCK), floats(cut, BLOCK), floats(cut, BLOCK), floats(cut, BLOCK),
         sems((2, owners)), sems((2, 3))],
        2, "give",
    )[0]


def prep_kernel(owned, bands, geometry_ref, angles_ref, coeffs_ref, coef_ref, part_ref, basis_ref, terms_ref,
                geo, ang, coe, rows):
    def relay(b, _):
        for h in range(BLOCK // 128):
            at = pl.ds(pl.multiple_of(b * BLOCK + h * 128, 128), 128)
            geo[h, pl.ds(pl.multiple_of(b * 8, 8), 6), :] = geometry_ref[:, at]
            ang[h, pl.ds(pl.multiple_of(b * 8, 8), 2), :] = angles_ref[:, at]
            coe[h, pl.ds(pl.multiple_of(b * 16, 8), 3 * bands), :] = coeffs_ref[:, at]
        return 0

    lax.fori_loop(0, owned, relay, 0, unroll=4)

    def plane(ref, k, pitch):
        halves = [ref[h, pl.ds(k, owned, stride=pitch), :] for h in range(BLOCK // 128)]
        return jnp.concatenate(halves, axis=1)

    terms = splat_terms([plane(geo, k, 8) for k in range(6)])
    for k, value in enumerate(terms):
        terms_ref[k] = value
    for k, value in enumerate(exponent_rows(terms)):
        coef_ref[k * owned : (k + 1) * owned, :] = value
    for k, value in enumerate(sh_basis([plane(ang, k, 8) for k in range(2)])):
        rows[k] = value
    first = lax.axis_index("attr") * bands
    total = [jnp.zeros((owned, BLOCK), jnp.float32) for _ in range(3)]
    for k in range(bands):
        value = rows[first + k]
        basis_ref[k] = value
        for c in range(3):
            total[c] = total[c] + value * plane(coe, 3 * k + c, 16)
    for c in range(3):
        part_ref[c * owned : (c + 1) * owned, :] = total[c]


def prep(geometry, view_angles, sh_coeffs, owned):
    bands = sh_coeffs.shape[0] // 3
    vmem = pl.BlockSpec(memory_space=pltpu.VMEM)
    shapes = ((6 * owned, BLOCK), (3 * owned, BLOCK), (bands, owned, BLOCK), (11, owned, BLOCK))
    return pl.pallas_call(
        functools.partial(prep_kernel, owned, bands),
        name="prep",
        out_shape=tuple(jax.ShapeDtypeStruct(o, jnp.float32) for o in shapes),
        in_specs=[vmem] * 3,
        out_specs=(vmem,) * 4,
        scratch_shapes=[
            floats(BLOCK // 128, 8 * owned, 128),
            floats(BLOCK // 128, 8 * owned, 128),
            floats(BLOCK // 128, 16 * owned, 128),
            floats(16, owned, BLOCK),
        ],
        compiler_params=pltpu.CompilerParams(vmem_limit_bytes=12 * 1024 * 1024),
    )(geometry, view_angles, sh_coeffs)


def final_kernel(owned, bands, sums_ref, terms_ref, basis_ref, geometry_ref, coeffs_ref, geo, coe):
    summed = [sums_ref[k * owned : (k + 1) * owned, :] for k in range(9)]

    def put(ref, k, pitch, value):
        for h in range(BLOCK // 128):
            ref[h, pl.ds(k, owned, stride=pitch), :] = value[:, h * 128 : (h + 1) * 128]

    for k, value in enumerate(geometry_grads([terms_ref[k] for k in range(11)], summed[:6])):
        put(geo, k, 8, value)
    for k in range(bands):
        for c in range(3):
            put(coe, 3 * k + c, 16, basis_ref[k] * summed[6 + c])

    def relay(b, _):
        for h in range(BLOCK // 128):
            at = pl.ds(pl.multiple_of(b * BLOCK + h * 128, 128), 128)
            geometry_ref[:, at] = geo[h, pl.ds(pl.multiple_of(b * 8, 8), 6), :]
            coeffs_ref[:, at] = coe[h, pl.ds(pl.multiple_of(b * 16, 8), 3 * bands), :]
        return 0

    lax.fori_loop(0, owned, relay, 0, unroll=4)


def final(sums, terms, basis, owned):
    bands = basis.shape[0]
    vmem = pl.BlockSpec(memory_space=pltpu.VMEM)
    shapes = ((6, owned * BLOCK), (3 * bands, owned * BLOCK))
    return pl.pallas_call(
        functools.partial(final_kernel, owned, bands),
        name="final",
        out_shape=tuple(jax.ShapeDtypeStruct(o, jnp.float32) for o in shapes),
        in_specs=[vmem] * 3,
        out_specs=(vmem,) * 2,
        scratch_shapes=[
            floats(BLOCK // 128, 8 * owned, 128),
            floats(BLOCK // 128, 16 * owned, 128),
        ],
        compiler_params=pltpu.CompilerParams(vmem_limit_bytes=12 * 1024 * 1024),
    )(sums, terms, basis)


def local_general(geometry, sh_coeffs, view_angles, visible, counts, order, image_cot):
    owners = lax.axis_size("tile")
    owned = geometry.shape[1] // BLOCK
    vis = visible.shape[1]
    cap = (vis + owners - 1) // owners
    coef, partial_colour, my_basis, terms = prep(geometry, view_angles, sh_coeffs, owned)

    ids = visible[0]
    owner_of, local_of = ids // owned, ids % owned
    position = jnp.arange(vis)
    rank = jnp.sum(((owner_of[None, :] == owner_of[:, None]) & (position[None, :] < position[:, None])).astype(jnp.int32), 1)
    slot = owner_of * cap + rank
    message = -(-9 * cap // 8) * 8
    stride = 16 if message <= 16 else 32
    dims = (owners, owned, cap, message, stride)
    lane = jnp.arange(128) - (lax.axis_index("tile") % (128 // stride)) * stride
    in_slot = lane[None, :, None] // 9 + jnp.arange(owners)[:, None, None] * cap
    hit = (slot[None, None, :] == in_slot) & (lane >= 0)[None, :, None] & (lane < 9 * cap)[None, :, None]
    want = jnp.sum(jnp.where(hit, 1 + local_of[None, None, :] + owned * (lane % 9)[None, :, None], 0), 2)
    want = jnp.broadcast_to(want.astype(jnp.float32)[:, None, :], (owners, 8, 128))
    slot_of = jnp.sum(jnp.where(visible[:, :, None] == ids[None, None, :], slot[None, None, :], 0), 2)
    seq = jnp.sum(jnp.where(order[:, :, None] == position[None, None, :], slot_of[:, None, :], 0), 2)

    held, asked = fetch(dims, want, coef, partial_colour)
    picture, grads = blend(seq, counts, held, image_cot)
    sums = give_back(dims, grads, asked)
    grad_geometry, grad_sh = final(sums, terms, my_basis, owned)
    return (picture, grad_geometry, grad_sh)


STEPS = 8
PAIR = 2
SLOTS = STEPS * PAIR
OWNED = 32
MSG = 24
TRIPLE = 3
LAG = 4
GIVEN = 9 * PAIR


def stack3(x):
    high, mid, low = split3(x)
    return jnp.concatenate([high, mid, low], axis=0)


def lane_halves(x):
    return [x[:, h * 128 : (h + 1) * 128] for h in range(BLOCK // 128)]


def put_rows(ref, rows, value):
    for h, part in enumerate(lane_halves(value)):
        ref[h, rows, :] = part


def get_rows(ref, rows):
    return jnp.concatenate([ref[h, rows, :] for h in range(BLOCK // 128)], axis=1)


def scatter(ref, at, pitch, value):
    put_rows(ref, pl.ds(at, STEPS, stride=pitch), value)


def gather(ref, at, pitch):
    return get_rows(ref, pl.ds(at, STEPS, stride=pitch))


def tile_of(ref, i, at):
    return jnp.concatenate([ref[i, h, at : at + 8, :] for h in range(BLOCK // 128)], axis=1)


def pixel_monomials(shape, dim):
    pixel = lax.broadcasted_iota(jnp.int32, shape, dim)
    kind = lax.broadcasted_iota(jnp.int32, shape, 1 - dim) & 7
    x = (pixel & (SIDE - 1)).astype(jnp.float32) + (0.5 - MID)
    y = (pixel // SIDE).astype(jnp.float32) + (0.5 - MID)
    out = jnp.where(kind == 0, 1.0, 0.0)
    for k, value in ((1, x), (2, y), (3, x * x), (4, x * y), (5, y * y)):
        out = jnp.where(kind == k, value, out)
    return out.astype(jnp.bfloat16)


def slot_tables(tile, visible, order, counts_ref):
    f32 = jnp.float32
    sub = lax.broadcasted_iota(jnp.int32, (SLOTS, SLOTS), 0)
    lane = lax.broadcasted_iota(jnp.int32, (SLOTS, SLOTS), 1)
    diagonal = sub == lane
    lane_f, sub_f = lane.astype(f32), sub.astype(f32)

    def to_column(row):
        return jnp.sum(jnp.where(diagonal, row, 0.0), axis=1, keepdims=True)

    def to_row(column):
        return jnp.sum(jnp.where(diagonal, column, 0.0), axis=0, keepdims=True)

    ids = visible[0:1]
    owner = ids // OWNED
    near = owner - tile
    near = jnp.where(near < 0, near + STEPS, near).astype(f32)
    ids_f = ids.astype(f32)
    inside = (ids - owner * OWNED).astype(f32)
    near_column = to_column(near)
    second = jnp.sum(jnp.where((near_column == near) & (sub < lane), 1.0, 0.0), axis=0, keepdims=True)
    slot = second * STEPS + near
    match = sub_f == slot
    local_id = jnp.sum(jnp.where(match, inside, 0.0), axis=1, keepdims=True)
    slot_id = jnp.sum(jnp.where(match, ids_f, 0.0), axis=1, keepdims=True)
    ahead, live = [], []
    for t in range(2):
        listed = to_column(visible[t : t + 1].astype(f32))
        here = sub == order[t : t + 1]
        sequence = jnp.sum(jnp.where(here, listed, 0.0), axis=0, keepdims=True)
        rank = jnp.sum(jnp.where(sequence == slot_id, lane_f, 0.0), axis=1, keepdims=True)
        ahead.append(jnp.where(to_row(rank) < rank, 1.0, 0.0))
        live.append(jnp.where(rank < counts_ref[t].astype(f32), 1.0, 0.0))
    return local_id, ahead, live


def fused_kernel(bands, geometry_hbm, angles_hbm, coeffs_hbm, visible_hbm, order_hbm, cot_hbm, counts_hbm,
                 pic_ref, basis_ref, terms_ref, out_ref,
                 geometry, angles, coeffs, visible, order, cot, counts_ref, geo, ang, coe, rows,
                 coef, part, first, summed, second, colour,
                 asks_out, asks, answer, held, w_ref, ratio_ref, c_ref, a_ref,
                 packed, landed, sums, got_core, all_picks, d_ref, columns_ref,
                 local_sems, ask_sems, back_sems, give_sems, share_sems, attr_sems):
    f32, bf16 = jnp.float32, jnp.bfloat16
    tile, attr = lax.axis_index("tile"), lax.axis_index("attr")
    core = attr + 1 - 2 * (attr % 2)
    across = (attr + 2) % 4
    mine = attr % 2
    greeted = greet((tile, attr, STEPS, (core, across, (core + 2) % 4)))

    pairs = ((visible_hbm, visible), (order_hbm, order), (counts_hbm, counts_ref), (angles_hbm, angles),
             (coeffs_hbm, coeffs), (geometry_hbm, geometry), (cot_hbm, cot))
    loads = [pltpu.make_async_copy(a, b, local_sems.at[n]) for n, (a, b) in enumerate(pairs)]
    for load in loads:
        load.start()

    asks_out[...] = jnp.zeros_like(asks_out)
    answer[...] = jnp.zeros_like(answer)
    for load in loads[:3]:
        load.wait()
    local_id, ahead, live = slot_tables(tile, visible[...], order[...], counts_ref)
    lane = lax.broadcasted_iota(jnp.int32, (SLOTS, 128), 1)
    block = (lane & (OWNED - 1)).astype(f32)
    wanted = jnp.where((block == local_id) & (lane < TRIPLE * OWNED), 1.0, 0.0)
    for k in range(PAIR):
        asks_out[pl.ds(k, STEPS, stride=8), :] = wanted[k * STEPS : (k + 1) * STEPS]
    for load in loads[3:]:
        load.wait()

    def relay(b, _):
        for h in range(BLOCK // 128):
            at = pl.ds(pl.multiple_of(b * BLOCK + h * 128, 128), 128)
            geo[h, pl.ds(pl.multiple_of(b * 8, 8), 6), :] = geometry[:, at]
            ang[h, pl.ds(pl.multiple_of(b * 8, 8), 2), :] = angles[:, at]
            coe[h, pl.ds(pl.multiple_of(b * 16, 8), 3 * bands), :] = coeffs[:, at]
        return 0

    lax.fori_loop(0, OWNED, relay, 0, unroll=4)

    def plane(ref, k, pitch):
        halves = [ref[h, pl.ds(k, OWNED, stride=pitch), :] for h in range(BLOCK // 128)]
        return jnp.concatenate(halves, axis=1)

    for k, value in enumerate(sh_basis([plane(ang, k, 8) for k in range(2)])):
        rows[k] = value
    first_band = attr * bands
    total = [jnp.zeros((OWNED, BLOCK), f32) for _ in range(3)]
    for k in range(bands):
        value = rows[first_band + k]
        basis_ref[k] = value
        for c in range(3):
            total[c] = total[c] + value * plane(coe, 3 * k + c, 16)
    for c in range(3):
        part[c * OWNED : (c + 1) * OWNED, :] = total[c]
    pl.semaphore_wait(*greeted)

    def ask(i):
        return pltpu.make_async_remote_copy(
            src_ref=asks_out.at[pl.ds(pl.multiple_of(i * 8, 8), 8)], dst_ref=asks.at[pl.ds(pl.multiple_of(i * 8, 8), 8)],
            send_sem=ask_sems.at[0, i], recv_sem=ask_sems.at[1, i],
            device_id=((tile + i) % STEPS, attr), device_id_type=MESH,
        )

    def back(i, part):
        at, size = ((0, 6 * PAIR), (16, 8))[part]
        return pltpu.make_async_remote_copy(
            src_ref=answer.at[:, pl.ds(pl.multiple_of(i * MSG + at, 8), size)], dst_ref=held.at[i, :, pl.ds(at, size)],
            send_sem=back_sems.at[0, part, i], recv_sem=back_sems.at[1, part, i],
            device_id=((tile + STEPS - i) % STEPS, attr), device_id_type=MESH,
        )

    def give(i, d):
        slot = d * STEPS + i
        return pltpu.make_async_remote_copy(
            src_ref=packed.at[i, (attr + d) % 2, pl.ds(0, GIVEN)],
            dst_ref=landed.at[pl.ds(pl.multiple_of(slot * MSG, 8), GIVEN)],
            send_sem=give_sems.at[0, slot], recv_sem=give_sems.at[1, slot],
            device_id=((tile + i) % STEPS, (attr + d) % 4), device_id_type=MESH,
        )

    def share(d):
        return exchange(all_picks.at[0], all_picks.at[d], share_sems, d, (tile, (attr + d) % 4))

    upper = tile // (STEPS // 2)

    def near(n):
        return (n + upper * (STEPS - 2 * n)) % STEPS

    def far(n):
        return (2 * STEPS - n + upper * (2 * n - STEPS)) % STEPS

    def each(act):
        def step(n, _):
            act(far(n))
            return 0

        lax.fori_loop(1, STEPS, step, 0)

    colour_one = exchange(part, first, attr_sems, 0, (tile, core))
    colour_one.start()
    each(lambda i: ask(i).start())
    asks[0:8, :] = asks_out[0:8, :]

    terms = splat_terms([plane(geo, k, 8) for k in range(6)])
    for k, value in enumerate(terms):
        terms_ref[k] = value
    for k, value in enumerate(exponent_rows(terms)):
        coef[k] = stack3(value)

    colour_one.wait()
    summed[...] = part[...] + first[...]
    colour_two = exchange(summed, second, attr_sems, 1, (tile, across))
    colour_two.start()

    each(lambda i: ask(i).wait_recv())
    picks = jnp.concatenate([asks[pl.ds(k, STEPS, stride=8), :] for k in range(PAIR)], axis=0)
    pick = picks.astype(bf16)[:, : TRIPLE * OWNED]
    all_picks[0] = picks
    for d in range(1, 4):
        share(d).start()

    def pick_row(values, at):
        found = dot(pick, values)
        for k in range(PAIR):
            scatter(answer, at[k], MSG, found[k * STEPS : (k + 1) * STEPS])

    for r in range(6):
        pick_row(coef[r], (r, 6 + r))
    each(lambda i: back(i, 0).start())
    held[0, :, 0:16] = answer[:, 0:16, :]

    row = lax.broadcasted_iota(jnp.int32, (2 * BLOCK, BLOCK), 0) & (BLOCK - 1)
    col = lax.broadcasted_iota(jnp.int32, (2 * BLOCK, BLOCK), 1)
    before = jnp.where(row < col, -1.0, 0.0).astype(bf16)
    upto = jnp.where(row <= col, 1.0, 0.0).astype(bf16)
    mono_cols = pixel_monomials((PIX, 32), 0)
    mono_rows = pixel_monomials((8, PIX), 1)
    eight = lax.broadcasted_iota(jnp.int32, (8, BLOCK), 0)
    own_rows = [(eight >= 4 * k) & (eight < 4 * k + 3) for k in range(PAIR)]

    def halves(x):
        high = x.astype(bf16).astype(f32)
        return high, x - high

    def powers_of(i):
        powers = []
        both = jnp.concatenate([tile_of(held, i, 0), tile_of(held, i, 8)], axis=0)
        for k in range(PAIR):
            rows = jnp.concatenate([both[6 * k : 6 * k + 6], jnp.zeros((2, BLOCK), f32)], axis=0)
            high, mid, low = [p.astype(f32) for p in split3(rows)]
            coefs = jnp.concatenate([high, mid, low, jnp.zeros_like(low)], axis=0).astype(bf16)
            powers.append(dot(mono_cols, coefs))
        return powers

    def shape_pair(i, powers):
        alphas, losses = [], []
        for k in range(PAIR):
            alpha = jnp.exp2(powers[k])
            loss = jnp.log(1.0 - alpha) * -LOG2E
            alphas.append(alpha)
            losses.append(split2(loss))
            ratio_ref[i, k] = alpha * jnp.exp2(loss)
        keep = dot(jnp.concatenate(losses, axis=0), before)
        for k in range(PAIR):
            w_ref[i, k] = split2(alphas[k] * jnp.exp2(keep[k * PIX : (k + 1) * PIX]))

    def show_pair(i):
        c_high, c_low = halves(tile_of(held, i, 16))
        seen = None
        for k in range(PAIR):
            w2 = w_ref[i, k]
            one = jnp.where(eight == 4 * k + 3, 1.0, 0.0)
            lhs = jnp.concatenate([jnp.where(own_rows[k], c_high, one), jnp.where(own_rows[k], c_low, 0.0)], axis=0)
            lhs = lhs.astype(bf16)
            contract = (((1,), (1,)), ((), ()))
            shown = lax.dot_general(lhs, w2[:, :BLOCK], contract, preferred_element_type=f32)
            shown = shown + lax.dot_general(lhs, w2[:, BLOCK:], contract, preferred_element_type=f32)
            shown = shown[:8] + shown[8:]
            seen = shown if seen is None else seen + shown
        put_rows(c_ref, pl.ds(pl.multiple_of(i * 8, 8), 8), seen)

    def forward_early(n, _):
        i = near(n)
        back(i, 0).wait_recv()
        shape_pair(i, powers_of(i))
        return 0

    def forward(n, _):
        i, shown = near(n), near(n - LAG)
        back(i, 0).wait_recv()

        @pl.when(n > LAG)
        def _():
            back(shown, 1).wait_recv()

        powers = powers_of(i)
        show_pair(shown)
        shape_pair(i, powers)
        return 0

    shape_pair(0, powers_of(0))
    colour_two.wait()
    for c in range(3):
        piece = slice(c * OWNED, (c + 1) * OWNED)
        pick_row(stack3(summed[piece] + second[piece] + 0.5), (16 + c, 20 + c))
    each(lambda i: back(i, 1).start())
    held[0, :, 16:24] = answer[:, 16:24, :]
    lax.fori_loop(1, LAG, forward_early, 0)
    lax.fori_loop(LAG, STEPS, forward, 0)
    for n in range(STEPS - LAG, STEPS):
        back(near(n), 1).wait_recv()
    for n in range(STEPS - LAG, STEPS):
        show_pair(near(n))

    def by_slot(ref, c):
        return jnp.concatenate([gather(ref, c + 4 * k, 8) for k in range(PAIR)], axis=0)

    local = [by_slot(c_ref, c) for c in range(4)]
    spread = [jnp.zeros((SLOTS, PIX), f32) for _ in range(4)]
    for t in range(2):
        def earlier(values):
            out = jnp.zeros((SLOTS, PIX), f32)
            for s in range(SLOTS):
                out = out + ahead[t][:, s : s + 1] * values[s : s + 1, :]
            return out

        through = jnp.broadcast_to(live[t], (SLOTS, PIX))
        for s in range(SLOTS):
            through = through * (1.0 - ahead[t][:, s : s + 1] * local[3][s : s + 1, :])
        shade = jnp.zeros((SLOTS, PIX), f32)
        for c in range(3):
            g = cot[c, t : t + 1, :]
            lit = through * local[c]
            pic_ref[c, t : t + 1, :] = jnp.sum(lit, axis=0, keepdims=True)
            shade = shade + lit * g
            spread[c] = spread[c] + through * g
        behind = earlier(shade) - jnp.sum(shade, axis=0, keepdims=True)
        spread[3] = spread[3] + live[t] * behind
    for c in range(4):
        for k in range(PAIR):
            scatter(a_ref, c + 4 * k, 8, spread[c][k * STEPS : (k + 1) * STEPS])

    def turn(i):
        a = get_rows(a_ref, pl.ds(pl.multiple_of(i * 8, 8), 8))
        a_high, a_low = halves(a)
        columns_ref[...] = jnp.transpose(jnp.concatenate([a_high, a_low, a_high, a], axis=0))

    def tints_of(i, columns):
        c_high, c_low = halves(tile_of(held, i, 16))
        tints = []
        for k in range(PAIR):
            ch, cl = jnp.where(own_rows[k], c_high, 0.0), jnp.where(own_rows[k], c_low, 0.0)
            tints.append(dot(columns.astype(bf16), jnp.concatenate([ch, ch, cl, jnp.zeros_like(cl)], axis=0).astype(bf16)))
        return tints

    def slope_pair(i, columns, tints):
        values = []
        for k in range(PAIR):
            w2 = w_ref[i, k]
            values.append((w2[:, :BLOCK].astype(f32) + w2[:, BLOCK:].astype(f32)) * tints[k])
        total = dot(jnp.concatenate([split2(value) for value in values], axis=0), upto)
        for k in range(PAIR):
            beyond = total[k * PIX : (k + 1) * PIX] + columns[:, 27 + 4 * k : 28 + 4 * k]
            d_ref[k] = split2(values[k] + ratio_ref[i, k] * beyond)

    def sum_pair(i):
        a_high, a_low = halves(get_rows(a_ref, pl.ds(pl.multiple_of(i * 8, 8), 8)))
        moments, tint = [], None
        for k in range(PAIR):
            d2, w2 = d_ref[k], w_ref[i, k]
            moments.append(dot(mono_rows, d2[:, :BLOCK]) + dot(mono_rows, d2[:, BLOCK:]))
            lhs = jnp.concatenate([jnp.where(own_rows[k], a_high, 0.0), jnp.where(own_rows[k], a_low, 0.0)], axis=0)
            lhs = lhs.astype(bf16)
            grads = dot(lhs, w2[:, :BLOCK]) + dot(lhs, w2[:, BLOCK:])
            grads = grads[:8] + grads[8:]
            tint = grads if tint is None else tint + grads
        pieces = [m[:6] for m in moments] + [tint[0:3], tint[4:7], jnp.zeros((6, BLOCK), f32)]
        put_rows(packed.at[i], pl.ds(0, MSG), jnp.concatenate(pieces, axis=0))

    def backward(n, _):
        i, after = far(n), far(n + 1)
        columns = columns_ref[...]
        tints = tints_of(after, columns)
        sum_pair(i)
        slope_pair(after, columns, tints)
        turn(far(n + 2))
        for d in (2, 1, 3, 0):
            give(i, d).start()
        return 0

    turn(far(1))
    columns = columns_ref[...]
    slope_pair(far(1), columns, tints_of(far(1), columns))
    turn(far(2))
    lax.fori_loop(1, STEPS, backward, 0)
    sum_pair(0)
    for d in range(1, 4):
        give(0, d).start()
    landed[0:MSG, :] = packed[0, mine]

    for d in range(1, 4):
        share(d).wait_recv()
    chosen = [all_picks[d, k * STEPS : (k + 1) * STEPS, :] for k in range(PAIR) for d in range(4)]
    tall = jnp.concatenate(chosen * TRIPLE + [jnp.zeros((256 - TRIPLE * 4 * SLOTS, 128), f32)], axis=0)
    put = jnp.transpose(tall)[:OWNED, : TRIPLE * 4 * SLOTS].astype(bf16)

    def take_give(n, _):
        for d in range(4):
            give(n, d).wait_recv()
        return 0

    lax.fori_loop(1, STEPS, take_give, 0)
    for d in range(1, 4):
        give(0, d).wait_recv()
    for r in range(0, 9, 2):
        both = []
        for q in range(r, min(r + 2, 9)):
            at = (q, 6 + q) if q < 6 else (6 + q, 9 + q)
            both.append(jnp.concatenate([landed[pl.ds(at[k], 4 * STEPS, stride=MSG), :] for k in range(PAIR)], axis=0))
        found = dot(put, stack3(jnp.concatenate(both, axis=1)))
        for q in range(len(both)):
            sums[(r + q) * OWNED : (r + q + 1) * OWNED, :] = found[:, q * 128 : (q + 1) * 128]

    swap = exchange(sums, got_core, attr_sems, 2, (tile, core))
    swap.start()
    out_ref[mine] = sums[...]
    for d in range(1, 4):
        share(d).wait_send()
        give(0, d).wait_send()

    def sent_give(n, _):
        for d in range(4):
            give(n, d).wait_send()
        return 0

    lax.fori_loop(1, STEPS, sent_give, 0)
    each(lambda i: ask(i).wait_send())
    each(lambda i: back(i, 0).wait_send())
    each(lambda i: back(i, 1).wait_send())
    swap.wait()
    out_ref[1 - mine] = got_core[...]


def fused(geometry, view_angles, sh_coeffs, visible, order, cot, counts):
    bands = sh_coeffs.shape[0] // 3
    sems = pltpu.SemaphoreType.DMA
    vmem = pl.BlockSpec(memory_space=pltpu.VMEM)
    ins = (geometry, view_angles, sh_coeffs, visible, order, cot, counts)
    colours = 3 * OWNED
    shapes = (cot.shape, (bands, OWNED, BLOCK), (11, OWNED, BLOCK), (2, 9 * OWNED, 128))
    return pl.pallas_call(
        functools.partial(fused_kernel, bands),
        name="splat",
        out_shape=tuple(jax.ShapeDtypeStruct(o, jnp.float32) for o in shapes),
        in_specs=[pl.BlockSpec(memory_space=pltpu.HBM)] * len(ins),
        out_specs=tuple(vmem for _ in shapes),
        scratch_shapes=[pltpu.VMEM(x.shape, x.dtype) for x in ins[:-1]] + [
            pltpu.SMEM(counts.shape, counts.dtype),
            floats(BLOCK // 128, 8 * OWNED, 128), floats(BLOCK // 128, 8 * OWNED, 128),
            floats(BLOCK // 128, 16 * OWNED, 128), floats(16, OWNED, BLOCK),
            pltpu.VMEM((6, TRIPLE * OWNED, BLOCK), jnp.bfloat16), floats(colours, BLOCK), floats(colours, BLOCK),
            floats(colours, BLOCK), floats(colours, BLOCK), floats(8, 128),
            floats(8 * STEPS, 128), floats(8 * STEPS, 128), floats(2, STEPS * MSG, 128), floats(STEPS, 2, MSG, 128),
            pltpu.VMEM((STEPS, PAIR, PIX, 2 * BLOCK), jnp.bfloat16), floats(STEPS, PAIR, PIX, BLOCK),
            floats(2, 8 * STEPS, 128), floats(2, 8 * STEPS, 128),
            floats(STEPS, 2, MSG, 128), floats(4 * STEPS * MSG, 128), floats(9 * OWNED, 128), floats(9 * OWNED, 128),
            floats(4, SLOTS, 128), pltpu.VMEM((PAIR, PIX, 2 * BLOCK), jnp.bfloat16), floats(PIX, 32),
            sems((len(ins),)), sems((2, STEPS)), sems((2, 2, STEPS)), sems((2, 4 * STEPS)), sems((2, 4)), sems((2, 3)),
        ],
        compiler_params=pltpu.CompilerParams(
            collective_id=3, has_side_effects=True, vmem_limit_bytes=40 * 1024 * 1024
        ),
    )(*[pltpu.with_memory_space_constraint(x, pltpu.HBM) for x in ins])


def finish_kernel(bands, sums_ref, terms_ref, basis_ref, pic_ref, geometry_hbm, coeffs_hbm, picture_hbm,
                  geo, coe, geometry_ref, coeffs_ref, sems):
    pairs = ((pic_ref, picture_hbm), (coeffs_ref, coeffs_hbm), (geometry_ref, geometry_hbm))
    stores = [pltpu.make_async_copy(a, b, sems.at[n]) for n, (a, b) in enumerate(pairs)]
    stores[0].start()

    def summed(r):
        return jnp.concatenate([sums_ref[h, r * OWNED : (r + 1) * OWNED, :] for h in range(BLOCK // 128)], axis=1)

    def put(ref, k, pitch, value):
        for h, part in enumerate(lane_halves(value)):
            ref[h, pl.ds(k, OWNED, stride=pitch), :] = part

    def relay(ref, out, pitch, count):
        def step(b, _):
            for h in range(BLOCK // 128):
                at = pl.ds(pl.multiple_of(b * BLOCK + h * 128, 128), 128)
                out[:, at] = ref[h, pl.ds(pl.multiple_of(b * pitch, 8), count), :]
            return 0

        lax.fori_loop(0, OWNED, step, 0, unroll=4)

    for c in range(3):
        tint = summed(6 + c)
        for k in range(bands):
            put(coe, 3 * k + c, 16, basis_ref[k] * tint)
    relay(coe, coeffs_ref, 16, 3 * bands)
    stores[1].start()
    grads = geometry_grads([terms_ref[k] for k in range(11)], [summed(r) for r in range(6)])
    for k, value in enumerate(grads):
        put(geo, k, 8, value)
    relay(geo, geometry_ref, 8, 6)
    stores[2].start()
    for store in stores:
        store.wait()


def finish(sums, terms, basis, pic):
    bands = basis.shape[0]
    vmem = pl.BlockSpec(memory_space=pltpu.VMEM)
    shapes = ((6, OWNED * BLOCK), (3 * bands, OWNED * BLOCK), pic.shape)
    return pl.pallas_call(
        functools.partial(finish_kernel, bands),
        name="finish",
        out_shape=tuple(jax.ShapeDtypeStruct(o, jnp.float32) for o in shapes),
        in_specs=[vmem] * 4,
        out_specs=tuple(pl.BlockSpec(memory_space=pltpu.HBM) for _ in shapes),
        scratch_shapes=[
            floats(BLOCK // 128, 8 * OWNED, 128),
            floats(BLOCK // 128, 16 * OWNED, 128),
            floats(*shapes[0]), floats(*shapes[1]), pltpu.SemaphoreType.DMA((3,)),
        ],
        compiler_params=pltpu.CompilerParams(vmem_limit_bytes=12 * 1024 * 1024),
    )(sums, terms, basis, pic)


def local_fused(geometry, sh_coeffs, view_angles, visible, counts, order, image_cot):
    cot = jnp.swapaxes(image_cot, 0, 1)
    pic, basis, terms, sums = fused(geometry, view_angles, sh_coeffs, visible, order, cot, counts)
    grad_geometry, grad_sh, picture = finish(sums, terms, basis, pic)
    return (jnp.swapaxes(picture, 0, 1), grad_geometry, grad_sh)


def local(geometry, sh_coeffs, view_angles, visible, counts, order, image_cot):
    owners = lax.axis_size("tile")
    tiles, vis = visible.shape
    owned = geometry.shape[1] // BLOCK
    fits = (owners, vis, tiles, owned, lax.axis_size("attr")) == (8, 16, 2, 32, 4)
    run = local_fused if fits else local_general
    return run(geometry, sh_coeffs, view_angles, visible, counts, order, image_cot)


def solution(mesh):
    in_specs = (
        P(None, "tile"),
        P("attr", "tile"),
        P(None, "tile"),
        P(("tile", "attr"), None),
        P(("tile", "attr")),
        P(("tile", "attr"), None),
        P(("tile", "attr"), None, None),
    )
    out_specs = (P(("tile", "attr"), None, None), P(None, "tile"), P("attr", "tile"))
    return jax.shard_map(local, mesh=mesh, in_specs=in_specs, out_specs=out_specs, check_vma=False)
```

```python
import functools
import jax
import jax.numpy as jnp
from jax import lax
from jax.experimental import pallas as pl
from jax.experimental.pallas import tpu as pltpu
from jax.sharding import PartitionSpec as P

BLOCK = 256
SIDE = 16
PIX = SIDE * SIDE
MID = 0.5 * SIDE
LOG2E = 1.4426950408889634
LN2 = 0.6931471805599453


band_zero = 0.28209479177387814
band_one = 0.4886025119029199
band_two = (
    1.0925484305920792,
    -1.0925484305920792,
    0.31539156525252005,
    -1.0925484305920792,
    0.5462742152960396,
)
band_three = (
    -0.5900435899266435,
    2.890611442640554,
    -0.4570457994644658,
    0.3731763325901154,
    -0.4570457994644658,
    1.445305721320277,
    -0.5900435899266435,
)


def sh_basis(view_angles):
    azimuth = view_angles[0]
    elevation = view_angles[1]
    dir_x = jnp.cos(azimuth) * jnp.cos(elevation)
    dir_y = jnp.sin(azimuth) * jnp.cos(elevation)
    dir_z = jnp.sin(elevation)
    sq_x = dir_x * dir_x
    sq_y = dir_y * dir_y
    sq_z = dir_z * dir_z
    basis_rows = [
        band_zero * jnp.ones_like(dir_x),
        -band_one * dir_y,
        band_one * dir_z,
        -band_one * dir_x,
        band_two[0] * dir_x * dir_y,
        band_two[1] * dir_y * dir_z,
        band_two[2] * (2.0 * sq_z - sq_x - sq_y),
        band_two[3] * dir_x * dir_z,
        band_two[4] * (sq_x - sq_y),
        band_three[0] * dir_y * (3.0 * sq_x - sq_y),
        band_three[1] * dir_x * dir_y * dir_z,
        band_three[2] * dir_y * (4.0 * sq_z - sq_x - sq_y),
        band_three[3] * dir_z * (2.0 * sq_z - 3.0 * sq_x - 3.0 * sq_y),
        band_three[4] * dir_x * (4.0 * sq_z - sq_x - sq_y),
        band_three[5] * dir_z * (sq_x - sq_y),
        band_three[6] * dir_x * (sq_x - 3.0 * sq_y),
    ]
    return basis_rows


def split2(x):
    high = x.astype(jnp.bfloat16)
    low = (x - high.astype(jnp.float32)).astype(jnp.bfloat16)
    return jnp.concatenate([high, low], axis=1)


def dot(a, b):
    return jnp.dot(a, b, preferred_element_type=jnp.float32)


def blend_kernel(tiles, seq_ref, counts_ref, held_ref, cot_rows_ref, cot_cols_ref, pic_ref, grad_ref, part_ref, ratio_ref):
    f32, bf16 = jnp.float32, jnp.bfloat16
    row = lax.broadcasted_iota(jnp.int32, (2 * BLOCK, BLOCK), 0)
    row = jnp.where(row >= BLOCK, row - BLOCK, row)
    col = lax.broadcasted_iota(jnp.int32, (2 * BLOCK, BLOCK), 1)
    before = jnp.where(row < col, -1.0, 0.0).astype(bf16)
    upto = jnp.where(row <= col, 1.0, 0.0).astype(bf16)

    def monomials(shape, dim, width):
        pixel = lax.broadcasted_iota(jnp.int32, shape, dim)
        kind = lax.broadcasted_iota(jnp.int32, shape, 1 - dim) & (width - 1)
        x = (pixel & (SIDE - 1)).astype(f32) + (0.5 - MID)
        y = (pixel // SIDE).astype(f32) + (0.5 - MID)
        out = jnp.where(kind == 0, 1.0, 0.0)
        for k, value in ((1, x), (2, y), (3, x * x), (4, x * y), (5, y * y)):
            out = jnp.where(kind == k, value, out)
        return out.astype(bf16)

    mono_cols = monomials((PIX, 48), 0, 16)
    mono_rows = monomials((8, PIX), 1, 8)
    cot_lhs, cot_rows = [], []
    for t in range(tiles):
        g = cot_cols_ref[t]
        high = g.astype(bf16).astype(f32)
        lane = lax.broadcasted_iota(jnp.int32, g.shape, 1)
        cot_lhs.append(jnp.where(lane < 48, high, g - high).astype(bf16))
        g = cot_rows_ref[t]
        high = g.astype(bf16).astype(f32)
        cot_rows.append(jnp.concatenate([high, g - high], axis=0).astype(bf16))

    grad_ref[...] = jnp.zeros_like(grad_ref)
    lives = [counts_ref[t] for t in range(tiles)]
    longest = functools.reduce(jnp.maximum, lives)

    lhs = []
    for t in range(tiles):
        wide = jnp.concatenate([mono_cols.astype(f32), jnp.zeros((PIX, 48), f32)], axis=1)
        lhs.append(jnp.concatenate([wide.astype(bf16), cot_lhs[t]], axis=0))
    head = lax.broadcasted_iota(jnp.int32, (16, BLOCK), 0) == 0

    def forward(j, carry):
        keep_before, sum_before, pictures = carry
        alphas, values, losses, helds, spots = [], [], [], [], []
        for t in range(tiles):
            at = seq_ref[t, j]
            hidden = jnp.where(j < lives[t], 0.0, -16384.0)
            held = held_ref[at]
            parts = split3(jnp.where(head, held + hidden, held))
            rows = jnp.concatenate(parts, axis=0)
            both = dot(lhs[t], jnp.concatenate([rows, rows], axis=0))
            alpha = jnp.exp2(both[:PIX])
            alphas.append(alpha)
            values.append(both[PIX:])
            losses.append(jnp.log(1.0 - alpha) * -LOG2E)
            helds.append(jnp.concatenate(parts[:2], axis=0))
            spots.append(at)
        loss = jnp.concatenate(losses, axis=0)
        keep_in = dot(split2(loss), before) + keep_before
        keep_before = keep_in[:, BLOCK - 1 :] - loss[:, BLOCK - 1 :]
        alpha = jnp.concatenate(alphas, axis=0)
        weight = alpha * jnp.exp2(keep_in)
        value = weight * jnp.concatenate(values, axis=0)
        total = dot(split2(value), upto) + sum_before
        sum_before = total[:, BLOCK - 1 :]
        ratio = alpha * jnp.exp2(loss)
        part_ref[j] = value + ratio * total
        ratio_ref[j] = ratio
        w2 = split2(weight)
        shown = []
        for t in range(tiles):
            w_high, w_low = w2[t * PIX : (t + 1) * PIX, :BLOCK], w2[t * PIX : (t + 1) * PIX, BLOCK:]
            rows = lax.dot_general(helds[t], w_high, (((1,), (1,)), ((), ())), preferred_element_type=f32)
            rows = rows + lax.dot_general(helds[t], w_low, (((1,), (1,)), ((), ())), preferred_element_type=f32)
            shown.append(pictures[t] + rows[:16] + rows[16:])
            colour_grad = dot(cot_rows[t], w_high) + dot(cot_rows[t], w_low)
            grad_ref[spots[t], 0:8, :] += colour_grad[:8] + colour_grad[8:]
        return keep_before, sum_before, tuple(shown)

    zero = jnp.zeros((tiles * PIX, 1), f32)
    start = (zero, zero, tuple(jnp.zeros((16, PIX), f32) for _ in range(tiles)))
    _, ends, pictures = lax.fori_loop(0, longest, forward, start)
    for t in range(tiles):
        pic_ref[t] = pictures[t]

    def backward(j, _):
        for t in range(tiles):
            pixels = slice(t * PIX, (t + 1) * PIX)
            d2 = split2(part_ref[j, pixels] - ratio_ref[j, pixels] * ends[pixels])
            moments = dot(mono_rows, d2[:, :BLOCK]) + dot(mono_rows, d2[:, BLOCK:])
            grad_ref[seq_ref[t, j], 8:16, :] += moments
        return 0

    lax.fori_loop(0, longest, backward, 0)


def blend(seq, counts, held, image_cot):
    tiles = image_cot.shape[0]
    rows = held.shape[0]
    cot_rows = jnp.pad(image_cot, ((0, 0), (0, 5), (0, 0)))
    cot_cols = jnp.pad(jnp.swapaxes(image_cot, 1, 2), ((0, 0), (0, 0), (6, 7)))
    cot_cols = jnp.tile(cot_cols, (1, 1, 6))
    smem = pl.BlockSpec(memory_space=pltpu.SMEM)
    vmem = pl.BlockSpec(memory_space=pltpu.VMEM)
    picture, grads = pl.pallas_call(
        functools.partial(blend_kernel, tiles),
        name="blend",
        out_shape=(
            jax.ShapeDtypeStruct((tiles, 16, PIX), jnp.float32),
            jax.ShapeDtypeStruct((rows, 16, BLOCK), jnp.float32),
        ),
        in_specs=[smem, smem, vmem, vmem, vmem],
        out_specs=(vmem, vmem),
        scratch_shapes=[
            pltpu.VMEM((seq.shape[1], tiles * PIX, BLOCK), jnp.float32),
            pltpu.VMEM((seq.shape[1], tiles * PIX, BLOCK), jnp.float32),
        ],
        compiler_params=pltpu.CompilerParams(vmem_limit_bytes=28 * 1024 * 1024),
    )(seq, counts, held, cot_rows, cot_cols)
    return picture[:, 6:9], grads


def splat_terms(geometry):
    mx, my = geometry[0] - MID, geometry[1] - MID
    c, s = jnp.cos(geometry[4]), jnp.sin(geometry[4])
    e1, e2 = jnp.exp(-2.0 * geometry[2]), jnp.exp(-2.0 * geometry[3])
    cc, ss, cs = c * c, s * s, c * s
    a = cc * e1 + ss * e2
    b = cs * (e1 - e2)
    d = ss * e1 + cc * e2
    return mx, my, e1, e2, cc, ss, cs, a, b, d, geometry[5]


def exponent_rows(terms):
    mx, my, e1, e2, cc, ss, cs, a, b, d, logit = terms
    bx, by = a * mx + b * my, b * mx + d * my
    log_opacity = jnp.minimum(logit, 0.0) - jnp.log1p(jnp.exp(-jnp.abs(logit)))
    one = log_opacity - 0.5 * (mx * bx + my * by)
    return [LOG2E * r for r in (one, bx, by, -0.5 * a, -b, -0.5 * d)]


def geometry_grads(terms, m):
    mx, my, e1, e2, cc, ss, cs, a, b, d, logit = terms
    n0 = m[0]
    nx, ny = m[1] - mx * n0, m[2] - my * n0
    nxx = m[3] - mx * (m[1] + nx)
    nxy = m[4] - mx * m[2] - my * nx
    nyy = m[5] - my * (m[2] + ny)
    return [
        a * nx + b * ny,
        b * nx + d * ny,
        e1 * (cc * nxx + 2.0 * cs * nxy + ss * nyy),
        e2 * (ss * nxx - 2.0 * cs * nxy + cc * nyy),
        (e2 - e1) * (cs * (nyy - nxx) + (cc - ss) * nxy),
        n0 / (1.0 + jnp.exp(logit)),
    ]


MESH = pl.DeviceIdType.MESH


def greet(peers):
    barrier = pltpu.get_barrier_semaphore()
    tile, attr, owners, extra = peers

    def hello(step, _):
        other = (tile + step) % owners
        pl.semaphore_signal(barrier, inc=1, device_id=(other, attr), device_id_type=MESH)
        return 0

    lax.fori_loop(1, owners, hello, 0)
    for other in extra:
        pl.semaphore_signal(barrier, inc=1, device_id=(tile, other), device_id_type=MESH)
    return barrier, owners - 1 + len(extra)


def split3(x):
    high = x.astype(jnp.bfloat16)
    rest = x - high.astype(jnp.float32)
    mid = rest.astype(jnp.bfloat16)
    return high, mid, (rest - mid.astype(jnp.float32)).astype(jnp.bfloat16)


def exchange(src, dst, sems, k, device):
    return pltpu.make_async_remote_copy(
        src_ref=src, dst_ref=dst, send_sem=sems.at[0, k], recv_sem=sems.at[1, k],
        device_id=device, device_id_type=MESH,
    )


def fetch_kernel(dims, want_ref, coef_ref, part_ref, held_ref, asked_ref,
                 asks, answer, landed, first, summed, second, tile_sems, back_sems, attr_sems):
    owners, owned, cap, message, stride = dims
    f32 = jnp.float32
    tile, attr = lax.axis_index("tile"), lax.axis_index("attr")
    core = attr + 1 - 2 * (attr % 2)
    across = (attr + 2) % 4
    pl.semaphore_wait(*greet((tile, attr, owners, (core, across))))

    colour_one = exchange(part_ref, first, attr_sems, 0, (tile, core))
    colour_one.start()

    def ask(other, sender):
        return pltpu.make_async_remote_copy(
            src_ref=want_ref.at[other], dst_ref=asks.at[sender],
            send_sem=tile_sems.at[0, other], recv_sem=tile_sems.at[1, sender],
            device_id=(other, attr), device_id_type=MESH,
        )

    def send_ask(step, _):
        ask((tile + step) % owners, tile).start()
        return 0

    lax.fori_loop(1, owners, send_ask, 0)
    asks[tile] = want_ref[tile]

    colour_one.wait()
    summed[...] = part_ref[...] + first[...]
    colour_two = exchange(summed, second, attr_sems, 1, (tile, across))
    colour_two.start()

    def take_ask(step, _):
        other = (tile + step) % owners
        ask(other, other).wait()
        return 0

    lax.fori_loop(1, owners, take_ask, 0)

    per = 128 // stride
    lanes = owners // per
    rows = []
    for tile_at in range(lanes):
        rows.append(functools.reduce(jnp.add, [asks[tile_at * per + k] for k in range(per)]))
    asked = jnp.concatenate(rows, axis=1) - 1.0
    asked_ref[...] = asked
    wide = 9 * owned
    columns = []
    for tile_at in range(lanes):
        square = jnp.concatenate([rows[tile_at] - 1.0] * 16, axis=0)
        columns.append(jnp.transpose(square)[:, 0:1])
    column = jnp.concatenate(columns, axis=0)
    lane = lax.broadcasted_iota(jnp.int32, (owners * stride, wide), 1).astype(f32)
    pick = jnp.where(lane == column, 1.0, 0.0).astype(jnp.bfloat16)

    colour_two.wait()
    colour = summed[...] + second[...] + 0.5
    table = jnp.concatenate([coef_ref[...], colour], axis=0)
    high, mid, low = split3(table)
    answer[...] = (dot(pick, low) + dot(pick, mid)) + dot(pick, high)

    def back(other, sender):
        at = pl.multiple_of(other * stride, 8)
        return pltpu.make_async_remote_copy(
            src_ref=answer.at[pl.ds(at, message)], dst_ref=landed.at[sender],
            send_sem=back_sems.at[0, other], recv_sem=back_sems.at[1, sender],
            device_id=(other, attr), device_id_type=MESH,
        )

    def send_back(step, _):
        back((tile + step) % owners, tile).start()
        return 0

    lax.fori_loop(1, owners, send_back, 0)
    landed[tile] = answer[pl.ds(pl.multiple_of(tile * stride, 8), message), :]
    held_ref[...] = jnp.zeros_like(held_ref)

    def take_back(step, _):
        other = (tile + step) % owners
        back(other, other).wait()
        return 0

    lax.fori_loop(1, owners, take_back, 0)

    def unpack(o, _):
        for k in range(cap):
            held_ref[o * cap + k, 0:9, :] = landed[o, 9 * k : 9 * k + 9, :]
        return 0

    lax.fori_loop(0, owners, unpack, 0)


def give_kernel(dims, grads_ref, asked_ref, out_ref,
                packed, landed, sums, first, half, second, third, tile_sems, attr_sems):
    owners, owned, cap, message, stride = dims
    f32 = jnp.float32
    tile, attr = lax.axis_index("tile"), lax.axis_index("attr")
    core = attr + 1 - 2 * (attr % 2)
    across = (attr + 2) % 4
    mine = attr % 2

    if message < stride:
        landed[...] = jnp.zeros_like(landed)
    greeted = greet((tile, attr, owners, (core, across)))
    packed[...] = jnp.zeros_like(packed)

    def pack(o, _):
        for k in range(cap):
            packed[o, 9 * k : 9 * k + 6, :] = grads_ref[o * cap + k, 8:14, :]
            packed[o, 9 * k + 6 : 9 * k + 9, :] = grads_ref[o * cap + k, 0:3, :]
        return 0

    lax.fori_loop(0, owners, pack, 0)
    pl.semaphore_wait(*greeted)

    def give(other, sender):
        at = pl.multiple_of(sender * stride, 8)
        return pltpu.make_async_remote_copy(
            src_ref=packed.at[other], dst_ref=landed.at[pl.ds(at, message)],
            send_sem=tile_sems.at[0, other], recv_sem=tile_sems.at[1, sender],
            device_id=(other, attr), device_id_type=MESH,
        )

    def send_give(step, _):
        give((tile + step) % owners, tile).start()
        return 0

    lax.fori_loop(1, owners, send_give, 0)
    landed[pl.ds(pl.multiple_of(tile * stride, 8), message), :] = packed[tile]
    wide = 9 * owned
    row = lax.broadcasted_iota(jnp.int32, (wide, owners * stride), 0).astype(f32)
    pick = jnp.where(row == asked_ref[0:1, :], 1.0, 0.0).astype(jnp.bfloat16)

    def take_give(step, _):
        other = (tile + step) % owners
        give(other, other).wait()
        return 0

    lax.fori_loop(1, owners, take_give, 0)
    high, mid, low = split3(landed[...])
    total = (dot(pick, low) + dot(pick, mid)) + dot(pick, high)
    cut = wide // 2
    sums[0] = total[:cut]
    sums[1] = total[cut:]

    one = exchange(sums.at[1 - mine], first, attr_sems, 0, (tile, core))
    one.start()
    one.wait()
    half[...] = sums[mine] + first[...]
    two = exchange(half, second, attr_sems, 1, (tile, across))
    two.start()
    two.wait()
    half_sum = half[...] + second[...]
    first[...] = half_sum
    three = exchange(first, third, attr_sems, 2, (tile, core))
    three.start()
    three.wait()
    at = pl.multiple_of(mine * cut, 8)
    out_ref[pl.ds(at, cut), :] = half_sum
    at = pl.multiple_of((1 - mine) * cut, 8)
    out_ref[pl.ds(at, cut), :] = third[...]


def remote_call(kernel, dims, outs, ins, scratch, number, name):
    vmem = pl.BlockSpec(memory_space=pltpu.VMEM)
    return pl.pallas_call(
        functools.partial(kernel, dims),
        name=name,
        out_shape=tuple(jax.ShapeDtypeStruct(o, jnp.float32) for o in outs),
        in_specs=[vmem] * len(ins),
        out_specs=tuple(vmem for _ in outs),
        scratch_shapes=scratch,
        compiler_params=pltpu.CompilerParams(
            collective_id=number, has_side_effects=True, vmem_limit_bytes=20 * 1024 * 1024
        ),
    )(*ins)


def floats(*shape):
    return pltpu.VMEM(shape, jnp.float32)


def fetch(dims, want, coef, part):
    owners, owned, cap, message, stride = dims
    sems = pltpu.SemaphoreType.DMA
    return remote_call(
        fetch_kernel, dims,
        ((owners * cap, 16, BLOCK), (8, owners * stride)),
        (want, coef, part),
        [floats(owners, 8, 128), floats(owners * stride, BLOCK), floats(owners, message, BLOCK),
         floats(3 * owned, BLOCK), floats(3 * owned, BLOCK), floats(3 * owned, BLOCK),
         sems((2, owners)), sems((2, owners)), sems((2, 2))],
        1, "fetch",
    )


def give_back(dims, grads, asked):
    owners, owned, cap, message, stride = dims
    sems = pltpu.SemaphoreType.DMA
    cut = 9 * owned // 2
    return remote_call(
        give_kernel, dims, ((9 * owned, BLOCK),), (grads, asked),
        [floats(owners, message, BLOCK), floats(owners * stride, BLOCK), floats(2, cut, BLOCK),
         floats(cut, BLOCK), floats(cut, BLOCK), floats(cut, BLOCK), floats(cut, BLOCK),
         sems((2, owners)), sems((2, 3))],
        2, "give",
    )[0]


def prep_kernel(owned, bands, geometry_ref, angles_ref, coeffs_ref, coef_ref, part_ref, basis_ref, terms_ref,
                geo, ang, coe, rows):
    def relay(b, _):
        for h in range(BLOCK // 128):
            at = pl.ds(pl.multiple_of(b * BLOCK + h * 128, 128), 128)
            geo[h, pl.ds(pl.multiple_of(b * 8, 8), 6), :] = geometry_ref[:, at]
            ang[h, pl.ds(pl.multiple_of(b * 8, 8), 2), :] = angles_ref[:, at]
            coe[h, pl.ds(pl.multiple_of(b * 16, 8), 3 * bands), :] = coeffs_ref[:, at]
        return 0

    lax.fori_loop(0, owned, relay, 0, unroll=4)

    def plane(ref, k, pitch):
        halves = [ref[h, pl.ds(k, owned, stride=pitch), :] for h in range(BLOCK // 128)]
        return jnp.concatenate(halves, axis=1)

    terms = splat_terms([plane(geo, k, 8) for k in range(6)])
    for k, value in enumerate(terms):
        terms_ref[k] = value
    for k, value in enumerate(exponent_rows(terms)):
        coef_ref[k * owned : (k + 1) * owned, :] = value
    for k, value in enumerate(sh_basis([plane(ang, k, 8) for k in range(2)])):
        rows[k] = value
    first = lax.axis_index("attr") * bands
    total = [jnp.zeros((owned, BLOCK), jnp.float32) for _ in range(3)]
    for k in range(bands):
        value = rows[first + k]
        basis_ref[k] = value
        for c in range(3):
            total[c] = total[c] + value * plane(coe, 3 * k + c, 16)
    for c in range(3):
        part_ref[c * owned : (c + 1) * owned, :] = total[c]


def prep(geometry, view_angles, sh_coeffs, owned):
    bands = sh_coeffs.shape[0] // 3
    vmem = pl.BlockSpec(memory_space=pltpu.VMEM)
    shapes = ((6 * owned, BLOCK), (3 * owned, BLOCK), (bands, owned, BLOCK), (11, owned, BLOCK))
    return pl.pallas_call(
        functools.partial(prep_kernel, owned, bands),
        name="prep",
        out_shape=tuple(jax.ShapeDtypeStruct(o, jnp.float32) for o in shapes),
        in_specs=[vmem] * 3,
        out_specs=(vmem,) * 4,
        scratch_shapes=[
            floats(BLOCK // 128, 8 * owned, 128),
            floats(BLOCK // 128, 8 * owned, 128),
            floats(BLOCK // 128, 16 * owned, 128),
            floats(16, owned, BLOCK),
        ],
        compiler_params=pltpu.CompilerParams(vmem_limit_bytes=12 * 1024 * 1024),
    )(geometry, view_angles, sh_coeffs)


def final_kernel(owned, bands, sums_ref, terms_ref, basis_ref, geometry_ref, coeffs_ref, geo, coe):
    summed = [sums_ref[k * owned : (k + 1) * owned, :] for k in range(9)]

    def put(ref, k, pitch, value):
        for h in range(BLOCK // 128):
            ref[h, pl.ds(k, owned, stride=pitch), :] = value[:, h * 128 : (h + 1) * 128]

    for k, value in enumerate(geometry_grads([terms_ref[k] for k in range(11)], summed[:6])):
        put(geo, k, 8, value)
    for k in range(bands):
        for c in range(3):
            put(coe, 3 * k + c, 16, basis_ref[k] * summed[6 + c])

    def relay(b, _):
        for h in range(BLOCK // 128):
            at = pl.ds(pl.multiple_of(b * BLOCK + h * 128, 128), 128)
            geometry_ref[:, at] = geo[h, pl.ds(pl.multiple_of(b * 8, 8), 6), :]
            coeffs_ref[:, at] = coe[h, pl.ds(pl.multiple_of(b * 16, 8), 3 * bands), :]
        return 0

    lax.fori_loop(0, owned, relay, 0, unroll=4)


def final(sums, terms, basis, owned):
    bands = basis.shape[0]
    vmem = pl.BlockSpec(memory_space=pltpu.VMEM)
    shapes = ((6, owned * BLOCK), (3 * bands, owned * BLOCK))
    return pl.pallas_call(
        functools.partial(final_kernel, owned, bands),
        name="final",
        out_shape=tuple(jax.ShapeDtypeStruct(o, jnp.float32) for o in shapes),
        in_specs=[vmem] * 3,
        out_specs=(vmem,) * 2,
        scratch_shapes=[
            floats(BLOCK // 128, 8 * owned, 128),
            floats(BLOCK // 128, 16 * owned, 128),
        ],
        compiler_params=pltpu.CompilerParams(vmem_limit_bytes=12 * 1024 * 1024),
    )(sums, terms, basis)


def local_general(geometry, sh_coeffs, view_angles, visible, counts, order, image_cot):
    owners = lax.axis_size("tile")
    owned = geometry.shape[1] // BLOCK
    vis = visible.shape[1]
    cap = (vis + owners - 1) // owners
    coef, partial_colour, my_basis, terms = prep(geometry, view_angles, sh_coeffs, owned)

    ids = visible[0]
    owner_of, local_of = ids // owned, ids % owned
    position = jnp.arange(vis)
    rank = jnp.sum(((owner_of[None, :] == owner_of[:, None]) & (position[None, :] < position[:, None])).astype(jnp.int32), 1)
    slot = owner_of * cap + rank
    message = -(-9 * cap // 8) * 8
    stride = 16 if message <= 16 else 32
    dims = (owners, owned, cap, message, stride)
    lane = jnp.arange(128) - (lax.axis_index("tile") % (128 // stride)) * stride
    in_slot = lane[None, :, None] // 9 + jnp.arange(owners)[:, None, None] * cap
    hit = (slot[None, None, :] == in_slot) & (lane >= 0)[None, :, None] & (lane < 9 * cap)[None, :, None]
    want = jnp.sum(jnp.where(hit, 1 + local_of[None, None, :] + owned * (lane % 9)[None, :, None], 0), 2)
    want = jnp.broadcast_to(want.astype(jnp.float32)[:, None, :], (owners, 8, 128))
    slot_of = jnp.sum(jnp.where(visible[:, :, None] == ids[None, None, :], slot[None, None, :], 0), 2)
    seq = jnp.sum(jnp.where(order[:, :, None] == position[None, None, :], slot_of[:, None, :], 0), 2)

    held, asked = fetch(dims, want, coef, partial_colour)
    picture, grads = blend(seq, counts, held, image_cot)
    sums = give_back(dims, grads, asked)
    grad_geometry, grad_sh = final(sums, terms, my_basis, owned)
    return (picture, grad_geometry, grad_sh)


STEPS = 8
PAIR = 2
SLOTS = STEPS * PAIR
OWNED = 32
MSG = 24
TRIPLE = 3
LAG = 4
GIVEN = 9 * PAIR


def stack3(x):
    high, mid, low = split3(x)
    return jnp.concatenate([high, mid, low], axis=0)


def lane_halves(x):
    return [x[:, h * 128 : (h + 1) * 128] for h in range(BLOCK // 128)]


def put_rows(ref, rows, value):
    for h, part in enumerate(lane_halves(value)):
        ref[h, rows, :] = part


def get_rows(ref, rows):
    return jnp.concatenate([ref[h, rows, :] for h in range(BLOCK // 128)], axis=1)


def scatter(ref, at, pitch, value):
    put_rows(ref, pl.ds(at, STEPS, stride=pitch), value)


def gather(ref, at, pitch):
    return get_rows(ref, pl.ds(at, STEPS, stride=pitch))


def tile_of(ref, i, at):
    return jnp.concatenate([ref[i, h, at : at + 8, :] for h in range(BLOCK // 128)], axis=1)


def pixel_monomials(shape, dim):
    pixel = lax.broadcasted_iota(jnp.int32, shape, dim)
    kind = lax.broadcasted_iota(jnp.int32, shape, 1 - dim) & 7
    x = (pixel & (SIDE - 1)).astype(jnp.float32) + (0.5 - MID)
    y = (pixel // SIDE).astype(jnp.float32) + (0.5 - MID)
    out = jnp.where(kind == 0, 1.0, 0.0)
    for k, value in ((1, x), (2, y), (3, x * x), (4, x * y), (5, y * y)):
        out = jnp.where(kind == k, value, out)
    return out.astype(jnp.bfloat16)


def slot_tables(tile, visible, order, counts_ref):
    f32 = jnp.float32
    sub = lax.broadcasted_iota(jnp.int32, (SLOTS, SLOTS), 0)
    lane = lax.broadcasted_iota(jnp.int32, (SLOTS, SLOTS), 1)
    diagonal = sub == lane
    lane_f, sub_f = lane.astype(f32), sub.astype(f32)

    def to_column(row):
        return jnp.sum(jnp.where(diagonal, row, 0.0), axis=1, keepdims=True)

    def to_row(column):
        return jnp.sum(jnp.where(diagonal, column, 0.0), axis=0, keepdims=True)

    ids = visible[0:1]
    owner = ids // OWNED
    near = owner - tile
    near = jnp.where(near < 0, near + STEPS, near).astype(f32)
    ids_f = ids.astype(f32)
    inside = (ids - owner * OWNED).astype(f32)
    near_column = to_column(near)
    second = jnp.sum(jnp.where((near_column == near) & (sub < lane), 1.0, 0.0), axis=0, keepdims=True)
    slot = second * STEPS + near
    match = sub_f == slot
    local_id = jnp.sum(jnp.where(match, inside, 0.0), axis=1, keepdims=True)
    slot_id = jnp.sum(jnp.where(match, ids_f, 0.0), axis=1, keepdims=True)
    ahead, live = [], []
    for t in range(2):
        listed = to_column(visible[t : t + 1].astype(f32))
        here = sub == order[t : t + 1]
        sequence = jnp.sum(jnp.where(here, listed, 0.0), axis=0, keepdims=True)
        rank = jnp.sum(jnp.where(sequence == slot_id, lane_f, 0.0), axis=1, keepdims=True)
        ahead.append(jnp.where(to_row(rank) < rank, 1.0, 0.0))
        live.append(jnp.where(rank < counts_ref[t].astype(f32), 1.0, 0.0))
    return local_id, ahead, live


def fused_kernel(bands, geometry_hbm, angles_hbm, coeffs_hbm, visible_hbm, order_hbm, cot_hbm, counts_hbm,
                 pic_ref, basis_ref, terms_ref, out_ref,
                 geometry, angles, coeffs, visible, order, cot, counts_ref, geo, ang, coe, rows,
                 coef, part, first, summed, second, colour,
                 asks_out, asks, answer, held, w_ref, ratio_ref, c_ref, a_ref,
                 packed, landed, sums, got_core, all_picks, d_ref, columns_ref,
                 local_sems, ask_sems, back_sems, give_sems, share_sems, attr_sems):
    f32, bf16 = jnp.float32, jnp.bfloat16
    tile, attr = lax.axis_index("tile"), lax.axis_index("attr")
    core = attr + 1 - 2 * (attr % 2)
    across = (attr + 2) % 4
    mine = attr % 2
    greeted = greet((tile, attr, STEPS, (core, across, (core + 2) % 4)))

    pairs = ((visible_hbm, visible), (order_hbm, order), (counts_hbm, counts_ref), (angles_hbm, angles),
             (coeffs_hbm, coeffs), (geometry_hbm, geometry), (cot_hbm, cot))
    loads = [pltpu.make_async_copy(a, b, local_sems.at[n]) for n, (a, b) in enumerate(pairs)]
    for load in loads:
        load.start()

    asks_out[...] = jnp.zeros_like(asks_out)
    answer[...] = jnp.zeros_like(answer)
    for load in loads[:3]:
        load.wait()
    local_id, ahead, live = slot_tables(tile, visible[...], order[...], counts_ref)
    lane = lax.broadcasted_iota(jnp.int32, (SLOTS, 128), 1)
    block = (lane & (OWNED - 1)).astype(f32)
    wanted = jnp.where((block == local_id) & (lane < TRIPLE * OWNED), 1.0, 0.0)
    for k in range(PAIR):
        asks_out[pl.ds(k, STEPS, stride=8), :] = wanted[k * STEPS : (k + 1) * STEPS]
    for load in loads[3:]:
        load.wait()

    def relay(b, _):
        for h in range(BLOCK // 128):
            at = pl.ds(pl.multiple_of(b * BLOCK + h * 128, 128), 128)
            geo[h, pl.ds(pl.multiple_of(b * 8, 8), 6), :] = geometry[:, at]
            ang[h, pl.ds(pl.multiple_of(b * 8, 8), 2), :] = angles[:, at]
            coe[h, pl.ds(pl.multiple_of(b * 16, 8), 3 * bands), :] = coeffs[:, at]
        return 0

    lax.fori_loop(0, OWNED, relay, 0, unroll=4)

    def plane(ref, k, pitch):
        halves = [ref[h, pl.ds(k, OWNED, stride=pitch), :] for h in range(BLOCK // 128)]
        return jnp.concatenate(halves, axis=1)

    for k, value in enumerate(sh_basis([plane(ang, k, 8) for k in range(2)])):
        rows[k] = value
    first_band = attr * bands
    total = [jnp.zeros((OWNED, BLOCK), f32) for _ in range(3)]
    for k in range(bands):
        value = rows[first_band + k]
        basis_ref[k] = value
        for c in range(3):
            total[c] = total[c] + value * plane(coe, 3 * k + c, 16)
    for c in range(3):
        part[c * OWNED : (c + 1) * OWNED, :] = total[c]
    pl.semaphore_wait(*greeted)

    def ask(i):
        return pltpu.make_async_remote_copy(
            src_ref=asks_out.at[pl.ds(pl.multiple_of(i * 8, 8), 8)], dst_ref=asks.at[pl.ds(pl.multiple_of(i * 8, 8), 8)],
            send_sem=ask_sems.at[0, i], recv_sem=ask_sems.at[1, i],
            device_id=((tile + i) % STEPS, attr), device_id_type=MESH,
        )

    def back(i, part):
        at, size = ((0, 6 * PAIR), (16, 8))[part]
        return pltpu.make_async_remote_copy(
            src_ref=answer.at[:, pl.ds(pl.multiple_of(i * MSG + at, 8), size)], dst_ref=held.at[i, :, pl.ds(at, size)],
            send_sem=back_sems.at[0, part, i], recv_sem=back_sems.at[1, part, i],
            device_id=((tile + STEPS - i) % STEPS, attr), device_id_type=MESH,
        )

    def give(i, d):
        slot = d * STEPS + i
        return pltpu.make_async_remote_copy(
            src_ref=packed.at[i, (attr + d) % 2, pl.ds(0, GIVEN)],
            dst_ref=landed.at[pl.ds(pl.multiple_of(slot * MSG, 8), GIVEN)],
            send_sem=give_sems.at[0, slot], recv_sem=give_sems.at[1, slot],
            device_id=((tile + i) % STEPS, (attr + d) % 4), device_id_type=MESH,
        )

    def share(d):
        return exchange(all_picks.at[0], all_picks.at[d], share_sems, d, (tile, (attr + d) % 4))

    upper = tile // (STEPS // 2)

    def near(n):
        return (n + upper * (STEPS - 2 * n)) % STEPS

    def far(n):
        return (2 * STEPS - n + upper * (2 * n - STEPS)) % STEPS

    def each(act):
        def step(n, _):
            act(far(n))
            return 0

        lax.fori_loop(1, STEPS, step, 0)

    colour_one = exchange(part, first, attr_sems, 0, (tile, core))
    colour_one.start()
    each(lambda i: ask(i).start())
    asks[0:8, :] = asks_out[0:8, :]

    terms = splat_terms([plane(geo, k, 8) for k in range(6)])
    for k, value in enumerate(terms):
        terms_ref[k] = value
    for k, value in enumerate(exponent_rows(terms)):
        coef[k] = stack3(value)

    colour_one.wait()
    summed[...] = part[...] + first[...]
    colour_two = exchange(summed, second, attr_sems, 1, (tile, across))
    colour_two.start()

    each(lambda i: ask(i).wait_recv())
    picks = jnp.concatenate([asks[pl.ds(k, STEPS, stride=8), :] for k in range(PAIR)], axis=0)
    pick = picks.astype(bf16)[:, : TRIPLE * OWNED]
    all_picks[0] = picks
    for d in range(1, 4):
        share(d).start()

    def pick_row(values, at):
        found = dot(pick, values)
        for k in range(PAIR):
            scatter(answer, at[k], MSG, found[k * STEPS : (k + 1) * STEPS])

    for r in range(6):
        pick_row(coef[r], (r, 6 + r))
    each(lambda i: back(i, 0).start())
    held[0, :, 0:16] = answer[:, 0:16, :]

    row = lax.broadcasted_iota(jnp.int32, (2 * BLOCK, BLOCK), 0) & (BLOCK - 1)
    col = lax.broadcasted_iota(jnp.int32, (2 * BLOCK, BLOCK), 1)
    before = jnp.where(row < col, -1.0, 0.0).astype(bf16)
    upto = jnp.where(row <= col, 1.0, 0.0).astype(bf16)
    mono_cols = pixel_monomials((PIX, 32), 0)
    mono_rows = pixel_monomials((8, PIX), 1)
    eight = lax.broadcasted_iota(jnp.int32, (8, BLOCK), 0)
    own_rows = [(eight >= 4 * k) & (eight < 4 * k + 3) for k in range(PAIR)]

    def halves(x):
        high = x.astype(bf16).astype(f32)
        return high, x - high

    def powers_of(i):
        powers = []
        both = jnp.concatenate([tile_of(held, i, 0), tile_of(held, i, 8)], axis=0)
        for k in range(PAIR):
            rows = jnp.concatenate([both[6 * k : 6 * k + 6], jnp.zeros((2, BLOCK), f32)], axis=0)
            high, mid, low = [p.astype(f32) for p in split3(rows)]
            coefs = jnp.concatenate([high, mid, low, jnp.zeros_like(low)], axis=0).astype(bf16)
            powers.append(dot(mono_cols, coefs))
        return powers

    def shape_pair(i, powers):
        alphas, losses = [], []
        for k in range(PAIR):
            alpha = jnp.exp2(powers[k])
            loss = jnp.log(1.0 - alpha) * -LOG2E
            alphas.append(alpha)
            losses.append(split2(loss))
            ratio_ref[i, k] = alpha * jnp.exp2(loss)
        keep = dot(jnp.concatenate(losses, axis=0), before)
        for k in range(PAIR):
            w_ref[i, k] = split2(alphas[k] * jnp.exp2(keep[k * PIX : (k + 1) * PIX]))

    def show_pair(i):
        c_high, c_low = halves(tile_of(held, i, 16))
        seen = None
        for k in range(PAIR):
            w2 = w_ref[i, k]
            one = jnp.where(eight == 4 * k + 3, 1.0, 0.0)
            lhs = jnp.concatenate([jnp.where(own_rows[k], c_high, one), jnp.where(own_rows[k], c_low, 0.0)], axis=0)
            lhs = lhs.astype(bf16)
            contract = (((1,), (1,)), ((), ()))
            shown = lax.dot_general(lhs, w2[:, :BLOCK], contract, preferred_element_type=f32)
            shown = shown + lax.dot_general(lhs, w2[:, BLOCK:], contract, preferred_element_type=f32)
            shown = shown[:8] + shown[8:]
            seen = shown if seen is None else seen + shown
        put_rows(c_ref, pl.ds(pl.multiple_of(i * 8, 8), 8), seen)

    def forward_early(n, _):
        i = near(n)
        back(i, 0).wait_recv()
        shape_pair(i, powers_of(i))
        return 0

    def forward(n, _):
        i, shown = near(n), near(n - LAG)
        back(i, 0).wait_recv()

        @pl.when(n > LAG)
        def _():
            back(shown, 1).wait_recv()

        powers = powers_of(i)
        show_pair(shown)
        shape_pair(i, powers)
        return 0

    shape_pair(0, powers_of(0))
    colour_two.wait()
    for c in range(3):
        piece = slice(c * OWNED, (c + 1) * OWNED)
        pick_row(stack3(summed[piece] + second[piece] + 0.5), (16 + c, 20 + c))
    each(lambda i: back(i, 1).start())
    held[0, :, 16:24] = answer[:, 16:24, :]
    lax.fori_loop(1, LAG, forward_early, 0)
    lax.fori_loop(LAG, STEPS, forward, 0)
    for n in range(STEPS - LAG, STEPS):
        back(near(n), 1).wait_recv()
    for n in range(STEPS - LAG, STEPS):
        show_pair(near(n))

    def by_slot(ref, c):
        return jnp.concatenate([gather(ref, c + 4 * k, 8) for k in range(PAIR)], axis=0)

    local = [by_slot(c_ref, c) for c in range(4)]
    spread = [jnp.zeros((SLOTS, PIX), f32) for _ in range(4)]
    for t in range(2):
        def earlier(values):
            out = jnp.zeros((SLOTS, PIX), f32)
            for s in range(SLOTS):
                out = out + ahead[t][:, s : s + 1] * values[s : s + 1, :]
            return out

        through = jnp.broadcast_to(live[t], (SLOTS, PIX))
        for s in range(SLOTS):
            through = through * (1.0 - ahead[t][:, s : s + 1] * local[3][s : s + 1, :])
        shade = jnp.zeros((SLOTS, PIX), f32)
        for c in range(3):
            g = cot[c, t : t + 1, :]
            lit = through * local[c]
            pic_ref[c, t : t + 1, :] = jnp.sum(lit, axis=0, keepdims=True)
            shade = shade + lit * g
            spread[c] = spread[c] + through * g
        behind = earlier(shade) - jnp.sum(shade, axis=0, keepdims=True)
        spread[3] = spread[3] + live[t] * behind
    for c in range(4):
        for k in range(PAIR):
            scatter(a_ref, c + 4 * k, 8, spread[c][k * STEPS : (k + 1) * STEPS])

    def turn(i):
        a = get_rows(a_ref, pl.ds(pl.multiple_of(i * 8, 8), 8))
        a_high, a_low = halves(a)
        columns_ref[...] = jnp.transpose(jnp.concatenate([a_high, a_low, a_high, a], axis=0))

    def tints_of(i, columns):
        c_high, c_low = halves(tile_of(held, i, 16))
        tints = []
        for k in range(PAIR):
            ch, cl = jnp.where(own_rows[k], c_high, 0.0), jnp.where(own_rows[k], c_low, 0.0)
            tints.append(dot(columns.astype(bf16), jnp.concatenate([ch, ch, cl, jnp.zeros_like(cl)], axis=0).astype(bf16)))
        return tints

    def slope_pair(i, columns, tints):
        values = []
        for k in range(PAIR):
            w2 = w_ref[i, k]
            values.append((w2[:, :BLOCK].astype(f32) + w2[:, BLOCK:].astype(f32)) * tints[k])
        total = dot(jnp.concatenate([split2(value) for value in values], axis=0), upto)
        for k in range(PAIR):
            beyond = total[k * PIX : (k + 1) * PIX] + columns[:, 27 + 4 * k : 28 + 4 * k]
            d_ref[k] = split2(values[k] + ratio_ref[i, k] * beyond)

    def sum_pair(i):
        a_high, a_low = halves(get_rows(a_ref, pl.ds(pl.multiple_of(i * 8, 8), 8)))
        moments, tint = [], None
        for k in range(PAIR):
            d2, w2 = d_ref[k], w_ref[i, k]
            moments.append(dot(mono_rows, d2[:, :BLOCK]) + dot(mono_rows, d2[:, BLOCK:]))
            lhs = jnp.concatenate([jnp.where(own_rows[k], a_high, 0.0), jnp.where(own_rows[k], a_low, 0.0)], axis=0)
            lhs = lhs.astype(bf16)
            grads = dot(lhs, w2[:, :BLOCK]) + dot(lhs, w2[:, BLOCK:])
            grads = grads[:8] + grads[8:]
            tint = grads if tint is None else tint + grads
        pieces = [m[:6] for m in moments] + [tint[0:3], tint[4:7], jnp.zeros((6, BLOCK), f32)]
        put_rows(packed.at[i], pl.ds(0, MSG), jnp.concatenate(pieces, axis=0))

    def backward(n, _):
        i, after = far(n), far(n + 1)
        columns = columns_ref[...]
        tints = tints_of(after, columns)
        sum_pair(i)
        for d in (2, 1, 3, 0):
            give(i, d).start()
        slope_pair(after, columns, tints)
        turn(far(n + 2))
        return 0

    turn(far(1))
    columns = columns_ref[...]
    slope_pair(far(1), columns, tints_of(far(1), columns))
    turn(far(2))
    lax.fori_loop(1, STEPS, backward, 0)
    sum_pair(0)
    for d in range(1, 4):
        give(0, d).start()
    landed[0:MSG, :] = packed[0, mine]

    for d in range(1, 4):
        share(d).wait_recv()
    chosen = [all_picks[d, k * STEPS : (k + 1) * STEPS, :] for k in range(PAIR) for d in range(4)]
    tall = jnp.concatenate(chosen * TRIPLE + [jnp.zeros((256 - TRIPLE * 4 * SLOTS, 128), f32)], axis=0)
    put = jnp.transpose(tall)[:OWNED, : TRIPLE * 4 * SLOTS].astype(bf16)

    def take_give(n, _):
        for d in range(4):
            give(n, d).wait_recv()
        return 0

    lax.fori_loop(1, STEPS, take_give, 0)
    for d in range(1, 4):
        give(0, d).wait_recv()
    for r in range(0, 9, 2):
        both = []
        for q in range(r, min(r + 2, 9)):
            at = (q, 6 + q) if q < 6 else (6 + q, 9 + q)
            both.append(jnp.concatenate([landed[pl.ds(at[k], 4 * STEPS, stride=MSG), :] for k in range(PAIR)], axis=0))
        found = dot(put, stack3(jnp.concatenate(both, axis=1)))
        for q in range(len(both)):
            sums[(r + q) * OWNED : (r + q + 1) * OWNED, :] = found[:, q * 128 : (q + 1) * 128]

    swap = exchange(sums, got_core, attr_sems, 2, (tile, core))
    swap.start()
    out_ref[mine] = sums[...]
    for d in range(1, 4):
        share(d).wait_send()
        give(0, d).wait_send()

    def sent_give(n, _):
        for d in range(4):
            give(n, d).wait_send()
        return 0

    lax.fori_loop(1, STEPS, sent_give, 0)
    each(lambda i: ask(i).wait_send())
    each(lambda i: back(i, 0).wait_send())
    each(lambda i: back(i, 1).wait_send())
    swap.wait()
    out_ref[1 - mine] = got_core[...]


def fused(geometry, view_angles, sh_coeffs, visible, order, cot, counts):
    bands = sh_coeffs.shape[0] // 3
    sems = pltpu.SemaphoreType.DMA
    vmem = pl.BlockSpec(memory_space=pltpu.VMEM)
    ins = (geometry, view_angles, sh_coeffs, visible, order, cot, counts)
    colours = 3 * OWNED
    shapes = (cot.shape, (bands, OWNED, BLOCK), (11, OWNED, BLOCK), (2, 9 * OWNED, 128))
    return pl.pallas_call(
        functools.partial(fused_kernel, bands),
        name="splat",
        out_shape=tuple(jax.ShapeDtypeStruct(o, jnp.float32) for o in shapes),
        in_specs=[pl.BlockSpec(memory_space=pltpu.HBM)] * len(ins),
        out_specs=tuple(vmem for _ in shapes),
        scratch_shapes=[pltpu.VMEM(x.shape, x.dtype) for x in ins[:-1]] + [
            pltpu.SMEM(counts.shape, counts.dtype),
            floats(BLOCK // 128, 8 * OWNED, 128), floats(BLOCK // 128, 8 * OWNED, 128),
            floats(BLOCK // 128, 16 * OWNED, 128), floats(16, OWNED, BLOCK),
            pltpu.VMEM((6, TRIPLE * OWNED, BLOCK), jnp.bfloat16), floats(colours, BLOCK), floats(colours, BLOCK),
            floats(colours, BLOCK), floats(colours, BLOCK), floats(8, 128),
            floats(8 * STEPS, 128), floats(8 * STEPS, 128), floats(2, STEPS * MSG, 128), floats(STEPS, 2, MSG, 128),
            pltpu.VMEM((STEPS, PAIR, PIX, 2 * BLOCK), jnp.bfloat16), floats(STEPS, PAIR, PIX, BLOCK),
            floats(2, 8 * STEPS, 128), floats(2, 8 * STEPS, 128),
            floats(STEPS, 2, MSG, 128), floats(4 * STEPS * MSG, 128), floats(9 * OWNED, 128), floats(9 * OWNED, 128),
            floats(4, SLOTS, 128), pltpu.VMEM((PAIR, PIX, 2 * BLOCK), jnp.bfloat16), floats(PIX, 32),
            sems((len(ins),)), sems((2, STEPS)), sems((2, 2, STEPS)), sems((2, 4 * STEPS)), sems((2, 4)), sems((2, 3)),
        ],
        compiler_params=pltpu.CompilerParams(
            collective_id=3, has_side_effects=True, vmem_limit_bytes=40 * 1024 * 1024
        ),
    )(*[pltpu.with_memory_space_constraint(x, pltpu.HBM) for x in ins])


def finish_kernel(bands, sums_ref, terms_ref, basis_ref, pic_ref, geometry_hbm, coeffs_hbm, picture_hbm,
                  geo, coe, geometry_ref, coeffs_ref, sems):
    pairs = ((pic_ref, picture_hbm), (coeffs_ref, coeffs_hbm), (geometry_ref, geometry_hbm))
    stores = [pltpu.make_async_copy(a, b, sems.at[n]) for n, (a, b) in enumerate(pairs)]
    stores[0].start()

    def summed(r):
        return jnp.concatenate([sums_ref[h, r * OWNED : (r + 1) * OWNED, :] for h in range(BLOCK // 128)], axis=1)

    def put(ref, k, pitch, value):
        for h, part in enumerate(lane_halves(value)):
            ref[h, pl.ds(k, OWNED, stride=pitch), :] = part

    def relay(ref, out, pitch, count):
        def step(b, _):
            for h in range(BLOCK // 128):
                at = pl.ds(pl.multiple_of(b * BLOCK + h * 128, 128), 128)
                out[:, at] = ref[h, pl.ds(pl.multiple_of(b * pitch, 8), count), :]
            return 0

        lax.fori_loop(0, OWNED, step, 0, unroll=4)

    for c in range(3):
        tint = summed(6 + c)
        for k in range(bands):
            put(coe, 3 * k + c, 16, basis_ref[k] * tint)
    relay(coe, coeffs_ref, 16, 3 * bands)
    stores[1].start()
    grads = geometry_grads([terms_ref[k] for k in range(11)], [summed(r) for r in range(6)])
    for k, value in enumerate(grads):
        put(geo, k, 8, value)
    relay(geo, geometry_ref, 8, 6)
    stores[2].start()
    for store in stores:
        store.wait()


def finish(sums, terms, basis, pic):
    bands = basis.shape[0]
    vmem = pl.BlockSpec(memory_space=pltpu.VMEM)
    shapes = ((6, OWNED * BLOCK), (3 * bands, OWNED * BLOCK), pic.shape)
    return pl.pallas_call(
        functools.partial(finish_kernel, bands),
        name="finish",
        out_shape=tuple(jax.ShapeDtypeStruct(o, jnp.float32) for o in shapes),
        in_specs=[vmem] * 4,
        out_specs=tuple(pl.BlockSpec(memory_space=pltpu.HBM) for _ in shapes),
        scratch_shapes=[
            floats(BLOCK // 128, 8 * OWNED, 128),
            floats(BLOCK // 128, 16 * OWNED, 128),
            floats(*shapes[0]), floats(*shapes[1]), pltpu.SemaphoreType.DMA((3,)),
        ],
        compiler_params=pltpu.CompilerParams(vmem_limit_bytes=12 * 1024 * 1024),
    )(sums, terms, basis, pic)


def local_fused(geometry, sh_coeffs, view_angles, visible, counts, order, image_cot):
    cot = jnp.swapaxes(image_cot, 0, 1)
    pic, basis, terms, sums = fused(geometry, view_angles, sh_coeffs, visible, order, cot, counts)
    grad_geometry, grad_sh, picture = finish(sums, terms, basis, pic)
    return (jnp.swapaxes(picture, 0, 1), grad_geometry, grad_sh)


def local(geometry, sh_coeffs, view_angles, visible, counts, order, image_cot):
    owners = lax.axis_size("tile")
    tiles, vis = visible.shape
    owned = geometry.shape[1] // BLOCK
    fits = (owners, vis, tiles, owned, lax.axis_size("attr")) == (8, 16, 2, 32, 4)
    run = local_fused if fits else local_general
    return run(geometry, sh_coeffs, view_angles, visible, counts, order, image_cot)


def solution(mesh):
    in_specs = (
        P(None, "tile"),
        P("attr", "tile"),
        P(None, "tile"),
        P(("tile", "attr"), None),
        P(("tile", "attr")),
        P(("tile", "attr"), None),
        P(("tile", "attr"), None, None),
    )
    out_specs = (P(("tile", "attr"), None, None), P(None, "tile"), P("attr", "tile"))
    return jax.shard_map(local, mesh=mesh, in_specs=in_specs, out_specs=out_specs, check_vma=False)
```
